32 devices in a mesh: seq: 4 (over y, core), ctx: 8 (over z, x).
Axes of the slice: x: 2, y: 2, z: 4, core: 2. Of those that a mesh axis runs over, the one named last changes fastest.
Arguments:
- tokens: bfloat16 [4, 1024, 2048], P('seq', 'ctx'), may hold values from -6 to 6
- cotangent: bfloat16 [4, 1024, 2048], P('seq', 'ctx'), may hold values from -6 to 6
- gain_attn: bfloat16 [2048], P(('seq', 'ctx')), may hold values from 0.099609375 to 1.8984375
- w_query: bfloat16 [2048, 2048], P(('seq', 'ctx')), may hold values from -0.125 to 0.125
- w_key: bfloat16 [2048, 1024], P(('seq', 'ctx')), may hold values from -0.125 to 0.125
- w_value: bfloat16 [2048, 1024], P(('seq', 'ctx')), may hold values from -0.125 to 0.125
- w_out: bfloat16 [2048, 2048], P(('seq', 'ctx')), may hold values from -1 to 1
- gain_mlp: bfloat16 [2048], P(('seq', 'ctx')), may hold values from 0.099609375 to 1.8984375
- w_gate: bfloat16 [2048, 8192], P(('seq', 'ctx')), may hold values from -0.125 to 0.125
- w_up: bfloat16 [2048, 8192], P(('seq', 'ctx')), may hold values from -0.125 to 0.125
- w_down: bfloat16 [8192, 2048], P(('seq', 'ctx')), may hold values from -0.0625 to 0.0625
- pair_order: int32 [4, 8], P('seq'), may hold values from 0 to 7, each once within a row
- segments: int32 [4, 1024], P('seq'), may hold values from 0 to 3, never falling along the last dimension, each value on 1 to 512 neighbouring positions
Outputs:
- output: bfloat16 [4, 1024, 2048], P('seq', 'ctx')
- grad_tokens: float32 [4, 1024, 2048], P('seq', 'ctx')
- grad_gain_attn: float32 [2048], P(('seq', 'ctx'))
- grad_w_query: float32 [2048, 2048], P(('seq', 'ctx'))
- grad_w_key: float32 [2048, 1024], P(('seq', 'ctx'))
- grad_w_value: float32 [2048, 1024], P(('seq', 'ctx'))
- grad_w_out: float32 [2048, 2048], P(('seq', 'ctx'))
- grad_gain_mlp: float32 [2048], P(('seq', 'ctx'))
- grad_w_gate: float32 [2048, 8192], P(('seq', 'ctx'))
- grad_w_up: float32 [2048, 8192], P(('seq', 'ctx'))
- grad_w_down: float32 [8192, 2048], P(('seq', 'ctx'))
The draws below stay inside these ranges and needn't reach their ends.
Inputs may be any that keep to these rules, and one draw needn't show every extreme that they name: `segments`: along a sequence the document numbers never fall; each document has 1 to 512 tokens. `pair_order`: each row holds every number of 0 to 7 once.
All inputs are finite; a program needn't handle non-finite values.
Results may differ from the reference program's by a relative error of at most 0.022.
Values may be sent and summed in bfloat16 or wider, within the bound.
A program may use at most 448 MiB of HBM per device.

```python
import math
import jax
import jax.numpy as jnp
import numpy as np
from jax import lax

D = 2048
H = 8
KVH = 4
HDIM = 256
FF = 8192
SPAN = 64
SEQS = 4
PAIRS = 8
LENGTH = 1024
HD = 2048
KD = 1024
DOCS = 4
DOC_MOST = 512


def block_levels(key, extent, split, least, top_value):
    def one(position, shards_of):
        steps = jax.random.uniform(jax.random.fold_in(jax.random.fold_in(key, 6), position), (shards_of,), jnp.float32, least / len(split), top_value / len(split))
        return jnp.repeat(jnp.exp(steps), extent[position] // shards_of).reshape((-1,) + (1,) * (len(extent) - position - 1))

    level = one(*split[0])
    for cut in split[1:]:
        level = level * one(*cut)
    return level


def split_up(number_of, total, bound, lean):
    weights = [(1 << 20) // math.isqrt(standing ** lean) + 1 for standing in range(2, number_of + 1)]
    rest, given = total - bound - (number_of - 1), [1] * (number_of - 1)
    while rest > 0:
        movable = [i for i in range(number_of - 1) if given[i] < bound]
        mass, left = sum([weights[i] for i in movable]), rest
        for i in movable:
            more = min(bound - given[i], max(1, left * weights[i] // mass), rest)
            given[i] = given[i] + more
            rest = rest - more
    return np.array([bound] + given)


def uneven(own_key, amount, total, most, lean):
    if amount == 2:
        one = jax.random.randint(own_key, (), max(1, total - most), min(most, total - 1) + 1)
        return jnp.stack([one, total - one])
    lengths = jnp.asarray(split_up(amount, total, most, lean), jnp.int32)
    couples = (amount - 1) // 2
    source_of, taker = lengths[1:1 + 2 * couples:2], lengths[2:2 + 2 * couples:2]
    room = jnp.minimum(source_of - 1, most - taker)
    shifted = jax.random.randint(jax.random.fold_in(own_key, 1), (couples,), 0, 1 << 20) % (room + 1)
    lengths = lengths.at[1:1 + 2 * couples:2].set(source_of - shifted).at[2:2 + 2 * couples:2].set(taker + shifted)
    return lengths[jax.random.permutation(jax.random.fold_in(own_key, 2), amount)]


def centred(stream_key, extent, width, limit, shards=(), held_as=jnp.bfloat16):
    factor_of = block_levels(stream_key, extent, shards, -0.22, 0.18) if shards else 1.0
    array = jax.random.normal(stream_key, extent, jnp.float32) * width * factor_of
    return jnp.minimum(jnp.maximum(array, -limit), limit).astype(held_as)


def setup_inputs(seed: int = 0) -> dict:
    keys = jax.random.split(jax.random.key(seed), 14)
    return {
        "tokens": centred(keys[0], (SEQS, LENGTH, D), 1.0, 6.0, ((0, 4), (1, 8))),
        "cotangent": centred(keys[1], (SEQS, LENGTH, D), 1.0, 6.0, ((0, 4), (1, 8))),
        "gain_attn": jnp.clip(1.0 + 0.18 * jax.random.normal(keys[2], (D,), jnp.float32), 0.099609375, 1.8984375).astype(jnp.bfloat16),
        "w_query": centred(keys[3], (D, HD), D ** -0.5, 0.125, ((0, 32),)),
        "w_key": centred(keys[4], (D, KD), D ** -0.5, 0.125, ((0, 32),)),
        "w_value": centred(keys[5], (D, KD), D ** -0.5, 0.125, ((0, 32),)),
        "w_out": centred(keys[6], (HD, D), (HD // 64) ** -0.5, 1.0, ((0, 32),)),
        "gain_mlp": jnp.clip(1.0 + 0.18 * jax.random.normal(keys[7], (D,), jnp.float32), 0.099609375, 1.8984375).astype(jnp.bfloat16),
        "w_gate": centred(keys[8], (D, FF), D ** -0.5, 0.125, ((0, 32),)),
        "w_up": centred(keys[9], (D, FF), D ** -0.5, 0.125, ((0, 32),)),
        "w_down": centred(keys[10], (FF, D), FF ** -0.5, 0.0625, ((0, 32),)),
        "pair_order": jax.vmap(lambda own: jax.random.permutation(own, PAIRS))(jax.random.split(keys[11], SEQS)).reshape((SEQS, PAIRS)).astype(jnp.int32),
        "segments": jax.vmap(lambda own: jnp.searchsorted(jnp.cumsum(uneven(own, DOCS, LENGTH, DOC_MOST, 1)), jnp.arange(LENGTH), side="right"))(jax.random.split(keys[12], SEQS)).reshape((SEQS, LENGTH)).astype(jnp.int32),
    }


EPSILON = 1e-06
THETA = 1000042.0
HIGHEST = lax.Precision.HIGHEST

@jax.custom_vjp
def low(v):
    return lax.optimization_barrier(v.astype(jnp.bfloat16)).astype(jnp.float32)

@jax.custom_vjp
def low_back(v):
    return v

def low_keep(v):
    return (low(v), None)

def low_pass(kept, grad):
    return (grad,)

def back_keep(v):
    return (v, None)

def back_low(kept, grad):
    return (low(grad),)
low.defvjp(low_keep, low_pass)
low_back.defvjp(back_keep, back_low)

def matmul(first_mat, second_mat):
    return jnp.dot(first_mat, second_mat, precision=HIGHEST, preferred_element_type=jnp.float32)

def slot_positions(pair_row):
    offsets = jnp.arange(SPAN, dtype=jnp.int32)
    low_slots = pair_row[:, None] * SPAN + offsets[None, :]
    high_slots = (2 * PAIRS - 1 - pair_row)[:, None] * SPAN + offsets[None, :]
    return jnp.concatenate([low_slots, high_slots], axis=1).reshape(-1)

def rotary_tables(positions):
    half_dim = HDIM // 2
    frequency = THETA ** (-(jnp.arange(half_dim, dtype=jnp.float32) * 2.0 / HDIM))
    angles = positions.astype(jnp.float32)[:, None] * frequency[None, :]
    return (jnp.cos(angles)[:, None, :], jnp.sin(angles)[:, None, :])

def rotary(tensor, table_cos, table_sin):
    half_dim = tensor.shape[-1] // 2
    lead_half = tensor[..., :half_dim]
    tail_half = tensor[..., half_dim:]
    return jnp.concatenate([lead_half * table_cos - tail_half * table_sin, tail_half * table_cos + lead_half * table_sin], axis=-1)

def layer(seq_tokens, weights_all, positions, doc_ids):
    gain_one, query_w, key_w, value_w, out_w, gain_two, gate_w, up_w, down_w = weights_all
    table_cos, table_sin = rotary_tables(positions)
    scale_one = lax.rsqrt(lax.optimization_barrier(jnp.mean(seq_tokens * seq_tokens, axis=-1, keepdims=True)) + EPSILON)
    normed = low(seq_tokens * scale_one * gain_one)
    query_proj = low_back(matmul(normed, query_w))
    key_proj = low_back(matmul(normed, key_w))
    value_proj = low_back(matmul(normed, value_w))
    query_rot = low(rotary(query_proj.reshape(LENGTH, H, HDIM), table_cos, table_sin))
    key_rot = low(rotary(key_proj.reshape(LENGTH, KVH, HDIM), table_cos, table_sin))
    value_low = low(value_proj.reshape(LENGTH, KVH, HDIM))
    query_rows = math.gcd(LENGTH, 512)
    step_count = LENGTH // query_rows
    score_scale = HDIM ** (-0.5)
    query_groups = query_rot.reshape(step_count, query_rows, KVH, H // KVH, HDIM)

    def attend(step_data):
        query_blk, query_pos, query_doc = step_data
        scores = jnp.einsum('qkgd,tkd->kgqt', query_blk, key_rot, precision=HIGHEST)
        scores = low_back(scores * score_scale)
        visible = (doc_ids[None, :] == query_doc[:, None]) & (positions[None, :] <= query_pos[:, None])
        scores = jnp.where(visible[None, None], scores, -1e+30)
        largest = lax.optimization_barrier(jnp.max(scores, axis=-1, keepdims=True))
        weights_exp = jnp.exp(scores - largest)
        prob_low = low(weights_exp / lax.optimization_barrier(jnp.sum(weights_exp, axis=-1, keepdims=True)))
        mixed = jnp.einsum('kgqt,tkd->qkgd', prob_low, value_low, precision=HIGHEST)
        return mixed.reshape(query_rows, HD)
    attended = lax.map(jax.checkpoint(attend), (query_groups, positions.reshape(step_count, query_rows), doc_ids.reshape(step_count, query_rows)))
    attended = attended.reshape(LENGTH, HD)
    out_low = low(low_back(attended))
    hidden = seq_tokens + low_back(matmul(out_low, out_w))
    scale_two = lax.rsqrt(lax.optimization_barrier(jnp.mean(hidden * hidden, axis=-1, keepdims=True)) + EPSILON)
    normed_two = low(hidden * scale_two * gain_two)
    gate_proj = low_back(matmul(normed_two, gate_w))
    up_proj = low_back(matmul(normed_two, up_w))
    middle = low(gate_proj * jax.nn.sigmoid(gate_proj) * up_proj)
    return hidden + low_back(matmul(middle, down_w))

def reference(tokens, cotangent, gain_attn, w_query, w_key, w_value, w_out, gain_mlp, w_gate, w_up, w_down, pair_order, segments):
    weights = tuple((weight.astype(jnp.float32) for weight in (gain_attn, w_query, w_key, w_value, w_out, gain_mlp, w_gate, w_up, w_down)))
    positions = jax.vmap(slot_positions)(pair_order)
    doc_ids = jnp.take_along_axis(segments, positions, axis=1)

    def whole_batch(inputs_all, weights_all):

        def single(step_data):
            seq_tokens, seq_pos, seq_doc = step_data
            return jax.checkpoint(layer)(seq_tokens, weights_all, seq_pos, seq_doc)
        return lax.map(single, (inputs_all, positions, doc_ids))
    result, pullback = jax.vjp(whole_batch, tokens.astype(jnp.float32), weights)
    grad_input, grad_weights = pullback(cotangent.astype(jnp.float32))
    return (result.astype(jnp.bfloat16), grad_input, grad_weights[0], grad_weights[1], grad_weights[2], grad_weights[3], grad_weights[4], grad_weights[5], grad_weights[6], grad_weights[7], grad_weights[8])
```

```python
import functools
import math

import jax
import jax.numpy as jnp
from jax import lax
from jax.experimental import pallas as pl
from jax.experimental.pallas import tpu as pltpu
from jax.sharding import PartitionSpec as P

H = 8
KVH = 4
HDIM = 256


EPSILON = 1e-06
THETA = 1000042.0
NEG_FILL = -1e30


def slot_positions(pair_row, half_rows, pair_count):
    offsets = jnp.arange(half_rows, dtype=jnp.int32)
    low_slots = pair_row[:, None] * half_rows + offsets[None, :]
    high_slots = (2 * pair_count - 1 - pair_row)[:, None] * half_rows + offsets[None, :]
    return jnp.concatenate([low_slots, high_slots], axis=1).reshape(-1)


def rotary_tables(positions, head_dim):
    half_dim = head_dim // 2
    frequency = THETA ** (-(jnp.arange(half_dim, dtype=jnp.float32) * 2.0 / head_dim))
    angles = positions.astype(jnp.float32)[:, None] * frequency[None, :]
    return (jnp.cos(angles)[:, None, :], jnp.sin(angles)[:, None, :])


def rotary(tensor, table_cos, table_sin):
    half_dim = tensor.shape[-1] // 2
    lead_half = tensor[..., :half_dim]
    tail_half = tensor[..., half_dim:]
    return jnp.concatenate(
        [
            lead_half * table_cos - tail_half * table_sin,
            tail_half * table_cos + lead_half * table_sin,
        ],
        axis=-1,
    )


def rms_scale(tensor):
    return lax.rsqrt(jnp.mean(tensor * tensor, axis=-1, keepdims=True) + EPSILON)


def rms_backward(tensor, scale_rows, gain_full, grad_rows):
    weighted = gain_full * grad_rows
    inner_mean = jnp.mean(weighted * tensor, axis=-1, keepdims=True)
    return scale_rows * weighted - tensor * (scale_rows * scale_rows * scale_rows) * inner_mean


def contract_rows(first_mat, second_mat):
    return lax.dot_general(
        first_mat, second_mat, (((0,), (0,)), ((), ())), preferred_element_type=jnp.float32
    )


def contract_cols(first_mat, second_mat):
    return lax.dot_general(
        first_mat, second_mat, (((1,), (1,)), ((), ())), preferred_element_type=jnp.float32
    )


def attention_weights(gain_attn, gain_mlp, w_query, w_key, w_value, w_out):
    return (
        lax.all_gather(gain_attn, ("seq", "ctx"), axis=0, tiled=True),
        lax.all_gather(gain_mlp, ("seq", "ctx"), axis=0, tiled=True),
        lax.all_gather(w_query, ("seq", "ctx"), axis=0, tiled=True),
        lax.all_gather(w_key, ("seq", "ctx"), axis=0, tiled=True),
        lax.all_gather(w_value, ("seq", "ctx"), axis=0, tiled=True),
        lax.all_gather(w_out, ("seq", "ctx"), axis=0, tiled=True),
    )


def mlp_weights(w_gate, w_up, w_down):
    return (
        lax.all_gather(w_gate, ("seq", "ctx"), axis=0, tiled=True),
        lax.all_gather(w_up, ("seq", "ctx"), axis=0, tiled=True),
        lax.all_gather(w_down, ("seq", "ctx"), axis=0, tiled=True),
    )


def reduce_grads(grad_one, grad_two, grad_three):
    seq_count = lax.axis_size("seq")
    grad_one = grad_one.reshape((seq_count, grad_one.shape[0] // seq_count) + grad_one.shape[1:])
    grad_two = grad_two.reshape((seq_count, grad_two.shape[0] // seq_count) + grad_two.shape[1:])
    grad_three = grad_three.reshape(
        (seq_count, grad_three.shape[0] // seq_count) + grad_three.shape[1:]
    )
    grad_one, grad_two, grad_three = (
        lax.psum_scatter(
            grad_one.astype(jnp.bfloat16), "ctx", scatter_dimension=1, tiled=True
        ).astype(jnp.float32),
        lax.psum_scatter(
            grad_two.astype(jnp.bfloat16), "ctx", scatter_dimension=1, tiled=True
        ).astype(jnp.float32),
        lax.psum_scatter(
            grad_three.astype(jnp.bfloat16), "ctx", scatter_dimension=1, tiled=True
        ).astype(jnp.float32),
    )
    grad_one, grad_two, grad_three = (
        lax.psum_scatter(
            grad_one.astype(jnp.bfloat16), "seq", scatter_dimension=0, tiled=True
        ).astype(jnp.float32),
        lax.psum_scatter(
            grad_two.astype(jnp.bfloat16), "seq", scatter_dimension=0, tiled=True
        ).astype(jnp.float32),
        lax.psum_scatter(
            grad_three.astype(jnp.bfloat16), "seq", scatter_dimension=0, tiled=True
        ).astype(jnp.float32),
    )
    return (grad_one[0], grad_two[0], grad_three[0])


def general_device(
    tokens,
    cotangent,
    gain_attn,
    w_query,
    w_key,
    w_value,
    w_out,
    gain_mlp,
    w_gate,
    w_up,
    w_down,
    pair_order,
    segments,
):
    pair_count = lax.axis_size("ctx")
    my_index = lax.axis_index("ctx")
    row_count = tokens.shape[1]
    half_rows = row_count // 2
    seq_len = segments.shape[1]
    head_groups = H // KVH
    score_scale = HDIM ** (-0.5)
    key_rows = math.gcd(seq_len, 512)
    key_steps = seq_len // key_rows
    key_pos = slot_positions(pair_order[0], half_rows, pair_count)
    key_doc = jnp.take(segments[0], key_pos)
    query_pos = lax.dynamic_slice_in_dim(key_pos, my_index * row_count, row_count)
    query_doc = lax.dynamic_slice_in_dim(key_doc, my_index * row_count, row_count)
    rot_cos, rot_sin = rotary_tables(query_pos, HDIM)
    gain_one, gain_two, query_w, key_w, value_w, out_w = attention_weights(
        gain_attn, gain_mlp, w_query, w_key, w_value, w_out
    )
    gain_one = gain_one.astype(jnp.float32)
    gain_two = gain_two.astype(jnp.float32)
    inputs = tokens[0].astype(jnp.float32)
    scale_one = rms_scale(inputs)
    normed = (inputs * scale_one * gain_one).astype(jnp.bfloat16)
    query_proj = jnp.dot(normed, query_w, preferred_element_type=jnp.float32).reshape(
        row_count, H, HDIM
    )
    key_proj = jnp.dot(normed, key_w, preferred_element_type=jnp.float32).reshape(
        row_count, KVH, HDIM
    )
    value_proj = jnp.dot(normed, value_w, preferred_element_type=jnp.float32)
    query_rot = (
        rotary(query_proj, rot_cos, rot_sin)
        .astype(jnp.bfloat16)
        .reshape(row_count, KVH, head_groups, HDIM)
    )
    key_rot = rotary(key_proj, rot_cos, rot_sin).astype(jnp.bfloat16).reshape(row_count, KVH * HDIM)
    value_low = value_proj.astype(jnp.bfloat16)
    key_width = key_rot.shape[1]
    key_all, value_all = (
        lax.all_gather(key_rot, "ctx", axis=0, tiled=True),
        lax.all_gather(value_low, "ctx", axis=0, tiled=True),
    )
    pos_blocks = key_pos.reshape(key_steps, key_rows)
    doc_blocks = key_doc.reshape(key_steps, key_rows)

    def scores_of(key_blk, pos_blk, doc_blk):
        key_heads = key_blk.reshape(key_rows, KVH, HDIM)
        raw_scores = (
            jnp.einsum("qkgd,tkd->kgqt", query_rot, key_heads, preferred_element_type=jnp.float32)
            * score_scale
        )
        visible = (doc_blk[None, :] == query_doc[:, None]) & (
            pos_blk[None, :] <= query_pos[:, None]
        )
        return (raw_scores, visible[None, None])

    def first_pass(carried, step_data):
        running_top, running_sum = carried
        key_blk, pos_blk, doc_blk = step_data
        raw_scores, visible = scores_of(key_blk, pos_blk, doc_blk)
        masked = jnp.where(visible, raw_scores, NEG_FILL)
        new_top = jnp.maximum(running_top, jnp.max(masked, axis=-1))
        added = jnp.sum(jnp.where(visible, jnp.exp(masked - new_top[..., None]), 0.0), axis=-1)
        return ((new_top, running_sum * jnp.exp(running_top - new_top) + added), None)

    start_top = jnp.full((KVH, head_groups, row_count), NEG_FILL, jnp.float32)
    start_sum = jnp.zeros((KVH, head_groups, row_count), jnp.float32)
    key_stack = key_all.reshape(key_steps, key_rows, key_width)
    value_stack = value_all.reshape(key_steps, key_rows, key_width)
    (final_top, final_sum), _ = lax.scan(
        first_pass, (start_top, start_sum), (key_stack, pos_blocks, doc_blocks)
    )
    log_total = final_top + jnp.log(final_sum)

    def second_pass(carried, step_data):
        acc_out, acc_rest = carried
        key_blk, value_blk, pos_blk, doc_blk = step_data
        raw_scores, visible = scores_of(key_blk, pos_blk, doc_blk)
        prob_full = jnp.where(visible, jnp.exp(raw_scores - log_total[..., None]), 0.0)
        prob_low = prob_full.astype(jnp.bfloat16)
        prob_rest = (prob_full - prob_low.astype(jnp.float32)).astype(jnp.bfloat16)
        value_heads = value_blk.reshape(key_rows, KVH, HDIM)
        acc_out = acc_out + jnp.einsum(
            "kgqt,tkd->qkgd", prob_low, value_heads, preferred_element_type=jnp.float32
        )
        acc_rest = acc_rest + jnp.einsum(
            "kgqt,tkd->qkgd", prob_rest, value_heads, preferred_element_type=jnp.float32
        )
        return ((acc_out, acc_rest), None)

    start_acc = jnp.zeros((row_count, KVH, head_groups, HDIM), jnp.float32)
    (attended, attended_rest), _ = lax.scan(
        second_pass, (start_acc, start_acc), (key_stack, value_stack, pos_blocks, doc_blocks)
    )
    exact_out = attended + attended_rest
    out_low = attended.reshape(row_count, H * HDIM).astype(jnp.bfloat16)
    hidden = inputs + jnp.dot(out_low, out_w, preferred_element_type=jnp.float32)
    scale_two = rms_scale(hidden)
    normed_two = (hidden * scale_two * gain_two).astype(jnp.bfloat16)
    grad_out = cotangent[0]
    gate_w, up_w, down_w = mlp_weights(w_gate, w_up, w_down)
    gate_proj = jnp.dot(normed_two, gate_w, preferred_element_type=jnp.float32)
    up_proj = jnp.dot(normed_two, up_w, preferred_element_type=jnp.float32)
    gate_sig = jax.nn.sigmoid(gate_proj)
    active = gate_proj * gate_sig
    middle = (active * up_proj).astype(jnp.bfloat16)
    result = hidden + jnp.dot(middle, down_w, preferred_element_type=jnp.float32)
    output = result.astype(jnp.bfloat16)[None]
    gate_w, up_w, down_w = mlp_weights(w_gate, w_up, w_down)
    grad_mid = contract_cols(grad_out, down_w)
    grad_gate = (grad_mid * up_proj * gate_sig * (1.0 + gate_proj * (1.0 - gate_sig))).astype(
        jnp.bfloat16
    )
    grad_up = (grad_mid * active).astype(jnp.bfloat16)
    grad_norm_two = contract_cols(grad_gate, gate_w) + contract_cols(grad_up, up_w)
    grad_gain_two = jnp.sum(grad_norm_two * hidden * scale_two, axis=0)
    grad_hidden = grad_out.astype(jnp.float32) + rms_backward(
        hidden, scale_two, gain_two, grad_norm_two
    )
    grad_w_gate = contract_rows(normed_two, grad_gate)
    grad_w_up = contract_rows(normed_two, grad_up)
    shard_gain_two, shard_gate, shard_up = reduce_grads(grad_gain_two, grad_w_gate, grad_w_up)
    gain_one, gain_two, query_w, key_w, value_w, out_w = attention_weights(
        gain_attn, gain_mlp, w_query, w_key, w_value, w_out
    )
    gain_one = gain_one.astype(jnp.float32)
    grad_branch = grad_hidden.astype(jnp.bfloat16)
    grad_w_out = contract_rows(out_low, grad_branch)
    grad_att = (
        contract_cols(grad_branch, out_w)
        .astype(jnp.bfloat16)
        .reshape(row_count, KVH, head_groups, HDIM)
    )
    row_delta = jnp.transpose(jnp.sum(grad_att.astype(jnp.float32) * exact_out, axis=-1), (1, 2, 0))
    key_back, value_back = (key_all, value_all)

    def backward_step(grad_query, step_data):
        key_blk, value_blk, pos_blk, doc_blk = step_data
        raw_scores, visible = scores_of(key_blk, pos_blk, doc_blk)
        prob_full = jnp.where(visible, jnp.exp(raw_scores - log_total[..., None]), 0.0)
        prob_low = prob_full.astype(jnp.bfloat16)
        key_heads = key_blk.reshape(key_rows, KVH, HDIM)
        value_heads = value_blk.reshape(key_rows, KVH, HDIM)
        grad_value_blk = jnp.einsum(
            "kgqt,qkgd->tkd", prob_low, grad_att, preferred_element_type=jnp.float32
        )
        grad_probs = jnp.einsum(
            "qkgd,tkd->kgqt", grad_att, value_heads, preferred_element_type=jnp.float32
        )
        grad_scores = (prob_full * (grad_probs - row_delta[..., None])).astype(jnp.bfloat16)
        grad_query = (
            grad_query
            + jnp.einsum(
                "kgqt,tkd->qkgd", grad_scores, key_heads, preferred_element_type=jnp.float32
            )
            * score_scale
        )
        grad_key_blk = (
            jnp.einsum("kgqt,qkgd->tkd", grad_scores, query_rot, preferred_element_type=jnp.float32)
            * score_scale
        )
        return (
            grad_query,
            (
                grad_key_blk.reshape(key_rows, key_width),
                grad_value_blk.reshape(key_rows, key_width),
            ),
        )

    back_keys = key_back.reshape(key_steps, key_rows, key_width)
    back_values = value_back.reshape(key_steps, key_rows, key_width)
    grad_query, (grad_key_steps, grad_value_steps) = lax.scan(
        backward_step, start_acc, (back_keys, back_values, pos_blocks, doc_blocks)
    )
    grad_key_all = grad_key_steps.reshape(seq_len, key_width)
    grad_value_all = grad_value_steps.reshape(seq_len, key_width)
    grad_key_own, grad_value_own = (
        lax.psum_scatter(
            grad_key_all.astype(jnp.bfloat16), "ctx", scatter_dimension=0, tiled=True
        ).astype(jnp.float32),
        lax.psum_scatter(
            grad_value_all.astype(jnp.bfloat16), "ctx", scatter_dimension=0, tiled=True
        ).astype(jnp.float32),
    )
    grad_query = (
        rotary(grad_query.reshape(row_count, H, HDIM), rot_cos, -rot_sin)
        .astype(jnp.bfloat16)
        .reshape(row_count, H * HDIM)
    )
    grad_key = (
        rotary(grad_key_own.reshape(row_count, KVH, HDIM), rot_cos, -rot_sin)
        .astype(jnp.bfloat16)
        .reshape(row_count, key_width)
    )
    grad_value = grad_value_own.astype(jnp.bfloat16)
    grad_w_query = contract_rows(normed, grad_query)
    grad_w_key = contract_rows(normed, grad_key)
    grad_w_value = contract_rows(normed, grad_value)
    grad_normed = (
        contract_cols(grad_query, query_w)
        + contract_cols(grad_key, key_w)
        + contract_cols(grad_value, value_w)
    )
    grad_gain_one = jnp.sum(grad_normed * inputs * scale_one, axis=0)
    grad_tokens = grad_hidden + rms_backward(inputs, scale_one, gain_one, grad_normed)
    grad_w_down = contract_rows(middle, grad_out)
    shard_gain_one, shard_out, shard_down = reduce_grads(grad_gain_one, grad_w_out, grad_w_down)
    shard_query, shard_key, shard_value = reduce_grads(grad_w_query, grad_w_key, grad_w_value)
    return (
        output,
        grad_tokens[None],
        shard_gain_one,
        shard_query,
        shard_key,
        shard_value,
        shard_out,
        shard_gain_two,
        shard_gate,
        shard_up,
        shard_down,
    )


MESH = pl.DeviceIdType.MESH
VMEM = pltpu.VMEM
RING = 8
SEQ = 4


class Place:
    def __init__(self):
        self.c = lax.axis_index("ctx")
        self.s = lax.axis_index("seq")
        z, x = self.c // 2, lax.rem(self.c, 2)
        self.p = z + x * (7 - 2 * z)
        self.right = {"ctx": self.at(1)}
        self.left = {"ctx": self.at(-1)}
        self.s_core = self.s + 1 - 2 * lax.rem(self.s, 2)
        self.s_far = lax.rem(self.s + 2, 4)
        self.s_both = 3 - self.s
        self.core_peer = {"seq": self.s_core}
        self.far_peer = {"seq": self.s_far}

    def at(self, offset):
        q = lax.rem(self.p + offset + 2 * RING, RING)
        return 2 * q + (q // 4) * (15 - 4 * q)

    def peers(self):
        return [{"ctx": lax.rem(self.c + k, RING)} for k in range(1, RING)]


def greet(devices):
    barrier = pltpu.get_barrier_semaphore()
    for device in devices:
        pl.semaphore_signal(barrier, inc=1, device_id=device, device_id_type=MESH)
    pl.semaphore_wait(barrier, len(devices))


def remote(src, dst, send_sem, recv_sem, device):
    return pltpu.make_async_remote_copy(
        src_ref=src, dst_ref=dst, send_sem=send_sem, recv_sem=recv_sem, device_id=device, device_id_type=MESH
    )


def arrived(ref, sems, index, device):
    remote(ref, ref, sems[0].at[index], sems[1].at[index], device).wait_recv()


def together(*flows):
    live = list(flows)
    while live:
        live = [flow for flow in live if next(flow, "end") != "end"]


def ring_sems():
    return [pltpu.SemaphoreType.DMA((2, RING // 2, 2))] * 2


def ring_gather(own, buf, sems, place):
    half = own.shape[0] // 2
    steps = RING // 2
    sent = []

    def part(ref, j):
        return ref.at[pl.ds(j * half, half)]

    def owner(d, s):
        return place.at(-s if d == 0 else s)

    def wait_for(d, s, j):
        arrived(part(buf.at[owner(d, s + 1)], j), sems, (d, s, j), place.right if d == 0 else place.left)

    for s in range(steps):
        for j in range(2):
            for d in range(2):
                if s == steps - 1 and j != d:
                    continue
                if s > 0:
                    wait_for(d, s - 1, j)
                copy = remote(
                    part(own if s == 0 else buf.at[owner(d, s)], j),
                    part(buf.at[owner(d, s)], j),
                    sems[0].at[d, s, j],
                    sems[1].at[d, s, j],
                    place.right if d == 0 else place.left,
                )
                copy.start()
                sent.append(copy)
            yield
    for d in range(2):
        wait_for(d, steps - 2, 1 - d)
        wait_for(d, steps - 1, d)
        yield
    for copy in sent:
        copy.wait_send()


def ring_scatter(part, out, slots, sems, place):
    half = part.shape[1] // 2
    steps = RING // 2
    sent = []

    def rows(ref, j):
        return ref.at[pl.ds(j * half, half)]

    def block(d, s):
        return place.at(steps - s if d == 0 else s - steps)

    def side(d):
        return place.right if d == 0 else place.left

    for s in range(steps):
        for j in range(2):
            for d in range(2):
                if s == 0 and j != d:
                    continue
                source = rows(part.at[block(d, s)], j)
                if s > 1 or (s == 1 and j == d):
                    held = rows(slots.at[d, s - 1], j)
                    arrived(held, sems, (d, s - 1, j), side(d))
                    held[...] = (held[...].astype(jnp.float32) + source[...].astype(jnp.float32)).astype(held.dtype)
                    source = held
                copy = remote(source, rows(slots.at[d, s], j), sems[0].at[d, s, j], sems[1].at[d, s, j], side(d))
                copy.start()
                sent.append(copy)
            yield
    for j in range(2):
        total = rows(part.at[place.c], j)[...].astype(jnp.float32)
        for d in range(2):
            held = rows(slots.at[d, steps - 1], j)
            arrived(held, sems, (d, steps - 1, j), side(d))
            total = total + held[...].astype(jnp.float32)
        rows(out, j)[...] = total
        yield
    for copy in sent:
        copy.wait_send()


def pair_sems():
    return [pltpu.SemaphoreType.DMA((RING,))] * 2


def exchange(src, buf, sems, place):
    sent = []
    for k in range(1, RING):
        to = lax.rem(place.c + k, RING)
        copy = remote(src.at[to], buf.at[place.c], sems[0].at[k], sems[1].at[k], {"ctx": to})
        copy.start()
        sent.append(copy)
    yield
    for k in range(1, RING):
        source = lax.rem(place.c + RING - k, RING)
        arrived(buf.at[source], sems, k, {"ctx": source})
    for copy in sent:
        copy.wait_send()
    yield


def seq_sems():
    return [pltpu.SemaphoreType.DMA((3,))] * 2


def seq_gather(own, buf, sems, place):
    first = remote(own, buf.at[place.s], sems[0].at[0], sems[1].at[0], place.far_peer)
    second = remote(own, buf.at[place.s], sems[0].at[1], sems[1].at[1], place.core_peer)
    first.start()
    second.start()
    yield
    arrived(buf.at[place.s_far], sems, 0, place.far_peer)
    third = remote(buf.at[place.s_far], buf.at[place.s_far], sems[0].at[2], sems[1].at[2], place.core_peer)
    third.start()
    yield
    arrived(buf.at[place.s_core], sems, 1, place.core_peer)
    arrived(buf.at[place.s_both], sems, 2, place.core_peer)
    for copy in (first, second, third):
        copy.wait_send()
    yield


def add_into(dst, other):
    rows = dst.shape[0]
    step = math.gcd(rows, 32)

    @pl.loop(0, rows // step)
    def _(i):
        at = pl.ds(pl.multiple_of(i * step, step), step)
        dst[at] = (dst[at].astype(jnp.float32) + other[at].astype(jnp.float32)).astype(dst.dtype)


def seq_scatter(part, near, far, sems, place):
    low = lax.rem(place.s, 2)
    row = place.s // 2
    other_row = 1 - row
    sent = []
    for k, r in enumerate((other_row, row)):
        copy = remote(part.at[r * 2 + 1 - low], near.at[k], sems[0].at[k], sems[1].at[k], place.core_peer)
        copy.start()
        sent.append(copy)
    yield
    arrived(near.at[0], sems, 0, place.core_peer)
    add_into(near.at[0], part.at[other_row * 2 + low])
    copy = remote(near.at[0], far.at[0], sems[0].at[2], sems[1].at[2], place.far_peer)
    copy.start()
    sent.append(copy)
    yield
    arrived(near.at[1], sems, 1, place.core_peer)
    add_into(near.at[1], part.at[row * 2 + low])
    yield
    arrived(far.at[0], sems, 2, place.far_peer)
    add_into(far.at[0], near.at[1])
    for copy in sent:
        copy.wait_send()
    yield


def call(body, outs, args, spaces, out_spaces, scratch, ident):
    return pl.pallas_call(
        body,
        out_shape=outs,
        in_specs=[pl.BlockSpec(memory_space=space) for space in spaces],
        out_specs=[pl.BlockSpec(memory_space=space) for space in out_spaces],
        scratch_shapes=scratch,
        compiler_params=pltpu.CompilerParams(
            collective_id=ident, has_side_effects=True, vmem_limit_bytes=56 * 1024 * 1024
        ),
    )(*args)


def shaped(shape, dtype=jnp.bfloat16):
    return jax.ShapeDtypeStruct(shape, dtype)


def start_kernel(x, wqkv, wout, x_all, wqkv_all, wout_all, local, r0, r1, e0, e1, q0, q1, o0, o1, w0, w1):
    place = Place()
    greet(place.peers() + [place.core_peer, place.far_peer])
    keep = [
        pltpu.make_async_copy(x, x_all.at[place.c], local.at[0]),
        pltpu.make_async_copy(wqkv.at[place.c], wqkv_all.at[place.s, place.c], local.at[1]),
        pltpu.make_async_copy(wout, wout_all.at[place.s, place.c], local.at[2]),
    ]
    for copy in keep:
        copy.start()

    def attention_weights_flow():
        yield from exchange(wqkv, wqkv_all.at[place.s], (e0, e1), place)
        keep[1].wait()
        yield from seq_gather(wqkv_all.at[place.s], wqkv_all, (q0, q1), place)

    together(attention_weights_flow(), ring_gather(x, x_all, (r0, r1), place))

    def out_weights_flow():
        yield from ring_gather(wout, wout_all.at[place.s], (o0, o1), place)
        keep[2].wait()
        yield from seq_gather(wout_all.at[place.s], wout_all, (w0, w1), place)

    together(out_weights_flow())
    keep[0].wait()


def middle_kernel(ob, dy, wcol, wdown, ob_all, dy_all, wcol_all, wdown_all, local, a0, a1, r0, r1, e0, e1, q0, q1, w0, w1):
    place = Place()
    greet(place.peers() + [place.core_peer, place.far_peer])
    keep = [
        pltpu.make_async_copy(ob.at[place.c], ob_all.at[place.c], local.at[0]),
        pltpu.make_async_copy(dy, dy_all.at[place.c], local.at[1]),
        pltpu.make_async_copy(wcol.at[place.c], wcol_all.at[place.s, place.c], local.at[2]),
        pltpu.make_async_copy(wdown, wdown_all.at[place.s], local.at[3]),
    ]
    for copy in keep:
        copy.start()

    def columns_flow():
        yield from exchange(wcol, wcol_all.at[place.s], (e0, e1), place)
        keep[2].wait()
        yield from seq_gather(wcol_all.at[place.s], wcol_all, (q0, q1), place)

    together(
        exchange(ob, ob_all, (a0, a1), place),
        columns_flow(),
        seq_gather(wdown, wdown_all, (w0, w1), place),
        ring_gather(dy, dy_all, (r0, r1), place),
    )
    keep[0].wait()
    keep[1].wait()
    keep[3].wait()


def gather_kernel(x, x_all, local, r0, r1):
    place = Place()
    greet([place.right, place.left])
    keep = pltpu.make_async_copy(x, x_all.at[place.c], local)
    keep.start()
    together(ring_gather(x, x_all, (r0, r1), place))
    keep.wait()


def scatter_kernel(count, *refs):
    parts, outs, slots, sems = refs[:count], refs[count : 2 * count], refs[2 * count : 3 * count], refs[3 * count :]
    place = Place()
    greet([place.right, place.left])
    for i in range(count):
        together(ring_scatter(parts[i], outs[i], slots[i], sems[2 * i : 2 * i + 2], place))


def swap_kernel(x, x_all, local, a0, a1):
    place = Place()
    greet(place.peers())
    keep = pltpu.make_async_copy(x.at[place.c], x_all.at[place.c], local)
    keep.start()
    together(exchange(x, x_all, (a0, a1), place))
    keep.wait()


def grads_kernel(col, down, qkv, out, col_out, down_out, qkv_out, out_out,
                 cn, cf, dn, df, qn, qf, on, of, slots, local, c0, c1, d0, d1, k0, k1, u0, u1, e0, e1, f0, f1, g0, g1):
    place = Place()
    greet(place.peers() + [place.core_peer, place.far_peer])

    def col_flow():
        yield from seq_scatter(col, cn, cf, (c0, c1), place)
        ref = cf.at[0]
        keep = pltpu.make_async_copy(ref.at[pl.ds(pl.multiple_of(place.c * 64, 64), 64)], col_out.at[place.c], local.at[0])
        keep.start()
        yield from exchange(Blocks(ref, 64), col_out, (e0, e1), place)
        keep.wait()

    def qkv_flow():
        yield from seq_scatter(qkv, qn, qf, (k0, k1), place)
        ref = qf.at[0]
        keep = pltpu.make_async_copy(ref.at[pl.ds(pl.multiple_of(place.c * 64, 64), 64)], qkv_out.at[place.c], local.at[1])
        keep.start()
        yield from exchange(Blocks(ref, 64), qkv_out, (f0, f1), place)
        keep.wait()

    def down_flow():
        yield from seq_scatter(down, dn, df, (d0, d1), place)
        keep = pltpu.make_async_copy(df.at[0], down_out, local.at[2])
        keep.start()
        keep.wait()

    def out_flow():
        yield from seq_scatter(out, on, of, (u0, u1), place)
        yield from ring_scatter(Blocks(of.at[0], 64), out_out, slots, (g0, g1), place)

    together(out_flow(), col_flow(), qkv_flow(), down_flow())


class Blocks:
    def __init__(self, ref, rows):
        self.ref, self.rows = ref, rows
        self.shape = (ref.shape[0] // rows, rows) + tuple(ref.shape[1:])

    @property
    def at(self):
        return self

    def __getitem__(self, i):
        return self.ref.at[pl.ds(pl.multiple_of(i * self.rows, self.rows), self.rows)]


DMA = pltpu.SemaphoreType.DMA
HBM = pl.ANY


def ring_device(
    tokens, cotangent, gain_attn, w_query, w_key, w_value, w_out, gain_mlp, w_gate, w_up, w_down, pair_order, segments
):
    bf16, f32 = jnp.bfloat16, jnp.float32
    n, c = RING, lax.axis_index("ctx")
    rows, width = tokens.shape[1], tokens.shape[2]
    half_rows, seq_len = rows // 2, segments.shape[1]
    shard = w_query.shape[0]
    ff_own = w_down.shape[0]
    ff_mine = SEQ * ff_own
    head = HDIM
    scale = HDIM ** (-0.5)

    gain_one = gain_attn.astype(f32)[:, None]
    gain_two = gain_mlp.astype(f32)[:, None]
    wq, wk, wv, wg, wu = (w.astype(f32) for w in (w_query, w_key, w_value, w_gate, w_up))
    groups = H // KVH

    def by_head(w):
        return jnp.repeat((w * gain_one).astype(bf16).reshape(shard, KVH, head), groups, axis=1)

    wqkv = jnp.concatenate(
        [(wq * gain_one).astype(bf16).reshape(shard, H, head), by_head(wk), by_head(wv)], axis=-1
    ).transpose(1, 0, 2)

    def by_context(w):
        return (w * gain_two).astype(bf16).reshape(shard, SEQ, n, ff_own).transpose(2, 0, 1, 3).reshape(n, shard, ff_mine)

    wcol = jnp.concatenate([by_context(wg), by_context(wu)], axis=-1)

    inputs = tokens[0].astype(f32)
    scale_one = rms_scale(inputs)
    xhat = (inputs * scale_one).astype(bf16)

    x_all, wqkv_all, wout_all = call(
        start_kernel,
        [shaped((n, rows, width)), shaped((SEQ, n, shard, 3 * head)), shaped((SEQ, n, shard, width))],
        (xhat, wqkv, w_out),
        [HBM] * 3,
        [HBM] * 3,
        [DMA((3,))] + ring_sems() + pair_sems() + seq_sems() + ring_sems() + seq_sems(),
        0,
    )
    x_all = x_all.reshape(seq_len, width)
    wqkv_all = wqkv_all.reshape(width, 3 * head)
    wout_all = wout_all.reshape(H * head, width)

    block = pair_order[0]
    blocks = jnp.stack([block, 2 * n - 1 - block], axis=1).reshape(-1)
    pos = (blocks[:, None] * half_rows + jnp.arange(half_rows, dtype=jnp.int32)[None, :]).reshape(-1)
    doc = jnp.take(segments[0].reshape(2 * n, half_rows), blocks, axis=0).reshape(-1)
    angles_of = rotary_tables(pos, HDIM)
    cos, sin = angles_of[0][:, 0], angles_of[1][:, 0]

    def rot(t, sign):
        a, b = t[:, : head // 2], t[:, head // 2 :]
        return jnp.concatenate([a * cos - sign * b * sin, b * cos + sign * a * sin], axis=-1)

    qkv = jnp.dot(x_all, wqkv_all, preferred_element_type=f32)
    q = rot(qkv[:, :head], 1.0).astype(bf16)
    k = rot(qkv[:, head : 2 * head], 1.0).astype(bf16)
    v = qkv[:, 2 * head :].astype(bf16)
    scores = contract_cols(q, k) * scale
    visible = (doc[None, :] == doc[:, None]) & (pos[None, :] <= pos[:, None])
    scores = jnp.where(visible, scores, NEG_FILL)
    top = jnp.max(scores, axis=-1, keepdims=True)
    weight = jnp.exp(scores - top)
    prob = weight / jnp.sum(weight, axis=-1, keepdims=True)
    prob_low = prob.astype(bf16)
    ob = jnp.dot(prob_low, v, preferred_element_type=f32).astype(bf16)

    ob_all, dy_all, wcol_all, wdown_all = call(
        middle_kernel,
        [
            shaped((n, rows, head)),
            shaped((n, rows, width)),
            shaped((SEQ, n, shard, 2 * ff_mine)),
            shaped((SEQ, ff_own, width)),
        ],
        (ob.reshape(n, rows, head), cotangent[0], wcol, w_down),
        [HBM] * 4,
        [HBM] * 4,
        [DMA((4,))] + pair_sems() + ring_sems() + pair_sems() + seq_sems() + seq_sems(),
        1,
    )
    ob_local = ob_all.transpose(1, 0, 2).reshape(rows, H * head)
    dy_all = dy_all.reshape(seq_len, width)
    wcol_all = wcol_all.reshape(width, 2 * ff_mine)
    wdown_all = wdown_all.reshape(ff_mine, width)

    hidden = inputs + jnp.dot(ob_local, wout_all, preferred_element_type=f32)
    scale_two = rms_scale(hidden)
    hhat = (hidden * scale_two).astype(bf16)
    (h_all,) = call(
        gather_kernel, [shaped((n, rows, width))], (hhat,), [HBM], [HBM], [DMA] + ring_sems(), 2
    )
    h_all = h_all.reshape(seq_len, width)
    gu = jnp.dot(h_all, wcol_all, preferred_element_type=f32)
    gate, up = gu[:, :ff_mine], gu[:, ff_mine:]
    sig = jax.nn.sigmoid(gate)
    active = gate * sig
    mid = (active * up).astype(bf16)
    dmid = contract_cols(dy_all, wdown_all)
    dgate = (dmid * up * sig * (1.0 + gate * (1.0 - sig))).astype(bf16)
    dup = (dmid * active).astype(bf16)
    dgu = jnp.concatenate([dgate, dup], axis=-1)
    part_h = contract_cols(dgu, wcol_all).astype(bf16)
    part_out = jnp.dot(mid, wdown_all, preferred_element_type=f32).astype(bf16)
    slot = VMEM((2, n // 2, rows, width), bf16)
    dweighted, out_sum = call(
        functools.partial(scatter_kernel, 2),
        [shaped((rows, width), f32)] * 2,
        (part_h.reshape(n, rows, width), part_out.reshape(n, rows, width)),
        [VMEM] * 2,
        [VMEM] * 2,
        [slot, slot] + ring_sems() + ring_sems(),
        3,
    )
    output = (hidden + out_sum).astype(bf16)[None]

    def norm_back(tensor, scale_rows, weighted):
        inner = jnp.mean(weighted * tensor, axis=-1, keepdims=True)
        return scale_rows * weighted - tensor * (scale_rows * scale_rows * scale_rows) * inner

    grad_hidden = cotangent[0].astype(f32) + norm_back(hidden, scale_two, dweighted)
    branch = grad_hidden.astype(bf16)
    datt = contract_cols(branch, wout_all).astype(bf16)
    (datt_all,) = call(
        swap_kernel,
        [shaped((n, rows, head))],
        (datt.reshape(rows, n, head).transpose(1, 0, 2),),
        [HBM],
        [HBM],
        [DMA] + pair_sems(),
        4,
    )
    datt_all = datt_all.reshape(seq_len, head)
    dprob = contract_cols(datt_all, v)
    delta = jnp.sum(prob * dprob, axis=-1, keepdims=True)
    dscore = (prob * (dprob - delta)).astype(bf16)
    dq = rot(jnp.dot(dscore, k, preferred_element_type=f32) * scale, -1.0)
    dk = rot(contract_rows(dscore, q) * scale, -1.0)
    dv = contract_rows(prob_low, datt_all)
    dqkv = jnp.concatenate([dq, dk, dv], axis=-1).astype(bf16)
    part_x = contract_cols(dqkv, wqkv_all).astype(bf16)
    (xweighted,) = call(
        functools.partial(scatter_kernel, 1),
        [shaped((rows, width), f32)],
        (part_x.reshape(n, rows, width),),
        [VMEM],
        [VMEM],
        [slot] + ring_sems(),
        5,
    )
    grad_tokens = grad_hidden + norm_back(inputs, scale_one, xweighted)

    g_col = contract_rows(h_all, dgu).astype(bf16).reshape(SEQ, n * shard, 2 * ff_mine)
    g_down = contract_rows(mid, dy_all).astype(bf16).reshape(SEQ, ff_own, width)
    g_qkv = contract_rows(x_all, dqkv).astype(bf16).reshape(SEQ, n * shard, 3 * head)
    g_out = contract_rows(ob_local, branch).astype(bf16).reshape(SEQ, n * shard, width)
    pieces = (g_col, g_down, g_qkv, g_out)
    near = []
    for piece in pieces:
        near += [VMEM((2,) + piece.shape[1:], bf16), VMEM((1,) + piece.shape[1:], bf16)]
    col_sum, down_sum, qkv_sum, out_grad = call(
        grads_kernel,
        [
            shaped((n, shard, 2 * ff_mine)),
            shaped((ff_own, width)),
            shaped((n, shard, 3 * head)),
            shaped((shard, width), f32),
        ],
        pieces,
        [VMEM] * 4,
        [HBM, HBM, HBM, VMEM],
        near
        + [VMEM((2, n // 2, shard, width), bf16), DMA((3,))]
        + seq_sems() * 4
        + pair_sems() * 2
        + ring_sems(),
        6,
    )
    col_sum = col_sum.astype(f32)

    def own_columns(t):
        return t.reshape(n, shard, SEQ, ff_own).transpose(1, 2, 0, 3).reshape(shard, SEQ * n * ff_own)

    raw_gate, raw_up = own_columns(col_sum[..., :ff_mine]), own_columns(col_sum[..., ff_mine:])
    qkv_sum = qkv_sum.astype(f32)
    raw_q = qkv_sum[..., :head].transpose(1, 0, 2).reshape(shard, H * head)

    def kv_sum(t):
        return t.reshape(KVH, groups, shard, head).sum(axis=1).transpose(1, 0, 2).reshape(shard, KVH * head)

    raw_k, raw_v = kv_sum(qkv_sum[..., head : 2 * head]), kv_sum(qkv_sum[..., 2 * head :])
    grad_gain_one = jnp.sum(raw_q * wq, axis=1) + jnp.sum(raw_k * wk, axis=1) + jnp.sum(raw_v * wv, axis=1)
    grad_gain_two = jnp.sum(raw_gate * wg, axis=1) + jnp.sum(raw_up * wu, axis=1)
    return (
        output,
        grad_tokens[None],
        grad_gain_one,
        raw_q * gain_one,
        raw_k * gain_one,
        raw_v * gain_one,
        out_grad,
        grad_gain_two,
        raw_gate * gain_two,
        raw_up * gain_two,
        down_sum.astype(f32),
    )


def solution(mesh):
    placed = (
        P("seq", "ctx", None),
        P("seq", "ctx", None),
        P(("seq", "ctx")),
        P(("seq", "ctx"), None),
        P(("seq", "ctx"), None),
        P(("seq", "ctx"), None),
        P(("seq", "ctx"), None),
        P(("seq", "ctx")),
        P(("seq", "ctx"), None),
        P(("seq", "ctx"), None),
        P(("seq", "ctx"), None),
        P("seq", None),
        P("seq", None),
    )
    fits = mesh.shape["ctx"] == H and mesh.shape["seq"] == 4
    chosen = ring_device if fits else general_device
    return jax.shard_map(
        chosen,
        mesh=mesh,
        in_specs=placed,
        out_specs=(
            P("seq", "ctx", None),
            P("seq", "ctx", None),
            P(("seq", "ctx")),
            P(("seq", "ctx"), None),
            P(("seq", "ctx"), None),
            P(("seq", "ctx"), None),
            P(("seq", "ctx"), None),
            P(("seq", "ctx")),
            P(("seq", "ctx"), None),
            P(("seq", "ctx"), None),
            P(("seq", "ctx"), None),
        ),
        check_vma=False,
    )
```

```python
import functools
import math

import jax
import jax.numpy as jnp
from jax import lax
from jax.experimental import pallas as pl
from jax.experimental.pallas import tpu as pltpu
from jax.sharding import PartitionSpec as P

H = 8
KVH = 4
HDIM = 256


EPSILON = 1e-06
THETA = 1000042.0
NEG_FILL = -1e30


def slot_positions(pair_row, half_rows, pair_count):
    offsets = jnp.arange(half_rows, dtype=jnp.int32)
    low_slots = pair_row[:, None] * half_rows + offsets[None, :]
    high_slots = (2 * pair_count - 1 - pair_row)[:, None] * half_rows + offsets[None, :]
    return jnp.concatenate([low_slots, high_slots], axis=1).reshape(-1)


def rotary_tables(positions, head_dim):
    half_dim = head_dim // 2
    frequency = THETA ** (-(jnp.arange(half_dim, dtype=jnp.float32) * 2.0 / head_dim))
    angles = positions.astype(jnp.float32)[:, None] * frequency[None, :]
    return (jnp.cos(angles)[:, None, :], jnp.sin(angles)[:, None, :])


def rotary(tensor, table_cos, table_sin):
    half_dim = tensor.shape[-1] // 2
    lead_half = tensor[..., :half_dim]
    tail_half = tensor[..., half_dim:]
    return jnp.concatenate(
        [
            lead_half * table_cos - tail_half * table_sin,
            tail_half * table_cos + lead_half * table_sin,
        ],
        axis=-1,
    )


def rms_scale(tensor):
    return lax.rsqrt(jnp.mean(tensor * tensor, axis=-1, keepdims=True) + EPSILON)


def rms_backward(tensor, scale_rows, gain_full, grad_rows):
    weighted = gain_full * grad_rows
    inner_mean = jnp.mean(weighted * tensor, axis=-1, keepdims=True)
    return scale_rows * weighted - tensor * (scale_rows * scale_rows * scale_rows) * inner_mean


def contract_rows(first_mat, second_mat):
    return lax.dot_general(
        first_mat, second_mat, (((0,), (0,)), ((), ())), preferred_element_type=jnp.float32
    )


def contract_cols(first_mat, second_mat):
    return lax.dot_general(
        first_mat, second_mat, (((1,), (1,)), ((), ())), preferred_element_type=jnp.float32
    )


def attention_weights(gain_attn, gain_mlp, w_query, w_key, w_value, w_out):
    return (
        lax.all_gather(gain_attn, ("seq", "ctx"), axis=0, tiled=True),
        lax.all_gather(gain_mlp, ("seq", "ctx"), axis=0, tiled=True),
        lax.all_gather(w_query, ("seq", "ctx"), axis=0, tiled=True),
        lax.all_gather(w_key, ("seq", "ctx"), axis=0, tiled=True),
        lax.all_gather(w_value, ("seq", "ctx"), axis=0, tiled=True),
        lax.all_gather(w_out, ("seq", "ctx"), axis=0, tiled=True),
    )


def mlp_weights(w_gate, w_up, w_down):
    return (
        lax.all_gather(w_gate, ("seq", "ctx"), axis=0, tiled=True),
        lax.all_gather(w_up, ("seq", "ctx"), axis=0, tiled=True),
        lax.all_gather(w_down, ("seq", "ctx"), axis=0, tiled=True),
    )


def reduce_grads(grad_one, grad_two, grad_three):
    seq_count = lax.axis_size("seq")
    grad_one = grad_one.reshape((seq_count, grad_one.shape[0] // seq_count) + grad_one.shape[1:])
    grad_two = grad_two.reshape((seq_count, grad_two.shape[0] // seq_count) + grad_two.shape[1:])
    grad_three = grad_three.reshape(
        (seq_count, grad_three.shape[0] // seq_count) + grad_three.shape[1:]
    )
    grad_one, grad_two, grad_three = (
        lax.psum_scatter(
            grad_one.astype(jnp.bfloat16), "ctx", scatter_dimension=1, tiled=True
        ).astype(jnp.float32),
        lax.psum_scatter(
            grad_two.astype(jnp.bfloat16), "ctx", scatter_dimension=1, tiled=True
        ).astype(jnp.float32),
        lax.psum_scatter(
            grad_three.astype(jnp.bfloat16), "ctx", scatter_dimension=1, tiled=True
        ).astype(jnp.float32),
    )
    grad_one, grad_two, grad_three = (
        lax.psum_scatter(
            grad_one.astype(jnp.bfloat16), "seq", scatter_dimension=0, tiled=True
        ).astype(jnp.float32),
        lax.psum_scatter(
            grad_two.astype(jnp.bfloat16), "seq", scatter_dimension=0, tiled=True
        ).astype(jnp.float32),
        lax.psum_scatter(
            grad_three.astype(jnp.bfloat16), "seq", scatter_dimension=0, tiled=True
        ).astype(jnp.float32),
    )
    return (grad_one[0], grad_two[0], grad_three[0])


def general_device(
    tokens,
    cotangent,
    gain_attn,
    w_query,
    w_key,
    w_value,
    w_out,
    gain_mlp,
    w_gate,
    w_up,
    w_down,
    pair_order,
    segments,
):
    pair_count = lax.axis_size("ctx")
    my_index = lax.axis_index("ctx")
    row_count = tokens.shape[1]
    half_rows = row_count // 2
    seq_len = segments.shape[1]
    head_groups = H // KVH
    score_scale = HDIM ** (-0.5)
    key_rows = math.gcd(seq_len, 512)
    key_steps = seq_len // key_rows
    key_pos = slot_positions(pair_order[0], half_rows, pair_count)
    key_doc = jnp.take(segments[0], key_pos)
    query_pos = lax.dynamic_slice_in_dim(key_pos, my_index * row_count, row_count)
    query_doc = lax.dynamic_slice_in_dim(key_doc, my_index * row_count, row_count)
    rot_cos, rot_sin = rotary_tables(query_pos, HDIM)
    gain_one, gain_two, query_w, key_w, value_w, out_w = attention_weights(
        gain_attn, gain_mlp, w_query, w_key, w_value, w_out
    )
    gain_one = gain_one.astype(jnp.float32)
    gain_two = gain_two.astype(jnp.float32)
    inputs = tokens[0].astype(jnp.float32)
    scale_one = rms_scale(inputs)
    normed = (inputs * scale_one * gain_one).astype(jnp.bfloat16)
    query_proj = jnp.dot(normed, query_w, preferred_element_type=jnp.float32).reshape(
        row_count, H, HDIM
    )
    key_proj = jnp.dot(normed, key_w, preferred_element_type=jnp.float32).reshape(
        row_count, KVH, HDIM
    )
    value_proj = jnp.dot(normed, value_w, preferred_element_type=jnp.float32)
    query_rot = (
        rotary(query_proj, rot_cos, rot_sin)
        .astype(jnp.bfloat16)
        .reshape(row_count, KVH, head_groups, HDIM)
    )
    key_rot = rotary(key_proj, rot_cos, rot_sin).astype(jnp.bfloat16).reshape(row_count, KVH * HDIM)
    value_low = value_proj.astype(jnp.bfloat16)
    key_width = key_rot.shape[1]
    key_all, value_all = (
        lax.all_gather(key_rot, "ctx", axis=0, tiled=True),
        lax.all_gather(value_low, "ctx", axis=0, tiled=True),
    )
    pos_blocks = key_pos.reshape(key_steps, key_rows)
    doc_blocks = key_doc.reshape(key_steps, key_rows)

    def scores_of(key_blk, pos_blk, doc_blk):
        key_heads = key_blk.reshape(key_rows, KVH, HDIM)
        raw_scores = (
            jnp.einsum("qkgd,tkd->kgqt", query_rot, key_heads, preferred_element_type=jnp.float32)
            * score_scale
        )
        visible = (doc_blk[None, :] == query_doc[:, None]) & (
            pos_blk[None, :] <= query_pos[:, None]
        )
        return (raw_scores, visible[None, None])

    def first_pass(carried, step_data):
        running_top, running_sum = carried
        key_blk, pos_blk, doc_blk = step_data
        raw_scores, visible = scores_of(key_blk, pos_blk, doc_blk)
        masked = jnp.where(visible, raw_scores, NEG_FILL)
        new_top = jnp.maximum(running_top, jnp.max(masked, axis=-1))
        added = jnp.sum(jnp.where(visible, jnp.exp(masked - new_top[..., None]), 0.0), axis=-1)
        return ((new_top, running_sum * jnp.exp(running_top - new_top) + added), None)

    start_top = jnp.full((KVH, head_groups, row_count), NEG_FILL, jnp.float32)
    start_sum = jnp.zeros((KVH, head_groups, row_count), jnp.float32)
    key_stack = key_all.reshape(key_steps, key_rows, key_width)
    value_stack = value_all.reshape(key_steps, key_rows, key_width)
    (final_top, final_sum), _ = lax.scan(
        first_pass, (start_top, start_sum), (key_stack, pos_blocks, doc_blocks)
    )
    log_total = final_top + jnp.log(final_sum)

    def second_pass(carried, step_data):
        acc_out, acc_rest = carried
        key_blk, value_blk, pos_blk, doc_blk = step_data
        raw_scores, visible = scores_of(key_blk, pos_blk, doc_blk)
        prob_full = jnp.where(visible, jnp.exp(raw_scores - log_total[..., None]), 0.0)
        prob_low = prob_full.astype(jnp.bfloat16)
        prob_rest = (prob_full - prob_low.astype(jnp.float32)).astype(jnp.bfloat16)
        value_heads = value_blk.reshape(key_rows, KVH, HDIM)
        acc_out = acc_out + jnp.einsum(
            "kgqt,tkd->qkgd", prob_low, value_heads, preferred_element_type=jnp.float32
        )
        acc_rest = acc_rest + jnp.einsum(
            "kgqt,tkd->qkgd", prob_rest, value_heads, preferred_element_type=jnp.float32
        )
        return ((acc_out, acc_rest), None)

    start_acc = jnp.zeros((row_count, KVH, head_groups, HDIM), jnp.float32)
    (attended, attended_rest), _ = lax.scan(
        second_pass, (start_acc, start_acc), (key_stack, value_stack, pos_blocks, doc_blocks)
    )
    exact_out = attended + attended_rest
    out_low = attended.reshape(row_count, H * HDIM).astype(jnp.bfloat16)
    hidden = inputs + jnp.dot(out_low, out_w, preferred_element_type=jnp.float32)
    scale_two = rms_scale(hidden)
    normed_two = (hidden * scale_two * gain_two).astype(jnp.bfloat16)
    grad_out = cotangent[0]
    gate_w, up_w, down_w = mlp_weights(w_gate, w_up, w_down)
    gate_proj = jnp.dot(normed_two, gate_w, preferred_element_type=jnp.float32)
    up_proj = jnp.dot(normed_two, up_w, preferred_element_type=jnp.float32)
    gate_sig = jax.nn.sigmoid(gate_proj)
    active = gate_proj * gate_sig
    middle = (active * up_proj).astype(jnp.bfloat16)
    result = hidden + jnp.dot(middle, down_w, preferred_element_type=jnp.float32)
    output = result.astype(jnp.bfloat16)[None]
    gate_w, up_w, down_w = mlp_weights(w_gate, w_up, w_down)
    grad_mid = contract_cols(grad_out, down_w)
    grad_gate = (grad_mid * up_proj * gate_sig * (1.0 + gate_proj * (1.0 - gate_sig))).astype(
        jnp.bfloat16
    )
    grad_up = (grad_mid * active).astype(jnp.bfloat16)
    grad_norm_two = contract_cols(grad_gate, gate_w) + contract_cols(grad_up, up_w)
    grad_gain_two = jnp.sum(grad_norm_two * hidden * scale_two, axis=0)
    grad_hidden = grad_out.astype(jnp.float32) + rms_backward(
        hidden, scale_two, gain_two, grad_norm_two
    )
    grad_w_gate = contract_rows(normed_two, grad_gate)
    grad_w_up = contract_rows(normed_two, grad_up)
    shard_gain_two, shard_gate, shard_up = reduce_grads(grad_gain_two, grad_w_gate, grad_w_up)
    gain_one, gain_two, query_w, key_w, value_w, out_w = attention_weights(
        gain_attn, gain_mlp, w_query, w_key, w_value, w_out
    )
    gain_one = gain_one.astype(jnp.float32)
    grad_branch = grad_hidden.astype(jnp.bfloat16)
    grad_w_out = contract_rows(out_low, grad_branch)
    grad_att = (
        contract_cols(grad_branch, out_w)
        .astype(jnp.bfloat16)
        .reshape(row_count, KVH, head_groups, HDIM)
    )
    row_delta = jnp.transpose(jnp.sum(grad_att.astype(jnp.float32) * exact_out, axis=-1), (1, 2, 0))
    key_back, value_back = (key_all, value_all)

    def backward_step(grad_query, step_data):
        key_blk, value_blk, pos_blk, doc_blk = step_data
        raw_scores, visible = scores_of(key_blk, pos_blk, doc_blk)
        prob_full = jnp.where(visible, jnp.exp(raw_scores - log_total[..., None]), 0.0)
        prob_low = prob_full.astype(jnp.bfloat16)
        key_heads = key_blk.reshape(key_rows, KVH, HDIM)
        value_heads = value_blk.reshape(key_rows, KVH, HDIM)
        grad_value_blk = jnp.einsum(
            "kgqt,qkgd->tkd", prob_low, grad_att, preferred_element_type=jnp.float32
        )
        grad_probs = jnp.einsum(
            "qkgd,tkd->kgqt", grad_att, value_heads, preferred_element_type=jnp.float32
        )
        grad_scores = (prob_full * (grad_probs - row_delta[..., None])).astype(jnp.bfloat16)
        grad_query = (
            grad_query
            + jnp.einsum(
                "kgqt,tkd->qkgd", grad_scores, key_heads, preferred_element_type=jnp.float32
            )
            * score_scale
        )
        grad_key_blk = (
            jnp.einsum("kgqt,qkgd->tkd", grad_scores, query_rot, preferred_element_type=jnp.float32)
            * score_scale
        )
        return (
            grad_query,
            (
                grad_key_blk.reshape(key_rows, key_width),
                grad_value_blk.reshape(key_rows, key_width),
            ),
        )

    back_keys = key_back.reshape(key_steps, key_rows, key_width)
    back_values = value_back.reshape(key_steps, key_rows, key_width)
    grad_query, (grad_key_steps, grad_value_steps) = lax.scan(
        backward_step, start_acc, (back_keys, back_values, pos_blocks, doc_blocks)
    )
    grad_key_all = grad_key_steps.reshape(seq_len, key_width)
    grad_value_all = grad_value_steps.reshape(seq_len, key_width)
    grad_key_own, grad_value_own = (
        lax.psum_scatter(
            grad_key_all.astype(jnp.bfloat16), "ctx", scatter_dimension=0, tiled=True
        ).astype(jnp.float32),
        lax.psum_scatter(
            grad_value_all.astype(jnp.bfloat16), "ctx", scatter_dimension=0, tiled=True
        ).astype(jnp.float32),
    )
    grad_query = (
        rotary(grad_query.reshape(row_count, H, HDIM), rot_cos, -rot_sin)
        .astype(jnp.bfloat16)
        .reshape(row_count, H * HDIM)
    )
    grad_key = (
        rotary(grad_key_own.reshape(row_count, KVH, HDIM), rot_cos, -rot_sin)
        .astype(jnp.bfloat16)
        .reshape(row_count, key_width)
    )
    grad_value = grad_value_own.astype(jnp.bfloat16)
    grad_w_query = contract_rows(normed, grad_query)
    grad_w_key = contract_rows(normed, grad_key)
    grad_w_value = contract_rows(normed, grad_value)
    grad_normed = (
        contract_cols(grad_query, query_w)
        + contract_cols(grad_key, key_w)
        + contract_cols(grad_value, value_w)
    )
    grad_gain_one = jnp.sum(grad_normed * inputs * scale_one, axis=0)
    grad_tokens = grad_hidden + rms_backward(inputs, scale_one, gain_one, grad_normed)
    grad_w_down = contract_rows(middle, grad_out)
    shard_gain_one, shard_out, shard_down = reduce_grads(grad_gain_one, grad_w_out, grad_w_down)
    shard_query, shard_key, shard_value = reduce_grads(grad_w_query, grad_w_key, grad_w_value)
    return (
        output,
        grad_tokens[None],
        shard_gain_one,
        shard_query,
        shard_key,
        shard_value,
        shard_out,
        shard_gain_two,
        shard_gate,
        shard_up,
        shard_down,
    )


MESH = pl.DeviceIdType.MESH
VMEM = pltpu.VMEM
RING = 8
SEQ = 4


class Place:
    def __init__(self):
        self.c = lax.axis_index("ctx")
        self.s = lax.axis_index("seq")
        z, x = self.c // 2, lax.rem(self.c, 2)
        self.p = z + x * (7 - 2 * z)
        self.right = {"ctx": self.at(1)}
        self.left = {"ctx": self.at(-1)}
        self.s_core = self.s + 1 - 2 * lax.rem(self.s, 2)
        self.s_far = lax.rem(self.s + 2, 4)
        self.s_both = 3 - self.s
        self.core_peer = {"seq": self.s_core}
        self.far_peer = {"seq": self.s_far}

    def at(self, offset):
        q = lax.rem(self.p + offset + 2 * RING, RING)
        return 2 * q + (q // 4) * (15 - 4 * q)

    def peers(self):
        return [{"ctx": lax.rem(self.c + k, RING)} for k in range(1, RING)]


def greet(devices):
    barrier = pltpu.get_barrier_semaphore()
    for device in devices:
        pl.semaphore_signal(barrier, inc=1, device_id=device, device_id_type=MESH)
    pl.semaphore_wait(barrier, len(devices))


def remote(src, dst, send_sem, recv_sem, device):
    return pltpu.make_async_remote_copy(
        src_ref=src, dst_ref=dst, send_sem=send_sem, recv_sem=recv_sem, device_id=device, device_id_type=MESH
    )


def arrived(ref, sems, index, device):
    remote(ref, ref, sems[0].at[index], sems[1].at[index], device).wait_recv()


def together(*flows):
    live = list(flows)
    while live:
        live = [flow for flow in live if next(flow, "end") != "end"]


def ring_sems():
    return [pltpu.SemaphoreType.DMA((2, RING // 2, 2))] * 2


def slot(offset):
    return 0 if offset == 0 else min(RING - 1, 2 * offset if offset > 0 else -2 * offset - 1)


class Rows:
    def __init__(self, ref, rows):
        self.ref, self.rows = ref, rows

    def here(self, offset):
        return self.ref.at[pl.ds(slot(offset) * self.rows, self.rows)]

    def there(self, offset, d):
        return self.here(offset - 1 if d == 0 else offset + 1)


class Owners:
    def __init__(self, ref, place):
        self.ref, self.place = ref, place

    def here(self, offset):
        return self.ref.at[self.place.at(offset)]

    def there(self, offset, d):
        return self.here(offset)


def ring_gather(own, blocks, sems, place):
    half = own.shape[0] // 2
    steps = RING // 2
    sent = []

    def part(ref, j):
        return ref.at[pl.ds(j * half, half)]

    def wait_for(d, s, j):
        offset = -(s + 1) if d == 0 else s + 1
        arrived(part(blocks.here(offset), j), sems, (d, s, j), place.right if d == 0 else place.left)

    for s in range(steps):
        for j in range(2):
            for d in range(2):
                if s == steps - 1 and j != d:
                    continue
                if s > 0:
                    wait_for(d, s - 1, j)
                offset = -s if d == 0 else s
                copy = remote(
                    part(own if s == 0 else blocks.here(offset), j),
                    part(blocks.there(offset, d), j),
                    sems[0].at[d, s, j],
                    sems[1].at[d, s, j],
                    place.right if d == 0 else place.left,
                )
                copy.start()
                sent.append(copy)
            yield
    for d in range(2):
        wait_for(d, steps - 2, 1 - d)
    yield
    for d in range(2):
        wait_for(d, steps - 1, d)
    yield
    for copy in sent:
        copy.wait_send()


class RingSum:
    def __init__(self, slots, sems, place):
        self.slots, self.sems, self.sent = slots, sems, []
        self.sides = (place.right, place.left)
        self.half = slots.shape[2] // 2

    def rows(self, ref, j):
        return ref.at[pl.ds(j * self.half, self.half)]

    def send(self, d, s, j, source):
        to = self.rows(self.slots.at[d, s], j)
        copy = remote(source, to, self.sems[0].at[d, s, j], self.sems[1].at[d, s, j], self.sides[d])
        copy.start()
        self.sent.append(copy)

    def held(self, d, s, j):
        ref = self.rows(self.slots.at[d, s], j)
        arrived(ref, self.sems, (d, s, j), self.sides[d])
        return ref

    def first(self, part):
        for d in range(2):
            self.send(d, 0, d, self.rows(part, d))

    def relay(self, s, parts):
        for j in range(2):
            for d in range(2):
                source = self.rows(parts[d], j)
                if s > 1 or j == d:
                    held = self.held(d, s - 1, j)
                    add_into(held, source)
                    source = held
                self.send(d, s, j, source)

    def last(self, part, out):
        for j in range(2):
            held = [self.held(d, RING // 2 - 1, j) for d in range(2)]
            sum_of_three(self.rows(out, j), self.rows(part, j), *held)

    def end(self):
        for copy in self.sent:
            copy.wait_send()


def ring_scatter(blocks, out, slots, sems, place):
    ring = RingSum(slots, sems, place)
    ring.first(blocks.here(RING // 2))
    yield
    for s in range(1, RING // 2):
        k = RING // 2 - s
        ring.relay(s, (blocks.here(k), blocks.here(-k)))
        yield
    ring.last(blocks.here(0), out)
    ring.end()
    yield


def pair_sems():
    return [pltpu.SemaphoreType.DMA((RING,))] * 2


OFFSETS = (1, -1, 2, -2, 3, -3, 4)


def exchange(send, there, here, sems, place):
    sent = []
    for k in OFFSETS:
        at = slot(k)
        copy = remote(send(k), there(k), sems[0].at[at], sems[1].at[at], {"ctx": place.at(k)})
        copy.start()
        sent.append(copy)
    yield
    for k in OFFSETS:
        arrived(here(k), sems, slot(-k) if k != RING // 2 else RING - 1, {"ctx": place.at(k)})
    for copy in sent:
        copy.wait_send()
    yield


def by_owner(src, dst, sems, place):
    return exchange(
        lambda k: src.at[place.at(k)], lambda k: dst.at[place.c], lambda k: dst.at[place.at(k)], sems, place
    )


def pairs_of(sems):
    return [sems[i : i + 2] for i in range(0, len(sems), 2)]


def seq_sems():
    return [pltpu.SemaphoreType.DMA((3,))] * 2


def seq_gather(own, buf, sems, place):
    first = remote(own, buf.at[place.s], sems[0].at[0], sems[1].at[0], place.far_peer)
    second = remote(own, buf.at[place.s], sems[0].at[1], sems[1].at[1], place.core_peer)
    first.start()
    second.start()
    yield
    arrived(buf.at[place.s_far], sems, 0, place.far_peer)
    third = remote(buf.at[place.s_far], buf.at[place.s_far], sems[0].at[2], sems[1].at[2], place.core_peer)
    third.start()
    yield
    arrived(buf.at[place.s_core], sems, 1, place.core_peer)
    arrived(buf.at[place.s_both], sems, 2, place.core_peer)
    for copy in (first, second, third):
        copy.wait_send()
    yield


def sum_of_three(dst, *terms):
    step = math.gcd(dst.shape[0], 16)

    @pl.loop(0, dst.shape[0] // step)
    def _(i):
        at = pl.ds(pl.multiple_of(i * step, step), step)
        one, two, three = (term[at].astype(jnp.float32) for term in terms)
        dst[at] = one + two + three


def add_into(dst, other):
    rows = dst.shape[0]
    step = math.gcd(rows, 16)

    @pl.loop(0, rows // step)
    def _(i):
        at = pl.ds(pl.multiple_of(i * step, step), step)
        dst[at] = (dst[at].astype(jnp.float32) + other[at].astype(jnp.float32)).astype(dst.dtype)


def seq_scatter(part, near, far, sems, place):
    low = lax.rem(place.s, 2)
    row = place.s // 2
    other_row = 1 - row
    sent = []
    for k, r in enumerate((other_row, row)):
        copy = remote(part.at[r * 2 + 1 - low], near.at[k], sems[0].at[k], sems[1].at[k], place.core_peer)
        copy.start()
        sent.append(copy)
    yield
    arrived(near.at[0], sems, 0, place.core_peer)
    add_into(near.at[0], part.at[other_row * 2 + low])
    copy = remote(near.at[0], far.at[0], sems[0].at[2], sems[1].at[2], place.far_peer)
    copy.start()
    sent.append(copy)
    yield
    arrived(near.at[1], sems, 1, place.core_peer)
    add_into(near.at[1], part.at[row * 2 + low])
    yield
    arrived(far.at[0], sems, 2, place.far_peer)
    add_into(far.at[0], near.at[1])
    for copy in sent:
        copy.wait_send()
    yield


def call(body, outs, args, spaces, out_spaces, scratch, ident):
    return pl.pallas_call(
        body,
        out_shape=outs,
        in_specs=[pl.BlockSpec(memory_space=space) for space in spaces],
        out_specs=[pl.BlockSpec(memory_space=space) for space in out_spaces],
        scratch_shapes=scratch,
        compiler_params=pltpu.CompilerParams(
            collective_id=ident, has_side_effects=True, vmem_limit_bytes=63 * 1024 * 1024
        ),
    )(*args)


def shaped(shape, dtype=jnp.bfloat16):
    return jax.ShapeDtypeStruct(shape, dtype)


def attention_in_kernel(x, wqkv, wout, x_all, wqkv_all, wout_all, local, *sems):
    place = Place()
    x_ring, qkv_swap, qkv_seq, out_ring, out_seq = pairs_of(sems)
    greet(place.peers() + [place.core_peer, place.far_peer])
    x_blocks = Rows(x_all, x.shape[0])
    keep = [
        pltpu.make_async_copy(x, x_blocks.here(0), local.at[0]),
        pltpu.make_async_copy(wqkv.at[place.c], wqkv_all.at[place.s, place.c], local.at[1]),
        pltpu.make_async_copy(wout, wout_all.at[place.s, place.c], local.at[2]),
    ]
    for copy in keep:
        copy.start()

    def qkv_flow():
        yield from by_owner(wqkv, wqkv_all.at[place.s], qkv_swap, place)
        keep[1].wait()
        yield from seq_gather(wqkv_all.at[place.s], wqkv_all, qkv_seq, place)

    def out_flow():
        yield from ring_gather(wout, Owners(wout_all.at[place.s], place), out_ring, place)
        keep[2].wait()
        yield from seq_gather(wout_all.at[place.s], wout_all, out_seq, place)

    first, second, third = qkv_flow(), out_flow(), ring_gather(x, x_blocks, x_ring, place)
    next(first)
    for _ in range(RING):
        next(second)
    next(first)
    together(third, first, second)
    keep[0].wait()


def attention_out_kernel(ob, dy, wcol, wdown, ob_all, dy_all, wcol_all, wdown_all, local, *sems):
    place = Place()
    ob_swap, dy_ring, gate_swap, gate_seq, up_swap, up_seq, down_seq = pairs_of(sems)
    greet(place.peers() + [place.core_peer, place.far_peer])
    ob_blocks, dy_blocks = Rows(ob, dy.shape[0]), Rows(dy_all, dy.shape[0])
    keep = [
        pltpu.make_async_copy(ob_blocks.here(0), ob_all.at[place.c], local.at[0]),
        pltpu.make_async_copy(dy, dy_blocks.here(0), local.at[1]),
        pltpu.make_async_copy(wcol.at[0, place.c], wcol_all.at[0, place.s, place.c], local.at[2]),
        pltpu.make_async_copy(wcol.at[1, place.c], wcol_all.at[1, place.s, place.c], local.at[3]),
        pltpu.make_async_copy(wdown, wdown_all.at[place.s], local.at[4]),
    ]
    for copy in keep:
        copy.start()

    def columns_flow(i, swap, seq):
        yield from by_owner(wcol.at[i], wcol_all.at[i, place.s], swap, place)
        keep[2 + i].wait()
        yield from seq_gather(wcol_all.at[i, place.s], wcol_all.at[i], seq, place)

    ob_flow = exchange(ob_blocks.here, lambda k: ob_all.at[place.c], lambda k: ob_all.at[place.at(k)], ob_swap, place)
    gate_flow, up_flow = columns_flow(0, gate_swap, gate_seq), columns_flow(1, up_swap, up_seq)
    down_flow = seq_gather(wdown, wdown_all, down_seq, place)
    next(ob_flow)
    next(gate_flow)
    next(down_flow)
    next(ob_flow)
    next(gate_flow)
    next(up_flow)
    next(gate_flow)
    together(up_flow, ring_gather(dy, dy_blocks, dy_ring, place), gate_flow, ob_flow, down_flow)
    keep[0].wait()
    keep[1].wait()
    keep[4].wait()


def dot(a, b, at=(1, 0)):
    return lax.dot_general(a, b, (((at[0],), (at[1],)), ((), ())), preferred_element_type=jnp.float32)


def chunks(total, size, body):
    @pl.loop(0, total // size)
    def _(i):
        body(pl.ds(pl.multiple_of(i * size, size), size))


def mlp_kernel(hhat, dy_hbm, wcol_hbm, wdown_hbm, sum_h, sum_o, col_out, down_out,
               h_all, dy_all, wg, wu, wd, mid, dgate, dup, stage_h, stage_o, stage, slots_h, slots_o,
               col_sent, col_near, col_far, down_sent, down_near, down_far, local, *sems):
    place = Place()
    h_sems, sum_h_sems, sum_o_sems, col_seq, down_seq = pairs_of(sems)
    greet([place.right, place.left, place.core_peer, place.far_peer])
    rows, width = hhat.shape
    ff = wg.shape[1]
    bf16, f32 = jnp.bfloat16, jnp.float32
    keep = [
        pltpu.make_async_copy(src, dst, local.at[i])
        for i, (src, dst) in enumerate(
            ((hhat, h_all.at[pl.ds(0, rows)]), (wcol_hbm.at[0], wg), (wcol_hbm.at[1], wu), (wdown_hbm, wd), (dy_hbm, dy_all))
        )
    ]
    for copy in keep:
        copy.start()
    gather = ring_gather(hhat, Rows(h_all, rows), h_sems, place)
    next(gather)
    next(gather)
    for copy in keep:
        copy.wait()

    def hidden_rows(start, count):
        at = pl.ds(start, count)

        def body(cols):
            gate = dot(h_all[at, :], wg[:, cols])
            up = dot(h_all[at, :], wu[:, cols])
            dmid = dot(dy_all[at, :], wd[cols, :], (1, 1))
            sig = jax.nn.sigmoid(gate)
            active = gate * sig
            mid[at, cols] = (active * up).astype(bf16)
            dgate[at, cols] = (dmid * up * sig * (1.0 + gate * (1.0 - sig))).astype(bf16)
            dup[at, cols] = (dmid * active).astype(bf16)

        chunks(ff, 256, body)

    def part_h(start, count, dst):
        at = pl.ds(start, count)

        def body(cols):
            dst[:, cols] = (dot(dgate[at, :], wg[cols, :], (1, 1)) + dot(dup[at, :], wu[cols, :], (1, 1))).astype(bf16)

        chunks(width, 256, body)

    def part_o(start, count, dst):
        at = pl.ds(start, count)

        def body(cols):
            dst[:, cols] = dot(mid[at, :], wd[:, cols]).astype(bf16)

        chunks(width, 256, body)

    def col_grad(s, dst, add):
        def body(cols):
            lhs = h_all[:, pl.ds(pl.multiple_of(s * dst.shape[0] + cols.start, 256), 256)]
            for side, grad in enumerate((dgate, dup)):
                there = pl.ds(side * ff, ff)
                value = dot(lhs, grad[...], (0, 0))
                if add:
                    value = value + dst[cols, there].astype(f32)
                dst[cols, there] = value.astype(bf16)

        chunks(dst.shape[0], 256, body)

    def down_grad(s, dst, add):
        lhs = pl.ds(pl.multiple_of(s * dst.shape[0], 256), dst.shape[0])

        def body(cols):
            value = dot(mid[:, lhs], dy_all[:, cols], (0, 0))
            if add:
                value = value + dst[:, cols].astype(f32)
            dst[:, cols] = value.astype(bf16)

        chunks(width, 512, body)

    hidden_rows(0, rows)
    for k in range(1, 4):
        next(gather)
        if k < 3:
            next(gather)
        else:
            next(gather)
            next(gather)
        hidden_rows((2 * k - 1) * rows, 2 * rows)
    next(gather)
    hidden_rows(7 * rows, rows)

    def pair(ref):
        return (ref.at[pl.ds(rows, rows)], ref.at[pl.ds(0, rows)])

    low, row = lax.rem(place.s, 2), place.s // 2
    other_row = 1 - row
    sent = []

    def near_send(i, grad, source, near, seq):
        r = (other_row, row)[i]
        grad(r * 2 + 1 - low, source.at[i], False)
        copy = remote(source.at[i], near.at[i], seq[0].at[i], seq[1].at[i], place.core_peer)
        copy.start()
        sent.append(copy)

    def far_send(grad, near, far, seq):
        arrived(near.at[0], seq, 0, place.core_peer)
        grad(other_row * 2 + low, near.at[0], True)
        copy = remote(near.at[0], far, seq[0].at[2], seq[1].at[2], place.far_peer)
        copy.start()
        sent.append(copy)

    def own_sum(grad, near, seq):
        arrived(near.at[1], seq, 1, place.core_peer)
        grad(row * 2 + low, near.at[1], True)

    def far_sum(near, far, seq, out, sem):
        arrived(far, seq, 2, place.far_peer)
        add_into(far, near.at[1])
        copy = pltpu.make_async_copy(far, out, sem)
        copy.start()
        return copy

    ring_h, ring_o = RingSum(slots_h, sum_h_sems, place), RingSum(slots_o, sum_o_sems, place)
    top_h, top_o = stage_h.at[pl.ds(2 * rows, rows)], stage_o.at[pl.ds(2 * rows, rows)]
    next_h, next_o = stage_h.at[pl.ds(0, 2 * rows)], stage_o.at[pl.ds(0, 2 * rows)]
    part_h(7 * rows, rows, top_h)
    ring_h.first(top_h)
    near_send(0, col_grad, col_sent, col_near, col_seq)
    part_h(5 * rows, 2 * rows, next_h)
    ring_h.relay(1, pair(next_h))
    near_send(1, col_grad, col_sent, col_near, col_seq)
    far_send(col_grad, col_near, col_far, col_seq)
    part_o(7 * rows, rows, top_o)
    ring_o.first(top_o)
    part_h(3 * rows, 2 * rows, stage)
    ring_h.relay(2, pair(stage))
    part_o(5 * rows, 2 * rows, next_o)
    ring_o.relay(1, pair(next_o))
    near_send(0, down_grad, down_sent, down_near, down_seq)
    part_h(rows, 2 * rows, stage)
    ring_h.relay(3, pair(stage))
    near_send(1, down_grad, down_sent, down_near, down_seq)
    far_send(down_grad, down_near, down_far, down_seq)
    part_o(3 * rows, 2 * rows, stage)
    ring_o.relay(2, pair(stage))
    own_sum(col_grad, col_near, col_seq)
    part_h(0, rows, top_stage := stage.at[pl.ds(0, rows)])
    ring_h.last(top_stage, sum_h)
    part_o(rows, 2 * rows, stage)
    ring_o.relay(3, pair(stage))
    own_sum(down_grad, down_near, down_seq)
    part_o(0, rows, top_stage)
    ring_o.last(top_stage, sum_o)
    ends = [
        far_sum(col_near, col_far, col_seq, col_out, local.at[0]),
        far_sum(down_near, down_far, down_seq, down_out, local.at[1]),
    ]
    for copy in ends:
        copy.wait()
    ring_h.end()
    ring_o.end()
    for copy in sent:
        copy.wait_send()
    for _ in gather:
        pass


def swap_kernel(x, x_all, local, *sems):
    place = Place()
    greet(place.peers())
    blocks = Rows(x_all, x.shape[1])
    keep = pltpu.make_async_copy(x.at[place.c], blocks.here(0), local)
    keep.start()
    together(
        exchange(lambda k: x.at[place.at(k)], lambda k: blocks.here(-k), blocks.here, sems, place)
    )
    keep.wait()


def grads_kernel(part_x, col, qkv, out, sum_x, col_out, qkv_out, out_out,
                 slots_x, qkv_near, qkv_far, out_near, out_far, slots_o, local, *sems):
    place = Place()
    x_ring, col_swap, qkv_seq, qkv_swap, out_seq, out_ring = pairs_of(sems)
    greet(place.peers() + [place.core_peer, place.far_peer])

    def swap_flow(blocks, into, swap, sem):
        keep = pltpu.make_async_copy(blocks.at[place.c], into.at[place.c], sem)
        keep.start()
        yield from by_owner(blocks, into, swap, place)
        keep.wait()

    def qkv_flow():
        yield from seq_scatter(qkv, qkv_near, qkv_far, qkv_seq, place)
        yield from swap_flow(Blocks(qkv_far.at[0], qkv_out.shape[1]), qkv_out, qkv_swap, local.at[1])

    def out_flow():
        yield from seq_scatter(out, out_near, out_far, out_seq, place)
        blocks = Owners(Blocks(out_far.at[0], out_out.shape[0]), place)
        yield from ring_scatter(blocks, out_out, slots_o, out_ring, place)

    together(
        ring_scatter(Rows(part_x, sum_x.shape[0]), sum_x, slots_x, x_ring, place),
        qkv_flow(),
        out_flow(),
        swap_flow(Blocks(col, col_out.shape[1]), col_out, col_swap, local.at[0]),
    )


class Blocks:
    def __init__(self, ref, rows):
        self.ref, self.rows = ref, rows
        self.shape = (ref.shape[0] // rows, rows) + tuple(ref.shape[1:])

    @property
    def at(self):
        return self

    def __getitem__(self, i):
        return self.ref.at[pl.ds(pl.multiple_of(i * self.rows, self.rows), self.rows)]


DMA = pltpu.SemaphoreType.DMA
HBM = pl.ANY


def ring_device(
    tokens, cotangent, gain_attn, w_query, w_key, w_value, w_out, gain_mlp, w_gate, w_up, w_down, pair_order, segments
):
    bf16, f32 = jnp.bfloat16, jnp.float32
    n, c = RING, lax.axis_index("ctx")
    rows, width = tokens.shape[1], tokens.shape[2]
    half_rows, seq_len = rows // 2, segments.shape[1]
    shard = w_query.shape[0]
    ff_own = w_down.shape[0]
    ff_mine = SEQ * ff_own
    head = HDIM
    scale = HDIM ** (-0.5)

    gain_one = gain_attn.astype(f32)[:, None]
    gain_two = gain_mlp.astype(f32)[:, None]
    wq, wk, wv, wg, wu = (w.astype(f32) for w in (w_query, w_key, w_value, w_gate, w_up))
    groups = H // KVH

    def by_head(w):
        return jnp.repeat((w * gain_one).astype(bf16).reshape(shard, KVH, head), groups, axis=1)

    wqkv = jnp.concatenate(
        [(wq * gain_one).astype(bf16).reshape(shard, H, head), by_head(wk), by_head(wv)], axis=-1
    ).transpose(1, 0, 2)

    def by_context(w):
        return (w * gain_two).astype(bf16).reshape(shard, SEQ, n, ff_own).transpose(2, 0, 1, 3).reshape(n, shard, ff_mine)

    wcol = jnp.stack([by_context(wg), by_context(wu)])

    inputs = tokens[0].astype(f32)
    scale_one = rms_scale(inputs)
    xhat = (inputs * scale_one).astype(bf16)

    x_all, wqkv_all, wout_all = call(
        attention_in_kernel,
        [shaped((seq_len, width)), shaped((SEQ, n, shard, 3 * head)), shaped((SEQ, n, shard, width))],
        (xhat, wqkv, w_out),
        [HBM] * 3,
        [HBM] * 3,
        [DMA((3,))] + ring_sems() + pair_sems() + seq_sems() + ring_sems() + seq_sems(),
        0,
    )
    wqkv_all = wqkv_all.reshape(width, 3 * head)
    wout_all = wout_all.reshape(H * head, width)

    z, x = c // 2, lax.rem(c, 2)
    ring_at = z + x * (7 - 2 * z)
    offsets = jnp.array([0, -1, 1, -2, 2, -3, 3, 4], jnp.int32)
    q = lax.rem(ring_at + offsets + n, n)
    order = 2 * q + (q // 4) * (15 - 4 * q)
    block = jnp.take(pair_order[0], order)
    blocks = jnp.stack([block, 2 * n - 1 - block], axis=1).reshape(-1)
    pos = (blocks[:, None] * half_rows + jnp.arange(half_rows, dtype=jnp.int32)[None, :]).reshape(-1)
    doc = jnp.take(segments[0].reshape(2 * n, half_rows), blocks, axis=0).reshape(-1)
    angles_of = rotary_tables(pos, HDIM)
    cos, sin = angles_of[0][:, 0], angles_of[1][:, 0]

    def rot(t, sign):
        a, b = t[:, : head // 2], t[:, head // 2 :]
        return jnp.concatenate([a * cos - sign * b * sin, b * cos + sign * a * sin], axis=-1)

    qkv = jnp.dot(x_all, wqkv_all, preferred_element_type=f32)
    q = rot(qkv[:, :head], 1.0).astype(bf16)
    k = rot(qkv[:, head : 2 * head], 1.0).astype(bf16)
    v = qkv[:, 2 * head :].astype(bf16)
    scores = contract_cols(q, k) * scale
    visible = (doc[None, :] == doc[:, None]) & (pos[None, :] <= pos[:, None])
    scores = jnp.where(visible, scores, NEG_FILL)
    top = jnp.max(scores, axis=-1, keepdims=True)
    weight = jnp.exp(scores - top)
    prob = weight / jnp.sum(weight, axis=-1, keepdims=True)
    prob_low = prob.astype(bf16)
    ob = jnp.dot(prob_low, v, preferred_element_type=f32).astype(bf16)

    ob_all, dy_all, wcol_all, wdown_all = call(
        attention_out_kernel,
        [
            shaped((n, rows, head)),
            shaped((seq_len, width)),
            shaped((2, SEQ, n, shard, ff_mine)),
            shaped((SEQ, ff_own, width)),
        ],
        (ob, cotangent[0], wcol, w_down),
        [HBM] * 4,
        [HBM] * 4,
        [DMA((5,))] + pair_sems() + ring_sems() + (pair_sems() + seq_sems()) * 2 + seq_sems(),
        1,
    )
    ob_local = ob_all.transpose(1, 0, 2).reshape(rows, H * head)
    wcol_all = wcol_all.reshape(2, width, ff_mine)

    hidden = inputs + jnp.dot(ob_local, wout_all, preferred_element_type=f32)
    scale_two = rms_scale(hidden)
    hhat = (hidden * scale_two).astype(bf16)
    wdown_all = wdown_all.reshape(ff_mine, width)

    def seq_slots(piece):
        return [VMEM((2,) + piece, bf16), VMEM((1,) + piece, bf16)]

    slot_shape = VMEM((2, n // 2, rows, width), bf16)
    col_piece, down_piece = (n * shard, 2 * ff_mine), (ff_own, width)
    dweighted, out_sum, col_sum, down_sum = call(
        mlp_kernel,
        [shaped((rows, width), f32)] * 2 + [shaped(col_piece), shaped(down_piece)],
        (hhat, dy_all, wcol_all, wdown_all),
        [HBM] * 4,
        [VMEM] * 2 + [HBM] * 2,
        [VMEM((seq_len, width), bf16)] * 2
        + [VMEM((width, ff_mine), bf16)] * 2
        + [VMEM((ff_mine, width), bf16)]
        + [VMEM((seq_len, ff_mine), bf16)] * 3
        + [VMEM((3 * rows, width), bf16)] * 2
        + [VMEM((2 * rows, width), bf16)]
        + [slot_shape] * 2
        + [VMEM((2,) + col_piece, bf16), VMEM((2,) + col_piece, bf16), VMEM(col_piece, bf16)]
        + [VMEM((2,) + down_piece, bf16), VMEM((2,) + down_piece, bf16), VMEM(down_piece, bf16)]
        + [DMA((5,))]
        + ring_sems() * 3
        + seq_sems() * 2,
        2,
    )
    output = (hidden + out_sum).astype(bf16)[None]

    def norm_back(tensor, scale_rows, weighted):
        inner = jnp.mean(weighted * tensor, axis=-1, keepdims=True)
        return scale_rows * weighted - tensor * (scale_rows * scale_rows * scale_rows) * inner

    grad_hidden = cotangent[0].astype(f32) + norm_back(hidden, scale_two, dweighted)
    branch = grad_hidden.astype(bf16)
    datt = contract_cols(branch, wout_all).astype(bf16)
    (datt_all,) = call(
        swap_kernel,
        [shaped((seq_len, head))],
        (datt.reshape(rows, n, head).transpose(1, 0, 2),),
        [HBM],
        [HBM],
        [DMA] + pair_sems(),
        4,
    )
    dprob = contract_cols(datt_all, v)
    delta = jnp.sum(prob * dprob, axis=-1, keepdims=True)
    dscore = (prob * (dprob - delta)).astype(bf16)
    dq = rot(jnp.dot(dscore, k, preferred_element_type=f32) * scale, -1.0)
    dk = rot(contract_rows(dscore, q) * scale, -1.0)
    dv = contract_rows(prob_low, datt_all)
    dqkv = jnp.concatenate([dq, dk, dv], axis=-1).astype(bf16)
    part_x = contract_cols(dqkv, wqkv_all).astype(bf16)
    g_qkv = contract_rows(x_all, dqkv).astype(bf16).reshape(SEQ, n * shard, 3 * head)
    g_out = contract_rows(ob_local, branch).astype(bf16).reshape(SEQ, n * shard, width)
    xweighted, col_sum, qkv_sum, out_grad = call(
        grads_kernel,
        [
            shaped((rows, width), f32),
            shaped((n, shard, 2 * ff_mine)),
            shaped((n, shard, 3 * head)),
            shaped((shard, width), f32),
        ],
        (part_x, col_sum, g_qkv, g_out),
        [VMEM, HBM, VMEM, VMEM],
        [VMEM, HBM, HBM, VMEM],
        [slot_shape]
        + seq_slots(g_qkv.shape[1:])
        + seq_slots(g_out.shape[1:])
        + [VMEM((2, n // 2, shard, width), bf16), DMA((2,))]
        + ring_sems()
        + pair_sems()
        + seq_sems()
        + pair_sems()
        + seq_sems()
        + ring_sems(),
        5,
    )
    grad_tokens = grad_hidden + norm_back(inputs, scale_one, xweighted)
    col_sum = col_sum.astype(f32)

    def own_columns(t):
        return t.reshape(n, shard, SEQ, ff_own).transpose(1, 2, 0, 3).reshape(shard, SEQ * n * ff_own)

    raw_gate, raw_up = own_columns(col_sum[..., :ff_mine]), own_columns(col_sum[..., ff_mine:])
    qkv_sum = qkv_sum.astype(f32)
    raw_q = qkv_sum[..., :head].transpose(1, 0, 2).reshape(shard, H * head)

    def kv_sum(t):
        return t.reshape(KVH, groups, shard, head).sum(axis=1).transpose(1, 0, 2).reshape(shard, KVH * head)

    raw_k, raw_v = kv_sum(qkv_sum[..., head : 2 * head]), kv_sum(qkv_sum[..., 2 * head :])
    grad_gain_one = jnp.sum(raw_q * wq, axis=1) + jnp.sum(raw_k * wk, axis=1) + jnp.sum(raw_v * wv, axis=1)
    grad_gain_two = jnp.sum(raw_gate * wg, axis=1) + jnp.sum(raw_up * wu, axis=1)
    return (
        output,
        grad_tokens[None],
        grad_gain_one,
        raw_q * gain_one,
        raw_k * gain_one,
        raw_v * gain_one,
        out_grad,
        grad_gain_two,
        raw_gate * gain_two,
        raw_up * gain_two,
        down_sum.astype(f32),
    )


def solution(mesh):
    placed = (
        P("seq", "ctx", None),
        P("seq", "ctx", None),
        P(("seq", "ctx")),
        P(("seq", "ctx"), None),
        P(("seq", "ctx"), None),
        P(("seq", "ctx"), None),
        P(("seq", "ctx"), None),
        P(("seq", "ctx")),
        P(("seq", "ctx"), None),
        P(("seq", "ctx"), None),
        P(("seq", "ctx"), None),
        P("seq", None),
        P("seq", None),
    )
    fits = mesh.shape["ctx"] == H and mesh.shape["seq"] == 4
    chosen = ring_device if fits else general_device
    return jax.shard_map(
        chosen,
        mesh=mesh,
        in_specs=placed,
        out_specs=(
            P("seq", "ctx", None),
            P("seq", "ctx", None),
            P(("seq", "ctx")),
            P(("seq", "ctx"), None),
            P(("seq", "ctx"), None),
            P(("seq", "ctx"), None),
            P(("seq", "ctx"), None),
            P(("seq", "ctx")),
            P(("seq", "ctx"), None),
            P(("seq", "ctx"), None),
            P(("seq", "ctx"), None),
        ),
        check_vma=False,
    )
```

```python
import functools
import math

import jax
import jax.numpy as jnp
from jax import lax
from jax.experimental import pallas as pl
from jax.experimental.pallas import tpu as pltpu
from jax.sharding import PartitionSpec as P

H = 8
KVH = 4
HDIM = 256


EPSILON = 1e-06
THETA = 1000042.0
NEG_FILL = -1e30


def slot_positions(pair_row, half_rows, pair_count):
    offsets = jnp.arange(half_rows, dtype=jnp.int32)
    low_slots = pair_row[:, None] * half_rows + offsets[None, :]
    high_slots = (2 * pair_count - 1 - pair_row)[:, None] * half_rows + offsets[None, :]
    return jnp.concatenate([low_slots, high_slots], axis=1).reshape(-1)


def rotary_tables(positions, head_dim):
    half_dim = head_dim // 2
    frequency = THETA ** (-(jnp.arange(half_dim, dtype=jnp.float32) * 2.0 / head_dim))
    angles = positions.astype(jnp.float32)[:, None] * frequency[None, :]
    return (jnp.cos(angles)[:, None, :], jnp.sin(angles)[:, None, :])


def rotary(tensor, table_cos, table_sin):
    half_dim = tensor.shape[-1] // 2
    lead_half = tensor[..., :half_dim]
    tail_half = tensor[..., half_dim:]
    return jnp.concatenate(
        [
            lead_half * table_cos - tail_half * table_sin,
            tail_half * table_cos + lead_half * table_sin,
        ],
        axis=-1,
    )


def rms_scale(tensor):
    return lax.rsqrt(jnp.mean(tensor * tensor, axis=-1, keepdims=True) + EPSILON)


def rms_backward(tensor, scale_rows, gain_full, grad_rows):
    weighted = gain_full * grad_rows
    inner_mean = jnp.mean(weighted * tensor, axis=-1, keepdims=True)
    return scale_rows * weighted - tensor * (scale_rows * scale_rows * scale_rows) * inner_mean


def contract_rows(first_mat, second_mat):
    return lax.dot_general(
        first_mat, second_mat, (((0,), (0,)), ((), ())), preferred_element_type=jnp.float32
    )


def contract_cols(first_mat, second_mat):
    return lax.dot_general(
        first_mat, second_mat, (((1,), (1,)), ((), ())), preferred_element_type=jnp.float32
    )


def attention_weights(gain_attn, gain_mlp, w_query, w_key, w_value, w_out):
    return (
        lax.all_gather(gain_attn, ("seq", "ctx"), axis=0, tiled=True),
        lax.all_gather(gain_mlp, ("seq", "ctx"), axis=0, tiled=True),
        lax.all_gather(w_query, ("seq", "ctx"), axis=0, tiled=True),
        lax.all_gather(w_key, ("seq", "ctx"), axis=0, tiled=True),
        lax.all_gather(w_value, ("seq", "ctx"), axis=0, tiled=True),
        lax.all_gather(w_out, ("seq", "ctx"), axis=0, tiled=True),
    )


def mlp_weights(w_gate, w_up, w_down):
    return (
        lax.all_gather(w_gate, ("seq", "ctx"), axis=0, tiled=True),
        lax.all_gather(w_up, ("seq", "ctx"), axis=0, tiled=True),
        lax.all_gather(w_down, ("seq", "ctx"), axis=0, tiled=True),
    )


def reduce_grads(grad_one, grad_two, grad_three):
    seq_count = lax.axis_size("seq")
    grad_one = grad_one.reshape((seq_count, grad_one.shape[0] // seq_count) + grad_one.shape[1:])
    grad_two = grad_two.reshape((seq_count, grad_two.shape[0] // seq_count) + grad_two.shape[1:])
    grad_three = grad_three.reshape(
        (seq_count, grad_three.shape[0] // seq_count) + grad_three.shape[1:]
    )
    grad_one, grad_two, grad_three = (
        lax.psum_scatter(
            grad_one.astype(jnp.bfloat16), "ctx", scatter_dimension=1, tiled=True
        ).astype(jnp.float32),
        lax.psum_scatter(
            grad_two.astype(jnp.bfloat16), "ctx", scatter_dimension=1, tiled=True
        ).astype(jnp.float32),
        lax.psum_scatter(
            grad_three.astype(jnp.bfloat16), "ctx", scatter_dimension=1, tiled=True
        ).astype(jnp.float32),
    )
    grad_one, grad_two, grad_three = (
        lax.psum_scatter(
            grad_one.astype(jnp.bfloat16), "seq", scatter_dimension=0, tiled=True
        ).astype(jnp.float32),
        lax.psum_scatter(
            grad_two.astype(jnp.bfloat16), "seq", scatter_dimension=0, tiled=True
        ).astype(jnp.float32),
        lax.psum_scatter(
            grad_three.astype(jnp.bfloat16), "seq", scatter_dimension=0, tiled=True
        ).astype(jnp.float32),
    )
    return (grad_one[0], grad_two[0], grad_three[0])


def general_device(
    tokens,
    cotangent,
    gain_attn,
    w_query,
    w_key,
    w_value,
    w_out,
    gain_mlp,
    w_gate,
    w_up,
    w_down,
    pair_order,
    segments,
):
    pair_count = lax.axis_size("ctx")
    my_index = lax.axis_index("ctx")
    row_count = tokens.shape[1]
    half_rows = row_count // 2
    seq_len = segments.shape[1]
    head_groups = H // KVH
    score_scale = HDIM ** (-0.5)
    key_rows = math.gcd(seq_len, 512)
    key_steps = seq_len // key_rows
    key_pos = slot_positions(pair_order[0], half_rows, pair_count)
    key_doc = jnp.take(segments[0], key_pos)
    query_pos = lax.dynamic_slice_in_dim(key_pos, my_index * row_count, row_count)
    query_doc = lax.dynamic_slice_in_dim(key_doc, my_index * row_count, row_count)
    rot_cos, rot_sin = rotary_tables(query_pos, HDIM)
    gain_one, gain_two, query_w, key_w, value_w, out_w = attention_weights(
        gain_attn, gain_mlp, w_query, w_key, w_value, w_out
    )
    gain_one = gain_one.astype(jnp.float32)
    gain_two = gain_two.astype(jnp.float32)
    inputs = tokens[0].astype(jnp.float32)
    scale_one = rms_scale(inputs)
    normed = (inputs * scale_one * gain_one).astype(jnp.bfloat16)
    query_proj = jnp.dot(normed, query_w, preferred_element_type=jnp.float32).reshape(
        row_count, H, HDIM
    )
    key_proj = jnp.dot(normed, key_w, preferred_element_type=jnp.float32).reshape(
        row_count, KVH, HDIM
    )
    value_proj = jnp.dot(normed, value_w, preferred_element_type=jnp.float32)
    query_rot = (
        rotary(query_proj, rot_cos, rot_sin)
        .astype(jnp.bfloat16)
        .reshape(row_count, KVH, head_groups, HDIM)
    )
    key_rot = rotary(key_proj, rot_cos, rot_sin).astype(jnp.bfloat16).reshape(row_count, KVH * HDIM)
    value_low = value_proj.astype(jnp.bfloat16)
    key_width = key_rot.shape[1]
    key_all, value_all = (
        lax.all_gather(key_rot, "ctx", axis=0, tiled=True),
        lax.all_gather(value_low, "ctx", axis=0, tiled=True),
    )
    pos_blocks = key_pos.reshape(key_steps, key_rows)
    doc_blocks = key_doc.reshape(key_steps, key_rows)

    def scores_of(key_blk, pos_blk, doc_blk):
        key_heads = key_blk.reshape(key_rows, KVH, HDIM)
        raw_scores = (
            jnp.einsum("qkgd,tkd->kgqt", query_rot, key_heads, preferred_element_type=jnp.float32)
            * score_scale
        )
        visible = (doc_blk[None, :] == query_doc[:, None]) & (
            pos_blk[None, :] <= query_pos[:, None]
        )
        return (raw_scores, visible[None, None])

    def first_pass(carried, step_data):
        running_top, running_sum = carried
        key_blk, pos_blk, doc_blk = step_data
        raw_scores, visible = scores_of(key_blk, pos_blk, doc_blk)
        masked = jnp.where(visible, raw_scores, NEG_FILL)
        new_top = jnp.maximum(running_top, jnp.max(masked, axis=-1))
        added = jnp.sum(jnp.where(visible, jnp.exp(masked - new_top[..., None]), 0.0), axis=-1)
        return ((new_top, running_sum * jnp.exp(running_top - new_top) + added), None)

    start_top = jnp.full((KVH, head_groups, row_count), NEG_FILL, jnp.float32)
    start_sum = jnp.zeros((KVH, head_groups, row_count), jnp.float32)
    key_stack = key_all.reshape(key_steps, key_rows, key_width)
    value_stack = value_all.reshape(key_steps, key_rows, key_width)
    (final_top, final_sum), _ = lax.scan(
        first_pass, (start_top, start_sum), (key_stack, pos_blocks, doc_blocks)
    )
    log_total = final_top + jnp.log(final_sum)

    def second_pass(carried, step_data):
        acc_out, acc_rest = carried
        key_blk, value_blk, pos_blk, doc_blk = step_data
        raw_scores, visible = scores_of(key_blk, pos_blk, doc_blk)
        prob_full = jnp.where(visible, jnp.exp(raw_scores - log_total[..., None]), 0.0)
        prob_low = prob_full.astype(jnp.bfloat16)
        prob_rest = (prob_full - prob_low.astype(jnp.float32)).astype(jnp.bfloat16)
        value_heads = value_blk.reshape(key_rows, KVH, HDIM)
        acc_out = acc_out + jnp.einsum(
            "kgqt,tkd->qkgd", prob_low, value_heads, preferred_element_type=jnp.float32
        )
        acc_rest = acc_rest + jnp.einsum(
            "kgqt,tkd->qkgd", prob_rest, value_heads, preferred_element_type=jnp.float32
        )
        return ((acc_out, acc_rest), None)

    start_acc = jnp.zeros((row_count, KVH, head_groups, HDIM), jnp.float32)
    (attended, attended_rest), _ = lax.scan(
        second_pass, (start_acc, start_acc), (key_stack, value_stack, pos_blocks, doc_blocks)
    )
    exact_out = attended + attended_rest
    out_low = attended.reshape(row_count, H * HDIM).astype(jnp.bfloat16)
    hidden = inputs + jnp.dot(out_low, out_w, preferred_element_type=jnp.float32)
    scale_two = rms_scale(hidden)
    normed_two = (hidden * scale_two * gain_two).astype(jnp.bfloat16)
    grad_out = cotangent[0]
    gate_w, up_w, down_w = mlp_weights(w_gate, w_up, w_down)
    gate_proj = jnp.dot(normed_two, gate_w, preferred_element_type=jnp.float32)
    up_proj = jnp.dot(normed_two, up_w, preferred_element_type=jnp.float32)
    gate_sig = jax.nn.sigmoid(gate_proj)
    active = gate_proj * gate_sig
    middle = (active * up_proj).astype(jnp.bfloat16)
    result = hidden + jnp.dot(middle, down_w, preferred_element_type=jnp.float32)
    output = result.astype(jnp.bfloat16)[None]
    gate_w, up_w, down_w = mlp_weights(w_gate, w_up, w_down)
    grad_mid = contract_cols(grad_out, down_w)
    grad_gate = (grad_mid * up_proj * gate_sig * (1.0 + gate_proj * (1.0 - gate_sig))).astype(
        jnp.bfloat16
    )
    grad_up = (grad_mid * active).astype(jnp.bfloat16)
    grad_norm_two = contract_cols(grad_gate, gate_w) + contract_cols(grad_up, up_w)
    grad_gain_two = jnp.sum(grad_norm_two * hidden * scale_two, axis=0)
    grad_hidden = grad_out.astype(jnp.float32) + rms_backward(
        hidden, scale_two, gain_two, grad_norm_two
    )
    grad_w_gate = contract_rows(normed_two, grad_gate)
    grad_w_up = contract_rows(normed_two, grad_up)
    shard_gain_two, shard_gate, shard_up = reduce_grads(grad_gain_two, grad_w_gate, grad_w_up)
    gain_one, gain_two, query_w, key_w, value_w, out_w = attention_weights(
        gain_attn, gain_mlp, w_query, w_key, w_value, w_out
    )
    gain_one = gain_one.astype(jnp.float32)
    grad_branch = grad_hidden.astype(jnp.bfloat16)
    grad_w_out = contract_rows(out_low, grad_branch)
    grad_att = (
        contract_cols(grad_branch, out_w)
        .astype(jnp.bfloat16)
        .reshape(row_count, KVH, head_groups, HDIM)
    )
    row_delta = jnp.transpose(jnp.sum(grad_att.astype(jnp.float32) * exact_out, axis=-1), (1, 2, 0))
    key_back, value_back = (key_all, value_all)

    def backward_step(grad_query, step_data):
        key_blk, value_blk, pos_blk, doc_blk = step_data
        raw_scores, visible = scores_of(key_blk, pos_blk, doc_blk)
        prob_full = jnp.where(visible, jnp.exp(raw_scores - log_total[..., None]), 0.0)
        prob_low = prob_full.astype(jnp.bfloat16)
        key_heads = key_blk.reshape(key_rows, KVH, HDIM)
        value_heads = value_blk.reshape(key_rows, KVH, HDIM)
        grad_value_blk = jnp.einsum(
            "kgqt,qkgd->tkd", prob_low, grad_att, preferred_element_type=jnp.float32
        )
        grad_probs = jnp.einsum(
            "qkgd,tkd->kgqt", grad_att, value_heads, preferred_element_type=jnp.float32
        )
        grad_scores = (prob_full * (grad_probs - row_delta[..., None])).astype(jnp.bfloat16)
        grad_query = (
            grad_query
            + jnp.einsum(
                "kgqt,tkd->qkgd", grad_scores, key_heads, preferred_element_type=jnp.float32
            )
            * score_scale
        )
        grad_key_blk = (
            jnp.einsum("kgqt,qkgd->tkd", grad_scores, query_rot, preferred_element_type=jnp.float32)
            * score_scale
        )
        return (
            grad_query,
            (
                grad_key_blk.reshape(key_rows, key_width),
                grad_value_blk.reshape(key_rows, key_width),
            ),
        )

    back_keys = key_back.reshape(key_steps, key_rows, key_width)
    back_values = value_back.reshape(key_steps, key_rows, key_width)
    grad_query, (grad_key_steps, grad_value_steps) = lax.scan(
        backward_step, start_acc, (back_keys, back_values, pos_blocks, doc_blocks)
    )
    grad_key_all = grad_key_steps.reshape(seq_len, key_width)
    grad_value_all = grad_value_steps.reshape(seq_len, key_width)
    grad_key_own, grad_value_own = (
        lax.psum_scatter(
            grad_key_all.astype(jnp.bfloat16), "ctx", scatter_dimension=0, tiled=True
        ).astype(jnp.float32),
        lax.psum_scatter(
            grad_value_all.astype(jnp.bfloat16), "ctx", scatter_dimension=0, tiled=True
        ).astype(jnp.float32),
    )
    grad_query = (
        rotary(grad_query.reshape(row_count, H, HDIM), rot_cos, -rot_sin)
        .astype(jnp.bfloat16)
        .reshape(row_count, H * HDIM)
    )
    grad_key = (
        rotary(grad_key_own.reshape(row_count, KVH, HDIM), rot_cos, -rot_sin)
        .astype(jnp.bfloat16)
        .reshape(row_count, key_width)
    )
    grad_value = grad_value_own.astype(jnp.bfloat16)
    grad_w_query = contract_rows(normed, grad_query)
    grad_w_key = contract_rows(normed, grad_key)
    grad_w_value = contract_rows(normed, grad_value)
    grad_normed = (
        contract_cols(grad_query, query_w)
        + contract_cols(grad_key, key_w)
        + contract_cols(grad_value, value_w)
    )
    grad_gain_one = jnp.sum(grad_normed * inputs * scale_one, axis=0)
    grad_tokens = grad_hidden + rms_backward(inputs, scale_one, gain_one, grad_normed)
    grad_w_down = contract_rows(middle, grad_out)
    shard_gain_one, shard_out, shard_down = reduce_grads(grad_gain_one, grad_w_out, grad_w_down)
    shard_query, shard_key, shard_value = reduce_grads(grad_w_query, grad_w_key, grad_w_value)
    return (
        output,
        grad_tokens[None],
        shard_gain_one,
        shard_query,
        shard_key,
        shard_value,
        shard_out,
        shard_gain_two,
        shard_gate,
        shard_up,
        shard_down,
    )


MESH = pl.DeviceIdType.MESH
VMEM = pltpu.VMEM
RING = 8
SEQ = 4


class Place:
    def __init__(self):
        self.c = lax.axis_index("ctx")
        self.s = lax.axis_index("seq")
        z, x = self.c // 2, lax.rem(self.c, 2)
        self.p = z + x * (7 - 2 * z)
        self.right = {"ctx": self.at(1)}
        self.left = {"ctx": self.at(-1)}
        self.s_core = self.s + 1 - 2 * lax.rem(self.s, 2)
        self.s_far = lax.rem(self.s + 2, 4)
        self.s_both = 3 - self.s
        self.core_peer = {"seq": self.s_core}
        self.far_peer = {"seq": self.s_far}

    def at(self, offset):
        q = lax.rem(self.p + offset + 2 * RING, RING)
        return 2 * q + (q // 4) * (15 - 4 * q)

    def peers(self):
        return [{"ctx": lax.rem(self.c + k, RING)} for k in range(1, RING)]


def greet(devices):
    barrier = pltpu.get_barrier_semaphore()
    for device in devices:
        pl.semaphore_signal(barrier, inc=1, device_id=device, device_id_type=MESH)
    pl.semaphore_wait(barrier, len(devices))


def remote(src, dst, send_sem, recv_sem, device):
    return pltpu.make_async_remote_copy(
        src_ref=src, dst_ref=dst, send_sem=send_sem, recv_sem=recv_sem, device_id=device, device_id_type=MESH
    )


def arrived(ref, sems, index, device):
    remote(ref, ref, sems[0].at[index], sems[1].at[index], device).wait_recv()


def together(*flows):
    live = list(flows)
    while live:
        live = [flow for flow in live if next(flow, "end") != "end"]


def ring_sems():
    return [pltpu.SemaphoreType.DMA((2, RING // 2, 2))] * 2


def slot(offset):
    return 0 if offset == 0 else min(RING - 1, 2 * offset if offset > 0 else -2 * offset - 1)


class Rows:
    def __init__(self, ref, rows):
        self.ref, self.rows = ref, rows

    def here(self, offset):
        return self.ref.at[pl.ds(slot(offset) * self.rows, self.rows)]

    def there(self, offset, d):
        return self.here(offset - 1 if d == 0 else offset + 1)


class Owners:
    def __init__(self, ref, place):
        self.ref, self.place = ref, place

    def here(self, offset):
        return self.ref.at[self.place.at(offset)]

    def there(self, offset, d):
        return self.here(offset)


def ring_gather(own, blocks, sems, place):
    half = own.shape[0] // 2
    steps = RING // 2
    sent = []

    def part(ref, j):
        return ref.at[pl.ds(j * half, half)]

    def wait_for(d, s, j):
        offset = -(s + 1) if d == 0 else s + 1
        arrived(part(blocks.here(offset), j), sems, (d, s, j), place.right if d == 0 else place.left)

    for s in range(steps):
        for j in range(2):
            for d in range(2):
                if s == steps - 1 and j != d:
                    continue
                if s > 0:
                    wait_for(d, s - 1, j)
                offset = -s if d == 0 else s
                copy = remote(
                    part(own if s == 0 else blocks.here(offset), j),
                    part(blocks.there(offset, d), j),
                    sems[0].at[d, s, j],
                    sems[1].at[d, s, j],
                    place.right if d == 0 else place.left,
                )
                copy.start()
                sent.append(copy)
            yield
    for d in range(2):
        wait_for(d, steps - 2, 1 - d)
    yield
    for d in range(2):
        wait_for(d, steps - 1, d)
    yield
    for copy in sent:
        copy.wait_send()


class RingSum:
    def __init__(self, slots, sems, place):
        self.slots, self.sems, self.sent = slots, sems, []
        self.sides = (place.right, place.left)
        self.half = slots.shape[2] // 2

    def rows(self, ref, j):
        return ref.at[pl.ds(j * self.half, self.half)]

    def send(self, d, s, j, source):
        to = self.rows(self.slots.at[d, s], j)
        copy = remote(source, to, self.sems[0].at[d, s, j], self.sems[1].at[d, s, j], self.sides[d])
        copy.start()
        self.sent.append(copy)

    def held(self, d, s, j):
        ref = self.rows(self.slots.at[d, s], j)
        arrived(ref, self.sems, (d, s, j), self.sides[d])
        return ref

    def first(self, part):
        for d in range(2):
            self.send(d, 0, d, self.rows(part, d))

    def relay(self, s, parts):
        for j in range(2):
            for d in range(2):
                source = self.rows(parts[d], j)
                if s > 1 or j == d:
                    held = self.held(d, s - 1, j)
                    add_into(held, source)
                    source = held
                self.send(d, s, j, source)

    def last(self, part, out):
        for j in range(2):
            held = [self.held(d, RING // 2 - 1, j) for d in range(2)]
            sum_of_three(self.rows(out, j), self.rows(part, j), *held)

    def end(self):
        for copy in self.sent:
            copy.wait_send()


def ring_scatter(blocks, out, slots, sems, place):
    ring = RingSum(slots, sems, place)
    ring.first(blocks.here(RING // 2))
    yield
    for s in range(1, RING // 2):
        k = RING // 2 - s
        ring.relay(s, (blocks.here(k), blocks.here(-k)))
        yield
    ring.last(blocks.here(0), out)
    ring.end()
    yield


def pair_sems():
    return [pltpu.SemaphoreType.DMA((RING,))] * 2


OFFSETS = (1, -1, 2, -2, 3, -3, 4)


def exchange(send, there, here, sems, place):
    sent = []
    for k in OFFSETS:
        at = slot(k)
        copy = remote(send(k), there(k), sems[0].at[at], sems[1].at[at], {"ctx": place.at(k)})
        copy.start()
        sent.append(copy)
    yield
    for k in OFFSETS:
        arrived(here(k), sems, slot(-k) if k != RING // 2 else RING - 1, {"ctx": place.at(k)})
    for copy in sent:
        copy.wait_send()
    yield


def by_owner(src, dst, sems, place):
    return exchange(
        lambda k: src.at[place.at(k)], lambda k: dst.at[place.c], lambda k: dst.at[place.at(k)], sems, place
    )


def pairs_of(sems):
    return [sems[i : i + 2] for i in range(0, len(sems), 2)]


def seq_sems():
    return [pltpu.SemaphoreType.DMA((3,))] * 2


def seq_gather(own, buf, sems, place):
    first = remote(own, buf.at[place.s], sems[0].at[0], sems[1].at[0], place.far_peer)
    second = remote(own, buf.at[place.s], sems[0].at[1], sems[1].at[1], place.core_peer)
    first.start()
    second.start()
    yield
    arrived(buf.at[place.s_far], sems, 0, place.far_peer)
    third = remote(buf.at[place.s_far], buf.at[place.s_far], sems[0].at[2], sems[1].at[2], place.core_peer)
    third.start()
    yield
    arrived(buf.at[place.s_core], sems, 1, place.core_peer)
    arrived(buf.at[place.s_both], sems, 2, place.core_peer)
    for copy in (first, second, third):
        copy.wait_send()
    yield


def sum_of_three(dst, *terms):
    step = math.gcd(dst.shape[0], 16)

    @pl.loop(0, dst.shape[0] // step)
    def _(i):
        at = pl.ds(pl.multiple_of(i * step, step), step)
        one, two, three = (term[at].astype(jnp.float32) for term in terms)
        dst[at] = one + two + three


def add_into(dst, other):
    rows = dst.shape[0]
    step = math.gcd(rows, 16)

    @pl.loop(0, rows // step)
    def _(i):
        at = pl.ds(pl.multiple_of(i * step, step), step)
        dst[at] = (dst[at].astype(jnp.float32) + other[at].astype(jnp.float32)).astype(dst.dtype)


class SeqSum:
    def __init__(self, grad, block, near, far, sems, place):
        self.grad, self.block, self.near_ref, self.far, self.sems, self.place = grad, block, near, far, sems, place
        self.low, self.row = lax.rem(place.s, 2), place.s // 2
        self.sent = []

    def send(self, src, dst, i, device):
        copy = remote(src, dst, self.sems[0].at[i], self.sems[1].at[i], device)
        copy.start()
        self.sent.append(copy)

    def near(self, i):
        r = (1 - self.row, self.row)[i]
        self.grad(r * 2 + 1 - self.low, self.block.at[i], False)
        self.send(self.block.at[i], self.near_ref.at[i], i, self.place.core_peer)

    def across(self):
        arrived(self.near_ref.at[0], self.sems, 0, self.place.core_peer)
        self.grad((1 - self.row) * 2 + self.low, self.near_ref.at[0], True)
        self.send(self.near_ref.at[0], self.far, 2, self.place.far_peer)

    def own(self):
        arrived(self.near_ref.at[1], self.sems, 1, self.place.core_peer)
        self.grad(self.row * 2 + self.low, self.near_ref.at[1], True)

    def last(self):
        arrived(self.far, self.sems, 2, self.place.far_peer)
        add_into(self.far, self.near_ref.at[1])

    def end(self):
        for copy in self.sent:
            copy.wait_send()


def call(body, outs, args, spaces, out_spaces, scratch, ident):
    return pl.pallas_call(
        body,
        out_shape=outs,
        in_specs=[pl.BlockSpec(memory_space=space) for space in spaces],
        out_specs=[pl.BlockSpec(memory_space=space) for space in out_spaces],
        scratch_shapes=scratch,
        compiler_params=pltpu.CompilerParams(
            collective_id=ident, has_side_effects=True, vmem_limit_bytes=63 * 1024 * 1024
        ),
    )(*args)


def shaped(shape, dtype=jnp.bfloat16):
    return jax.ShapeDtypeStruct(shape, dtype)


def dot(a, b, at=(1, 0)):
    return lax.dot_general(a, b, (((at[0],), (at[1],)), ((), ())), preferred_element_type=jnp.float32)


def chunks(total, size, body):
    @pl.loop(0, total // size)
    def _(i):
        body(pl.ds(pl.multiple_of(i * size, size), size))


def turned(t, cos, sin, sign):
    half = t.shape[1] // 2
    a, b = t[:, :half], t[:, half:]
    return jnp.concatenate([a * cos - sign * b * sin, b * cos + sign * a * sin], axis=-1)


def probabilities(q, k, pos_rows, doc_rows, pos_cols, doc_cols):
    scores = dot(q, k, (1, 1)) * HDIM ** (-0.5)
    visible = (doc_cols == doc_rows) & (pos_cols <= pos_rows)
    scores = jnp.where(visible, scores, NEG_FILL)
    weight = jnp.exp(scores - jnp.max(scores, axis=-1, keepdims=True))
    return weight / jnp.sum(weight, axis=-1, keepdims=True)


def attention_kernel(x, xhat, dy, wqkv, wout, wcol, wdown, cos, sin, pos_rows, doc_rows, pos_cols, doc_cols,
                     hidden, hhat, ob_local, q_out, k_out, v_out, x_all, dy_all, wqkv_all, wout_all, wcol_all, wdown_all,
                     x_v, wqkv_v, wout_v, q, k, v, ob, local, loads, *sems):
    place = Place()
    x_ring, qkv_swap, qkv_seq, out_ring, out_seq, ob_swap, dy_ring, gate_swap, gate_seq, up_swap, up_seq, down_seq = pairs_of(sems)
    greet(place.peers() + [place.core_peer, place.far_peer])
    bf16, f32 = jnp.bfloat16, jnp.float32
    rows, width = x.shape
    head = ob.shape[1]
    x_blocks, dy_blocks, ob_blocks = Rows(x_all, rows), Rows(dy_all, rows), Rows(ob, rows)
    keep = [
        pltpu.make_async_copy(src, dst, local.at[i])
        for i, (src, dst) in enumerate(
            (
                (xhat, x_blocks.here(0)),
                (dy, dy_blocks.here(0)),
                (wqkv.at[place.c], wqkv_all.at[place.s, place.c]),
                (wout, wout_all.at[place.s, place.c]),
                (wdown, wdown_all.at[place.s]),
                (wcol.at[0, place.c], wcol_all.at[0, place.s, place.c]),
                (wcol.at[1, place.c], wcol_all.at[1, place.s, place.c]),
            )
        )
    ]
    for copy in keep:
        copy.start()

    def spread(src, dst, own, swap, seq):
        yield from by_owner(src, dst.at[place.s], swap, place)
        keep[own].wait()
        yield from seq_gather(dst.at[place.s], dst, seq, place)

    def out_flow():
        yield from ring_gather(wout, Owners(wout_all.at[place.s], place), out_ring, place)
        keep[3].wait()
        yield from seq_gather(wout_all.at[place.s], wout_all, out_seq, place)

    def steps(flow, count):
        for _ in range(count):
            next(flow)

    qkv_w = spread(wqkv, wqkv_all, 2, qkv_swap, qkv_seq)
    gate_w = spread(wcol.at[0], wcol_all.at[0], 5, gate_swap, gate_seq)
    up_w = spread(wcol.at[1], wcol_all.at[1], 6, up_swap, up_seq)
    down_w = seq_gather(wdown, wdown_all, down_seq, place)
    out_w = out_flow()
    x_flow, dy_flow = ring_gather(xhat, x_blocks, x_ring, place), ring_gather(dy, dy_blocks, dy_ring, place)

    steps(qkv_w, 1)
    steps(down_w, 1)
    steps(out_w, 2)
    steps(gate_w, 1)
    steps(out_w, 2)
    steps(up_w, 1)
    steps(out_w, 4)
    steps(qkv_w, 2)
    steps(x_flow, 2)
    steps(out_w, 3)
    steps(down_w, 1)
    steps(x_flow, 2)
    steps(gate_w, 2)
    steps(x_flow, 2)
    steps(up_w, 2)
    steps(qkv_w, 1)
    steps(x_flow, 4)
    steps(dy_flow, 2)
    steps(qkv_w, 1)
    keep[0].wait()
    load = [
        pltpu.make_async_copy(x_all, x_v, loads.at[0]),
        pltpu.make_async_copy(wqkv_all, wqkv_v, loads.at[1]),
    ]
    for copy in load:
        copy.start()
    for copy in load:
        copy.wait()

    def project(at):
        qkv = dot(x_v[at, :], wqkv_v[...].reshape(width, 3 * head))
        c, s = cos[at, :], sin[at, :]
        q[at, :] = turned(qkv[:, :head], c, s, 1.0).astype(bf16)
        k[at, :] = turned(qkv[:, head : 2 * head], c, s, 1.0).astype(bf16)
        v[at, :] = qkv[:, 2 * head :].astype(bf16)

    chunks(x_v.shape[0], 256, project)
    steps(dy_flow, 2)

    def attend(at):
        prob = probabilities(q[at, :], k[...], pos_rows[at, :], doc_rows[at, :], pos_cols[...], doc_cols[...])
        ob[at, :] = dot(prob.astype(bf16), v[...]).astype(bf16)

    chunks(x_v.shape[0], 256, attend)
    mine = pl.ds(pl.multiple_of(place.c * head, head), head)

    def from_head(k_offset):
        return ob_local.at[:, pl.ds(pl.multiple_of(place.at(k_offset) * head, head), head)]

    ob_flow = exchange(ob_blocks.here, lambda k_offset: ob_local.at[:, mine], from_head, ob_swap, place)
    steps(ob_flow, 1)
    ob_local[:, mine] = ob[pl.ds(0, rows), :]
    saves = [pltpu.make_async_copy(src, dst, loads.at[2 + i]) for i, (src, dst) in enumerate(((q, q_out), (k, k_out), (v, v_out)))]
    for copy in saves:
        copy.start()
    steps(dy_flow, 2)
    steps(out_w, 1)
    steps(dy_flow, 4)
    for _ in out_w:
        pass
    load_out = pltpu.make_async_copy(wout_all, wout_v, loads.at[0])
    load_out.start()
    steps(gate_w, 1)
    steps(up_w, 1)
    steps(ob_flow, 1)
    load_out.wait()

    def residual(cols):
        part = dot(ob_local[...], wout_v[:, :, :, cols].reshape(width, cols.size))
        hidden[:, cols] = x[:, cols].astype(f32) + part

    chunks(width, 256, residual)
    mean = jnp.mean(hidden[...] * hidden[...], axis=-1, keepdims=True)
    hhat[...] = (hidden[...] * lax.rsqrt(mean + EPSILON)).astype(bf16)
    for flow in (gate_w, up_w, down_w, qkv_w, x_flow, dy_flow, ob_flow):
        for _ in flow:
            pass
    for copy in saves:
        copy.wait()
    keep[1].wait()
    keep[4].wait()


def mlp_kernel(hhat, dy_hbm, wcol_hbm, wdown_hbm, sum_h, sum_o, col_out, down_out,
               h_all, dy_all, wg, wu, wd, mid, dgate, dup, stage_h, stage_o, stage, slots_h, slots_o,
               col_sent, col_near, col_far, down_sent, down_near, down_far, local, *sems):
    place = Place()
    h_sems, sum_h_sems, sum_o_sems, col_seq, down_seq = pairs_of(sems)
    greet([place.right, place.left, place.core_peer, place.far_peer])
    rows, width = hhat.shape
    ff = wg.shape[1]
    bf16, f32 = jnp.bfloat16, jnp.float32
    keep = [
        pltpu.make_async_copy(src, dst, local.at[i])
        for i, (src, dst) in enumerate(
            ((hhat, h_all.at[pl.ds(0, rows)]), (wcol_hbm.at[0], wg), (wcol_hbm.at[1], wu), (wdown_hbm, wd), (dy_hbm, dy_all))
        )
    ]
    for copy in keep:
        copy.start()
    gather = ring_gather(hhat, Rows(h_all, rows), h_sems, place)
    next(gather)
    next(gather)
    for copy in keep:
        copy.wait()

    def hidden_rows(start, count):
        at = pl.ds(start, count)

        def body(cols):
            gate = dot(h_all[at, :], wg[:, cols])
            up = dot(h_all[at, :], wu[:, cols])
            dmid = dot(dy_all[at, :], wd[cols, :], (1, 1))
            sig = jax.nn.sigmoid(gate)
            active = gate * sig
            mid[at, cols] = (active * up).astype(bf16)
            dgate[at, cols] = (dmid * up * sig * (1.0 + gate * (1.0 - sig))).astype(bf16)
            dup[at, cols] = (dmid * active).astype(bf16)

        chunks(ff, 256, body)

    def part_h(start, count, dst):
        at = pl.ds(start, count)

        def body(cols):
            dst[:, cols] = (dot(dgate[at, :], wg[cols, :], (1, 1)) + dot(dup[at, :], wu[cols, :], (1, 1))).astype(bf16)

        chunks(width, 256, body)

    def part_o(start, count, dst):
        at = pl.ds(start, count)

        def body(cols):
            dst[:, cols] = dot(mid[at, :], wd[:, cols]).astype(bf16)

        chunks(width, 256, body)

    def col_grad(s, dst, add):
        def body(cols):
            lhs = h_all[:, pl.ds(pl.multiple_of(s * dst.shape[0] + cols.start, 256), 256)]
            for side, grad in enumerate((dgate, dup)):
                there = pl.ds(side * ff, ff)
                value = dot(lhs, grad[...], (0, 0))
                if add:
                    value = value + dst[cols, there].astype(f32)
                dst[cols, there] = value.astype(bf16)

        chunks(dst.shape[0], 256, body)

    def down_grad(s, dst, add):
        lhs = pl.ds(pl.multiple_of(s * dst.shape[0], 256), dst.shape[0])

        def body(cols):
            value = dot(mid[:, lhs], dy_all[:, cols], (0, 0))
            if add:
                value = value + dst[:, cols].astype(f32)
            dst[:, cols] = value.astype(bf16)

        chunks(width, 512, body)

    hidden_rows(0, rows)
    for k in range(1, 4):
        next(gather)
        if k < 3:
            next(gather)
        else:
            next(gather)
            next(gather)
        hidden_rows((2 * k - 1) * rows, 2 * rows)
    next(gather)
    hidden_rows(7 * rows, rows)

    def pair(ref):
        return (ref.at[pl.ds(rows, rows)], ref.at[pl.ds(0, rows)])

    col_sum = SeqSum(col_grad, col_sent, col_near, col_far, col_seq, place)
    down_sum = SeqSum(down_grad, down_sent, down_near, down_far, down_seq, place)
    ring_h, ring_o = RingSum(slots_h, sum_h_sems, place), RingSum(slots_o, sum_o_sems, place)
    top_h, top_o = stage_h.at[pl.ds(2 * rows, rows)], stage_o.at[pl.ds(2 * rows, rows)]
    next_h, next_o = stage_h.at[pl.ds(0, 2 * rows)], stage_o.at[pl.ds(0, 2 * rows)]
    part_h(7 * rows, rows, top_h)
    ring_h.first(top_h)
    col_sum.near(0)
    part_h(5 * rows, 2 * rows, next_h)
    ring_h.relay(1, pair(next_h))
    col_sum.near(1)
    col_sum.across()
    part_o(7 * rows, rows, top_o)
    ring_o.first(top_o)
    part_h(3 * rows, 2 * rows, stage)
    ring_h.relay(2, pair(stage))
    part_o(5 * rows, 2 * rows, next_o)
    ring_o.relay(1, pair(next_o))
    down_sum.near(0)
    part_h(rows, 2 * rows, stage)
    ring_h.relay(3, pair(stage))
    down_sum.near(1)
    down_sum.across()
    part_o(3 * rows, 2 * rows, stage)
    ring_o.relay(2, pair(stage))
    col_sum.own()
    part_h(0, rows, top_stage := stage.at[pl.ds(0, rows)])
    ring_h.last(top_stage, sum_h)
    part_o(rows, 2 * rows, stage)
    ring_o.relay(3, pair(stage))
    down_sum.own()
    part_o(0, rows, top_stage)
    ring_o.last(top_stage, sum_o)
    ends = []
    for i, (total, out) in enumerate(((col_sum, col_out), (down_sum, down_out))):
        total.last()
        ends.append(pltpu.make_async_copy(total.far, out, local.at[i]))
        ends[-1].start()
    for copy in ends:
        copy.wait()
    for flow in (ring_h, ring_o, col_sum, down_sum):
        flow.end()
    for _ in gather:
        pass


def backward_kernel(weighted, hidden, dy, x, q, k, v, ob_local, cos, sin, pos_rows, doc_rows, pos_cols, doc_cols,
                    x_all, wqkv_all, wout_all, col,
                    grad_x, out_grad, col_out, qkv_out,
                    x_v, wqkv_v, wout_v, grad_h, branch, datt_own, datt, dqkv, dk, dv, part_7, part_3, part, sum_x, slots_x,
                    qkv_sent, qkv_near, qkv_far, out_sent, out_near, out_far, slots_o, local, *sems):
    place = Place()
    att_swap, x_ring, col_swap, qkv_seq, qkv_swap, out_seq, out_ring = pairs_of(sems)
    greet(place.peers() + [place.core_peer, place.far_peer])
    bf16, f32 = jnp.bfloat16, jnp.float32
    rows, width = x.shape
    head = q.shape[1]
    seq_len = q.shape[0]

    loads = [
        pltpu.make_async_copy(src, dst, local.at[i])
        for i, (src, dst) in enumerate(((wout_all, wout_v), (x_all, x_v), (wqkv_all, wqkv_v)))
    ]
    for copy in loads:
        copy.start()

    def swap_flow(blocks, into, swap, sem):
        keep = pltpu.make_async_copy(blocks.at[place.c], into.at[place.c], sem)
        keep.start()
        yield from by_owner(blocks, into, swap, place)
        keep.wait()

    col_flow = swap_flow(Blocks(col, col_out.shape[1]), col_out, col_swap, local.at[3])
    next(col_flow)

    def norm_back(tensor, grads):
        scale = lax.rsqrt(jnp.mean(tensor * tensor, axis=-1, keepdims=True) + EPSILON)
        inner = jnp.mean(grads * tensor, axis=-1, keepdims=True)
        return scale * grads - tensor * (scale * scale * scale) * inner

    def hidden_back(at):
        grads = dy[at, :].astype(f32) + norm_back(hidden[at, :], weighted[at, :])
        grad_h[at, :] = grads
        branch[at, :] = grads.astype(bf16)

    chunks(rows, 16, hidden_back)
    loads[0].wait()

    def att_back(cols):
        datt_own[:, cols] = dot(branch[...], wout_v[cols, :], (1, 1)).astype(bf16)

    chunks(width, head, att_back)

    def head_cols(offset):
        return pl.ds(pl.multiple_of(place.at(offset) * head, head), head)

    blocks = Rows(datt, rows)
    att_flow = exchange(lambda o: datt_own.at[:, head_cols(o)], lambda o: blocks.here(-o), blocks.here, att_swap, place)
    next(att_flow)
    datt[pl.ds(0, rows), :] = datt_own[:, head_cols(0)]

    def out_block(s, dst, add):
        def body(cols):
            lhs = ob_local[:, pl.ds(pl.multiple_of(s * dst.shape[0] + cols.start, 256), 256)]
            value = dot(lhs, branch[...], (0, 0))
            if add:
                value = value + dst[cols, :].astype(f32)
            dst[cols, :] = value.astype(bf16)

        chunks(dst.shape[0], 256, body)

    def qkv_block(s, dst, add):
        def body(cols):
            lhs = x_v[:, pl.ds(pl.multiple_of(s * dst.shape[0] + cols.start, 256), 256)]
            value = dot(lhs, dqkv[...], (0, 0))
            if add:
                value = value + dst[cols, :].astype(f32)
            dst[cols, :] = value.astype(bf16)

        chunks(dst.shape[0], 256, body)

    out_sum = SeqSum(out_block, out_sent, out_near, out_far, out_seq, place)
    qkv_sum = SeqSum(qkv_block, qkv_sent, qkv_near, qkv_far, qkv_seq, place)
    out_sum.near(0)
    out_sum.near(1)
    out_sum.across()
    dk[...] = jnp.zeros_like(dk)
    dv[...] = jnp.zeros_like(dv)
    for copy in loads[1:]:
        copy.wait()
    next(att_flow)

    def attend_back(at):
        prob = probabilities(q[at, :], k[...], pos_rows[at, :], doc_rows[at, :], pos_cols[...], doc_cols[...])
        dprob = dot(datt[at, :], v[...], (1, 1))
        delta = jnp.sum(prob * dprob, axis=-1, keepdims=True)
        dscore = (prob * (dprob - delta)).astype(bf16)
        dq = dot(dscore, k[...]) * HDIM ** (-0.5)
        dqkv[at, pl.ds(0, head)] = turned(dq, cos[at, :], sin[at, :], -1.0).astype(bf16)
        dk[...] += dot(dscore, q[at, :], (0, 0))
        dv[...] += dot(prob.astype(bf16), datt[at, :], (0, 0))

    chunks(seq_len, 256, attend_back)

    def finish_back(at):
        turned_dk = turned(dk[at, :] * HDIM ** (-0.5), cos[at, :], sin[at, :], -1.0)
        dqkv[at, pl.ds(head, head)] = turned_dk.astype(bf16)
        dqkv[at, pl.ds(2 * head, head)] = dv[at, :].astype(bf16)

    chunks(seq_len, 128, finish_back)

    def part_x(start, count, dst):
        at = pl.ds(start, count)

        def body(cols):
            dst[:, cols] = dot(dqkv[at, :], wqkv_v[cols, :], (1, 1)).astype(bf16)

        chunks(width, 256, body)

    def pair(ref):
        return (ref.at[pl.ds(rows, rows)], ref.at[pl.ds(0, rows)])

    ring = RingSum(slots_x, x_ring, place)
    part_x(7 * rows, rows, part_7)
    ring.first(part_7)
    qkv_sum.near(0)
    qkv_sum.near(1)
    part_x(5 * rows, 2 * rows, part_3)
    ring.relay(1, pair(part_3))
    qkv_sum.across()
    part_x(3 * rows, 2 * rows, part)
    ring.relay(2, pair(part))
    out_sum.own()
    qkv_sum.own()
    part_x(rows, 2 * rows, part)
    out_sum.last()
    out_blocks = Owners(Blocks(out_far, out_grad.shape[0]), place)
    out_flow = ring_scatter(out_blocks, out_grad, slots_o, out_ring, place)
    next(out_flow)
    ring.relay(3, pair(part))
    next(out_flow)
    qkv_sum.last()
    qkv_flow = swap_flow(Blocks(qkv_far, qkv_out.shape[1]), qkv_out, qkv_swap, local.at[4])
    next(qkv_flow)
    part_x(0, rows, part.at[pl.ds(0, rows)])
    next(out_flow)
    ring.last(part.at[pl.ds(0, rows)], sum_x)

    def token_back(at):
        grad_x[at, :] = grad_h[at, :] + norm_back(x[at, :].astype(f32), sum_x[at, :])

    chunks(rows, 16, token_back)
    for flow in (out_flow, col_flow, qkv_flow, att_flow):
        for _ in flow:
            pass
    for flow in (ring, out_sum, qkv_sum):
        flow.end()


class Blocks:
    def __init__(self, ref, rows):
        self.ref, self.rows = ref, rows
        self.shape = (ref.shape[0] // rows, rows) + tuple(ref.shape[1:])

    @property
    def at(self):
        return self

    def __getitem__(self, i):
        return self.ref.at[pl.ds(pl.multiple_of(i * self.rows, self.rows), self.rows)]


DMA = pltpu.SemaphoreType.DMA
HBM = pl.ANY


def ring_device(
    tokens, cotangent, gain_attn, w_query, w_key, w_value, w_out, gain_mlp, w_gate, w_up, w_down, pair_order, segments
):
    bf16, f32 = jnp.bfloat16, jnp.float32
    n, c = RING, lax.axis_index("ctx")
    rows, width = tokens.shape[1], tokens.shape[2]
    half_rows, seq_len = rows // 2, segments.shape[1]
    shard = w_query.shape[0]
    ff_own = w_down.shape[0]
    ff_mine = SEQ * ff_own
    head = HDIM
    scale = HDIM ** (-0.5)

    gain_one = gain_attn.astype(f32)[:, None]
    gain_two = gain_mlp.astype(f32)[:, None]
    wq, wk, wv, wg, wu = (w.astype(f32) for w in (w_query, w_key, w_value, w_gate, w_up))
    groups = H // KVH

    def by_head(w):
        return jnp.repeat((w * gain_one).astype(bf16).reshape(shard, KVH, head), groups, axis=1)

    wqkv = jnp.concatenate(
        [(wq * gain_one).astype(bf16).reshape(shard, H, head), by_head(wk), by_head(wv)], axis=-1
    ).transpose(1, 0, 2)

    def by_context(w):
        return (w * gain_two).astype(bf16).reshape(shard, SEQ, n, ff_own).transpose(2, 0, 1, 3).reshape(n, shard, ff_mine)

    wcol = jnp.stack([by_context(wg), by_context(wu)])

    inputs = tokens[0].astype(f32)
    scale_one = rms_scale(inputs)
    xhat = (inputs * scale_one).astype(bf16)

    z, x = c // 2, lax.rem(c, 2)
    ring_at = z + x * (7 - 2 * z)
    offsets = jnp.array([0, -1, 1, -2, 2, -3, 3, 4], jnp.int32)
    q = lax.rem(ring_at + offsets + n, n)
    order = 2 * q + (q // 4) * (15 - 4 * q)
    block = jnp.take(pair_order[0], order)
    blocks = jnp.stack([block, 2 * n - 1 - block], axis=1).reshape(-1)
    pos = (blocks[:, None] * half_rows + jnp.arange(half_rows, dtype=jnp.int32)[None, :]).reshape(-1)
    doc = jnp.take(segments[0].reshape(2 * n, half_rows), blocks, axis=0).reshape(-1)
    angles_of = rotary_tables(pos, HDIM)
    cos, sin = angles_of[0][:, 0], angles_of[1][:, 0]

    def rot(t, sign):
        a, b = t[:, : head // 2], t[:, head // 2 :]
        return jnp.concatenate([a * cos - sign * b * sin, b * cos + sign * a * sin], axis=-1)

    hidden, hhat, ob_local, q, k, v, x_all, dy_all, wqkv_all, wout_all, wcol_all, wdown_all = call(
        attention_kernel,
        [
            shaped((rows, width), f32),
            shaped((rows, width)),
            shaped((rows, H * head)),
            shaped((seq_len, head)),
            shaped((seq_len, head)),
            shaped((seq_len, head)),
            shaped((seq_len, width)),
            shaped((seq_len, width)),
            shaped((SEQ, n, shard, 3 * head)),
            shaped((SEQ, n, shard, width)),
            shaped((2, SEQ, n, shard, ff_mine)),
            shaped((SEQ, ff_own, width)),
        ],
        (
            tokens[0],
            xhat,
            cotangent[0],
            wqkv,
            w_out,
            wcol,
            w_down,
            cos,
            sin,
            pos[:, None],
            doc[:, None],
            pos[None, :],
            doc[None, :],
        ),
        [VMEM] + [HBM] * 6 + [VMEM] * 6,
        [VMEM] * 3 + [HBM] * 9,
        [
            VMEM((seq_len, width), bf16),
            VMEM((SEQ, n, shard, 3 * head), bf16),
            VMEM((SEQ, n, shard, width), bf16),
        ]
        + [VMEM((seq_len, head), bf16)] * 4
        + [DMA((7,)), DMA((5,))]
        + ring_sems()
        + pair_sems()
        + seq_sems()
        + ring_sems()
        + seq_sems()
        + pair_sems()
        + ring_sems()
        + (pair_sems() + seq_sems()) * 2
        + seq_sems(),
        1,
    )
    wqkv_all = wqkv_all.reshape(width, 3 * head)
    wout_all = wout_all.reshape(H * head, width)
    wcol_all = wcol_all.reshape(2, width, ff_mine)
    wdown_all = wdown_all.reshape(ff_mine, width)

    slot_shape = VMEM((2, n // 2, rows, width), bf16)
    col_piece, down_piece = (n * shard, 2 * ff_mine), (ff_own, width)
    dweighted, out_sum, col_sum, down_sum = call(
        mlp_kernel,
        [shaped((rows, width), f32)] * 2 + [shaped(col_piece), shaped(down_piece)],
        (hhat, dy_all, wcol_all, wdown_all),
        [HBM] * 4,
        [VMEM] * 2 + [HBM] * 2,
        [VMEM((seq_len, width), bf16)] * 2
        + [VMEM((width, ff_mine), bf16)] * 2
        + [VMEM((ff_mine, width), bf16)]
        + [VMEM((seq_len, ff_mine), bf16)] * 3
        + [VMEM((3 * rows, width), bf16)] * 2
        + [VMEM((2 * rows, width), bf16)]
        + [slot_shape] * 2
        + [VMEM((2,) + col_piece, bf16), VMEM((2,) + col_piece, bf16), VMEM(col_piece, bf16)]
        + [VMEM((2,) + down_piece, bf16), VMEM((2,) + down_piece, bf16), VMEM(down_piece, bf16)]
        + [DMA((5,))]
        + ring_sems() * 3
        + seq_sems() * 2,
        2,
    )
    output = (hidden + out_sum).astype(bf16)[None]

    piece = (n * shard, width)
    qkv_piece = (n * shard, 3 * head)
    grad_tokens, out_grad, col_sum, qkv_sum = call(
        backward_kernel,
        [
            shaped((rows, width), f32),
            shaped((shard, width), f32),
            shaped((n, shard, 2 * ff_mine)),
            shaped((n, shard, 3 * head)),
        ],
        (dweighted, hidden, cotangent[0], tokens[0], q, k, v, ob_local, cos, sin)
        + (pos[:, None], doc[:, None], pos[None, :], doc[None, :], x_all, wqkv_all, wout_all, col_sum),
        [VMEM] * 14 + [HBM] * 4,
        [VMEM] * 2 + [HBM] * 2,
        [
            VMEM((seq_len, width), bf16),
            VMEM((width, 3 * head), bf16),
            VMEM((H * head, width), bf16),
            VMEM((rows, width), f32),
            VMEM((rows, width), bf16),
            VMEM((rows, width), bf16),
            VMEM((seq_len, head), bf16),
            VMEM((seq_len, 3 * head), bf16),
            VMEM((seq_len, head), f32),
            VMEM((seq_len, head), f32),
            VMEM((rows, width), bf16),
            VMEM((2 * rows, width), bf16),
            VMEM((2 * rows, width), bf16),
            VMEM((rows, width), f32),
            slot_shape,
        ]
        + [VMEM((2,) + qkv_piece, bf16), VMEM((2,) + qkv_piece, bf16), VMEM(qkv_piece, bf16)]
        + [VMEM((2,) + piece, bf16), VMEM((2,) + piece, bf16), VMEM(piece, bf16)]
        + [VMEM((2, n // 2, shard, width), bf16), DMA((5,))]
        + pair_sems()
        + ring_sems()
        + pair_sems()
        + seq_sems()
        + pair_sems()
        + seq_sems()
        + ring_sems(),
        5,
    )
    col_sum = col_sum.astype(f32)

    def own_columns(t):
        return t.reshape(n, shard, SEQ, ff_own).transpose(1, 2, 0, 3).reshape(shard, SEQ * n * ff_own)

    raw_gate, raw_up = own_columns(col_sum[..., :ff_mine]), own_columns(col_sum[..., ff_mine:])
    qkv_sum = qkv_sum.astype(f32)
    raw_q = qkv_sum[..., :head].transpose(1, 0, 2).reshape(shard, H * head)

    def kv_sum(t):
        return t.reshape(KVH, groups, shard, head).sum(axis=1).transpose(1, 0, 2).reshape(shard, KVH * head)

    raw_k, raw_v = kv_sum(qkv_sum[..., head : 2 * head]), kv_sum(qkv_sum[..., 2 * head :])
    grad_gain_one = jnp.sum(raw_q * wq, axis=1) + jnp.sum(raw_k * wk, axis=1) + jnp.sum(raw_v * wv, axis=1)
    grad_gain_two = jnp.sum(raw_gate * wg, axis=1) + jnp.sum(raw_up * wu, axis=1)
    return (
        output,
        grad_tokens[None],
        grad_gain_one,
        raw_q * gain_one,
        raw_k * gain_one,
        raw_v * gain_one,
        out_grad,
        grad_gain_two,
        raw_gate * gain_two,
        raw_up * gain_two,
        down_sum.astype(f32),
    )


def solution(mesh):
    placed = (
        P("seq", "ctx", None),
        P("seq", "ctx", None),
        P(("seq", "ctx")),
        P(("seq", "ctx"), None),
        P(("seq", "ctx"), None),
        P(("seq", "ctx"), None),
        P(("seq", "ctx"), None),
        P(("seq", "ctx")),
        P(("seq", "ctx"), None),
        P(("seq", "ctx"), None),
        P(("seq", "ctx"), None),
        P("seq", None),
        P("seq", None),
    )
    fits = mesh.shape["ctx"] == H and mesh.shape["seq"] == 4
    chosen = ring_device if fits else general_device
    return jax.shard_map(
        chosen,
        mesh=mesh,
        in_specs=placed,
        out_specs=(
            P("seq", "ctx", None),
            P("seq", "ctx", None),
            P(("seq", "ctx")),
            P(("seq", "ctx"), None),
            P(("seq", "ctx"), None),
            P(("seq", "ctx"), None),
            P(("seq", "ctx"), None),
            P(("seq", "ctx")),
            P(("seq", "ctx"), None),
            P(("seq", "ctx"), None),
            P(("seq", "ctx"), None),
        ),
        check_vma=False,
    )
```

```python
import functools
import math

import jax
import jax.numpy as jnp
import numpy as np
from jax import lax
from jax.experimental import pallas as pl
from jax.experimental.pallas import tpu as pltpu
from jax.sharding import PartitionSpec as P

H = 8
KVH = 4
HDIM = 256
DOCS = 4


EPSILON = 1e-06
THETA = 1000042.0
NEG_FILL = -1e30


def slot_positions(pair_row, half_rows, pair_count):
    offsets = jnp.arange(half_rows, dtype=jnp.int32)
    low_slots = pair_row[:, None] * half_rows + offsets[None, :]
    high_slots = (2 * pair_count - 1 - pair_row)[:, None] * half_rows + offsets[None, :]
    return jnp.concatenate([low_slots, high_slots], axis=1).reshape(-1)


def rotary_tables(positions, head_dim):
    half_dim = head_dim // 2
    frequency = THETA ** (-(jnp.arange(half_dim, dtype=jnp.float32) * 2.0 / head_dim))
    angles = positions.astype(jnp.float32)[:, None] * frequency[None, :]
    return (jnp.cos(angles)[:, None, :], jnp.sin(angles)[:, None, :])


def rotary(tensor, table_cos, table_sin):
    half_dim = tensor.shape[-1] // 2
    lead_half = tensor[..., :half_dim]
    tail_half = tensor[..., half_dim:]
    return jnp.concatenate(
        [
            lead_half * table_cos - tail_half * table_sin,
            tail_half * table_cos + lead_half * table_sin,
        ],
        axis=-1,
    )


def rms_scale(tensor):
    return lax.rsqrt(jnp.mean(tensor * tensor, axis=-1, keepdims=True) + EPSILON)


def rms_backward(tensor, scale_rows, gain_full, grad_rows):
    weighted = gain_full * grad_rows
    inner_mean = jnp.mean(weighted * tensor, axis=-1, keepdims=True)
    return scale_rows * weighted - tensor * (scale_rows * scale_rows * scale_rows) * inner_mean


def contract_rows(first_mat, second_mat):
    return lax.dot_general(
        first_mat, second_mat, (((0,), (0,)), ((), ())), preferred_element_type=jnp.float32
    )


def contract_cols(first_mat, second_mat):
    return lax.dot_general(
        first_mat, second_mat, (((1,), (1,)), ((), ())), preferred_element_type=jnp.float32
    )


def attention_weights(gain_attn, gain_mlp, w_query, w_key, w_value, w_out):
    return (
        lax.all_gather(gain_attn, ("seq", "ctx"), axis=0, tiled=True),
        lax.all_gather(gain_mlp, ("seq", "ctx"), axis=0, tiled=True),
        lax.all_gather(w_query, ("seq", "ctx"), axis=0, tiled=True),
        lax.all_gather(w_key, ("seq", "ctx"), axis=0, tiled=True),
        lax.all_gather(w_value, ("seq", "ctx"), axis=0, tiled=True),
        lax.all_gather(w_out, ("seq", "ctx"), axis=0, tiled=True),
    )


def mlp_weights(w_gate, w_up, w_down):
    return (
        lax.all_gather(w_gate, ("seq", "ctx"), axis=0, tiled=True),
        lax.all_gather(w_up, ("seq", "ctx"), axis=0, tiled=True),
        lax.all_gather(w_down, ("seq", "ctx"), axis=0, tiled=True),
    )


def reduce_grads(grad_one, grad_two, grad_three):
    seq_count = lax.axis_size("seq")
    grad_one = grad_one.reshape((seq_count, grad_one.shape[0] // seq_count) + grad_one.shape[1:])
    grad_two = grad_two.reshape((seq_count, grad_two.shape[0] // seq_count) + grad_two.shape[1:])
    grad_three = grad_three.reshape(
        (seq_count, grad_three.shape[0] // seq_count) + grad_three.shape[1:]
    )
    grad_one, grad_two, grad_three = (
        lax.psum_scatter(
            grad_one.astype(jnp.bfloat16), "ctx", scatter_dimension=1, tiled=True
        ).astype(jnp.float32),
        lax.psum_scatter(
            grad_two.astype(jnp.bfloat16), "ctx", scatter_dimension=1, tiled=True
        ).astype(jnp.float32),
        lax.psum_scatter(
            grad_three.astype(jnp.bfloat16), "ctx", scatter_dimension=1, tiled=True
        ).astype(jnp.float32),
    )
    grad_one, grad_two, grad_three = (
        lax.psum_scatter(
            grad_one.astype(jnp.bfloat16), "seq", scatter_dimension=0, tiled=True
        ).astype(jnp.float32),
        lax.psum_scatter(
            grad_two.astype(jnp.bfloat16), "seq", scatter_dimension=0, tiled=True
        ).astype(jnp.float32),
        lax.psum_scatter(
            grad_three.astype(jnp.bfloat16), "seq", scatter_dimension=0, tiled=True
        ).astype(jnp.float32),
    )
    return (grad_one[0], grad_two[0], grad_three[0])


def general_device(
    tokens,
    cotangent,
    gain_attn,
    w_query,
    w_key,
    w_value,
    w_out,
    gain_mlp,
    w_gate,
    w_up,
    w_down,
    pair_order,
    segments,
):
    pair_count = lax.axis_size("ctx")
    my_index = lax.axis_index("ctx")
    row_count = tokens.shape[1]
    half_rows = row_count // 2
    seq_len = segments.shape[1]
    head_groups = H // KVH
    score_scale = HDIM ** (-0.5)
    key_rows = math.gcd(seq_len, 512)
    key_steps = seq_len // key_rows
    key_pos = slot_positions(pair_order[0], half_rows, pair_count)
    key_doc = jnp.take(segments[0], key_pos)
    query_pos = lax.dynamic_slice_in_dim(key_pos, my_index * row_count, row_count)
    query_doc = lax.dynamic_slice_in_dim(key_doc, my_index * row_count, row_count)
    rot_cos, rot_sin = rotary_tables(query_pos, HDIM)
    gain_one, gain_two, query_w, key_w, value_w, out_w = attention_weights(
        gain_attn, gain_mlp, w_query, w_key, w_value, w_out
    )
    gain_one = gain_one.astype(jnp.float32)
    gain_two = gain_two.astype(jnp.float32)
    inputs = tokens[0].astype(jnp.float32)
    scale_one = rms_scale(inputs)
    normed = (inputs * scale_one * gain_one).astype(jnp.bfloat16)
    query_proj = jnp.dot(normed, query_w, preferred_element_type=jnp.float32).reshape(
        row_count, H, HDIM
    )
    key_proj = jnp.dot(normed, key_w, preferred_element_type=jnp.float32).reshape(
        row_count, KVH, HDIM
    )
    value_proj = jnp.dot(normed, value_w, preferred_element_type=jnp.float32)
    query_rot = (
        rotary(query_proj, rot_cos, rot_sin)
        .astype(jnp.bfloat16)
        .reshape(row_count, KVH, head_groups, HDIM)
    )
    key_rot = rotary(key_proj, rot_cos, rot_sin).astype(jnp.bfloat16).reshape(row_count, KVH * HDIM)
    value_low = value_proj.astype(jnp.bfloat16)
    key_width = key_rot.shape[1]
    key_all, value_all = (
        lax.all_gather(key_rot, "ctx", axis=0, tiled=True),
        lax.all_gather(value_low, "ctx", axis=0, tiled=True),
    )
    pos_blocks = key_pos.reshape(key_steps, key_rows)
    doc_blocks = key_doc.reshape(key_steps, key_rows)

    def scores_of(key_blk, pos_blk, doc_blk):
        key_heads = key_blk.reshape(key_rows, KVH, HDIM)
        raw_scores = (
            jnp.einsum("qkgd,tkd->kgqt", query_rot, key_heads, preferred_element_type=jnp.float32)
            * score_scale
        )
        visible = (doc_blk[None, :] == query_doc[:, None]) & (
            pos_blk[None, :] <= query_pos[:, None]
        )
        return (raw_scores, visible[None, None])

    def first_pass(carried, step_data):
        running_top, running_sum = carried
        key_blk, pos_blk, doc_blk = step_data
        raw_scores, visible = scores_of(key_blk, pos_blk, doc_blk)
        masked = jnp.where(visible, raw_scores, NEG_FILL)
        new_top = jnp.maximum(running_top, jnp.max(masked, axis=-1))
        added = jnp.sum(jnp.where(visible, jnp.exp(masked - new_top[..., None]), 0.0), axis=-1)
        return ((new_top, running_sum * jnp.exp(running_top - new_top) + added), None)

    start_top = jnp.full((KVH, head_groups, row_count), NEG_FILL, jnp.float32)
    start_sum = jnp.zeros((KVH, head_groups, row_count), jnp.float32)
    key_stack = key_all.reshape(key_steps, key_rows, key_width)
    value_stack = value_all.reshape(key_steps, key_rows, key_width)
    (final_top, final_sum), _ = lax.scan(
        first_pass, (start_top, start_sum), (key_stack, pos_blocks, doc_blocks)
    )
    log_total = final_top + jnp.log(final_sum)

    def second_pass(carried, step_data):
        acc_out, acc_rest = carried
        key_blk, value_blk, pos_blk, doc_blk = step_data
        raw_scores, visible = scores_of(key_blk, pos_blk, doc_blk)
        prob_full = jnp.where(visible, jnp.exp(raw_scores - log_total[..., None]), 0.0)
        prob_low = prob_full.astype(jnp.bfloat16)
        prob_rest = (prob_full - prob_low.astype(jnp.float32)).astype(jnp.bfloat16)
        value_heads = value_blk.reshape(key_rows, KVH, HDIM)
        acc_out = acc_out + jnp.einsum(
            "kgqt,tkd->qkgd", prob_low, value_heads, preferred_element_type=jnp.float32
        )
        acc_rest = acc_rest + jnp.einsum(
            "kgqt,tkd->qkgd", prob_rest, value_heads, preferred_element_type=jnp.float32
        )
        return ((acc_out, acc_rest), None)

    start_acc = jnp.zeros((row_count, KVH, head_groups, HDIM), jnp.float32)
    (attended, attended_rest), _ = lax.scan(
        second_pass, (start_acc, start_acc), (key_stack, value_stack, pos_blocks, doc_blocks)
    )
    exact_out = attended + attended_rest
    out_low = attended.reshape(row_count, H * HDIM).astype(jnp.bfloat16)
    hidden = inputs + jnp.dot(out_low, out_w, preferred_element_type=jnp.float32)
    scale_two = rms_scale(hidden)
    normed_two = (hidden * scale_two * gain_two).astype(jnp.bfloat16)
    grad_out = cotangent[0]
    gate_w, up_w, down_w = mlp_weights(w_gate, w_up, w_down)
    gate_proj = jnp.dot(normed_two, gate_w, preferred_element_type=jnp.float32)
    up_proj = jnp.dot(normed_two, up_w, preferred_element_type=jnp.float32)
    gate_sig = jax.nn.sigmoid(gate_proj)
    active = gate_proj * gate_sig
    middle = (active * up_proj).astype(jnp.bfloat16)
    result = hidden + jnp.dot(middle, down_w, preferred_element_type=jnp.float32)
    output = result.astype(jnp.bfloat16)[None]
    gate_w, up_w, down_w = mlp_weights(w_gate, w_up, w_down)
    grad_mid = contract_cols(grad_out, down_w)
    grad_gate = (grad_mid * up_proj * gate_sig * (1.0 + gate_proj * (1.0 - gate_sig))).astype(
        jnp.bfloat16
    )
    grad_up = (grad_mid * active).astype(jnp.bfloat16)
    grad_norm_two = contract_cols(grad_gate, gate_w) + contract_cols(grad_up, up_w)
    grad_gain_two = jnp.sum(grad_norm_two * hidden * scale_two, axis=0)
    grad_hidden = grad_out.astype(jnp.float32) + rms_backward(
        hidden, scale_two, gain_two, grad_norm_two
    )
    grad_w_gate = contract_rows(normed_two, grad_gate)
    grad_w_up = contract_rows(normed_two, grad_up)
    shard_gain_two, shard_gate, shard_up = reduce_grads(grad_gain_two, grad_w_gate, grad_w_up)
    gain_one, gain_two, query_w, key_w, value_w, out_w = attention_weights(
        gain_attn, gain_mlp, w_query, w_key, w_value, w_out
    )
    gain_one = gain_one.astype(jnp.float32)
    grad_branch = grad_hidden.astype(jnp.bfloat16)
    grad_w_out = contract_rows(out_low, grad_branch)
    grad_att = (
        contract_cols(grad_branch, out_w)
        .astype(jnp.bfloat16)
        .reshape(row_count, KVH, head_groups, HDIM)
    )
    row_delta = jnp.transpose(jnp.sum(grad_att.astype(jnp.float32) * exact_out, axis=-1), (1, 2, 0))
    key_back, value_back = (key_all, value_all)

    def backward_step(grad_query, step_data):
        key_blk, value_blk, pos_blk, doc_blk = step_data
        raw_scores, visible = scores_of(key_blk, pos_blk, doc_blk)
        prob_full = jnp.where(visible, jnp.exp(raw_scores - log_total[..., None]), 0.0)
        prob_low = prob_full.astype(jnp.bfloat16)
        key_heads = key_blk.reshape(key_rows, KVH, HDIM)
        value_heads = value_blk.reshape(key_rows, KVH, HDIM)
        grad_value_blk = jnp.einsum(
            "kgqt,qkgd->tkd", prob_low, grad_att, preferred_element_type=jnp.float32
        )
        grad_probs = jnp.einsum(
            "qkgd,tkd->kgqt", grad_att, value_heads, preferred_element_type=jnp.float32
        )
        grad_scores = (prob_full * (grad_probs - row_delta[..., None])).astype(jnp.bfloat16)
        grad_query = (
            grad_query
            + jnp.einsum(
                "kgqt,tkd->qkgd", grad_scores, key_heads, preferred_element_type=jnp.float32
            )
            * score_scale
        )
        grad_key_blk = (
            jnp.einsum("kgqt,qkgd->tkd", grad_scores, query_rot, preferred_element_type=jnp.float32)
            * score_scale
        )
        return (
            grad_query,
            (
                grad_key_blk.reshape(key_rows, key_width),
                grad_value_blk.reshape(key_rows, key_width),
            ),
        )

    back_keys = key_back.reshape(key_steps, key_rows, key_width)
    back_values = value_back.reshape(key_steps, key_rows, key_width)
    grad_query, (grad_key_steps, grad_value_steps) = lax.scan(
        backward_step, start_acc, (back_keys, back_values, pos_blocks, doc_blocks)
    )
    grad_key_all = grad_key_steps.reshape(seq_len, key_width)
    grad_value_all = grad_value_steps.reshape(seq_len, key_width)
    grad_key_own, grad_value_own = (
        lax.psum_scatter(
            grad_key_all.astype(jnp.bfloat16), "ctx", scatter_dimension=0, tiled=True
        ).astype(jnp.float32),
        lax.psum_scatter(
            grad_value_all.astype(jnp.bfloat16), "ctx", scatter_dimension=0, tiled=True
        ).astype(jnp.float32),
    )
    grad_query = (
        rotary(grad_query.reshape(row_count, H, HDIM), rot_cos, -rot_sin)
        .astype(jnp.bfloat16)
        .reshape(row_count, H * HDIM)
    )
    grad_key = (
        rotary(grad_key_own.reshape(row_count, KVH, HDIM), rot_cos, -rot_sin)
        .astype(jnp.bfloat16)
        .reshape(row_count, key_width)
    )
    grad_value = grad_value_own.astype(jnp.bfloat16)
    grad_w_query = contract_rows(normed, grad_query)
    grad_w_key = contract_rows(normed, grad_key)
    grad_w_value = contract_rows(normed, grad_value)
    grad_normed = (
        contract_cols(grad_query, query_w)
        + contract_cols(grad_key, key_w)
        + contract_cols(grad_value, value_w)
    )
    grad_gain_one = jnp.sum(grad_normed * inputs * scale_one, axis=0)
    grad_tokens = grad_hidden + rms_backward(inputs, scale_one, gain_one, grad_normed)
    grad_w_down = contract_rows(middle, grad_out)
    shard_gain_one, shard_out, shard_down = reduce_grads(grad_gain_one, grad_w_out, grad_w_down)
    shard_query, shard_key, shard_value = reduce_grads(grad_w_query, grad_w_key, grad_w_value)
    return (
        output,
        grad_tokens[None],
        shard_gain_one,
        shard_query,
        shard_key,
        shard_value,
        shard_out,
        shard_gain_two,
        shard_gate,
        shard_up,
        shard_down,
    )


MESH = pl.DeviceIdType.MESH
VMEM = pltpu.VMEM
RING = 8
SEQ = 4


class Place:
    def __init__(self):
        self.c = lax.axis_index("ctx")
        self.s = lax.axis_index("seq")
        self.z, self.x = self.c // 2, lax.rem(self.c, 2)
        self.p = self.z + self.x * (7 - 2 * self.z)
        self.up, self.down = {"ctx": self.c + 2}, {"ctx": self.c - 2}
        self.side = {"ctx": self.c + 1 - 2 * self.x}
        self.right = {"ctx": self.at(1)}
        self.left = {"ctx": self.at(-1)}
        self.s_core = self.s + 1 - 2 * lax.rem(self.s, 2)
        self.s_far = lax.rem(self.s + 2, 4)
        self.s_both = 3 - self.s
        self.core_peer = {"seq": self.s_core}
        self.far_peer = {"seq": self.s_far}

    def at(self, offset):
        q = lax.rem(self.p + offset + 2 * RING, RING)
        return 2 * q + (q // 4) * (15 - 4 * q)

    def peers(self):
        return [{"ctx": lax.rem(self.c + k, RING)} for k in range(1, RING)]


def greet(devices):
    barrier = pltpu.get_barrier_semaphore()
    for device in devices:
        pl.semaphore_signal(barrier, inc=1, device_id=device, device_id_type=MESH)
    pl.semaphore_wait(barrier, len(devices))


def remote(src, dst, send_sem, recv_sem, device):
    return pltpu.make_async_remote_copy(
        src_ref=src, dst_ref=dst, send_sem=send_sem, recv_sem=recv_sem, device_id=device, device_id_type=MESH
    )


def arrived(ref, sems, index, device):
    remote(ref, ref, sems[0].at[index], sems[1].at[index], device).wait_recv()


def together(*flows):
    live = list(flows)
    while live:
        live = [flow for flow in live if next(flow, "end") != "end"]


def ring_sems():
    return [pltpu.SemaphoreType.DMA((2, RING // 2, 2))] * 2


def slot(offset):
    return 0 if offset == 0 else min(RING - 1, 2 * offset if offset > 0 else -2 * offset - 1)


class Rows:
    def __init__(self, ref, rows):
        self.ref, self.rows = ref, rows

    def here(self, offset):
        return self.ref.at[pl.ds(slot(offset) * self.rows, self.rows)]

    def there(self, offset, d):
        return self.here(offset - 1 if d == 0 else offset + 1)


class Owners:
    def __init__(self, ref, place):
        self.ref, self.place = ref, place

    def here(self, offset):
        return self.ref.at[self.place.at(offset)]

    def there(self, offset, d):
        return self.here(offset)


def ring_gather(own, blocks, sems, place):
    half = own.shape[0] // 2
    steps = RING // 2
    sent = []

    def part(ref, j):
        return ref.at[pl.ds(j * half, half)]

    def wait_for(d, s, j):
        offset = -(s + 1) if d == 0 else s + 1
        arrived(part(blocks.here(offset), j), sems, (d, s, j), place.right if d == 0 else place.left)

    for s in range(steps):
        for j in range(2):
            for d in range(2):
                if s == steps - 1 and j != d:
                    continue
                if s > 0:
                    wait_for(d, s - 1, j)
                offset = -s if d == 0 else s
                copy = remote(
                    part(own if s == 0 else blocks.here(offset), j),
                    part(blocks.there(offset, d), j),
                    sems[0].at[d, s, j],
                    sems[1].at[d, s, j],
                    place.right if d == 0 else place.left,
                )
                copy.start()
                sent.append(copy)
            yield
    for d in range(2):
        wait_for(d, steps - 2, 1 - d)
    yield
    for d in range(2):
        wait_for(d, steps - 1, d)
    yield
    for copy in sent:
        copy.wait_send()


class RingSum:
    def __init__(self, slots, sems, place):
        self.slots, self.sems, self.sent = slots, sems, []
        self.sides = (place.right, place.left)
        self.half = slots.shape[2] // 2

    def rows(self, ref, j):
        return ref.at[pl.ds(j * self.half, self.half)]

    def send(self, d, s, j, source):
        to = self.rows(self.slots.at[d, s], j)
        copy = remote(source, to, self.sems[0].at[d, s, j], self.sems[1].at[d, s, j], self.sides[d])
        copy.start()
        self.sent.append(copy)

    def held(self, d, s, j):
        ref = self.rows(self.slots.at[d, s], j)
        arrived(ref, self.sems, (d, s, j), self.sides[d])
        return ref

    def first(self, part):
        for d in range(2):
            self.send(d, 0, d, self.rows(part, d))

    def relay(self, s, parts):
        for j in range(2):
            for d in range(2):
                source = self.rows(parts[d], j)
                if s > 1 or j == d:
                    held = self.held(d, s - 1, j)
                    add_into(held, source)
                    source = held
                self.send(d, s, j, source)

    def last(self, part, out):
        for j in range(2):
            held = [self.held(d, RING // 2 - 1, j) for d in range(2)]
            sum_of_three(self.rows(out, j), self.rows(part, j), *held)

    def end(self):
        for copy in self.sent:
            copy.wait_send()


def ring_scatter(blocks, out, slots, sems, place):
    ring = RingSum(slots, sems, place)
    ring.first(blocks.here(RING // 2))
    yield
    for s in range(1, RING // 2):
        k = RING // 2 - s
        ring.relay(s, (blocks.here(k), blocks.here(-k)))
        yield
    ring.last(blocks.here(0), out)
    ring.end()
    yield


def pair_sems():
    return [pltpu.SemaphoreType.DMA((RING,))] * 2


OFFSETS = (1, -1, 2, -2, 3, -3, 4)


def exchange(pieces, here, sems, place, group=RING):
    for i in range(0, len(OFFSETS), group):
        for k in OFFSETS[i : i + group]:
            at = slot(k)
            for src, dst in pieces(k):
                remote(src, dst, sems[0].at[at], sems[1].at[at], {"ctx": place.at(k)}).start()
        yield
    for k in OFFSETS:
        arrived(here(k), sems, RING - 1 if k == RING // 2 else slot(-k), {"ctx": place.at(k)})
    for k in OFFSETS:
        remote(here(k), here(k), sems[0].at[slot(k)], sems[1].at[slot(k)], {"ctx": place.at(k)}).wait_send()
    yield


def by_owner(src, dst, sems, place, group=RING):
    return exchange(lambda k: [(src.at[place.at(k)], dst.at[place.c])], lambda k: dst.at[place.at(k)], sems, place, group)


def block_at(i, size):
    return pl.ds(pl.multiple_of(i * size, size), size)


class ByOwner:
    def __init__(self, ref, rows):
        self.ref, self.rows = ref, rows

    def owner(self, c, side=None):
        return self.ref.at[block_at(c, self.rows)]


class ByArrival:
    def __init__(self, ref, rows, place):
        self.ref, self.rows, self.place = ref, rows, place

    def owner(self, c, side="here"):
        far = {"here": 0, "up": 2, "down": -2, "side": 1 - 2 * self.place.x}[side]
        mine = self.place.c + far
        z, x = mine // 2, lax.rem(mine, 2)
        p = z + x * (7 - 2 * z)
        z, x = c // 2, lax.rem(c, 2)
        k = lax.rem(z + x * (7 - 2 * z) - p + 2 * RING, RING)
        late = jnp.where(k == RING // 2, RING - 1, 2 * (RING - k) - 1)
        return self.ref.at[block_at(jnp.where(k < RING // 2, 2 * k, late), self.rows)]


def grid_sems():
    return [pltpu.SemaphoreType.DMA((2, 3))] * 2 + [pltpu.SemaphoreType.DMA((4,))] * 2


def grid_gather(own, blocks, sems, place):
    z_sems, x_sems = sems[:2], sems[2:]
    z, x = place.z, place.x
    sent = []

    def send(when, src, c, side, pair, index, device):
        copy = remote(src, blocks.owner(c, side), pair[0].at[index], pair[1].at[index], device)
        pl.when(when)(copy.start)
        sent.append((when, copy))

    def across(when, src, line):
        send(when, src, 2 * line + x, "side", x_sems, line, place.side)

    send(z < 3, own, place.c, "up", z_sems, (0, 0), place.up)
    send(z > 0, own, place.c, "down", z_sems, (1, 0), place.down)
    across(z >= 0, own, z)
    yield
    for hop in range(1, 4):
        for d, (line, here, further) in enumerate(((z - hop, z >= hop, z < 3), (z + hop, z <= 3 - hop, z > 0))):
            index = 2 * line + x
            ref = blocks.owner(jnp.clip(index, 0, RING - 1))
            device = (place.down, place.up)[d]

            @pl.when(here)
            def _():
                arrived(ref, z_sems, (d, hop - 1), device)

            if hop < 3:
                send(here & further, ref, jnp.clip(index, 0, RING - 1), ("up", "down")[d], z_sems, (d, hop), (place.up, place.down)[d])
            across_line = jnp.clip(line, 0, 3)
            send(here, ref, 2 * across_line + x, "side", x_sems, across_line, place.side)
        yield
    for line in range(4):
        arrived(blocks.owner(2 * line + 1 - x), x_sems, line, place.side)
    for when, copy in sent:
        pl.when(when)(copy.wait_send)
    yield


def grid_sum_sems():
    return [pltpu.SemaphoreType.DMA((4,))] * 2 + [pltpu.SemaphoreType.DMA((2, 4))] * 2


class GridSum:
    def __init__(self, part, over, line, sems, place):
        self.part, self.over, self.line, self.place = part, over, line, place
        self.x_sems, self.z_sems = sems[:2], sems[2:]
        self.rows = over.shape[1]
        self.sent = []

    def plane(self, i):
        z = self.place.z
        inner = jnp.where((z == 1) | (z == 2), 1, 0)
        plain, mid = (3, 2, 1, 0)[i], (3, 0, 2, 1)[i]
        order = plain + inner * (mid - plain)
        return jnp.where(z < 2, order, 3 - order)

    def send(self, when, src, dst, pair, index, device):
        copy = remote(src, dst, pair[0].at[index], pair[1].at[index], device)
        pl.when(when)(copy.start)
        self.sent.append((when, copy))

    def mine(self, z, x):
        return self.part.at[block_at(2 * z + x, self.rows)]

    def across(self, i):
        z = self.plane(i)
        self.send(self.place.z >= 0, self.mine(z, 1 - self.place.x), self.over.at[z], self.x_sems, z, self.place.side)

    def along(self, i):
        z, me = self.plane(i), self.place.z
        held = self.over.at[z]
        arrived(held, self.x_sems, z, self.place.side)
        add_into(held, self.mine(z, self.place.x))
        for d, (when, more, source, device) in enumerate(
            (
                (z > me, me > 0, self.place.down, self.place.up),
                (z < me, me < 3, self.place.up, self.place.down),
            )
        ):

            @pl.when(when & more)
            def _():
                arrived(self.line.at[d, z], self.z_sems, (d, z), source)
                add_into(held, self.line.at[d, z])

            self.send(when, held, self.line.at[d, z], self.z_sems, (d, z), device)

    def last(self, out):
        z = self.place.z
        held = self.over.at[z]
        arrived(held, self.x_sems, z, self.place.side)
        add_to(out, held, self.mine(z, self.place.x))
        for d, (when, source) in enumerate(((z > 0, self.place.down), (z < 3, self.place.up))):

            @pl.when(when)
            def _():
                arrived(self.line.at[d, z], self.z_sems, (d, z), source)
                add_to(out, out, self.line.at[d, z])

    def end(self):
        for when, copy in self.sent:
            pl.when(when)(copy.wait_send)


def pairs_of(sems):
    return [sems[i : i + 2] for i in range(0, len(sems), 2)]


def seq_sems():
    return [pltpu.SemaphoreType.DMA((3,))] * 2


def seq_gather(own, buf, sems, place):
    first = remote(own, buf.at[place.s], sems[0].at[0], sems[1].at[0], place.far_peer)
    second = remote(own, buf.at[place.s], sems[0].at[1], sems[1].at[1], place.core_peer)
    first.start()
    second.start()
    yield
    arrived(buf.at[place.s_far], sems, 0, place.far_peer)
    third = remote(buf.at[place.s_far], buf.at[place.s_far], sems[0].at[2], sems[1].at[2], place.core_peer)
    third.start()
    yield
    arrived(buf.at[place.s_core], sems, 1, place.core_peer)
    arrived(buf.at[place.s_both], sems, 2, place.core_peer)
    for copy in (first, second, third):
        copy.wait_send()
    yield


def sum_of_three(dst, *terms):
    step = math.gcd(dst.shape[0], 16)

    @pl.loop(0, dst.shape[0] // step)
    def _(i):
        at = pl.ds(pl.multiple_of(i * step, step), step)
        one, two, three = (term[at].astype(jnp.float32) for term in terms)
        dst[at] = one + two + three


def add_to(dst, one, two):
    step = math.gcd(dst.shape[0], 16)

    @pl.loop(0, dst.shape[0] // step)
    def _(i):
        at = pl.ds(pl.multiple_of(i * step, step), step)
        dst[at] = one[at].astype(jnp.float32) + two[at].astype(jnp.float32)


def add_into(dst, other):
    rows = dst.shape[0]
    step = math.gcd(rows, 16)

    @pl.loop(0, rows // step)
    def _(i):
        at = pl.ds(pl.multiple_of(i * step, step), step)
        dst[at] = (dst[at].astype(jnp.float32) + other[at].astype(jnp.float32)).astype(dst.dtype)


class SeqSum:
    def __init__(self, grad, block, near, far, sems, place):
        self.grad, self.block, self.near_ref, self.far, self.sems, self.place = grad, block, near, far, sems, place
        self.low, self.row = lax.rem(place.s, 2), place.s // 2
        self.sent = []

    def send(self, src, dst, i, device):
        copy = remote(src, dst, self.sems[0].at[i], self.sems[1].at[i], device)
        copy.start()
        self.sent.append(copy)

    def near(self, i):
        r = (1 - self.row, self.row)[i]
        self.grad(r * 2 + 1 - self.low, self.block.at[i], False)
        self.send(self.block.at[i], self.near_ref.at[i], i, self.place.core_peer)

    def across(self):
        arrived(self.near_ref.at[0], self.sems, 0, self.place.core_peer)
        self.grad((1 - self.row) * 2 + self.low, self.near_ref.at[0], True)
        self.send(self.near_ref.at[0], self.far, 2, self.place.far_peer)

    def own(self):
        arrived(self.near_ref.at[1], self.sems, 1, self.place.core_peer)
        self.grad(self.row * 2 + self.low, self.near_ref.at[1], True)

    def last(self):
        arrived(self.far, self.sems, 2, self.place.far_peer)
        add_into(self.far, self.near_ref.at[1])

    def end(self):
        for copy in self.sent:
            copy.wait_send()


def call(body, outs, args, spaces, out_spaces, scratch, ident):
    return pl.pallas_call(
        body,
        out_shape=outs,
        in_specs=[pl.BlockSpec(memory_space=space) for space in spaces],
        out_specs=[pl.BlockSpec(memory_space=space) for space in out_spaces],
        scratch_shapes=scratch,
        compiler_params=pltpu.CompilerParams(
            collective_id=ident, has_side_effects=True, vmem_limit_bytes=63 * 1024 * 1024
        ),
    )(*args)


def shaped(shape, dtype=jnp.bfloat16):
    return jax.ShapeDtypeStruct(shape, dtype)


def dot(a, b, at=(1, 0)):
    return lax.dot_general(a, b, (((at[0],), (at[1],)), ((), ())), preferred_element_type=jnp.float32)


def chunks(total, size, body):
    @pl.loop(0, total // size)
    def _(i):
        body(pl.ds(pl.multiple_of(i * size, size), size))


def turned(t, cos, sin, sign):
    half = t.shape[1] // 2
    a, b = t[:, :half], t[:, half:]
    return jnp.concatenate([a * cos - sign * b * sin, b * cos + sign * a * sin], axis=-1)


def probabilities(q, k, pos_rows, start_rows, pos_cols):
    scores = dot(q, k, (1, 1)) * HDIM ** (-0.5)
    visible = (pos_cols >= start_rows) & (pos_cols <= pos_rows)
    scores = jnp.where(visible, scores, NEG_FILL)
    weight = jnp.exp(scores - jnp.max(scores, axis=-1, keepdims=True))
    return weight / jnp.sum(weight, axis=-1, keepdims=True)


def place_rows(pairs, segments, block_cos, block_sin, row_cos, row_sin, cos, sin, pos_rows, start_rows, pos_cols):
    f32 = jnp.float32
    half = row_cos.shape[0]
    bounds = [
        jnp.sum(jnp.where(segments[...] < d, 1.0, 0.0).astype(f32), axis=1, keepdims=True) for d in range(1, DOCS)
    ]
    numbers = lax.broadcasted_iota(jnp.int32, block_cos.shape, 0)
    for c in range(RING):
        blocks = (pairs[0, c], 2 * RING - 1 - pairs[0, c])
        lanes = lax.broadcasted_iota(jnp.int32, (1, 2 * half), 1)
        low = blocks[0] * half + lanes
        pos_cols[:, pl.ds(c * 2 * half, 2 * half)] = jnp.where(lanes < half, low, blocks[1] * half + lanes - half).astype(f32)
        for j, block in enumerate(blocks):
            at = pl.ds((2 * c + j) * half, half)
            near_cos = jnp.sum(jnp.where(numbers == block, block_cos[...], 0.0), axis=0, keepdims=True)
            near_sin = jnp.sum(jnp.where(numbers == block, block_sin[...], 0.0), axis=0, keepdims=True)
            cos[at, :] = near_cos * row_cos[...] - near_sin * row_sin[...]
            sin[at, :] = near_sin * row_cos[...] + near_cos * row_sin[...]
            pos = (block * half + lax.broadcasted_iota(jnp.int32, (half, 1), 0)).astype(f32)
            start = jnp.zeros((half, 1), f32)
            for bound in bounds:
                start = jnp.where(pos >= bound, bound, start)
            pos_rows[at, :] = pos
            start_rows[at, :] = start


def column(row):
    n = row.shape[1]
    same = lax.broadcasted_iota(jnp.int32, (n, n), 0) == lax.broadcasted_iota(jnp.int32, (n, n), 1)
    return jnp.sum(jnp.where(same, row, 0.0), axis=1, keepdims=True)


def attention_kernel(plan, x, gain_one, gain_two, pairs, segments, block_cos, block_sin, row_cos, row_sin,
                     dy, w_query, w_key, w_value, wout, w_gate, w_up, wdown,
                     hidden, hhat, ob_local, cos, sin, pos_rows, start_rows, pos_cols,
                     q_out, k_out, v_out, x_all, dy_all, wqkv_all, wout_all, wg_all, wu_own, wdown_all,
                     xhat, wq, wk, wv, wg, wu, x_v, wqkv_v, wout_v, q, k, v, ob, local, loads, *sems):
    place = Place()
    qkv_swap, qkv_seq, out_ring, out_seq, ob_swap, gate_swap, gate_seq, up_swap, down_seq = pairs_of(sems[:18])
    x_grid, dy_grid = sems[18:22], sems[22:26]
    bf16, f32 = jnp.bfloat16, jnp.float32
    rows, width = x.shape
    head, shard = ob.shape[1], wout.shape[0]
    groups = H // KVH
    fetch = [
        pltpu.make_async_copy(src, dst, loads.at[i])
        for i, (src, dst) in enumerate(((w_query, wq), (w_key, wk), (w_value, wv), (w_gate, wg), (w_up, wu)))
    ]
    for copy in fetch:
        copy.start()
    keep = [
        pltpu.make_async_copy(wout, wout_all.at[place.s, place.c], local.at[0]),
        pltpu.make_async_copy(wdown, wdown_all.at[place.s], local.at[1]),
        pltpu.make_async_copy(dy, ByArrival(dy_all, rows, place).owner(place.c), local.at[2]),
    ]
    for copy in keep:
        copy.start()

    def normed(at):
        t = x[at, :].astype(f32)
        xhat[at, :] = (t * lax.rsqrt(jnp.mean(t * t, axis=-1, keepdims=True) + EPSILON)).astype(bf16)

    chunks(rows, 16, normed)
    greet(place.peers() + [place.core_peer, place.far_peer])
    down_w = seq_gather(wdown, wdown_all, down_seq, place)
    x_blocks, dy_blocks = ByOwner(x_all, rows), ByArrival(dy_all, rows, place)

    def out_flow():
        yield from ring_gather(wout, Owners(wout_all.at[place.s], place), out_ring, place)
        keep[0].wait()
        yield from seq_gather(wout_all.at[place.s], wout_all, out_seq, place)

    out_w = out_flow()

    def scale(ref, gain):
        def body(cols):
            ref[:, cols] = (ref[:, cols].astype(f32) * gain).astype(bf16)

        chunks(ref.shape[1], 512, body)

    for copy in fetch[:3]:
        copy.wait()
    gain = column(gain_one[...].astype(f32))
    for ref in (wq, wk, wv):
        scale(ref, gain)

    def spread(pieces, dst, i, swap, seq, group=RING):
        def to(c, into):
            cols = pieces(c)
            each = into.shape[1] // len(cols)
            return [(src, into.at[:, pl.ds(j * each, each)]) for j, src in enumerate(cols)]

        rows_of_s = dst if seq is None else dst.at[place.s]
        own = rows_of_s.at[place.c]
        for src, into in to(place.c, own):
            pltpu.make_async_copy(src, into, local.at[i]).start()
        yield from exchange(lambda o: to(place.at(o), own), lambda o: rows_of_s.at[place.at(o)], swap, place, group)
        pltpu.make_async_copy(own, own, local.at[i]).wait()
        if seq is not None:
            yield from seq_gather(rows_of_s, dst, seq, place)

    def head_columns(t):
        kv = block_at(t // groups, head)
        return [wq.at[:, block_at(t, head)], wk.at[:, kv], wv.at[:, kv]]

    def unit_columns(ref):
        own = wdown.shape[0]
        return lambda t: [ref.at[:, block_at(i * RING + t, own)] for i in range(SEQ)]

    qkv_w = spread(head_columns, wqkv_all, 3, qkv_swap, qkv_seq)
    gate_w = spread(unit_columns(wg), wg_all, 4, gate_swap, gate_seq, 2)
    up_w = spread(unit_columns(wu), wu_own, 5, up_swap, None, 2)
    x_flow = grid_gather(xhat, x_blocks, x_grid, place)
    dy_flow = grid_gather(dy, dy_blocks, dy_grid, place)
    own_x = pltpu.make_async_copy(xhat, x_blocks.owner(place.c), local.at[6])

    flows = {"q": qkv_w, "g": gate_w, "u": up_w, "d": down_w, "o": out_w, "x": x_flow, "y": dy_flow}
    mine = block_at(place.c, head)
    flows["b"] = exchange(
        lambda o: [(ob.at[block_at(place.at(o), rows)], ob_local.at[:, mine])],
        lambda o: ob_local.at[:, block_at(place.at(o), head)],
        ob_swap,
        place,
    )
    load = [pltpu.make_async_copy(x_all, x_v, loads.at[0]), pltpu.make_async_copy(wqkv_all, wqkv_v, loads.at[1])]
    saves = [pltpu.make_async_copy(src, dst, loads.at[2 + i]) for i, (src, dst) in enumerate(((q, q_out), (k, k_out), (v, v_out)))]
    load_out = pltpu.make_async_copy(wout_all, wout_v, local.at[0])

    def scale_units():
        for copy in fetch[3:]:
            copy.wait()
        gain = column(gain_two[...].astype(f32))
        scale(wg, gain)
        scale(wu, gain)

    def find_rows():
        place_rows(
            pairs, segments, block_cos, block_sin, row_cos, row_sin, cos, sin, pos_rows, start_rows, pos_cols
        )

    def load_attention():
        own_x.start()
        own_x.wait()
        for copy in load:
            copy.start()

    def project_all():
        for copy in load:
            copy.wait()

        def project(at):
            qkv = dot(x_v[at, :], wqkv_v[...].reshape(width, 3 * head))
            c, s = cos[at, :], sin[at, :]
            q[at, :] = turned(qkv[:, :head], c, s, 1.0).astype(bf16)
            k[at, :] = turned(qkv[:, head : 2 * head], c, s, 1.0).astype(bf16)
            v[at, :] = qkv[:, 2 * head :].astype(bf16)

        chunks(x_v.shape[0], 256, project)
        for copy in saves:
            copy.start()

    def attend_all():
        def attend(at):
            prob = probabilities(q[at, :], k[...], pos_rows[at, :], start_rows[at, :], pos_cols[...])
            ob[at, :] = dot(prob.astype(bf16), v[...]).astype(bf16)

        chunks(x_v.shape[0], 256, attend)
        ob_local[:, mine] = ob[block_at(place.c, rows), :]

    def finish_hidden():
        load_out.wait()

        def residual(cols):
            part = dot(ob_local[...], wout_v[:, :, :, cols].reshape(width, cols.size))
            hidden[:, cols] = x[:, cols].astype(f32) + part

        chunks(width, 256, residual)

        def normed_two(at):
            t = hidden[at, :]
            hhat[at, :] = (t * lax.rsqrt(jnp.mean(t * t, axis=-1, keepdims=True) + EPSILON)).astype(bf16)

        chunks(rows, 16, normed_two)

    works = {
        "S": scale_units, "R": find_rows, "L": load_attention, "P": project_all,
        "A": attend_all, "W": load_out.start, "H": finish_hidden,
    }
    for step in plan:
        if step in flows:
            next(flows[step], None)
        else:
            works[step]()
    for name, flow in flows.items():
        if name in plan:
            for _ in flow:
                pass
    if "P" in plan:
        for copy in saves:
            copy.wait()
    elif "L" in plan:
        for copy in load:
            copy.wait()
    if "S" not in plan:
        for copy in fetch[3:]:
            copy.wait()
    if "o" not in plan:
        keep[0].wait()
    if "W" in plan and "H" not in plan:
        load_out.wait()
    keep[1].wait()
    keep[2].wait()


def mlp_kernel(plan, hhat, dy_hbm, wg_hbm, wu_own, wdown_hbm, sum_h, sum_o, col_out, down_out,
               h_all, dy_all, wg, wu, wd, mid, dgate, dup, stage_h, stage_o, stage, stage_2, slots_h, slots_o,
               col_sent, col_near, col_far, down_sent, down_near, down_far, local, *sems):
    place = Place()
    h_sems, sum_h_sems, sum_o_sems, col_seq, down_seq, up_seq = pairs_of(sems)
    greet([place.right, place.left, place.core_peer, place.far_peer])
    rows, width = hhat.shape
    ff = wg.shape[1]
    bf16, f32 = jnp.bfloat16, jnp.float32
    up_blocks = Blocks(wu, wu_own.shape[0])
    keep = [
        pltpu.make_async_copy(src, dst, local.at[i])
        for i, (src, dst) in enumerate(
            ((hhat, h_all.at[pl.ds(0, rows)]), (wg_hbm, wg), (wu_own, up_blocks[place.s]), (wdown_hbm, wd), (dy_hbm, dy_all))
        )
    ]
    for copy in keep:
        copy.start()
    gather = ring_gather(hhat, Rows(h_all, rows), h_sems, place)
    up_flow = seq_gather(wu_own, up_blocks, up_seq, place)

    def hidden_rows(start, count):
        at = pl.ds(start, count)

        def body(cols):
            gate = dot(h_all[at, :], wg[:, cols])
            up = dot(h_all[at, :], wu[:, cols])
            dmid = dot(dy_all[at, :], wd[cols, :], (1, 1))
            sig = jax.nn.sigmoid(gate)
            active = gate * sig
            mid[at, cols] = (active * up).astype(bf16)
            dgate[at, cols] = (dmid * up * sig * (1.0 + gate * (1.0 - sig))).astype(bf16)
            dup[at, cols] = (dmid * active).astype(bf16)

        chunks(ff, 512, body)

    def part_h(start, count, dst):
        at = pl.ds(start, count)

        def body(cols):
            dst[:, cols] = (dot(dgate[at, :], wg[cols, :], (1, 1)) + dot(dup[at, :], wu[cols, :], (1, 1))).astype(bf16)

        chunks(width, 512, body)

    def part_o(start, count, dst):
        at = pl.ds(start, count)

        def body(cols):
            dst[:, cols] = dot(mid[at, :], wd[:, cols]).astype(bf16)

        chunks(width, 1024, body)

    def col_grad(s, dst, add):
        def body(cols):
            lhs = h_all[:, pl.ds(pl.multiple_of(s * dst.shape[0] + cols.start, 256), 256)]
            for side, grad in enumerate((dgate, dup)):
                there = pl.ds(side * ff, ff)
                value = dot(lhs, grad[...], (0, 0))
                if add:
                    value = value + dst[cols, there].astype(f32)
                dst[cols, there] = value.astype(bf16)

        chunks(dst.shape[0], 256, body)

    def down_grad(s, dst, add):
        lhs = pl.ds(pl.multiple_of(s * dst.shape[0], 256), dst.shape[0])

        def body(cols):
            value = dot(mid[:, lhs], dy_all[:, cols], (0, 0))
            if add:
                value = value + dst[:, cols].astype(f32)
            dst[:, cols] = value.astype(bf16)

        chunks(width, 1024, body)

    def pair(ref):
        return (ref.at[pl.ds(rows, rows)], ref.at[pl.ds(0, rows)])

    col_sum = SeqSum(col_grad, col_sent, col_near, col_far, col_seq, place)
    down_sum = SeqSum(down_grad, down_sent, down_near, down_far, down_seq, place)
    ring_h, ring_o = RingSum(slots_h, sum_h_sems, place), RingSum(slots_o, sum_o_sems, place)
    top_h, top_o = stage_h.at[pl.ds(2 * rows, rows)], stage_o.at[pl.ds(2 * rows, rows)]
    next_h, next_o = stage_h.at[pl.ds(0, 2 * rows)], stage_o.at[pl.ds(0, 2 * rows)]

    def in_turn(*actions):
        return iter(actions)

    def parts(part, top, following, later):
        return in_turn(
            lambda: part(7 * rows, rows, top),
            lambda: part(5 * rows, 2 * rows, following),
            lambda: part(3 * rows, 2 * rows, later),
            lambda: part(rows, 2 * rows, later),
            lambda: part(0, rows, later.at[pl.ds(0, rows)]),
        )

    def sums(ring, top, following, later, out):
        return in_turn(
            lambda: ring.first(top),
            lambda: ring.relay(1, pair(following)),
            lambda: ring.relay(2, pair(later)),
            lambda: ring.relay(3, pair(later)),
            lambda: ring.last(later.at[pl.ds(0, rows)], out),
        )

    def wait_loads():
        for copy in keep:
            copy.wait()

    turns = {
        "k": in_turn(wait_loads),
        "a": in_turn(lambda: hidden_rows(0, rows)),
        "b": in_turn(lambda: hidden_rows(rows, 2 * rows)),
        "c": in_turn(lambda: hidden_rows(3 * rows, 2 * rows)),
        "d": in_turn(lambda: hidden_rows(5 * rows, 2 * rows)),
        "e": in_turn(lambda: hidden_rows(7 * rows, rows)),
        "P": parts(part_h, top_h, next_h, stage),
        "r": sums(ring_h, top_h, next_h, stage, sum_h),
        "O": parts(part_o, top_o, next_o, stage_2),
        "s": sums(ring_o, top_o, next_o, stage_2, sum_o),
        "n": in_turn(lambda: col_sum.near(0), lambda: col_sum.near(1)),
        "m": in_turn(col_sum.across),
        "w": in_turn(col_sum.own),
        "l": in_turn(col_sum.last),
        "N": in_turn(lambda: down_sum.near(0), lambda: down_sum.near(1)),
        "M": in_turn(down_sum.across),
        "W": in_turn(down_sum.own),
        "L": in_turn(down_sum.last),
    }
    for step in plan:
        if step == "x":
            next(gather)
        elif step == "u":
            next(up_flow)
        else:
            next(turns[step])()
    ends = []
    for i, (total, out) in enumerate(((col_sum, col_out), (down_sum, down_out))):
        ends.append(pltpu.make_async_copy(total.far, out, local.at[i]))
        ends[-1].start()
    for copy in ends:
        copy.wait()
    for flow in (ring_h, ring_o, col_sum, down_sum):
        flow.end()
    for flow in (gather, up_flow):
        for _ in flow:
            pass


def backward_kernel(plan, weighted, hidden, dy, x, q, k, v, ob_local, cos, sin, pos_rows, start_rows, pos_cols,
                    x_all, wqkv_all, wout_all, col,
                    grad_x, out_grad, qkv_raw, gate_raw, up_raw, col_in,
                    x_v, wqkv_v, wout_v, branch, datt_own, datt, dqkv, dk, dv, sum_x, over_x, line_x,
                    qkv_sent, qkv_near, qkv_far, qkv_in, out_sent, out_near, out_far, slots_o, local, *sems):
    place = Place()
    att_swap, col_swap, qkv_seq, qkv_swap, out_seq, out_ring = pairs_of(sems[:12])
    x_grid = sems[12:]
    bf16, f32 = jnp.bfloat16, jnp.float32
    rows, width = x.shape
    head = q.shape[1]
    seq_len = q.shape[0]
    shard = out_grad.shape[0]
    loads = [
        pltpu.make_async_copy(src, dst, local.at[i])
        for i, (src, dst) in enumerate(((wout_all, wout_v), (x_all, x_v), (wqkv_all, wqkv_v)))
    ]
    for copy in loads:
        copy.start()
    col_blocks, qkv_blocks = Blocks(col, shard), Blocks(qkv_far, shard)
    own_col = pltpu.make_async_copy(col_blocks[place.c], col_in.at[place.c], local.at[3])
    own_col.start()
    greet(place.peers() + [place.core_peer, place.far_peer])
    def norm_back(tensor, grads):
        scale = lax.rsqrt(jnp.mean(tensor * tensor, axis=-1, keepdims=True) + EPSILON)
        inner = jnp.mean(grads * tensor, axis=-1, keepdims=True)
        return scale * grads - tensor * (scale * scale * scale) * inner

    def hidden_back(at):
        grads = dy[at, :].astype(f32) + norm_back(hidden[at, :], weighted[at, :])
        grad_x[at, :] = grads
        branch[at, :] = grads.astype(bf16)

    def heads_back():
        chunks(rows, 16, hidden_back)
        loads[0].wait()

        def att_back(cols):
            datt_own[:, cols] = dot(branch[...], wout_v[cols, :], (1, 1)).astype(bf16)

        chunks(width, head, att_back)

    mine = block_at(place.c, rows)
    att_flow = exchange(
        lambda o: [(datt_own.at[:, block_at(place.at(o), head)], datt.at[mine])],
        lambda o: datt.at[block_at(place.at(o), rows)],
        att_swap,
        place,
    )
    def rows_grad(left, right):
        def grad(s, dst, add):
            def body(cols):
                lhs = left[:, pl.ds(pl.multiple_of(s * dst.shape[0] + cols.start, 256), 256)]
                value = dot(lhs, right[...], (0, 0))
                if add:
                    value = value + dst[cols, :].astype(f32)
                dst[cols, :] = value.astype(bf16)

            chunks(dst.shape[0], 256, body)

        return grad

    out_sum = SeqSum(rows_grad(ob_local, branch), out_sent, out_near, out_far, out_seq, place)
    qkv_sum = SeqSum(rows_grad(x_v, dqkv), qkv_sent, qkv_near, qkv_far, qkv_seq, place)
    def attend_back(at):
        prob = probabilities(q[at, :], k[...], pos_rows[at, :], start_rows[at, :], pos_cols[...])
        dprob = dot(datt[at, :], v[...], (1, 1))
        delta = jnp.sum(prob * dprob, axis=-1, keepdims=True)
        dscore = (prob * (dprob - delta)).astype(bf16)
        dq = dot(dscore, k[...]) * HDIM ** (-0.5)
        dqkv[at, pl.ds(0, head)] = turned(dq, cos[at, :], sin[at, :], -1.0).astype(bf16)
        dk[...] += dot(dscore, q[at, :], (0, 0))
        dv[...] += dot(prob.astype(bf16), datt[at, :], (0, 0))

    def finish_back(at):
        turned_dk = turned(dk[at, :] * HDIM ** (-0.5), cos[at, :], sin[at, :], -1.0)
        dqkv[at, pl.ds(head, head)] = turned_dk.astype(bf16)
        dqkv[at, pl.ds(2 * head, head)] = dv[at, :].astype(bf16)

    def all_back():
        dk[...] = jnp.zeros_like(dk)
        dv[...] = jnp.zeros_like(dv)
        datt[mine, :] = datt_own[:, block_at(place.c, head)]
        for copy in loads[1:]:
            copy.wait()
        chunks(seq_len, 256, attend_back)
        chunks(seq_len, 128, finish_back)

    part = wout_v.at[pl.ds(0, seq_len)]
    total = GridSum(part, over_x, line_x, x_grid, place)

    def part_x(i):
        at = block_at(total.plane(i), 2 * rows)

        def body(cols):
            part[at, cols] = dot(dqkv[at, :], wqkv_v[cols, :], (1, 1)).astype(bf16)

        chunks(width, 1024, body)
        total.across(i)

    unit = gate_raw.shape[1] // (RING * SEQ)
    groups = H // KVH

    def move_columns():
        own_col.wait()
        for c in range(RING):
            for side, raw in enumerate((gate_raw, up_raw)):
                for i in range(SEQ):
                    src = col_in.at[c, :, pl.ds((side * SEQ + i) * unit, unit)]
                    into = raw.at[:, pl.ds((i * RING + c) * unit, unit)]
                    pltpu.make_async_copy(src, into, local.at[4 + side]).start()

    own_qkv = pltpu.make_async_copy(qkv_blocks[place.c], qkv_in.at[place.c], local.at[6])

    def qkv_last():
        qkv_sum.last()
        own_qkv.start()

    def tokens_back():
        total.last(sum_x)

        def token_back(at):
            grad_x[at, :] = grad_x[at, :] + norm_back(x[at, :].astype(f32), sum_x[at, :])

        chunks(rows, 16, token_back)

    def finish_qkv():
        own_qkv.wait()
        for t in range(H):
            qkv_raw[:, pl.ds(t * head, head)] = qkv_in[t, :, pl.ds(0, head)].astype(f32)
        for side in (1, 2):
            for t in range(KVH):
                value = sum(qkv_in[t * groups + g, :, pl.ds(side * head, head)].astype(f32) for g in range(groups))
                qkv_raw[:, pl.ds((H + (side - 1) * KVH + t) * head, head)] = value

    def each(action, count=4):
        return iter([functools.partial(action, i) for i in range(count)])

    out_blocks = Owners(Blocks(out_far, shard), place)
    flows = {
        "a": att_flow,
        "c": by_owner(col_blocks, col_in, col_swap, place, 2),
        "o": ring_scatter(out_blocks, out_grad, slots_o, out_ring, place),
        "t": by_owner(qkv_blocks, qkv_in, qkv_swap, place),
    }
    works = {
        "h": heads_back, "B": all_back, "m": out_sum.across, "w": out_sum.own, "e": out_sum.last,
        "M": qkv_sum.across, "W": qkv_sum.own, "E": qkv_last, "V": move_columns, "Z": tokens_back, "F": finish_qkv,
    }
    turns = {"n": each(out_sum.near, 2), "N": each(qkv_sum.near, 2), "p": each(part_x), "l": each(total.along, 3)}
    for step in plan:
        if step in flows:
            next(flows[step])
        elif step in turns:
            next(turns[step])()
        else:
            works[step]()
    if "V" in plan:
        for raw, sem in ((gate_raw, local.at[4]), (up_raw, local.at[5])):
            pltpu.make_async_copy(raw, raw, sem).wait()
    else:
        own_col.wait()
    for name, flow in flows.items():
        if name in plan:
            for _ in flow:
                pass
    for flow in (total, out_sum, qkv_sum):
        flow.end()


class Blocks:
    def __init__(self, ref, rows):
        self.ref, self.rows = ref, rows
        self.shape = (ref.shape[0] // rows, rows) + tuple(ref.shape[1:])

    @property
    def at(self):
        return self

    def __getitem__(self, i):
        return self.ref.at[pl.ds(pl.multiple_of(i * self.rows, self.rows), self.rows)]


DMA = pltpu.SemaphoreType.DMA
HBM = pl.ANY


ATTENTION_PLAN = "dqxoooxoooxooRqqoooxxSggggqqLyPAbygggyuuuuyooWyybHdgu"


def attention_stage(
    tokens, cotangent, gain_attn, w_query, w_key, w_value, w_out, gain_mlp, w_gate, w_up, w_down, pair_order, segments, plan
):
    bf16, f32 = jnp.bfloat16, jnp.float32
    n = RING
    rows, width = tokens.shape[1], tokens.shape[2]
    seq_len = segments.shape[1]
    shard = w_query.shape[0]
    ff_own = w_down.shape[0]
    ff_mine = SEQ * ff_own
    head = HDIM
    frequency = THETA ** (-(np.arange(head // 2) * 2.0 / head))
    half = rows // 2
    block_angles = np.arange(2 * n)[:, None] * half * frequency[None, :]
    row_angles = np.arange(half)[:, None] * frequency[None, :]
    tables = tuple(jnp.asarray(f(angles), f32) for angles in (block_angles, row_angles) for f in (np.cos, np.sin))

    return call(
        functools.partial(attention_kernel, plan),
        [
            shaped((rows, width), f32),
            shaped((rows, width)),
            shaped((rows, H * head)),
            shaped((seq_len, head // 2), f32),
            shaped((seq_len, head // 2), f32),
            shaped((seq_len, 1), f32),
            shaped((seq_len, 1), f32),
            shaped((1, seq_len), f32),
            shaped((seq_len, head)),
            shaped((seq_len, head)),
            shaped((seq_len, head)),
            shaped((seq_len, width)),
            shaped((seq_len, width)),
            shaped((SEQ, n, shard, 3 * head)),
            shaped((SEQ, n, shard, width)),
            shaped((SEQ, n, shard, ff_mine)),
            shaped((n, shard, ff_mine)),
            shaped((SEQ, ff_own, width)),
        ],
        (tokens[0], gain_attn[None], gain_mlp[None], pair_order, segments)
        + tables
        + (cotangent[0], w_query, w_key, w_value, w_out, w_gate, w_up, w_down),
        [VMEM] * 3 + [pltpu.SMEM] + [VMEM] * 5 + [HBM] * 8,
        [VMEM] * 8 + [HBM] * 10,
        [
            VMEM((rows, width), bf16),
            VMEM(w_query.shape, bf16),
            VMEM(w_key.shape, bf16),
            VMEM(w_value.shape, bf16),
            VMEM(w_gate.shape, bf16),
            VMEM(w_up.shape, bf16),
            VMEM((seq_len, width), bf16),
            VMEM((SEQ, n, shard, 3 * head), bf16),
            VMEM((SEQ, n, shard, width), bf16),
        ]
        + [VMEM((seq_len, head), bf16)] * 4
        + [DMA((7,)), DMA((5,))]
        + pair_sems()
        + seq_sems()
        + ring_sems()
        + seq_sems()
        + pair_sems()
        + (pair_sems() + seq_sems()) * 2
        + grid_sems() * 2,
        1,
    )


MLP_PLAN = "xuxkxxuxxuabxxxcdxePrnPrnmOsPrOsNPrNMOsPwrOsOWslL"


def mlp_stage(hhat, dy_all, wg_all, wu_own, wdown_all, plan):
    bf16, f32, n = jnp.bfloat16, jnp.float32, RING
    (rows, width), seq_len = hhat.shape, dy_all.shape[0]
    ff_mine = wg_all.shape[1]
    shard, ff_own = width // (SEQ * n), ff_mine // SEQ
    slot_shape = VMEM((2, n // 2, rows, width), bf16)
    col_piece, down_piece = (n * shard, 2 * ff_mine), (ff_own, width)
    return call(
        functools.partial(mlp_kernel, plan),
        [shaped((rows, width), f32)] * 2 + [shaped(col_piece), shaped(down_piece)],
        (hhat, dy_all, wg_all, wu_own, wdown_all),
        [HBM] * 5,
        [VMEM] * 2 + [HBM] * 2,
        [VMEM((seq_len, width), bf16)] * 2
        + [VMEM((width, ff_mine), bf16)] * 2
        + [VMEM((ff_mine, width), bf16)]
        + [VMEM((seq_len, ff_mine), bf16)] * 3
        + [VMEM((3 * rows, width), bf16)] * 2
        + [VMEM((2 * rows, width), bf16)] * 2
        + [slot_shape] * 2
        + [VMEM((2,) + col_piece, bf16), VMEM((2,) + col_piece, bf16), VMEM(col_piece, bf16)]
        + [VMEM((2,) + down_piece, bf16), VMEM((2,) + down_piece, bf16), VMEM(down_piece, bf16)]
        + [DMA((5,))]
        + ring_sems() * 3
        + seq_sems() * 3,
        2,
    )


BACKWARD_PLAN = "channmacccBppNpNplMlwWclEtVZteooooFo"


def backward_stage(args, columns, plan):
    bf16, f32, n, head = jnp.bfloat16, jnp.float32, RING, HDIM
    (rows, width), seq_len, shard = args[0].shape, args[4].shape[0], columns[0]
    ff_mine = columns[1] // n
    piece = (n * shard, width)
    qkv_piece = (n * shard, 3 * head)
    outs = call(
        functools.partial(backward_kernel, plan),
        [
            shaped((rows, width), f32),
            shaped((shard, width), f32),
            shaped((shard, (H + 2 * KVH) * head), f32),
            shaped(columns),
            shaped(columns),
            shaped((n, shard, 2 * ff_mine)),
        ],
        args,
        [VMEM] * 13 + [HBM] * 4,
        [VMEM] * 3 + [HBM] * 3,
        [
            VMEM((seq_len, width), bf16),
            VMEM((width, 3 * head), bf16),
            VMEM((H * head, width), bf16),
            VMEM((rows, width), bf16),
            VMEM((rows, width), bf16),
            VMEM((seq_len, head), bf16),
            VMEM((seq_len, 3 * head), bf16),
            VMEM((seq_len, head), f32),
            VMEM((seq_len, head), f32),
            VMEM((rows, width), f32),
            VMEM((n // 2, rows, width), bf16),
            VMEM((2, n // 2, rows, width), bf16),
        ]
        + [VMEM((2,) + qkv_piece, bf16), VMEM((2,) + qkv_piece, bf16), VMEM(qkv_piece, bf16)]
        + [VMEM((n, shard, 3 * head), bf16)]
        + [VMEM((2,) + piece, bf16), VMEM((2,) + piece, bf16), VMEM(piece, bf16)]
        + [VMEM((2, n // 2, shard, width), bf16), DMA((7,))]
        + pair_sems() * 2
        + seq_sems()
        + pair_sems()
        + seq_sems()
        + ring_sems()
        + grid_sum_sems(),
        5,
    )
    return outs[:-1]


def ring_device(
    tokens, cotangent, gain_attn, w_query, w_key, w_value, w_out, gain_mlp, w_gate, w_up, w_down, pair_order, segments
):
    bf16, f32 = jnp.bfloat16, jnp.float32
    n = RING
    rows, width = tokens.shape[1], tokens.shape[2]
    seq_len = segments.shape[1]
    shard = w_query.shape[0]
    ff_own = w_down.shape[0]
    ff_mine = SEQ * ff_own
    head = HDIM
    outs = attention_stage(
        tokens, cotangent, gain_attn, w_query, w_key, w_value, w_out, gain_mlp, w_gate, w_up, w_down,
        pair_order, segments, ATTENTION_PLAN,
    )
    hidden, hhat, ob_local = outs[:3]
    where = outs[3:8]
    q, k, v, x_all, dy_all, wqkv_all, wout_all, wg_all, wu_own, wdown_all = outs[8:]
    wqkv_all = wqkv_all.reshape(width, 3 * head)
    wout_all = wout_all.reshape(H * head, width)
    wg_all = wg_all.reshape(width, ff_mine)
    wu_own = wu_own.reshape(n * shard, ff_mine)
    wdown_all = wdown_all.reshape(ff_mine, width)
    dweighted, out_sum, col_sum, down_sum = mlp_stage(hhat, dy_all, wg_all, wu_own, wdown_all, MLP_PLAN)
    output = (hidden + out_sum).astype(bf16)[None]

    grad_tokens, out_grad, qkv_raw, gate_raw, up_raw = backward_stage(
        (dweighted, hidden, cotangent[0], tokens[0], q, k, v, ob_local)
        + tuple(where)
        + (x_all, wqkv_all, wout_all, col_sum),
        w_gate.shape, BACKWARD_PLAN,
    )
    gain_one = gain_attn.astype(f32)[:, None]
    gain_two = gain_mlp.astype(f32)[:, None]
    raw_q = qkv_raw[:, : H * head]
    raw_k = qkv_raw[:, H * head : (H + KVH) * head]
    raw_v = qkv_raw[:, (H + KVH) * head :]

    def gain_part(raw, w):
        return jnp.sum(raw.astype(f32) * w.astype(f32), axis=1)

    grad_gain_one = gain_part(raw_q, w_query) + gain_part(raw_k, w_key) + gain_part(raw_v, w_value)
    grad_gain_two = gain_part(gate_raw, w_gate) + gain_part(up_raw, w_up)
    return (
        output,
        grad_tokens[None],
        grad_gain_one,
        raw_q * gain_one,
        raw_k * gain_one,
        raw_v * gain_one,
        out_grad,
        grad_gain_two,
        gate_raw.astype(f32) * gain_two,
        up_raw.astype(f32) * gain_two,
        down_sum.astype(f32),
    )


def solution(mesh):
    placed = (
        P("seq", "ctx", None),
        P("seq", "ctx", None),
        P(("seq", "ctx")),
        P(("seq", "ctx"), None),
        P(("seq", "ctx"), None),
        P(("seq", "ctx"), None),
        P(("seq", "ctx"), None),
        P(("seq", "ctx")),
        P(("seq", "ctx"), None),
        P(("seq", "ctx"), None),
        P(("seq", "ctx"), None),
        P("seq", None),
        P("seq", None),
    )
    fits = mesh.shape["ctx"] == H and mesh.shape["seq"] == 4
    chosen = ring_device if fits else general_device
    return jax.shard_map(
        chosen,
        mesh=mesh,
        in_specs=placed,
        out_specs=(
            P("seq", "ctx", None),
            P("seq", "ctx", None),
            P(("seq", "ctx")),
            P(("seq", "ctx"), None),
            P(("seq", "ctx"), None),
            P(("seq", "ctx"), None),
            P(("seq", "ctx"), None),
            P(("seq", "ctx")),
            P(("seq", "ctx"), None),
            P(("seq", "ctx"), None),
            P(("seq", "ctx"), None),
        ),
        check_vma=False,
    )
```

```python
import functools
import math

import jax
import jax.numpy as jnp
import numpy as np
from jax import lax
from jax.experimental import pallas as pl
from jax.experimental.pallas import tpu as pltpu
from jax.sharding import PartitionSpec as P

H = 8
KVH = 4
HDIM = 256
DOCS = 4


EPSILON = 1e-06
THETA = 1000042.0
NEG_FILL = -1e30


def slot_positions(pair_row, half_rows, pair_count):
    offsets = jnp.arange(half_rows, dtype=jnp.int32)
    low_slots = pair_row[:, None] * half_rows + offsets[None, :]
    high_slots = (2 * pair_count - 1 - pair_row)[:, None] * half_rows + offsets[None, :]
    return jnp.concatenate([low_slots, high_slots], axis=1).reshape(-1)


def rotary_tables(positions, head_dim):
    half_dim = head_dim // 2
    frequency = THETA ** (-(jnp.arange(half_dim, dtype=jnp.float32) * 2.0 / head_dim))
    angles = positions.astype(jnp.float32)[:, None] * frequency[None, :]
    return (jnp.cos(angles)[:, None, :], jnp.sin(angles)[:, None, :])


def rotary(tensor, table_cos, table_sin):
    half_dim = tensor.shape[-1] // 2
    lead_half = tensor[..., :half_dim]
    tail_half = tensor[..., half_dim:]
    return jnp.concatenate(
        [
            lead_half * table_cos - tail_half * table_sin,
            tail_half * table_cos + lead_half * table_sin,
        ],
        axis=-1,
    )


def rms_scale(tensor):
    return lax.rsqrt(jnp.mean(tensor * tensor, axis=-1, keepdims=True) + EPSILON)


def rms_backward(tensor, scale_rows, gain_full, grad_rows):
    weighted = gain_full * grad_rows
    inner_mean = jnp.mean(weighted * tensor, axis=-1, keepdims=True)
    return scale_rows * weighted - tensor * (scale_rows * scale_rows * scale_rows) * inner_mean


def contract_rows(first_mat, second_mat):
    return lax.dot_general(
        first_mat, second_mat, (((0,), (0,)), ((), ())), preferred_element_type=jnp.float32
    )


def contract_cols(first_mat, second_mat):
    return lax.dot_general(
        first_mat, second_mat, (((1,), (1,)), ((), ())), preferred_element_type=jnp.float32
    )


def attention_weights(gain_attn, gain_mlp, w_query, w_key, w_value, w_out):
    return (
        lax.all_gather(gain_attn, ("seq", "ctx"), axis=0, tiled=True),
        lax.all_gather(gain_mlp, ("seq", "ctx"), axis=0, tiled=True),
        lax.all_gather(w_query, ("seq", "ctx"), axis=0, tiled=True),
        lax.all_gather(w_key, ("seq", "ctx"), axis=0, tiled=True),
        lax.all_gather(w_value, ("seq", "ctx"), axis=0, tiled=True),
        lax.all_gather(w_out, ("seq", "ctx"), axis=0, tiled=True),
    )


def mlp_weights(w_gate, w_up, w_down):
    return (
        lax.all_gather(w_gate, ("seq", "ctx"), axis=0, tiled=True),
        lax.all_gather(w_up, ("seq", "ctx"), axis=0, tiled=True),
        lax.all_gather(w_down, ("seq", "ctx"), axis=0, tiled=True),
    )


def reduce_grads(grad_one, grad_two, grad_three):
    seq_count = lax.axis_size("seq")
    grad_one = grad_one.reshape((seq_count, grad_one.shape[0] // seq_count) + grad_one.shape[1:])
    grad_two = grad_two.reshape((seq_count, grad_two.shape[0] // seq_count) + grad_two.shape[1:])
    grad_three = grad_three.reshape(
        (seq_count, grad_three.shape[0] // seq_count) + grad_three.shape[1:]
    )
    grad_one, grad_two, grad_three = (
        lax.psum_scatter(
            grad_one.astype(jnp.bfloat16), "ctx", scatter_dimension=1, tiled=True
        ).astype(jnp.float32),
        lax.psum_scatter(
            grad_two.astype(jnp.bfloat16), "ctx", scatter_dimension=1, tiled=True
        ).astype(jnp.float32),
        lax.psum_scatter(
            grad_three.astype(jnp.bfloat16), "ctx", scatter_dimension=1, tiled=True
        ).astype(jnp.float32),
    )
    grad_one, grad_two, grad_three = (
        lax.psum_scatter(
            grad_one.astype(jnp.bfloat16), "seq", scatter_dimension=0, tiled=True
        ).astype(jnp.float32),
        lax.psum_scatter(
            grad_two.astype(jnp.bfloat16), "seq", scatter_dimension=0, tiled=True
        ).astype(jnp.float32),
        lax.psum_scatter(
            grad_three.astype(jnp.bfloat16), "seq", scatter_dimension=0, tiled=True
        ).astype(jnp.float32),
    )
    return (grad_one[0], grad_two[0], grad_three[0])


def general_device(
    tokens,
    cotangent,
    gain_attn,
    w_query,
    w_key,
    w_value,
    w_out,
    gain_mlp,
    w_gate,
    w_up,
    w_down,
    pair_order,
    segments,
):
    pair_count = lax.axis_size("ctx")
    my_index = lax.axis_index("ctx")
    row_count = tokens.shape[1]
    half_rows = row_count // 2
    seq_len = segments.shape[1]
    head_groups = H // KVH
    score_scale = HDIM ** (-0.5)
    key_rows = math.gcd(seq_len, 512)
    key_steps = seq_len // key_rows
    key_pos = slot_positions(pair_order[0], half_rows, pair_count)
    key_doc = jnp.take(segments[0], key_pos)
    query_pos = lax.dynamic_slice_in_dim(key_pos, my_index * row_count, row_count)
    query_doc = lax.dynamic_slice_in_dim(key_doc, my_index * row_count, row_count)
    rot_cos, rot_sin = rotary_tables(query_pos, HDIM)
    gain_one, gain_two, query_w, key_w, value_w, out_w = attention_weights(
        gain_attn, gain_mlp, w_query, w_key, w_value, w_out
    )
    gain_one = gain_one.astype(jnp.float32)
    gain_two = gain_two.astype(jnp.float32)
    inputs = tokens[0].astype(jnp.float32)
    scale_one = rms_scale(inputs)
    normed = (inputs * scale_one * gain_one).astype(jnp.bfloat16)
    query_proj = jnp.dot(normed, query_w, preferred_element_type=jnp.float32).reshape(
        row_count, H, HDIM
    )
    key_proj = jnp.dot(normed, key_w, preferred_element_type=jnp.float32).reshape(
        row_count, KVH, HDIM
    )
    value_proj = jnp.dot(normed, value_w, preferred_element_type=jnp.float32)
    query_rot = (
        rotary(query_proj, rot_cos, rot_sin)
        .astype(jnp.bfloat16)
        .reshape(row_count, KVH, head_groups, HDIM)
    )
    key_rot = rotary(key_proj, rot_cos, rot_sin).astype(jnp.bfloat16).reshape(row_count, KVH * HDIM)
    value_low = value_proj.astype(jnp.bfloat16)
    key_width = key_rot.shape[1]
    key_all, value_all = (
        lax.all_gather(key_rot, "ctx", axis=0, tiled=True),
        lax.all_gather(value_low, "ctx", axis=0, tiled=True),
    )
    pos_blocks = key_pos.reshape(key_steps, key_rows)
    doc_blocks = key_doc.reshape(key_steps, key_rows)

    def scores_of(key_blk, pos_blk, doc_blk):
        key_heads = key_blk.reshape(key_rows, KVH, HDIM)
        raw_scores = (
            jnp.einsum("qkgd,tkd->kgqt", query_rot, key_heads, preferred_element_type=jnp.float32)
            * score_scale
        )
        visible = (doc_blk[None, :] == query_doc[:, None]) & (
            pos_blk[None, :] <= query_pos[:, None]
        )
        return (raw_scores, visible[None, None])

    def first_pass(carried, step_data):
        running_top, running_sum = carried
        key_blk, pos_blk, doc_blk = step_data
        raw_scores, visible = scores_of(key_blk, pos_blk, doc_blk)
        masked = jnp.where(visible, raw_scores, NEG_FILL)
        new_top = jnp.maximum(running_top, jnp.max(masked, axis=-1))
        added = jnp.sum(jnp.where(visible, jnp.exp(masked - new_top[..., None]), 0.0), axis=-1)
        return ((new_top, running_sum * jnp.exp(running_top - new_top) + added), None)

    start_top = jnp.full((KVH, head_groups, row_count), NEG_FILL, jnp.float32)
    start_sum = jnp.zeros((KVH, head_groups, row_count), jnp.float32)
    key_stack = key_all.reshape(key_steps, key_rows, key_width)
    value_stack = value_all.reshape(key_steps, key_rows, key_width)
    (final_top, final_sum), _ = lax.scan(
        first_pass, (start_top, start_sum), (key_stack, pos_blocks, doc_blocks)
    )
    log_total = final_top + jnp.log(final_sum)

    def second_pass(carried, step_data):
        acc_out, acc_rest = carried
        key_blk, value_blk, pos_blk, doc_blk = step_data
        raw_scores, visible = scores_of(key_blk, pos_blk, doc_blk)
        prob_full = jnp.where(visible, jnp.exp(raw_scores - log_total[..., None]), 0.0)
        prob_low = prob_full.astype(jnp.bfloat16)
        prob_rest = (prob_full - prob_low.astype(jnp.float32)).astype(jnp.bfloat16)
        value_heads = value_blk.reshape(key_rows, KVH, HDIM)
        acc_out = acc_out + jnp.einsum(
            "kgqt,tkd->qkgd", prob_low, value_heads, preferred_element_type=jnp.float32
        )
        acc_rest = acc_rest + jnp.einsum(
            "kgqt,tkd->qkgd", prob_rest, value_heads, preferred_element_type=jnp.float32
        )
        return ((acc_out, acc_rest), None)

    start_acc = jnp.zeros((row_count, KVH, head_groups, HDIM), jnp.float32)
    (attended, attended_rest), _ = lax.scan(
        second_pass, (start_acc, start_acc), (key_stack, value_stack, pos_blocks, doc_blocks)
    )
    exact_out = attended + attended_rest
    out_low = attended.reshape(row_count, H * HDIM).astype(jnp.bfloat16)
    hidden = inputs + jnp.dot(out_low, out_w, preferred_element_type=jnp.float32)
    scale_two = rms_scale(hidden)
    normed_two = (hidden * scale_two * gain_two).astype(jnp.bfloat16)
    grad_out = cotangent[0]
    gate_w, up_w, down_w = mlp_weights(w_gate, w_up, w_down)
    gate_proj = jnp.dot(normed_two, gate_w, preferred_element_type=jnp.float32)
    up_proj = jnp.dot(normed_two, up_w, preferred_element_type=jnp.float32)
    gate_sig = jax.nn.sigmoid(gate_proj)
    active = gate_proj * gate_sig
    middle = (active * up_proj).astype(jnp.bfloat16)
    result = hidden + jnp.dot(middle, down_w, preferred_element_type=jnp.float32)
    output = result.astype(jnp.bfloat16)[None]
    gate_w, up_w, down_w = mlp_weights(w_gate, w_up, w_down)
    grad_mid = contract_cols(grad_out, down_w)
    grad_gate = (grad_mid * up_proj * gate_sig * (1.0 + gate_proj * (1.0 - gate_sig))).astype(
        jnp.bfloat16
    )
    grad_up = (grad_mid * active).astype(jnp.bfloat16)
    grad_norm_two = contract_cols(grad_gate, gate_w) + contract_cols(grad_up, up_w)
    grad_gain_two = jnp.sum(grad_norm_two * hidden * scale_two, axis=0)
    grad_hidden = grad_out.astype(jnp.float32) + rms_backward(
        hidden, scale_two, gain_two, grad_norm_two
    )
    grad_w_gate = contract_rows(normed_two, grad_gate)
    grad_w_up = contract_rows(normed_two, grad_up)
    shard_gain_two, shard_gate, shard_up = reduce_grads(grad_gain_two, grad_w_gate, grad_w_up)
    gain_one, gain_two, query_w, key_w, value_w, out_w = attention_weights(
        gain_attn, gain_mlp, w_query, w_key, w_value, w_out
    )
    gain_one = gain_one.astype(jnp.float32)
    grad_branch = grad_hidden.astype(jnp.bfloat16)
    grad_w_out = contract_rows(out_low, grad_branch)
    grad_att = (
        contract_cols(grad_branch, out_w)
        .astype(jnp.bfloat16)
        .reshape(row_count, KVH, head_groups, HDIM)
    )
    row_delta = jnp.transpose(jnp.sum(grad_att.astype(jnp.float32) * exact_out, axis=-1), (1, 2, 0))
    key_back, value_back = (key_all, value_all)

    def backward_step(grad_query, step_data):
        key_blk, value_blk, pos_blk, doc_blk = step_data
        raw_scores, visible = scores_of(key_blk, pos_blk, doc_blk)
        prob_full = jnp.where(visible, jnp.exp(raw_scores - log_total[..., None]), 0.0)
        prob_low = prob_full.astype(jnp.bfloat16)
        key_heads = key_blk.reshape(key_rows, KVH, HDIM)
        value_heads = value_blk.reshape(key_rows, KVH, HDIM)
        grad_value_blk = jnp.einsum(
            "kgqt,qkgd->tkd", prob_low, grad_att, preferred_element_type=jnp.float32
        )
        grad_probs = jnp.einsum(
            "qkgd,tkd->kgqt", grad_att, value_heads, preferred_element_type=jnp.float32
        )
        grad_scores = (prob_full * (grad_probs - row_delta[..., None])).astype(jnp.bfloat16)
        grad_query = (
            grad_query
            + jnp.einsum(
                "kgqt,tkd->qkgd", grad_scores, key_heads, preferred_element_type=jnp.float32
            )
            * score_scale
        )
        grad_key_blk = (
            jnp.einsum("kgqt,qkgd->tkd", grad_scores, query_rot, preferred_element_type=jnp.float32)
            * score_scale
        )
        return (
            grad_query,
            (
                grad_key_blk.reshape(key_rows, key_width),
                grad_value_blk.reshape(key_rows, key_width),
            ),
        )

    back_keys = key_back.reshape(key_steps, key_rows, key_width)
    back_values = value_back.reshape(key_steps, key_rows, key_width)
    grad_query, (grad_key_steps, grad_value_steps) = lax.scan(
        backward_step, start_acc, (back_keys, back_values, pos_blocks, doc_blocks)
    )
    grad_key_all = grad_key_steps.reshape(seq_len, key_width)
    grad_value_all = grad_value_steps.reshape(seq_len, key_width)
    grad_key_own, grad_value_own = (
        lax.psum_scatter(
            grad_key_all.astype(jnp.bfloat16), "ctx", scatter_dimension=0, tiled=True
        ).astype(jnp.float32),
        lax.psum_scatter(
            grad_value_all.astype(jnp.bfloat16), "ctx", scatter_dimension=0, tiled=True
        ).astype(jnp.float32),
    )
    grad_query = (
        rotary(grad_query.reshape(row_count, H, HDIM), rot_cos, -rot_sin)
        .astype(jnp.bfloat16)
        .reshape(row_count, H * HDIM)
    )
    grad_key = (
        rotary(grad_key_own.reshape(row_count, KVH, HDIM), rot_cos, -rot_sin)
        .astype(jnp.bfloat16)
        .reshape(row_count, key_width)
    )
    grad_value = grad_value_own.astype(jnp.bfloat16)
    grad_w_query = contract_rows(normed, grad_query)
    grad_w_key = contract_rows(normed, grad_key)
    grad_w_value = contract_rows(normed, grad_value)
    grad_normed = (
        contract_cols(grad_query, query_w)
        + contract_cols(grad_key, key_w)
        + contract_cols(grad_value, value_w)
    )
    grad_gain_one = jnp.sum(grad_normed * inputs * scale_one, axis=0)
    grad_tokens = grad_hidden + rms_backward(inputs, scale_one, gain_one, grad_normed)
    grad_w_down = contract_rows(middle, grad_out)
    shard_gain_one, shard_out, shard_down = reduce_grads(grad_gain_one, grad_w_out, grad_w_down)
    shard_query, shard_key, shard_value = reduce_grads(grad_w_query, grad_w_key, grad_w_value)
    return (
        output,
        grad_tokens[None],
        shard_gain_one,
        shard_query,
        shard_key,
        shard_value,
        shard_out,
        shard_gain_two,
        shard_gate,
        shard_up,
        shard_down,
    )


MESH = pl.DeviceIdType.MESH
VMEM = pltpu.VMEM
RING = 8
SEQ = 4


class Place:
    def __init__(self):
        self.c = lax.axis_index("ctx")
        self.s = lax.axis_index("seq")
        self.z, self.x = self.c // 2, lax.rem(self.c, 2)
        self.p = self.z + self.x * (7 - 2 * self.z)
        self.up, self.down = {"ctx": self.c + 2}, {"ctx": self.c - 2}
        self.side = {"ctx": self.c + 1 - 2 * self.x}
        self.right = {"ctx": self.at(1)}
        self.left = {"ctx": self.at(-1)}
        self.s_core = self.s + 1 - 2 * lax.rem(self.s, 2)
        self.s_far = lax.rem(self.s + 2, 4)
        self.s_both = 3 - self.s
        self.core_peer = {"seq": self.s_core}
        self.far_peer = {"seq": self.s_far}

    def at(self, offset):
        q = lax.rem(self.p + offset + 2 * RING, RING)
        return 2 * q + (q // 4) * (15 - 4 * q)

    def peers(self):
        return [{"ctx": lax.rem(self.c + k, RING)} for k in range(1, RING)]


def greet(devices, work=None):
    barrier = pltpu.get_barrier_semaphore()
    for device in devices:
        pl.semaphore_signal(barrier, inc=1, device_id=device, device_id_type=MESH)
    if work is not None:
        work()
    pl.semaphore_wait(barrier, len(devices))


def remote(src, dst, send_sem, recv_sem, device):
    return pltpu.make_async_remote_copy(
        src_ref=src, dst_ref=dst, send_sem=send_sem, recv_sem=recv_sem, device_id=device, device_id_type=MESH
    )


def arrived(ref, sems, index, device):
    remote(ref, ref, sems[0].at[index], sems[1].at[index], device).wait_recv()


def together(*flows):
    live = list(flows)
    while live:
        live = [flow for flow in live if next(flow, "end") != "end"]


def ring_sems():
    return [pltpu.SemaphoreType.DMA((2, RING // 2, 2))] * 2


def slot(offset):
    return 0 if offset == 0 else min(RING - 1, 2 * offset if offset > 0 else -2 * offset - 1)


class Rows:
    def __init__(self, ref, rows):
        self.ref, self.rows = ref, rows

    def here(self, offset):
        return self.ref.at[pl.ds(slot(offset) * self.rows, self.rows)]

    def there(self, offset, d):
        return self.here(offset - 1 if d == 0 else offset + 1)


class Owners:
    def __init__(self, ref, place):
        self.ref, self.place = ref, place

    def here(self, offset):
        return self.ref.at[self.place.at(offset)]

    def there(self, offset, d):
        return self.here(offset)


def ring_gather(own, blocks, sems, place):
    half = own.shape[0] // 2
    steps = RING // 2
    sent = []

    def part(ref, j):
        return ref.at[pl.ds(j * half, half)]

    def wait_for(d, s, j):
        offset = -(s + 1) if d == 0 else s + 1
        arrived(part(blocks.here(offset), j), sems, (d, s, j), place.right if d == 0 else place.left)

    for s in range(steps):
        for j in range(2):
            for d in range(2):
                if s == steps - 1 and j != d:
                    continue
                if s > 0:
                    wait_for(d, s - 1, j)
                offset = -s if d == 0 else s
                copy = remote(
                    part(own if s == 0 else blocks.here(offset), j),
                    part(blocks.there(offset, d), j),
                    sems[0].at[d, s, j],
                    sems[1].at[d, s, j],
                    place.right if d == 0 else place.left,
                )
                copy.start()
                sent.append(copy)
            yield
    for d in range(2):
        wait_for(d, steps - 2, 1 - d)
    yield
    for d in range(2):
        wait_for(d, steps - 1, d)
    yield
    for copy in sent:
        copy.wait_send()


class RingSum:
    def __init__(self, slots, sems, place):
        self.slots, self.sems, self.sent = slots, sems, []
        self.sides = (place.right, place.left)
        self.half = slots.shape[2] // 2

    def rows(self, ref, j):
        return ref.at[pl.ds(j * self.half, self.half)]

    def send(self, d, s, j, source):
        to = self.rows(self.slots.at[d, s], j)
        copy = remote(source, to, self.sems[0].at[d, s, j], self.sems[1].at[d, s, j], self.sides[d])
        copy.start()
        self.sent.append(copy)

    def held(self, d, s, j):
        ref = self.rows(self.slots.at[d, s], j)
        arrived(ref, self.sems, (d, s, j), self.sides[d])
        return ref

    def first(self, part):
        for d in range(2):
            self.send(d, 0, d, self.rows(part, d))

    def relay(self, s, parts):
        for j in range(2):
            for d in range(2):
                source = self.rows(parts[d], j)
                if s > 1 or j == d:
                    held = self.held(d, s - 1, j)
                    add_into(held, source)
                    source = held
                self.send(d, s, j, source)

    def last(self, part, out):
        for j in range(2):
            held = [self.held(d, RING // 2 - 1, j) for d in range(2)]
            sum_of_three(self.rows(out, j), self.rows(part, j), *held)

    def end(self):
        for copy in self.sent:
            copy.wait_send()


def ring_scatter(blocks, out, slots, sems, place):
    ring = RingSum(slots, sems, place)
    ring.first(blocks.here(RING // 2))
    yield
    for s in range(1, RING // 2):
        k = RING // 2 - s
        ring.relay(s, (blocks.here(k), blocks.here(-k)))
        yield
    ring.last(blocks.here(0), out)
    ring.end()
    yield


def pair_sems():
    return [pltpu.SemaphoreType.DMA((RING,))] * 2


OFFSETS = (1, -1, 2, -2, 3, -3, 4)


def exchange(pieces, here, sems, place, group=RING):
    for i in range(0, len(OFFSETS), group):
        for k in OFFSETS[i : i + group]:
            at = slot(k)
            for src, dst in pieces(k):
                remote(src, dst, sems[0].at[at], sems[1].at[at], {"ctx": place.at(k)}).start()
        yield
    for k in OFFSETS:
        arrived(here(k), sems, RING - 1 if k == RING // 2 else slot(-k), {"ctx": place.at(k)})
    for k in OFFSETS:
        remote(here(k), here(k), sems[0].at[slot(k)], sems[1].at[slot(k)], {"ctx": place.at(k)}).wait_send()
    yield


def by_owner(src, dst, sems, place, group=RING):
    return exchange(lambda k: [(src.at[place.at(k)], dst.at[place.c])], lambda k: dst.at[place.at(k)], sems, place, group)


def block_at(i, size):
    return pl.ds(pl.multiple_of(i * size, size), size)


class ByOwner:
    def __init__(self, ref, rows):
        self.ref, self.rows = ref, rows

    def owner(self, c, side=None):
        return self.ref.at[block_at(c, self.rows)]


class ByArrival:
    def __init__(self, ref, rows, place):
        self.ref, self.rows, self.place = ref, rows, place

    def owner(self, c, side="here"):
        far = {"here": 0, "up": 2, "down": -2, "side": 1 - 2 * self.place.x}[side]
        mine = self.place.c + far
        z, x = mine // 2, lax.rem(mine, 2)
        p = z + x * (7 - 2 * z)
        z, x = c // 2, lax.rem(c, 2)
        k = lax.rem(z + x * (7 - 2 * z) - p + 2 * RING, RING)
        late = jnp.where(k == RING // 2, RING - 1, 2 * (RING - k) - 1)
        return self.ref.at[block_at(jnp.where(k < RING // 2, 2 * k, late), self.rows)]


def grid_sems():
    return [pltpu.SemaphoreType.DMA((2, 3))] * 2 + [pltpu.SemaphoreType.DMA((4,))] * 2


def grid_gather(own, blocks, sems, place, late=False):
    z_sems, x_sems = sems[:2], sems[2:]
    z, x = place.z, place.x
    sent = []

    def send(when, src, c, side, pair, index, device):
        copy = remote(src, blocks.owner(c, side), pair[0].at[index], pair[1].at[index], device)
        pl.when(when)(copy.start)
        sent.append((when, copy))

    def across(when, src, line):
        send(when, src, 2 * line + x, "side", x_sems, line, place.side)

    send(z < 3, own, place.c, "up", z_sems, (0, 0), place.up)
    send(z > 0, own, place.c, "down", z_sems, (1, 0), place.down)
    if not late:
        across(z >= 0, own, z)
    yield
    for hop in range(1, 4):
        for d, (line, here, further) in enumerate(((z - hop, z >= hop, z < 3), (z + hop, z <= 3 - hop, z > 0))):
            index = 2 * line + x
            ref = blocks.owner(jnp.clip(index, 0, RING - 1))
            device = (place.down, place.up)[d]

            @pl.when(here)
            def _():
                arrived(ref, z_sems, (d, hop - 1), device)

            if hop < 3:
                send(here & further, ref, jnp.clip(index, 0, RING - 1), ("up", "down")[d], z_sems, (d, hop), (place.up, place.down)[d])
            if not late:
                across_line = jnp.clip(line, 0, 3)
                send(here, ref, 2 * across_line + x, "side", x_sems, across_line, place.side)
        yield
    if late:
        across(z >= 0, own, z)
        for hop in range(1, 4):
            line = lax.rem(z + hop, 4)
            across(z >= 0, blocks.owner(2 * line + x), line)
        yield
    for line in range(4):
        arrived(blocks.owner(2 * line + 1 - x), x_sems, line, place.side)
    for when, copy in sent:
        pl.when(when)(copy.wait_send)
    yield


def grid_sum_sems():
    return [pltpu.SemaphoreType.DMA((4,))] * 2 + [pltpu.SemaphoreType.DMA((2, 4))] * 2


class GridSum:
    def __init__(self, part, over, line, sems, place):
        self.part, self.over, self.line, self.place = part, over, line, place
        self.x_sems, self.z_sems = sems[:2], sems[2:]
        self.rows = over.shape[1]
        self.sent = []

    def plane(self, i):
        z = self.place.z
        inner = jnp.where((z == 1) | (z == 2), 1, 0)
        plain, mid = (3, 2, 1, 0)[i], (3, 0, 2, 1)[i]
        order = plain + inner * (mid - plain)
        return jnp.where(z < 2, order, 3 - order)

    def send(self, when, src, dst, pair, index, device):
        copy = remote(src, dst, pair[0].at[index], pair[1].at[index], device)
        pl.when(when)(copy.start)
        self.sent.append((when, copy))

    def mine(self, z, x):
        return self.part.at[block_at(2 * z + x, self.rows)]

    def across(self, i):
        z = self.plane(i)
        self.send(self.place.z >= 0, self.mine(z, 1 - self.place.x), self.over.at[z], self.x_sems, z, self.place.side)

    def along(self, i):
        z, me = self.plane(i), self.place.z
        held = self.over.at[z]
        arrived(held, self.x_sems, z, self.place.side)
        add_into(held, self.mine(z, self.place.x))
        for d, (when, more, source, device) in enumerate(
            (
                (z > me, me > 0, self.place.down, self.place.up),
                (z < me, me < 3, self.place.up, self.place.down),
            )
        ):

            @pl.when(when & more)
            def _():
                arrived(self.line.at[d, z], self.z_sems, (d, z), source)
                add_into(held, self.line.at[d, z])

            self.send(when, held, self.line.at[d, z], self.z_sems, (d, z), device)

    def last(self, out):
        z = self.place.z
        held = self.over.at[z]
        arrived(held, self.x_sems, z, self.place.side)
        add_to(out, held, self.mine(z, self.place.x))
        for d, (when, source) in enumerate(((z > 0, self.place.down), (z < 3, self.place.up))):

            @pl.when(when)
            def _():
                arrived(self.line.at[d, z], self.z_sems, (d, z), source)
                add_to(out, out, self.line.at[d, z])

    def end(self):
        for when, copy in self.sent:
            pl.when(when)(copy.wait_send)


def pairs_of(sems):
    return [sems[i : i + 2] for i in range(0, len(sems), 2)]


def seq_sems():
    return [pltpu.SemaphoreType.DMA((3,))] * 2


def seq_gather(own, buf, sems, place):
    first = remote(own, buf.at[place.s], sems[0].at[0], sems[1].at[0], place.far_peer)
    second = remote(own, buf.at[place.s], sems[0].at[1], sems[1].at[1], place.core_peer)
    first.start()
    second.start()
    yield
    arrived(buf.at[place.s_far], sems, 0, place.far_peer)
    third = remote(buf.at[place.s_far], buf.at[place.s_far], sems[0].at[2], sems[1].at[2], place.core_peer)
    third.start()
    yield
    arrived(buf.at[place.s_core], sems, 1, place.core_peer)
    arrived(buf.at[place.s_both], sems, 2, place.core_peer)
    for copy in (first, second, third):
        copy.wait_send()
    yield


def sum_of_three(dst, *terms):
    step = math.gcd(dst.shape[0], 16)

    @pl.loop(0, dst.shape[0] // step)
    def _(i):
        at = pl.ds(pl.multiple_of(i * step, step), step)
        one, two, three = (term[at].astype(jnp.float32) for term in terms)
        dst[at] = one + two + three


def add_to(dst, one, two):
    step = math.gcd(dst.shape[0], 16)

    @pl.loop(0, dst.shape[0] // step)
    def _(i):
        at = pl.ds(pl.multiple_of(i * step, step), step)
        dst[at] = one[at].astype(jnp.float32) + two[at].astype(jnp.float32)


def add_into(dst, other):
    rows = dst.shape[0]
    step = math.gcd(rows, 16)

    @pl.loop(0, rows // step)
    def _(i):
        at = pl.ds(pl.multiple_of(i * step, step), step)
        dst[at] = (dst[at].astype(jnp.float32) + other[at].astype(jnp.float32)).astype(dst.dtype)


class SeqSum:
    def __init__(self, grad, block, near, far, sems, place):
        self.grad, self.block, self.near_ref, self.far, self.sems, self.place = grad, block, near, far, sems, place
        self.low, self.row = lax.rem(place.s, 2), place.s // 2
        self.sent = []

    def send(self, src, dst, i, device):
        copy = remote(src, dst, self.sems[0].at[i], self.sems[1].at[i], device)
        copy.start()
        self.sent.append(copy)

    def near(self, i):
        r = (1 - self.row, self.row)[i]
        self.grad(r * 2 + 1 - self.low, self.block.at[i], False)
        self.send(self.block.at[i], self.near_ref.at[i], i, self.place.core_peer)

    def across(self):
        arrived(self.near_ref.at[0], self.sems, 0, self.place.core_peer)
        self.grad((1 - self.row) * 2 + self.low, self.near_ref.at[0], True)
        self.send(self.near_ref.at[0], self.far, 2, self.place.far_peer)

    def own(self):
        arrived(self.near_ref.at[1], self.sems, 1, self.place.core_peer)
        self.grad(self.row * 2 + self.low, self.near_ref.at[1], True)

    def last(self):
        arrived(self.far, self.sems, 2, self.place.far_peer)
        add_into(self.far, self.near_ref.at[1])

    def end(self):
        for copy in self.sent:
            copy.wait_send()


def call(body, outs, args, spaces, out_spaces, scratch, ident):
    return pl.pallas_call(
        body,
        out_shape=outs,
        in_specs=[pl.BlockSpec(memory_space=space) for space in spaces],
        out_specs=[pl.BlockSpec(memory_space=space) for space in out_spaces],
        scratch_shapes=scratch,
        compiler_params=pltpu.CompilerParams(
            collective_id=ident, has_side_effects=True, vmem_limit_bytes=63 * 1024 * 1024
        ),
    )(*args)


def shaped(shape, dtype=jnp.bfloat16):
    return jax.ShapeDtypeStruct(shape, dtype)


def dot(a, b, at=(1, 0)):
    return lax.dot_general(a, b, (((at[0],), (at[1],)), ((), ())), preferred_element_type=jnp.float32)


def chunks(total, size, body):
    @pl.loop(0, total // size)
    def _(i):
        body(pl.ds(pl.multiple_of(i * size, size), size))


def turned(t, cos, sin, sign):
    half = t.shape[1] // 2
    a, b = t[:, :half], t[:, half:]
    return jnp.concatenate([a * cos - sign * b * sin, b * cos + sign * a * sin], axis=-1)


def probabilities(q, k, pos_rows, start_rows, pos_cols):
    scores = dot(q, k, (1, 1)) * HDIM ** (-0.5)
    visible = (pos_cols >= start_rows) & (pos_cols <= pos_rows)
    scores = jnp.where(visible, scores, NEG_FILL)
    weight = jnp.exp(scores - jnp.max(scores, axis=-1, keepdims=True))
    return weight / jnp.sum(weight, axis=-1, keepdims=True)


def place_rows(pairs, segments, block_cos, block_sin, row_cos, row_sin, cos, sin, pos_rows, start_rows, pos_cols):
    f32 = jnp.float32
    half = row_cos.shape[0]
    bounds = [
        jnp.sum(jnp.where(segments[...] < d, 1.0, 0.0).astype(f32), axis=1, keepdims=True) for d in range(1, DOCS)
    ]
    numbers = lax.broadcasted_iota(jnp.int32, block_cos.shape, 0)
    for c in range(RING):
        blocks = (pairs[0, c], 2 * RING - 1 - pairs[0, c])
        lanes = lax.broadcasted_iota(jnp.int32, (1, 2 * half), 1)
        low = blocks[0] * half + lanes
        pos_cols[:, pl.ds(c * 2 * half, 2 * half)] = jnp.where(lanes < half, low, blocks[1] * half + lanes - half).astype(f32)
        for j, block in enumerate(blocks):
            at = pl.ds((2 * c + j) * half, half)
            near_cos = jnp.sum(jnp.where(numbers == block, block_cos[...], 0.0), axis=0, keepdims=True)
            near_sin = jnp.sum(jnp.where(numbers == block, block_sin[...], 0.0), axis=0, keepdims=True)
            cos[at, :] = near_cos * row_cos[...] - near_sin * row_sin[...]
            sin[at, :] = near_sin * row_cos[...] + near_cos * row_sin[...]
            pos = (block * half + lax.broadcasted_iota(jnp.int32, (half, 1), 0)).astype(f32)
            start = jnp.zeros((half, 1), f32)
            for bound in bounds:
                start = jnp.where(pos >= bound, bound, start)
            pos_rows[at, :] = pos
            start_rows[at, :] = start


def column(row):
    n = row.shape[1]
    same = lax.broadcasted_iota(jnp.int32, (n, n), 0) == lax.broadcasted_iota(jnp.int32, (n, n), 1)
    return jnp.sum(jnp.where(same, row, 0.0), axis=1, keepdims=True)


def attention_kernel(plan, x, gain_one, gain_two, pairs, segments, block_cos, block_sin, row_cos, row_sin,
                     dy, w_query, w_key, w_value, wout, w_gate, w_up, wdown,
                     hidden, hhat, ob_local, cos, sin, pos_rows, start_rows, pos_cols,
                     q_out, k_out, v_out, x_all, dy_all, wqkv_all, wout_all, wg_all, wu_own, wdown_all,
                     xhat, wq, wk, wv, wg, wu, heads, gate_units, up_units, x_v, wqkv_v, wout_v, q, k, v, ob, local, loads, *sems):
    place = Place()
    qkv_swap, qkv_seq, out_ring, out_seq, ob_swap, gate_swap, gate_seq, up_swap, down_seq = pairs_of(sems[:18])
    x_grid, dy_grid = sems[18:22], sems[22:26]
    bf16, f32 = jnp.bfloat16, jnp.float32
    rows, width = x.shape
    head, shard = ob.shape[1], wout.shape[0]
    groups = H // KVH
    fetch = [
        pltpu.make_async_copy(src, dst, loads.at[i])
        for i, (src, dst) in enumerate(((w_query, wq), (w_key, wk), (w_value, wv), (w_gate, wg), (w_up, wu)))
    ]
    for copy in fetch:
        copy.start()
    keep = [
        pltpu.make_async_copy(wout, wout_all.at[place.s, place.c], local.at[0]),
        pltpu.make_async_copy(wdown, wdown_all.at[place.s], local.at[1]),
        pltpu.make_async_copy(dy, ByArrival(dy_all, rows, place).owner(place.c), local.at[2]),
    ]
    for copy in keep:
        copy.start()

    def normed(at):
        t = x[at, :].astype(f32)
        xhat[at, :] = (t * lax.rsqrt(jnp.mean(t * t, axis=-1, keepdims=True) + EPSILON)).astype(bf16)

    def scale(ref, gain, columns, into, at):
        @pl.loop(0, RING)
        def _(t):
            for j, cols in enumerate(columns(t)):
                part = (ref[:, cols].astype(f32) * gain).astype(bf16)
                into[t, :, pl.ds(at + j * cols.size, cols.size)] = part

    def prepare():
        chunks(rows, 16, normed)
        for copy in fetch[:3]:
            copy.wait()
        gain = column(gain_one[...].astype(f32))
        scale(wq, gain, lambda t: [block_at(t, head)], heads, 0)
        scale(wk, gain, lambda t: [block_at(t // groups, head)], heads, head)
        scale(wv, gain, lambda t: [block_at(t // groups, head)], heads, 2 * head)

    greet(place.peers() + [place.core_peer, place.far_peer], prepare)
    down_w = seq_gather(wdown, wdown_all, down_seq, place)
    x_blocks, dy_blocks = ByOwner(x_all, rows), ByArrival(dy_all, rows, place)

    def out_flow():
        yield from ring_gather(wout, Owners(wout_all.at[place.s], place), out_ring, place)
        keep[0].wait()
        yield from seq_gather(wout_all.at[place.s], wout_all, out_seq, place)

    out_w = out_flow()

    def spread(src, dst, swap, seq, sem, group=RING):
        rows_of_s = dst if seq is None else dst.at[place.s]
        own = pltpu.make_async_copy(src.at[place.c], rows_of_s.at[place.c], sem)
        own.start()
        yield from by_owner(src, rows_of_s, swap, place, group)
        own.wait()
        if seq is not None:
            yield from seq_gather(rows_of_s, dst, seq, place)

    qkv_w = spread(heads, wqkv_all, qkv_swap, qkv_seq, local.at[3])
    gate_w = spread(gate_units, wg_all, gate_swap, gate_seq, local.at[4], 2)
    up_w = spread(up_units, wu_own, up_swap, None, local.at[5], 2)
    x_flow = grid_gather(xhat, x_blocks, x_grid, place)
    dy_flow = grid_gather(dy, dy_blocks, dy_grid, place)
    own_x = pltpu.make_async_copy(xhat, x_blocks.owner(place.c), local.at[6])

    flows = {"q": qkv_w, "g": gate_w, "u": up_w, "d": down_w, "o": out_w, "x": x_flow, "y": dy_flow}
    mine = block_at(place.c, head)
    flows["b"] = exchange(
        lambda o: [(ob.at[block_at(place.at(o), rows)], ob_local.at[:, mine])],
        lambda o: ob_local.at[:, block_at(place.at(o), head)],
        ob_swap,
        place,
    )
    load = [pltpu.make_async_copy(x_all, x_v, loads.at[0]), pltpu.make_async_copy(wqkv_all, wqkv_v, loads.at[1])]
    saves = [pltpu.make_async_copy(src, dst, loads.at[2 + i]) for i, (src, dst) in enumerate(((q, q_out), (k, k_out), (v, v_out)))]
    load_out = pltpu.make_async_copy(wout_all, wout_v, local.at[0])

    def scale_units():
        for copy in fetch[3:]:
            copy.wait()
        gain = column(gain_two[...].astype(f32))
        own = wdown.shape[0]
        for ref, into in ((wg, gate_units), (wu, up_units)):
            scale(ref, gain, lambda t: [block_at(i * RING + t, own) for i in range(SEQ)], into, 0)

    def find_rows():
        place_rows(
            pairs, segments, block_cos, block_sin, row_cos, row_sin, cos, sin, pos_rows, start_rows, pos_cols
        )

    def load_attention():
        own_x.start()
        own_x.wait()
        for copy in load:
            copy.start()

    halves = x_v.shape[0] // 2

    def project(at):
        qkv = dot(x_v[at, :], wqkv_v[...].reshape(width, 3 * head))
        c, s = cos[at, :], sin[at, :]
        q[at, :] = turned(qkv[:, :head], c, s, 1.0).astype(bf16)
        k[at, :] = turned(qkv[:, head : 2 * head], c, s, 1.0).astype(bf16)
        v[at, :] = qkv[:, 2 * head :].astype(bf16)

    def project_half(i):
        if i == 0:
            for copy in load:
                copy.wait()
        chunks(halves, 256, lambda at: project(pl.ds(pl.multiple_of(i * halves + at.start, 256), 256)))
        if i == 1:
            for copy in saves:
                copy.start()

    def attend(at):
        prob = probabilities(q[at, :], k[...], pos_rows[at, :], start_rows[at, :], pos_cols[...])
        ob[at, :] = dot(prob.astype(bf16), v[...]).astype(bf16)

    def attend_half(i):
        chunks(halves, 256, lambda at: attend(pl.ds(pl.multiple_of(i * halves + at.start, 256), 256)))
        if i == 1:
            ob_local[:, mine] = ob[block_at(place.c, rows), :]

    def finish_hidden():
        load_out.wait()

        def residual(cols):
            part = dot(ob_local[...], wout_v[:, :, :, cols].reshape(width, cols.size))
            hidden[:, cols] = x[:, cols].astype(f32) + part

        chunks(width, 256, residual)

        def normed_two(at):
            t = hidden[at, :]
            hhat[at, :] = (t * lax.rsqrt(jnp.mean(t * t, axis=-1, keepdims=True) + EPSILON)).astype(bf16)

        chunks(rows, 16, normed_two)

    works = {
        "S": scale_units, "R": find_rows, "L": load_attention, "W": load_out.start, "H": finish_hidden,
    }
    turns = {"P": iter((0, 1)), "A": iter((0, 1))}
    for step in plan:
        if step in flows:
            next(flows[step], None)
        elif step in turns:
            (project_half if step == "P" else attend_half)(next(turns[step]))
        else:
            works[step]()
    for name, flow in flows.items():
        if name in plan:
            for _ in flow:
                pass
    if "P" in plan:
        for copy in saves:
            copy.wait()
    elif "L" in plan:
        for copy in load:
            copy.wait()
    if "S" not in plan:
        for copy in fetch[3:]:
            copy.wait()
    if "o" not in plan:
        keep[0].wait()
    if "W" in plan and "H" not in plan:
        load_out.wait()
    keep[1].wait()
    keep[2].wait()


def mlp_kernel(plan, hhat, dy_hbm, wg_hbm, wu_own, wdown_hbm, sum_h, sum_o, col_out, down_out,
               h_all, dy_all, wg, wu, wd, mid, dgate, dup, stage_h, stage_o, stage, stage_2, slots_h, slots_o,
               col_sent, col_near, col_far, down_sent, down_near, down_far, local, *sems):
    place = Place()
    h_sems, sum_h_sems, sum_o_sems, col_seq, down_seq, up_seq = pairs_of(sems)
    greet([place.right, place.left, place.core_peer, place.far_peer])
    rows, width = hhat.shape
    ff = wg.shape[1]
    bf16, f32 = jnp.bfloat16, jnp.float32
    up_blocks = Blocks(wu, wu_own.shape[0])
    keep = [
        pltpu.make_async_copy(src, dst, local.at[i])
        for i, (src, dst) in enumerate(
            ((hhat, h_all.at[pl.ds(0, rows)]), (wg_hbm, wg), (wu_own, up_blocks[place.s]), (wdown_hbm, wd), (dy_hbm, dy_all))
        )
    ]
    for copy in keep:
        copy.start()
    gather = ring_gather(hhat, Rows(h_all, rows), h_sems, place)
    up_flow = seq_gather(wu_own, up_blocks, up_seq, place)

    def hidden_rows(start, count):
        at = pl.ds(start, count)

        def body(cols):
            gate = dot(h_all[at, :], wg[:, cols])
            up = dot(h_all[at, :], wu[:, cols])
            dmid = dot(dy_all[at, :], wd[cols, :], (1, 1))
            sig = jax.nn.sigmoid(gate)
            active = gate * sig
            mid[at, cols] = (active * up).astype(bf16)
            dgate[at, cols] = (dmid * up * sig * (1.0 + gate * (1.0 - sig))).astype(bf16)
            dup[at, cols] = (dmid * active).astype(bf16)

        chunks(ff, 512, body)

    def part_h(start, count, dst):
        at = pl.ds(start, count)

        def body(cols):
            dst[:, cols] = (dot(dgate[at, :], wg[cols, :], (1, 1)) + dot(dup[at, :], wu[cols, :], (1, 1))).astype(bf16)

        chunks(width, 512, body)

    def part_o(start, count, dst):
        at = pl.ds(start, count)

        def body(cols):
            dst[:, cols] = dot(mid[at, :], wd[:, cols]).astype(bf16)

        chunks(width, 1024, body)

    def col_grad(s, dst, add):
        def body(cols):
            lhs = h_all[:, pl.ds(pl.multiple_of(s * dst.shape[0] + cols.start, 256), 256)]
            for side, grad in enumerate((dgate, dup)):
                there = pl.ds(side * ff, ff)
                value = dot(lhs, grad[...], (0, 0))
                if add:
                    value = value + dst[cols, there].astype(f32)
                dst[cols, there] = value.astype(bf16)

        chunks(dst.shape[0], 256, body)

    def down_grad(s, dst, add):
        lhs = pl.ds(pl.multiple_of(s * dst.shape[0], 256), dst.shape[0])

        def body(cols):
            value = dot(mid[:, lhs], dy_all[:, cols], (0, 0))
            if add:
                value = value + dst[:, cols].astype(f32)
            dst[:, cols] = value.astype(bf16)

        chunks(width, 1024, body)

    def pair(ref):
        return (ref.at[pl.ds(rows, rows)], ref.at[pl.ds(0, rows)])

    col_sum = SeqSum(col_grad, col_sent, col_near, col_far, col_seq, place)
    down_sum = SeqSum(down_grad, down_sent, down_near, down_far, down_seq, place)
    ring_h, ring_o = RingSum(slots_h, sum_h_sems, place), RingSum(slots_o, sum_o_sems, place)
    top_h, top_o = stage_h.at[pl.ds(2 * rows, rows)], stage_o.at[pl.ds(2 * rows, rows)]
    next_h, next_o = stage_h.at[pl.ds(0, 2 * rows)], stage_o.at[pl.ds(0, 2 * rows)]

    def in_turn(*actions):
        return iter(actions)

    def parts(part, top, following, later):
        return in_turn(
            lambda: part(7 * rows, rows, top),
            lambda: part(5 * rows, 2 * rows, following),
            lambda: part(3 * rows, 2 * rows, later),
            lambda: part(rows, 2 * rows, later),
            lambda: part(0, rows, later.at[pl.ds(0, rows)]),
        )

    def sums(ring, top, following, later, out):
        return in_turn(
            lambda: ring.first(top),
            lambda: ring.relay(1, pair(following)),
            lambda: ring.relay(2, pair(later)),
            lambda: ring.relay(3, pair(later)),
            lambda: ring.last(later.at[pl.ds(0, rows)], out),
        )

    def wait_loads():
        for copy in keep:
            copy.wait()

    turns = {
        "k": in_turn(wait_loads),
        "a": in_turn(lambda: hidden_rows(0, rows)),
        "b": in_turn(lambda: hidden_rows(rows, 2 * rows)),
        "c": in_turn(lambda: hidden_rows(3 * rows, 2 * rows)),
        "d": in_turn(lambda: hidden_rows(5 * rows, 2 * rows)),
        "e": in_turn(lambda: hidden_rows(7 * rows, rows)),
        "P": parts(part_h, top_h, next_h, stage),
        "r": sums(ring_h, top_h, next_h, stage, sum_h),
        "O": parts(part_o, top_o, next_o, stage_2),
        "s": sums(ring_o, top_o, next_o, stage_2, sum_o),
        "n": in_turn(lambda: col_sum.near(0), lambda: col_sum.near(1)),
        "m": in_turn(col_sum.across),
        "w": in_turn(col_sum.own),
        "l": in_turn(col_sum.last),
        "N": in_turn(lambda: down_sum.near(0), lambda: down_sum.near(1)),
        "M": in_turn(down_sum.across),
        "W": in_turn(down_sum.own),
        "L": in_turn(down_sum.last),
    }
    for step in plan:
        if step == "x":
            next(gather)
        elif step == "u":
            next(up_flow)
        else:
            next(turns[step])()
    ends = []
    for i, (total, out) in enumerate(((col_sum, col_out), (down_sum, down_out))):
        ends.append(pltpu.make_async_copy(total.far, out, local.at[i]))
        ends[-1].start()
    for copy in ends:
        copy.wait()
    for flow in (ring_h, ring_o, col_sum, down_sum):
        flow.end()
    for flow in (gather, up_flow):
        for _ in flow:
            pass


def backward_kernel(plan, weighted, hidden, dy, x, pos_cols, q_hbm, k_hbm, v_hbm, ob_hbm, cos_hbm, sin_hbm, pos_hbm, start_hbm,
                    x_all, wqkv_all, wout_all, col,
                    grad_x, out_grad, qkv_raw, gate_raw, up_raw, col_hbm,
                    q, k, v, ob_local, cos, sin, pos_rows, start_rows,
                    x_v, wqkv_v, wout_v, branch, datt_own, datt, dqkv, dk, dv, sum_x, over_x, line_x,
                    qkv_sent, qkv_near, qkv_far, qkv_in, out_sent, out_near, out_far, slots_o, local, early, *sems):
    place = Place()
    att_swap, qkv_seq, qkv_swap, out_seq, out_ring = pairs_of(sems[:10])
    x_grid, col_swap = sems[10:14], sems[14:]
    bf16, f32 = jnp.bfloat16, jnp.float32
    rows, width = x.shape
    seq_len, head = q.shape
    shard = out_grad.shape[0]
    loads = [
        pltpu.make_async_copy(src, dst, local.at[i])
        for i, (src, dst) in enumerate(((wout_all, wout_v), (x_all, x_v), (wqkv_all, wqkv_v)))
    ]
    for copy in loads:
        copy.start()
    qkv_blocks = Blocks(qkv_far, shard)
    fetched = [
        pltpu.make_async_copy(src, dst, early.at[i])
        for i, (src, dst) in enumerate(
            (
                (ob_hbm, ob_local), (q_hbm, q), (k_hbm, k), (v_hbm, v),
                (cos_hbm, cos), (sin_hbm, sin), (pos_hbm, pos_rows), (start_hbm, start_rows),
            )
        )
    ]
    for copy in fetched:
        copy.start()
    def norm_back(tensor, grads):
        scale = lax.rsqrt(jnp.mean(tensor * tensor, axis=-1, keepdims=True) + EPSILON)
        inner = jnp.mean(grads * tensor, axis=-1, keepdims=True)
        return scale * grads - tensor * (scale * scale * scale) * inner

    def hidden_back(at):
        grads = dy[at, :].astype(f32) + norm_back(hidden[at, :], weighted[at, :])
        grad_x[at, :] = grads
        branch[at, :] = grads.astype(bf16)

    greet(place.peers() + [place.core_peer, place.far_peer], lambda: chunks(rows, 16, hidden_back))

    def heads_back():
        loads[0].wait()
        fetched[0].wait()

        def att_back(cols):
            datt_own[:, cols] = dot(branch[...], wout_v[cols, :], (1, 1)).astype(bf16)

        chunks(width, head, att_back)

    mine = block_at(place.c, rows)
    att_flow = exchange(
        lambda o: [(datt_own.at[:, block_at(place.at(o), head)], datt.at[mine])],
        lambda o: datt.at[block_at(place.at(o), rows)],
        att_swap,
        place,
    )
    def rows_grad(left, right):
        def grad(s, dst, add):
            def body(cols):
                lhs = left[:, pl.ds(pl.multiple_of(s * dst.shape[0] + cols.start, 256), 256)]
                value = dot(lhs, right[...], (0, 0))
                if add:
                    value = value + dst[cols, :].astype(f32)
                dst[cols, :] = value.astype(bf16)

            chunks(dst.shape[0], 256, body)

        return grad

    out_sum = SeqSum(rows_grad(ob_local, branch), out_sent, out_near, out_far, out_seq, place)
    qkv_sum = SeqSum(rows_grad(x_v, dqkv), qkv_sent, qkv_near, qkv_far, qkv_seq, place)
    def attend_back(at):
        prob = probabilities(q[at, :], k[...], pos_rows[at, :], start_rows[at, :], pos_cols[...])
        dprob = dot(datt[at, :], v[...], (1, 1))
        delta = jnp.sum(prob * dprob, axis=-1, keepdims=True)
        dscore = (prob * (dprob - delta)).astype(bf16)
        dq = dot(dscore, k[...]) * HDIM ** (-0.5)
        dqkv[at, pl.ds(0, head)] = turned(dq, cos[at, :], sin[at, :], -1.0).astype(bf16)
        dk[...] += dot(dscore, q[at, :], (0, 0))
        dv[...] += dot(prob.astype(bf16), datt[at, :], (0, 0))

    def finish_back(at):
        turned_dk = turned(dk[at, :] * HDIM ** (-0.5), cos[at, :], sin[at, :], -1.0)
        dqkv[at, pl.ds(head, head)] = turned_dk.astype(bf16)
        dqkv[at, pl.ds(2 * head, head)] = dv[at, :].astype(bf16)

    def all_back():
        dk[...] = jnp.zeros_like(dk)
        dv[...] = jnp.zeros_like(dv)
        datt[mine, :] = datt_own[:, block_at(place.c, head)]
        for copy in loads[1:] + fetched[1:]:
            copy.wait()
        chunks(seq_len, 256, attend_back)
        chunks(seq_len, 128, finish_back)

    part = wout_v.at[pl.ds(0, seq_len)]
    col_in = wout_v.at[pl.ds(seq_len, RING * shard)]
    total = GridSum(part, over_x, line_x, x_grid, place)

    def part_x(i):
        at = block_at(total.plane(i), 2 * rows)

        def body(cols):
            part[at, cols] = dot(dqkv[at, :], wqkv_v[cols, :], (1, 1)).astype(bf16)

        chunks(width, 1024, body)
        total.across(i)

    unit = gate_raw.shape[1] // (RING * SEQ)
    groups = H // KVH

    own_col = pltpu.make_async_copy(Blocks(col, shard)[place.c], Blocks(col_hbm, shard)[place.c], local.at[3])
    own_col.start()
    load_col = pltpu.make_async_copy(col_hbm, col_in, local.at[4])

    def fetch_columns():
        own_col.wait()
        load_col.start()

    def move_columns():
        load_col.wait()
        for c in range(RING):
            for side, raw in enumerate((gate_raw, up_raw)):
                for i in range(SEQ):
                    value = col_in[pl.ds(c * shard, shard), pl.ds((side * SEQ + i) * unit, unit)]
                    raw[:, pl.ds((i * RING + c) * unit, unit)] = value

    own_qkv = pltpu.make_async_copy(qkv_blocks[place.c], qkv_in.at[place.c], local.at[6])

    def qkv_last():
        qkv_sum.last()
        own_qkv.start()

    def tokens_back():
        total.last(sum_x)

        def token_back(at):
            grad_x[at, :] = grad_x[at, :] + norm_back(x[at, :].astype(f32), sum_x[at, :])

        chunks(rows, 16, token_back)

    def finish_qkv():
        own_qkv.wait()
        for t in range(H):
            qkv_raw[:, pl.ds(t * head, head)] = qkv_in[t, :, pl.ds(0, head)].astype(f32)
        for side in (1, 2):
            for t in range(KVH):
                value = sum(qkv_in[t * groups + g, :, pl.ds(side * head, head)].astype(f32) for g in range(groups))
                qkv_raw[:, pl.ds((H + (side - 1) * KVH + t) * head, head)] = value

    def each(action, count=4):
        return iter([functools.partial(action, i) for i in range(count)])

    out_blocks = Owners(Blocks(out_far, shard), place)
    flows = {
        "a": att_flow,
        "c": by_owner(Blocks(col, shard), Blocks(col_hbm, shard), col_swap, place, 2),
        "o": ring_scatter(out_blocks, out_grad, slots_o, out_ring, place),
        "t": by_owner(qkv_blocks, qkv_in, qkv_swap, place),
    }
    works = {
        "h": heads_back, "B": all_back, "m": out_sum.across, "w": out_sum.own, "e": out_sum.last,
        "M": qkv_sum.across, "W": qkv_sum.own, "E": qkv_last, "C": fetch_columns, "V": move_columns, "Z": tokens_back, "F": finish_qkv,
    }
    turns = {"n": each(out_sum.near, 2), "N": each(qkv_sum.near, 2), "p": each(part_x), "l": each(total.along, 3)}
    for step in plan:
        if step in flows:
            next(flows[step])
        elif step in turns:
            next(turns[step])()
        else:
            works[step]()
    for name, flow in flows.items():
        if name in plan:
            for _ in flow:
                pass
    for flow in (total, out_sum, qkv_sum):
        flow.end()


class Blocks:
    def __init__(self, ref, rows):
        self.ref, self.rows = ref, rows
        self.shape = (ref.shape[0] // rows, rows) + tuple(ref.shape[1:])

    @property
    def at(self):
        return self

    def __getitem__(self, i):
        return self.ref.at[pl.ds(pl.multiple_of(i * self.rows, self.rows), self.rows)]


DMA = pltpu.SemaphoreType.DMA
HBM = pl.ANY


ATTENTION_PLAN = "dqxoooxoooxooRqqoooxxSggggqqLyPPAAbygggyuuuuyooWyybHdgu"


def attention_stage(
    tokens, cotangent, gain_attn, w_query, w_key, w_value, w_out, gain_mlp, w_gate, w_up, w_down, pair_order, segments, plan
):
    bf16, f32 = jnp.bfloat16, jnp.float32
    n = RING
    rows, width = tokens.shape[1], tokens.shape[2]
    seq_len = segments.shape[1]
    shard = w_query.shape[0]
    ff_own = w_down.shape[0]
    ff_mine = SEQ * ff_own
    head = HDIM
    frequency = THETA ** (-(np.arange(head // 2) * 2.0 / head))
    half = rows // 2
    block_angles = np.arange(2 * n)[:, None] * half * frequency[None, :]
    row_angles = np.arange(half)[:, None] * frequency[None, :]
    tables = tuple(jnp.asarray(f(angles), f32) for angles in (block_angles, row_angles) for f in (np.cos, np.sin))

    return call(
        functools.partial(attention_kernel, plan),
        [
            shaped((rows, width), f32),
            shaped((rows, width)),
            shaped((rows, H * head)),
            shaped((seq_len, head // 2), f32),
            shaped((seq_len, head // 2), f32),
            shaped((seq_len, 1), f32),
            shaped((seq_len, 1), f32),
            shaped((1, seq_len), f32),
            shaped((seq_len, head)),
            shaped((seq_len, head)),
            shaped((seq_len, head)),
            shaped((seq_len, width)),
            shaped((seq_len, width)),
            shaped((SEQ, n, shard, 3 * head)),
            shaped((SEQ, n, shard, width)),
            shaped((SEQ, n, shard, ff_mine)),
            shaped((n, shard, ff_mine)),
            shaped((SEQ, ff_own, width)),
        ],
        (tokens[0], gain_attn[None], gain_mlp[None], pair_order, segments)
        + tables
        + (cotangent[0], w_query, w_key, w_value, w_out, w_gate, w_up, w_down),
        [VMEM] * 3 + [pltpu.SMEM] + [VMEM] * 5 + [HBM] * 8,
        [VMEM] * 8 + [HBM] * 10,
        [
            VMEM((rows, width), bf16),
            VMEM(w_query.shape, bf16),
            VMEM(w_key.shape, bf16),
            VMEM(w_value.shape, bf16),
            VMEM(w_gate.shape, bf16),
            VMEM(w_up.shape, bf16),
            VMEM((n, shard, 3 * head), bf16),
            VMEM((n, shard, ff_mine), bf16),
            VMEM((n, shard, ff_mine), bf16),
            VMEM((seq_len, width), bf16),
            VMEM((SEQ, n, shard, 3 * head), bf16),
            VMEM((SEQ, n, shard, width), bf16),
        ]
        + [VMEM((seq_len, head), bf16)] * 4
        + [DMA((7,)), DMA((5,))]
        + pair_sems()
        + seq_sems()
        + ring_sems()
        + seq_sems()
        + pair_sems()
        + (pair_sems() + seq_sems()) * 2
        + grid_sems() * 2,
        1,
    )


MLP_PLAN = "xuxkxxuxxuabxxxcdxePrnPrnmOsPrOsNPrNMOsPwrOsOWslL"


def mlp_stage(hhat, dy_all, wg_all, wu_own, wdown_all, plan):
    bf16, f32, n = jnp.bfloat16, jnp.float32, RING
    (rows, width), seq_len = hhat.shape, dy_all.shape[0]
    ff_mine = wg_all.shape[1]
    shard, ff_own = width // (SEQ * n), ff_mine // SEQ
    slot_shape = VMEM((2, n // 2, rows, width), bf16)
    col_piece, down_piece = (n * shard, 2 * ff_mine), (ff_own, width)
    return call(
        functools.partial(mlp_kernel, plan),
        [shaped((rows, width), f32)] * 2 + [shaped(col_piece), shaped(down_piece)],
        (hhat, dy_all, wg_all, wu_own, wdown_all),
        [HBM] * 5,
        [VMEM] * 2 + [HBM] * 2,
        [VMEM((seq_len, width), bf16)] * 2
        + [VMEM((width, ff_mine), bf16)] * 2
        + [VMEM((ff_mine, width), bf16)]
        + [VMEM((seq_len, ff_mine), bf16)] * 3
        + [VMEM((3 * rows, width), bf16)] * 2
        + [VMEM((2 * rows, width), bf16)] * 2
        + [slot_shape] * 2
        + [VMEM((2,) + col_piece, bf16), VMEM((2,) + col_piece, bf16), VMEM(col_piece, bf16)]
        + [VMEM((2,) + down_piece, bf16), VMEM((2,) + down_piece, bf16), VMEM(down_piece, bf16)]
        + [DMA((5,))]
        + ring_sems() * 3
        + seq_sems() * 3,
        2,
    )


BACKWARD_PLAN = "hannmaccccBpNpNplMplwWlEtcCZVteoooooF"


def backward_stage(args, columns, plan):
    bf16, f32, n, head = jnp.bfloat16, jnp.float32, RING, HDIM
    (rows, width), seq_len, shard = args[0].shape, args[5].shape[0], columns[0]
    ff_mine = columns[1] // n
    piece = (n * shard, width)
    qkv_piece = (n * shard, 3 * head)
    outs = call(
        functools.partial(backward_kernel, plan),
        [
            shaped((rows, width), f32),
            shaped((shard, width), f32),
            shaped((shard, (H + 2 * KVH) * head), f32),
            shaped(columns),
            shaped(columns),
            shaped((n * shard, 2 * ff_mine)),
        ],
        args,
        [VMEM] * 5 + [HBM] * 12,
        [VMEM] * 5 + [HBM],
        [VMEM((seq_len, head), bf16)] * 3
        + [VMEM((rows, H * head), bf16)]
        + [VMEM((seq_len, head // 2), f32)] * 2
        + [VMEM((seq_len, 1), f32)] * 2
        + [
            VMEM((seq_len, width), bf16),
            VMEM((width, 3 * head), bf16),
            VMEM((H * head, width), bf16),
            VMEM((rows, width), bf16),
            VMEM((rows, width), bf16),
            VMEM((seq_len, head), bf16),
            VMEM((seq_len, 3 * head), bf16),
            VMEM((seq_len, head), f32),
            VMEM((seq_len, head), f32),
            VMEM((rows, width), f32),
            VMEM((n // 2, rows, width), bf16),
            VMEM((2, n // 2, rows, width), bf16),
        ]
        + [VMEM((2,) + qkv_piece, bf16), VMEM((2,) + qkv_piece, bf16), VMEM(qkv_piece, bf16)]
        + [VMEM((n, shard, 3 * head), bf16)]
        + [VMEM((2,) + piece, bf16), VMEM((2,) + piece, bf16), VMEM(piece, bf16)]
        + [VMEM((2, n // 2, shard, width), bf16), DMA((7,)), DMA((8,))]
        + pair_sems()
        + seq_sems()
        + pair_sems()
        + seq_sems()
        + ring_sems()
        + grid_sum_sems()
        + pair_sems(),
        5,
    )
    return outs[:-1]


def ring_device(
    tokens, cotangent, gain_attn, w_query, w_key, w_value, w_out, gain_mlp, w_gate, w_up, w_down, pair_order, segments
):
    bf16, f32 = jnp.bfloat16, jnp.float32
    n = RING
    rows, width = tokens.shape[1], tokens.shape[2]
    seq_len = segments.shape[1]
    shard = w_query.shape[0]
    ff_own = w_down.shape[0]
    ff_mine = SEQ * ff_own
    head = HDIM
    outs = attention_stage(
        tokens, cotangent, gain_attn, w_query, w_key, w_value, w_out, gain_mlp, w_gate, w_up, w_down,
        pair_order, segments, ATTENTION_PLAN,
    )
    hidden, hhat, ob_local = outs[:3]
    where = outs[3:8]
    q, k, v, x_all, dy_all, wqkv_all, wout_all, wg_all, wu_own, wdown_all = outs[8:]
    wqkv_all = wqkv_all.reshape(width, 3 * head)
    wout_all = wout_all.reshape(H * head, width)
    wg_all = wg_all.reshape(width, ff_mine)
    wu_own = wu_own.reshape(n * shard, ff_mine)
    wdown_all = wdown_all.reshape(ff_mine, width)
    dweighted, out_sum, col_sum, down_sum = mlp_stage(hhat, dy_all, wg_all, wu_own, wdown_all, MLP_PLAN)
    output = (hidden + out_sum).astype(bf16)[None]

    grad_tokens, out_grad, qkv_raw, gate_raw, up_raw = backward_stage(
        (dweighted, hidden, cotangent[0], tokens[0], where[4], q, k, v, ob_local)
        + tuple(where[:4])
        + (x_all, wqkv_all, wout_all, col_sum),
        w_gate.shape, BACKWARD_PLAN,
    )
    gain_one = gain_attn.astype(f32)[:, None]
    gain_two = gain_mlp.astype(f32)[:, None]
    raw_q = qkv_raw[:, : H * head]
    raw_k = qkv_raw[:, H * head : (H + KVH) * head]
    raw_v = qkv_raw[:, (H + KVH) * head :]

    def gain_part(raw, w):
        return jnp.sum(raw.astype(f32) * w.astype(f32), axis=1)

    grad_gain_one = gain_part(raw_q, w_query) + gain_part(raw_k, w_key) + gain_part(raw_v, w_value)
    grad_gain_two = gain_part(gate_raw, w_gate) + gain_part(up_raw, w_up)
    return (
        output,
        grad_tokens[None],
        grad_gain_one,
        raw_q * gain_one,
        raw_k * gain_one,
        raw_v * gain_one,
        out_grad,
        grad_gain_two,
        gate_raw.astype(f32) * gain_two,
        up_raw.astype(f32) * gain_two,
        down_sum.astype(f32),
    )


def solution(mesh):
    placed = (
        P("seq", "ctx", None),
        P("seq", "ctx", None),
        P(("seq", "ctx")),
        P(("seq", "ctx"), None),
        P(("seq", "ctx"), None),
        P(("seq", "ctx"), None),
        P(("seq", "ctx"), None),
        P(("seq", "ctx")),
        P(("seq", "ctx"), None),
        P(("seq", "ctx"), None),
        P(("seq", "ctx"), None),
        P("seq", None),
        P("seq", None),
    )
    fits = mesh.shape["ctx"] == H and mesh.shape["seq"] == 4
    chosen = ring_device if fits else general_device
    return jax.shard_map(
        chosen,
        mesh=mesh,
        in_specs=placed,
        out_specs=(
            P("seq", "ctx", None),
            P("seq", "ctx", None),
            P(("seq", "ctx")),
            P(("seq", "ctx"), None),
            P(("seq", "ctx"), None),
            P(("seq", "ctx"), None),
            P(("seq", "ctx"), None),
            P(("seq", "ctx")),
            P(("seq", "ctx"), None),
            P(("seq", "ctx"), None),
            P(("seq", "ctx"), None),
        ),
        check_vma=False,
    )
```

```python
import functools
import math

import jax
import jax.numpy as jnp
import numpy as np
from jax import lax
from jax.experimental import pallas as pl
from jax.experimental.pallas import tpu as pltpu
from jax.sharding import PartitionSpec as P

H = 8
KVH = 4
HDIM = 256
DOCS = 4


EPSILON = 1e-06
THETA = 1000042.0
NEG_FILL = -1e30


def slot_positions(pair_row, half_rows, pair_count):
    offsets = jnp.arange(half_rows, dtype=jnp.int32)
    low_slots = pair_row[:, None] * half_rows + offsets[None, :]
    high_slots = (2 * pair_count - 1 - pair_row)[:, None] * half_rows + offsets[None, :]
    return jnp.concatenate([low_slots, high_slots], axis=1).reshape(-1)


def rotary_tables(positions, head_dim):
    half_dim = head_dim // 2
    frequency = THETA ** (-(jnp.arange(half_dim, dtype=jnp.float32) * 2.0 / head_dim))
    angles = positions.astype(jnp.float32)[:, None] * frequency[None, :]
    return (jnp.cos(angles)[:, None, :], jnp.sin(angles)[:, None, :])


def rotary(tensor, table_cos, table_sin):
    half_dim = tensor.shape[-1] // 2
    lead_half = tensor[..., :half_dim]
    tail_half = tensor[..., half_dim:]
    return jnp.concatenate(
        [
            lead_half * table_cos - tail_half * table_sin,
            tail_half * table_cos + lead_half * table_sin,
        ],
        axis=-1,
    )


def rms_scale(tensor):
    return lax.rsqrt(jnp.mean(tensor * tensor, axis=-1, keepdims=True) + EPSILON)


def rms_backward(tensor, scale_rows, gain_full, grad_rows):
    weighted = gain_full * grad_rows
    inner_mean = jnp.mean(weighted * tensor, axis=-1, keepdims=True)
    return scale_rows * weighted - tensor * (scale_rows * scale_rows * scale_rows) * inner_mean


def contract_rows(first_mat, second_mat):
    return lax.dot_general(
        first_mat, second_mat, (((0,), (0,)), ((), ())), preferred_element_type=jnp.float32
    )


def contract_cols(first_mat, second_mat):
    return lax.dot_general(
        first_mat, second_mat, (((1,), (1,)), ((), ())), preferred_element_type=jnp.float32
    )


def attention_weights(gain_attn, gain_mlp, w_query, w_key, w_value, w_out):
    return (
        lax.all_gather(gain_attn, ("seq", "ctx"), axis=0, tiled=True),
        lax.all_gather(gain_mlp, ("seq", "ctx"), axis=0, tiled=True),
        lax.all_gather(w_query, ("seq", "ctx"), axis=0, tiled=True),
        lax.all_gather(w_key, ("seq", "ctx"), axis=0, tiled=True),
        lax.all_gather(w_value, ("seq", "ctx"), axis=0, tiled=True),
        lax.all_gather(w_out, ("seq", "ctx"), axis=0, tiled=True),
    )


def mlp_weights(w_gate, w_up, w_down):
    return (
        lax.all_gather(w_gate, ("seq", "ctx"), axis=0, tiled=True),
        lax.all_gather(w_up, ("seq", "ctx"), axis=0, tiled=True),
        lax.all_gather(w_down, ("seq", "ctx"), axis=0, tiled=True),
    )


def reduce_grads(grad_one, grad_two, grad_three):
    seq_count = lax.axis_size("seq")
    grad_one = grad_one.reshape((seq_count, grad_one.shape[0] // seq_count) + grad_one.shape[1:])
    grad_two = grad_two.reshape((seq_count, grad_two.shape[0] // seq_count) + grad_two.shape[1:])
    grad_three = grad_three.reshape(
        (seq_count, grad_three.shape[0] // seq_count) + grad_three.shape[1:]
    )
    grad_one, grad_two, grad_three = (
        lax.psum_scatter(
            grad_one.astype(jnp.bfloat16), "ctx", scatter_dimension=1, tiled=True
        ).astype(jnp.float32),
        lax.psum_scatter(
            grad_two.astype(jnp.bfloat16), "ctx", scatter_dimension=1, tiled=True
        ).astype(jnp.float32),
        lax.psum_scatter(
            grad_three.astype(jnp.bfloat16), "ctx", scatter_dimension=1, tiled=True
        ).astype(jnp.float32),
    )
    grad_one, grad_two, grad_three = (
        lax.psum_scatter(
            grad_one.astype(jnp.bfloat16), "seq", scatter_dimension=0, tiled=True
        ).astype(jnp.float32),
        lax.psum_scatter(
            grad_two.astype(jnp.bfloat16), "seq", scatter_dimension=0, tiled=True
        ).astype(jnp.float32),
        lax.psum_scatter(
            grad_three.astype(jnp.bfloat16), "seq", scatter_dimension=0, tiled=True
        ).astype(jnp.float32),
    )
    return (grad_one[0], grad_two[0], grad_three[0])


def general_device(
    tokens,
    cotangent,
    gain_attn,
    w_query,
    w_key,
    w_value,
    w_out,
    gain_mlp,
    w_gate,
    w_up,
    w_down,
    pair_order,
    segments,
):
    pair_count = lax.axis_size("ctx")
    my_index = lax.axis_index("ctx")
    row_count = tokens.shape[1]
    half_rows = row_count // 2
    seq_len = segments.shape[1]
    head_groups = H // KVH
    score_scale = HDIM ** (-0.5)
    key_rows = math.gcd(seq_len, 512)
    key_steps = seq_len // key_rows
    key_pos = slot_positions(pair_order[0], half_rows, pair_count)
    key_doc = jnp.take(segments[0], key_pos)
    query_pos = lax.dynamic_slice_in_dim(key_pos, my_index * row_count, row_count)
    query_doc = lax.dynamic_slice_in_dim(key_doc, my_index * row_count, row_count)
    rot_cos, rot_sin = rotary_tables(query_pos, HDIM)
    gain_one, gain_two, query_w, key_w, value_w, out_w = attention_weights(
        gain_attn, gain_mlp, w_query, w_key, w_value, w_out
    )
    gain_one = gain_one.astype(jnp.float32)
    gain_two = gain_two.astype(jnp.float32)
    inputs = tokens[0].astype(jnp.float32)
    scale_one = rms_scale(inputs)
    normed = (inputs * scale_one * gain_one).astype(jnp.bfloat16)
    query_proj = jnp.dot(normed, query_w, preferred_element_type=jnp.float32).reshape(
        row_count, H, HDIM
    )
    key_proj = jnp.dot(normed, key_w, preferred_element_type=jnp.float32).reshape(
        row_count, KVH, HDIM
    )
    value_proj = jnp.dot(normed, value_w, preferred_element_type=jnp.float32)
    query_rot = (
        rotary(query_proj, rot_cos, rot_sin)
        .astype(jnp.bfloat16)
        .reshape(row_count, KVH, head_groups, HDIM)
    )
    key_rot = rotary(key_proj, rot_cos, rot_sin).astype(jnp.bfloat16).reshape(row_count, KVH * HDIM)
    value_low = value_proj.astype(jnp.bfloat16)
    key_width = key_rot.shape[1]
    key_all, value_all = (
        lax.all_gather(key_rot, "ctx", axis=0, tiled=True),
        lax.all_gather(value_low, "ctx", axis=0, tiled=True),
    )
    pos_blocks = key_pos.reshape(key_steps, key_rows)
    doc_blocks = key_doc.reshape(key_steps, key_rows)

    def scores_of(key_blk, pos_blk, doc_blk):
        key_heads = key_blk.reshape(key_rows, KVH, HDIM)
        raw_scores = (
            jnp.einsum("qkgd,tkd->kgqt", query_rot, key_heads, preferred_element_type=jnp.float32)
            * score_scale
        )
        visible = (doc_blk[None, :] == query_doc[:, None]) & (
            pos_blk[None, :] <= query_pos[:, None]
        )
        return (raw_scores, visible[None, None])

    def first_pass(carried, step_data):
        running_top, running_sum = carried
        key_blk, pos_blk, doc_blk = step_data
        raw_scores, visible = scores_of(key_blk, pos_blk, doc_blk)
        masked = jnp.where(visible, raw_scores, NEG_FILL)
        new_top = jnp.maximum(running_top, jnp.max(masked, axis=-1))
        added = jnp.sum(jnp.where(visible, jnp.exp(masked - new_top[..., None]), 0.0), axis=-1)
        return ((new_top, running_sum * jnp.exp(running_top - new_top) + added), None)

    start_top = jnp.full((KVH, head_groups, row_count), NEG_FILL, jnp.float32)
    start_sum = jnp.zeros((KVH, head_groups, row_count), jnp.float32)
    key_stack = key_all.reshape(key_steps, key_rows, key_width)
    value_stack = value_all.reshape(key_steps, key_rows, key_width)
    (final_top, final_sum), _ = lax.scan(
        first_pass, (start_top, start_sum), (key_stack, pos_blocks, doc_blocks)
    )
    log_total = final_top + jnp.log(final_sum)

    def second_pass(carried, step_data):
        acc_out, acc_rest = carried
        key_blk, value_blk, pos_blk, doc_blk = step_data
        raw_scores, visible = scores_of(key_blk, pos_blk, doc_blk)
        prob_full = jnp.where(visible, jnp.exp(raw_scores - log_total[..., None]), 0.0)
        prob_low = prob_full.astype(jnp.bfloat16)
        prob_rest = (prob_full - prob_low.astype(jnp.float32)).astype(jnp.bfloat16)
        value_heads = value_blk.reshape(key_rows, KVH, HDIM)
        acc_out = acc_out + jnp.einsum(
            "kgqt,tkd->qkgd", prob_low, value_heads, preferred_element_type=jnp.float32
        )
        acc_rest = acc_rest + jnp.einsum(
            "kgqt,tkd->qkgd", prob_rest, value_heads, preferred_element_type=jnp.float32
        )
        return ((acc_out, acc_rest), None)

    start_acc = jnp.zeros((row_count, KVH, head_groups, HDIM), jnp.float32)
    (attended, attended_rest), _ = lax.scan(
        second_pass, (start_acc, start_acc), (key_stack, value_stack, pos_blocks, doc_blocks)
    )
    exact_out = attended + attended_rest
    out_low = attended.reshape(row_count, H * HDIM).astype(jnp.bfloat16)
    hidden = inputs + jnp.dot(out_low, out_w, preferred_element_type=jnp.float32)
    scale_two = rms_scale(hidden)
    normed_two = (hidden * scale_two * gain_two).astype(jnp.bfloat16)
    grad_out = cotangent[0]
    gate_w, up_w, down_w = mlp_weights(w_gate, w_up, w_down)
    gate_proj = jnp.dot(normed_two, gate_w, preferred_element_type=jnp.float32)
    up_proj = jnp.dot(normed_two, up_w, preferred_element_type=jnp.float32)
    gate_sig = jax.nn.sigmoid(gate_proj)
    active = gate_proj * gate_sig
    middle = (active * up_proj).astype(jnp.bfloat16)
    result = hidden + jnp.dot(middle, down_w, preferred_element_type=jnp.float32)
    output = result.astype(jnp.bfloat16)[None]
    gate_w, up_w, down_w = mlp_weights(w_gate, w_up, w_down)
    grad_mid = contract_cols(grad_out, down_w)
    grad_gate = (grad_mid * up_proj * gate_sig * (1.0 + gate_proj * (1.0 - gate_sig))).astype(
        jnp.bfloat16
    )
    grad_up = (grad_mid * active).astype(jnp.bfloat16)
    grad_norm_two = contract_cols(grad_gate, gate_w) + contract_cols(grad_up, up_w)
    grad_gain_two = jnp.sum(grad_norm_two * hidden * scale_two, axis=0)
    grad_hidden = grad_out.astype(jnp.float32) + rms_backward(
        hidden, scale_two, gain_two, grad_norm_two
    )
    grad_w_gate = contract_rows(normed_two, grad_gate)
    grad_w_up = contract_rows(normed_two, grad_up)
    shard_gain_two, shard_gate, shard_up = reduce_grads(grad_gain_two, grad_w_gate, grad_w_up)
    gain_one, gain_two, query_w, key_w, value_w, out_w = attention_weights(
        gain_attn, gain_mlp, w_query, w_key, w_value, w_out
    )
    gain_one = gain_one.astype(jnp.float32)
    grad_branch = grad_hidden.astype(jnp.bfloat16)
    grad_w_out = contract_rows(out_low, grad_branch)
    grad_att = (
        contract_cols(grad_branch, out_w)
        .astype(jnp.bfloat16)
        .reshape(row_count, KVH, head_groups, HDIM)
    )
    row_delta = jnp.transpose(jnp.sum(grad_att.astype(jnp.float32) * exact_out, axis=-1), (1, 2, 0))
    key_back, value_back = (key_all, value_all)

    def backward_step(grad_query, step_data):
        key_blk, value_blk, pos_blk, doc_blk = step_data
        raw_scores, visible = scores_of(key_blk, pos_blk, doc_blk)
        prob_full = jnp.where(visible, jnp.exp(raw_scores - log_total[..., None]), 0.0)
        prob_low = prob_full.astype(jnp.bfloat16)
        key_heads = key_blk.reshape(key_rows, KVH, HDIM)
        value_heads = value_blk.reshape(key_rows, KVH, HDIM)
        grad_value_blk = jnp.einsum(
            "kgqt,qkgd->tkd", prob_low, grad_att, preferred_element_type=jnp.float32
        )
        grad_probs = jnp.einsum(
            "qkgd,tkd->kgqt", grad_att, value_heads, preferred_element_type=jnp.float32
        )
        grad_scores = (prob_full * (grad_probs - row_delta[..., None])).astype(jnp.bfloat16)
        grad_query = (
            grad_query
            + jnp.einsum(
                "kgqt,tkd->qkgd", grad_scores, key_heads, preferred_element_type=jnp.float32
            )
            * score_scale
        )
        grad_key_blk = (
            jnp.einsum("kgqt,qkgd->tkd", grad_scores, query_rot, preferred_element_type=jnp.float32)
            * score_scale
        )
        return (
            grad_query,
            (
                grad_key_blk.reshape(key_rows, key_width),
                grad_value_blk.reshape(key_rows, key_width),
            ),
        )

    back_keys = key_back.reshape(key_steps, key_rows, key_width)
    back_values = value_back.reshape(key_steps, key_rows, key_width)
    grad_query, (grad_key_steps, grad_value_steps) = lax.scan(
        backward_step, start_acc, (back_keys, back_values, pos_blocks, doc_blocks)
    )
    grad_key_all = grad_key_steps.reshape(seq_len, key_width)
    grad_value_all = grad_value_steps.reshape(seq_len, key_width)
    grad_key_own, grad_value_own = (
        lax.psum_scatter(
            grad_key_all.astype(jnp.bfloat16), "ctx", scatter_dimension=0, tiled=True
        ).astype(jnp.float32),
        lax.psum_scatter(
            grad_value_all.astype(jnp.bfloat16), "ctx", scatter_dimension=0, tiled=True
        ).astype(jnp.float32),
    )
    grad_query = (
        rotary(grad_query.reshape(row_count, H, HDIM), rot_cos, -rot_sin)
        .astype(jnp.bfloat16)
        .reshape(row_count, H * HDIM)
    )
    grad_key = (
        rotary(grad_key_own.reshape(row_count, KVH, HDIM), rot_cos, -rot_sin)
        .astype(jnp.bfloat16)
        .reshape(row_count, key_width)
    )
    grad_value = grad_value_own.astype(jnp.bfloat16)
    grad_w_query = contract_rows(normed, grad_query)
    grad_w_key = contract_rows(normed, grad_key)
    grad_w_value = contract_rows(normed, grad_value)
    grad_normed = (
        contract_cols(grad_query, query_w)
        + contract_cols(grad_key, key_w)
        + contract_cols(grad_value, value_w)
    )
    grad_gain_one = jnp.sum(grad_normed * inputs * scale_one, axis=0)
    grad_tokens = grad_hidden + rms_backward(inputs, scale_one, gain_one, grad_normed)
    grad_w_down = contract_rows(middle, grad_out)
    shard_gain_one, shard_out, shard_down = reduce_grads(grad_gain_one, grad_w_out, grad_w_down)
    shard_query, shard_key, shard_value = reduce_grads(grad_w_query, grad_w_key, grad_w_value)
    return (
        output,
        grad_tokens[None],
        shard_gain_one,
        shard_query,
        shard_key,
        shard_value,
        shard_out,
        shard_gain_two,
        shard_gate,
        shard_up,
        shard_down,
    )


MESH = pl.DeviceIdType.MESH
VMEM = pltpu.VMEM
RING = 8
SEQ = 4


class Place:
    def __init__(self):
        self.c = lax.axis_index("ctx")
        self.s = lax.axis_index("seq")
        self.z, self.x = self.c // 2, lax.rem(self.c, 2)
        self.p = self.z + self.x * (7 - 2 * self.z)
        self.up, self.down = {"ctx": self.c + 2}, {"ctx": self.c - 2}
        self.side = {"ctx": self.c + 1 - 2 * self.x}
        self.right = {"ctx": self.at(1)}
        self.left = {"ctx": self.at(-1)}
        self.s_core = self.s + 1 - 2 * lax.rem(self.s, 2)
        self.s_far = lax.rem(self.s + 2, 4)
        self.s_both = 3 - self.s
        self.core_peer = {"seq": self.s_core}
        self.far_peer = {"seq": self.s_far}

    def at(self, offset):
        q = lax.rem(self.p + offset + 2 * RING, RING)
        return 2 * q + (q // 4) * (15 - 4 * q)

    def peers(self):
        return [{"ctx": lax.rem(self.c + k, RING)} for k in range(1, RING)]


def greet(devices, work=None):
    barrier = pltpu.get_barrier_semaphore()
    for device in devices:
        pl.semaphore_signal(barrier, inc=1, device_id=device, device_id_type=MESH)
    if work is not None:
        work()
    pl.semaphore_wait(barrier, len(devices))


def remote(src, dst, send_sem, recv_sem, device):
    return pltpu.make_async_remote_copy(
        src_ref=src, dst_ref=dst, send_sem=send_sem, recv_sem=recv_sem, device_id=device, device_id_type=MESH
    )


def arrived(ref, sems, index, device):
    remote(ref, ref, sems[0].at[index], sems[1].at[index], device).wait_recv()


def together(*flows):
    live = list(flows)
    while live:
        live = [flow for flow in live if next(flow, "end") != "end"]


def ring_sems():
    return [pltpu.SemaphoreType.DMA((2, RING // 2, 2))] * 2


def slot(offset):
    return 0 if offset == 0 else min(RING - 1, 2 * offset if offset > 0 else -2 * offset - 1)


class Rows:
    def __init__(self, ref, rows):
        self.ref, self.rows = ref, rows

    def here(self, offset):
        return self.ref.at[pl.ds(slot(offset) * self.rows, self.rows)]

    def there(self, offset, d):
        return self.here(offset - 1 if d == 0 else offset + 1)


class Owners:
    def __init__(self, ref, place):
        self.ref, self.place = ref, place

    def here(self, offset):
        return self.ref.at[self.place.at(offset)]

    def there(self, offset, d):
        return self.here(offset)


def ring_gather(own, blocks, sems, place):
    half = own.shape[0] // 2
    steps = RING // 2
    sent = []

    def part(ref, j):
        return ref.at[pl.ds(j * half, half)]

    def wait_for(d, s, j):
        offset = -(s + 1) if d == 0 else s + 1
        arrived(part(blocks.here(offset), j), sems, (d, s, j), place.right if d == 0 else place.left)

    for s in range(steps):
        for j in range(2):
            for d in range(2):
                if s == steps - 1 and j != d:
                    continue
                if s > 0:
                    wait_for(d, s - 1, j)
                offset = -s if d == 0 else s
                copy = remote(
                    part(own if s == 0 else blocks.here(offset), j),
                    part(blocks.there(offset, d), j),
                    sems[0].at[d, s, j],
                    sems[1].at[d, s, j],
                    place.right if d == 0 else place.left,
                )
                copy.start()
                sent.append(copy)
            yield
    for d in range(2):
        wait_for(d, steps - 2, 1 - d)
    yield
    for d in range(2):
        wait_for(d, steps - 1, d)
    yield
    for copy in sent:
        copy.wait_send()


class RingSum:
    def __init__(self, slots, sems, place):
        self.slots, self.sems, self.sent = slots, sems, []
        self.sides = (place.right, place.left)
        self.half = slots.shape[2] // 2

    def rows(self, ref, j):
        return ref.at[pl.ds(j * self.half, self.half)]

    def send(self, d, s, j, source):
        to = self.rows(self.slots.at[d, s], j)
        copy = remote(source, to, self.sems[0].at[d, s, j], self.sems[1].at[d, s, j], self.sides[d])
        copy.start()
        self.sent.append(copy)

    def held(self, d, s, j):
        ref = self.rows(self.slots.at[d, s], j)
        arrived(ref, self.sems, (d, s, j), self.sides[d])
        return ref

    def first(self, part):
        for d in range(2):
            self.send(d, 0, d, self.rows(part, d))

    def relay(self, s, parts):
        for j in range(2):
            for d in range(2):
                source = self.rows(parts[d], j)
                if s > 1 or j == d:
                    held = self.held(d, s - 1, j)
                    add_into(held, source)
                    source = held
                self.send(d, s, j, source)

    def last(self, part, out):
        for j in range(2):
            held = [self.held(d, RING // 2 - 1, j) for d in range(2)]
            sum_of_three(self.rows(out, j), self.rows(part, j), *held)

    def end(self):
        for copy in self.sent:
            copy.wait_send()


def ring_scatter(blocks, out, slots, sems, place):
    ring = RingSum(slots, sems, place)
    ring.first(blocks.here(RING // 2))
    yield
    for s in range(1, RING // 2):
        k = RING // 2 - s
        ring.relay(s, (blocks.here(k), blocks.here(-k)))
        yield
    ring.last(blocks.here(0), out)
    ring.end()
    yield


def pair_sems():
    return [pltpu.SemaphoreType.DMA((RING,))] * 2


OFFSETS = (1, -1, 2, -2, 3, -3, 4)


def exchange(pieces, here, sems, place, group=RING):
    for i in range(0, len(OFFSETS), group):
        for k in OFFSETS[i : i + group]:
            at = slot(k)
            for src, dst in pieces(k):
                remote(src, dst, sems[0].at[at], sems[1].at[at], {"ctx": place.at(k)}).start()
        yield
    for k in OFFSETS:
        arrived(here(k), sems, RING - 1 if k == RING // 2 else slot(-k), {"ctx": place.at(k)})
    for k in OFFSETS:
        remote(here(k), here(k), sems[0].at[slot(k)], sems[1].at[slot(k)], {"ctx": place.at(k)}).wait_send()
    yield


def by_owner(src, dst, sems, place, group=RING):
    return exchange(lambda k: [(src.at[place.at(k)], dst.at[place.c])], lambda k: dst.at[place.at(k)], sems, place, group)


def block_at(i, size):
    return pl.ds(pl.multiple_of(i * size, size), size)


class ByOwner:
    def __init__(self, ref, rows):
        self.ref, self.rows = ref, rows

    def owner(self, c, side=None):
        return self.ref.at[block_at(c, self.rows)]


class ByArrival:
    def __init__(self, ref, rows, place):
        self.ref, self.rows, self.place = ref, rows, place

    def owner(self, c, side="here"):
        far = {"here": 0, "up": 2, "down": -2, "side": 1 - 2 * self.place.x}[side]
        mine = self.place.c + far
        z, x = mine // 2, lax.rem(mine, 2)
        p = z + x * (7 - 2 * z)
        z, x = c // 2, lax.rem(c, 2)
        k = lax.rem(z + x * (7 - 2 * z) - p + 2 * RING, RING)
        late = jnp.where(k == RING // 2, RING - 1, 2 * (RING - k) - 1)
        return self.ref.at[block_at(jnp.where(k < RING // 2, 2 * k, late), self.rows)]


def grid_sems():
    return [pltpu.SemaphoreType.DMA((2, 3))] * 2 + [pltpu.SemaphoreType.DMA((4,))] * 2


def grid_gather(own, blocks, sems, place, late=False):
    z_sems, x_sems = sems[:2], sems[2:]
    z, x = place.z, place.x
    sent = []

    def send(when, src, c, side, pair, index, device):
        copy = remote(src, blocks.owner(c, side), pair[0].at[index], pair[1].at[index], device)
        pl.when(when)(copy.start)
        sent.append((when, copy))

    def across(when, src, line):
        send(when, src, 2 * line + x, "side", x_sems, line, place.side)

    send(z < 3, own, place.c, "up", z_sems, (0, 0), place.up)
    send(z > 0, own, place.c, "down", z_sems, (1, 0), place.down)
    if not late:
        across(z >= 0, own, z)
    yield
    for hop in range(1, 4):
        for d, (line, here, further) in enumerate(((z - hop, z >= hop, z < 3), (z + hop, z <= 3 - hop, z > 0))):
            index = 2 * line + x
            ref = blocks.owner(jnp.clip(index, 0, RING - 1))
            device = (place.down, place.up)[d]

            @pl.when(here)
            def _():
                arrived(ref, z_sems, (d, hop - 1), device)

            if hop < 3:
                send(here & further, ref, jnp.clip(index, 0, RING - 1), ("up", "down")[d], z_sems, (d, hop), (place.up, place.down)[d])
            if not late:
                across_line = jnp.clip(line, 0, 3)
                send(here, ref, 2 * across_line + x, "side", x_sems, across_line, place.side)
        yield
    if late:
        across(z >= 0, own, z)
        for hop in range(1, 4):
            line = lax.rem(z + hop, 4)
            across(z >= 0, blocks.owner(2 * line + x), line)
        yield
    for line in range(4):
        arrived(blocks.owner(2 * line + 1 - x), x_sems, line, place.side)
    for when, copy in sent:
        pl.when(when)(copy.wait_send)
    yield


def grid_sum_sems():
    return [pltpu.SemaphoreType.DMA((4,))] * 2 + [pltpu.SemaphoreType.DMA((2, 4))] * 2


class GridSum:
    def __init__(self, part, over, line, sems, place):
        self.part, self.over, self.line, self.place = part, over, line, place
        self.x_sems, self.z_sems = sems[:2], sems[2:]
        self.rows = over.shape[1]
        self.sent = []

    def plane(self, i):
        z = self.place.z
        inner = jnp.where((z == 1) | (z == 2), 1, 0)
        plain, mid = (3, 2, 1, 0)[i], (3, 0, 2, 1)[i]
        order = plain + inner * (mid - plain)
        return jnp.where(z < 2, order, 3 - order)

    def send(self, when, src, dst, pair, index, device):
        copy = remote(src, dst, pair[0].at[index], pair[1].at[index], device)
        pl.when(when)(copy.start)
        self.sent.append((when, copy))

    def mine(self, z, x):
        return self.part.at[block_at(2 * z + x, self.rows)]

    def across(self, i):
        z = self.plane(i)
        self.send(self.place.z >= 0, self.mine(z, 1 - self.place.x), self.over.at[z], self.x_sems, z, self.place.side)

    def along(self, i):
        z, me = self.plane(i), self.place.z
        held = self.over.at[z]
        arrived(held, self.x_sems, z, self.place.side)
        add_into(held, self.mine(z, self.place.x))
        for d, (when, more, source, device) in enumerate(
            (
                (z > me, me > 0, self.place.down, self.place.up),
                (z < me, me < 3, self.place.up, self.place.down),
            )
        ):

            @pl.when(when & more)
            def _():
                arrived(self.line.at[d, z], self.z_sems, (d, z), source)
                add_into(held, self.line.at[d, z])

            self.send(when, held, self.line.at[d, z], self.z_sems, (d, z), device)

    def last(self, out):
        z = self.place.z
        held = self.over.at[z]
        arrived(held, self.x_sems, z, self.place.side)
        add_to(out, held, self.mine(z, self.place.x))
        for d, (when, source) in enumerate(((z > 0, self.place.down), (z < 3, self.place.up))):

            @pl.when(when)
            def _():
                arrived(self.line.at[d, z], self.z_sems, (d, z), source)
                add_to(out, out, self.line.at[d, z])

    def end(self):
        for when, copy in self.sent:
            pl.when(when)(copy.wait_send)


def pairs_of(sems):
    return [sems[i : i + 2] for i in range(0, len(sems), 2)]


def seq_sems():
    return [pltpu.SemaphoreType.DMA((3,))] * 2


def seq_gather(own, buf, sems, place):
    first = remote(own, buf.at[place.s], sems[0].at[0], sems[1].at[0], place.far_peer)
    second = remote(own, buf.at[place.s], sems[0].at[1], sems[1].at[1], place.core_peer)
    first.start()
    second.start()
    yield
    arrived(buf.at[place.s_far], sems, 0, place.far_peer)
    third = remote(buf.at[place.s_far], buf.at[place.s_far], sems[0].at[2], sems[1].at[2], place.core_peer)
    third.start()
    yield
    arrived(buf.at[place.s_core], sems, 1, place.core_peer)
    arrived(buf.at[place.s_both], sems, 2, place.core_peer)
    for copy in (first, second, third):
        copy.wait_send()
    yield


def sum_of_three(dst, *terms):
    step = math.gcd(dst.shape[0], 16)

    @pl.loop(0, dst.shape[0] // step)
    def _(i):
        at = pl.ds(pl.multiple_of(i * step, step), step)
        one, two, three = (term[at].astype(jnp.float32) for term in terms)
        dst[at] = one + two + three


def add_to(dst, one, two):
    step = math.gcd(dst.shape[0], 16)

    @pl.loop(0, dst.shape[0] // step)
    def _(i):
        at = pl.ds(pl.multiple_of(i * step, step), step)
        dst[at] = one[at].astype(jnp.float32) + two[at].astype(jnp.float32)


def add_into(dst, other):
    rows = dst.shape[0]
    step = math.gcd(rows, 16)

    @pl.loop(0, rows // step)
    def _(i):
        at = pl.ds(pl.multiple_of(i * step, step), step)
        dst[at] = (dst[at].astype(jnp.float32) + other[at].astype(jnp.float32)).astype(dst.dtype)


class SeqSum:
    def __init__(self, grad, block, near, far, sems, place):
        self.grad, self.block, self.near_ref, self.far, self.sems, self.place = grad, block, near, far, sems, place
        self.low, self.row = lax.rem(place.s, 2), place.s // 2
        self.sent = []

    def send(self, src, dst, i, device):
        copy = remote(src, dst, self.sems[0].at[i], self.sems[1].at[i], device)
        copy.start()
        self.sent.append(copy)

    def near(self, i):
        r = (1 - self.row, self.row)[i]
        self.grad(r * 2 + 1 - self.low, self.block.at[i], False)
        self.send(self.block.at[i], self.near_ref.at[i], i, self.place.core_peer)

    def across(self):
        arrived(self.near_ref.at[0], self.sems, 0, self.place.core_peer)
        self.grad((1 - self.row) * 2 + self.low, self.near_ref.at[0], True)
        self.send(self.near_ref.at[0], self.far, 2, self.place.far_peer)

    def own(self):
        arrived(self.near_ref.at[1], self.sems, 1, self.place.core_peer)
        self.grad(self.row * 2 + self.low, self.near_ref.at[1], True)

    def last(self):
        arrived(self.far, self.sems, 2, self.place.far_peer)
        add_into(self.far, self.near_ref.at[1])

    def end(self):
        for copy in self.sent:
            copy.wait_send()


def call(body, outs, args, spaces, out_spaces, scratch, ident):
    return pl.pallas_call(
        body,
        out_shape=outs,
        in_specs=[pl.BlockSpec(memory_space=space) for space in spaces],
        out_specs=[pl.BlockSpec(memory_space=space) for space in out_spaces],
        scratch_shapes=scratch,
        compiler_params=pltpu.CompilerParams(
            collective_id=ident, has_side_effects=True, vmem_limit_bytes=63 * 1024 * 1024
        ),
    )(*args)


def shaped(shape, dtype=jnp.bfloat16):
    return jax.ShapeDtypeStruct(shape, dtype)


def dot(a, b, at=(1, 0)):
    return lax.dot_general(a, b, (((at[0],), (at[1],)), ((), ())), preferred_element_type=jnp.float32)


def chunks(total, size, body):
    @pl.loop(0, total // size)
    def _(i):
        body(pl.ds(pl.multiple_of(i * size, size), size))


def turned(t, cos, sin, sign):
    half = t.shape[1] // 2
    a, b = t[:, :half], t[:, half:]
    return jnp.concatenate([a * cos - sign * b * sin, b * cos + sign * a * sin], axis=-1)


def probabilities(q, k, pos_rows, start_rows, pos_cols):
    scores = dot(q, k, (1, 1)) * HDIM ** (-0.5)
    visible = (pos_cols >= start_rows) & (pos_cols <= pos_rows)
    scores = jnp.where(visible, scores, NEG_FILL)
    weight = jnp.exp(scores - jnp.max(scores, axis=-1, keepdims=True))
    return weight / jnp.sum(weight, axis=-1, keepdims=True)


def place_rows(pairs, segments, block_cos, block_sin, row_cos, row_sin, cos, sin, pos_rows, start_rows, pos_cols):
    f32 = jnp.float32
    half = row_cos.shape[0]
    bounds = [
        jnp.sum(jnp.where(segments[...] < d, 1.0, 0.0).astype(f32), axis=1, keepdims=True) for d in range(1, DOCS)
    ]
    numbers = lax.broadcasted_iota(jnp.int32, block_cos.shape, 0)
    for c in range(RING):
        blocks = (pairs[0, c], 2 * RING - 1 - pairs[0, c])
        lanes = lax.broadcasted_iota(jnp.int32, (1, 2 * half), 1)
        low = blocks[0] * half + lanes
        pos_cols[:, pl.ds(c * 2 * half, 2 * half)] = jnp.where(lanes < half, low, blocks[1] * half + lanes - half).astype(f32)
        for j, block in enumerate(blocks):
            at = pl.ds((2 * c + j) * half, half)
            near_cos = jnp.sum(jnp.where(numbers == block, block_cos[...], 0.0), axis=0, keepdims=True)
            near_sin = jnp.sum(jnp.where(numbers == block, block_sin[...], 0.0), axis=0, keepdims=True)
            cos[at, :] = near_cos * row_cos[...] - near_sin * row_sin[...]
            sin[at, :] = near_sin * row_cos[...] + near_cos * row_sin[...]
            pos = (block * half + lax.broadcasted_iota(jnp.int32, (half, 1), 0)).astype(f32)
            start = jnp.zeros((half, 1), f32)
            for bound in bounds:
                start = jnp.where(pos >= bound, bound, start)
            pos_rows[at, :] = pos
            start_rows[at, :] = start


def column(row):
    n = row.shape[1]
    same = lax.broadcasted_iota(jnp.int32, (n, n), 0) == lax.broadcasted_iota(jnp.int32, (n, n), 1)
    return jnp.sum(jnp.where(same, row, 0.0), axis=1, keepdims=True)


def attention_kernel(plan, x, gain_one, gain_two, pairs, segments, block_cos, block_sin, row_cos, row_sin,
                     dy, w_query, w_key, w_value, wout, w_gate, w_up, wdown,
                     hidden, hhat, ob_local, cos, sin, pos_rows, start_rows, pos_cols,
                     q_out, k_out, v_out, x_all, dy_all, wqkv_all, wout_all, wg_all, wu_own, wdown_all,
                     xhat, wq, wk, wv, wg, wu, wout_s, wdown_s, dy_s, heads, gate_units, up_units, x_v, wqkv_v, wout_v, q, k, v, ob, local, loads, *sems):
    place = Place()
    qkv_swap, qkv_seq, out_ring, out_seq, ob_swap, gate_swap, gate_seq, up_swap, down_seq = pairs_of(sems[:18])
    x_grid, dy_grid = sems[18:22], sems[22:26]
    bf16, f32 = jnp.bfloat16, jnp.float32
    rows, width = x.shape
    head, shard = ob.shape[1], wout.shape[0]
    groups = H // KVH
    fetch = [
        pltpu.make_async_copy(src, dst, loads.at[i])
        for i, (src, dst) in enumerate(
            (
                (w_query, wq), (w_key, wk), (w_value, wv), (w_gate, wg), (w_up, wu),
                (wout, wout_s), (wdown, wdown_s), (dy, dy_s),
            )
        )
    ]
    for copy in fetch:
        copy.start()
    keep = [
        pltpu.make_async_copy(wout_s, wout_all.at[place.s, place.c], local.at[0]),
        pltpu.make_async_copy(wdown_s, wdown_all.at[place.s], local.at[1]),
        pltpu.make_async_copy(dy_s, ByArrival(dy_all, rows, place).owner(place.c), local.at[2]),
    ]

    def normed(at):
        t = x[at, :].astype(f32)
        xhat[at, :] = (t * lax.rsqrt(jnp.mean(t * t, axis=-1, keepdims=True) + EPSILON)).astype(bf16)

    def scale(ref, gain, columns, into, at):
        @pl.loop(0, RING)
        def _(t):
            for j, cols in enumerate(columns(t)):
                part = (ref[:, cols].astype(f32) * gain).astype(bf16)
                into[t, :, pl.ds(at + j * cols.size, cols.size)] = part

    def prepare():
        chunks(rows, 16, normed)
        for loaded, kept in zip(fetch[5:], keep):
            loaded.wait()
            kept.start()
        for copy in fetch[:3]:
            copy.wait()
        gain = column(gain_one[...].astype(f32))
        scale(wq, gain, lambda t: [block_at(t, head)], heads, 0)
        scale(wk, gain, lambda t: [block_at(t // groups, head)], heads, head)
        scale(wv, gain, lambda t: [block_at(t // groups, head)], heads, 2 * head)

    greet(place.peers() + [place.core_peer, place.far_peer], prepare)
    down_w = seq_gather(wdown, wdown_all, down_seq, place)
    x_blocks, dy_blocks = ByOwner(x_all, rows), ByArrival(dy_all, rows, place)

    def out_flow():
        yield from ring_gather(wout, Owners(wout_all.at[place.s], place), out_ring, place)
        keep[0].wait()
        yield from seq_gather(wout_all.at[place.s], wout_all, out_seq, place)

    out_w = out_flow()

    def spread(src, dst, swap, seq, sem, group=RING):
        rows_of_s = dst if seq is None else dst.at[place.s]
        own = pltpu.make_async_copy(src.at[place.c], rows_of_s.at[place.c], sem)
        own.start()
        yield from by_owner(src, rows_of_s, swap, place, group)
        own.wait()
        if seq is not None:
            yield from seq_gather(rows_of_s, dst, seq, place)

    qkv_w = spread(heads, wqkv_all, qkv_swap, qkv_seq, local.at[3])
    gate_w = spread(gate_units, wg_all, gate_swap, gate_seq, local.at[4], 2)
    up_w = spread(up_units, wu_own, up_swap, None, local.at[5], 2)
    x_flow = grid_gather(xhat, x_blocks, x_grid, place)
    dy_flow = grid_gather(dy, dy_blocks, dy_grid, place)
    own_x = pltpu.make_async_copy(xhat, x_blocks.owner(place.c), local.at[6])

    flows = {"q": qkv_w, "g": gate_w, "u": up_w, "d": down_w, "o": out_w, "x": x_flow, "y": dy_flow}
    mine = block_at(place.c, head)
    flows["b"] = exchange(
        lambda o: [(ob.at[block_at(place.at(o), rows)], ob_local.at[:, mine])],
        lambda o: ob_local.at[:, block_at(place.at(o), head)],
        ob_swap,
        place,
    )
    load = [pltpu.make_async_copy(x_all, x_v, loads.at[0]), pltpu.make_async_copy(wqkv_all, wqkv_v, loads.at[1])]
    saves = [pltpu.make_async_copy(src, dst, loads.at[2 + i]) for i, (src, dst) in enumerate(((q, q_out), (k, k_out), (v, v_out)))]
    load_out = pltpu.make_async_copy(wout_all, wout_v, local.at[0])

    def scale_units():
        for copy in fetch[3:5]:
            copy.wait()
        gain = column(gain_two[...].astype(f32))
        own = wdown.shape[0]
        for ref, into in ((wg, gate_units), (wu, up_units)):
            scale(ref, gain, lambda t: [block_at(i * RING + t, own) for i in range(SEQ)], into, 0)

    def find_rows():
        place_rows(
            pairs, segments, block_cos, block_sin, row_cos, row_sin, cos, sin, pos_rows, start_rows, pos_cols
        )

    def load_attention():
        own_x.start()
        own_x.wait()
        for copy in load:
            copy.start()

    halves = x_v.shape[0] // 2

    def project(at):
        qkv = dot(x_v[at, :], wqkv_v[...].reshape(width, 3 * head))
        c, s = cos[at, :], sin[at, :]
        q[at, :] = turned(qkv[:, :head], c, s, 1.0).astype(bf16)
        k[at, :] = turned(qkv[:, head : 2 * head], c, s, 1.0).astype(bf16)
        v[at, :] = qkv[:, 2 * head :].astype(bf16)

    def project_half(i):
        if i == 0:
            for copy in load:
                copy.wait()
        chunks(halves, 256, lambda at: project(pl.ds(pl.multiple_of(i * halves + at.start, 256), 256)))
        if i == 1:
            for copy in saves:
                copy.start()

    def attend(at):
        prob = probabilities(q[at, :], k[...], pos_rows[at, :], start_rows[at, :], pos_cols[...])
        ob[at, :] = dot(prob.astype(bf16), v[...]).astype(bf16)

    def attend_half(i):
        chunks(halves, 256, lambda at: attend(pl.ds(pl.multiple_of(i * halves + at.start, 256), 256)))
        if i == 1:
            ob_local[:, mine] = ob[block_at(place.c, rows), :]

    def finish_hidden():
        load_out.wait()

        def residual(cols):
            part = dot(ob_local[...], wout_v[:, :, :, cols].reshape(width, cols.size))
            hidden[:, cols] = x[:, cols].astype(f32) + part

        chunks(width, 256, residual)

        def normed_two(at):
            t = hidden[at, :]
            hhat[at, :] = (t * lax.rsqrt(jnp.mean(t * t, axis=-1, keepdims=True) + EPSILON)).astype(bf16)

        chunks(rows, 16, normed_two)

    works = {
        "S": scale_units, "R": find_rows, "L": load_attention, "W": load_out.start, "H": finish_hidden,
    }
    turns = {"P": iter((0, 1)), "A": iter((0, 1))}
    for step in plan:
        if step in flows:
            next(flows[step], None)
        elif step in turns:
            (project_half if step == "P" else attend_half)(next(turns[step]))
        else:
            works[step]()
    for name, flow in flows.items():
        if name in plan:
            for _ in flow:
                pass
    if "P" in plan:
        for copy in saves:
            copy.wait()
    elif "L" in plan:
        for copy in load:
            copy.wait()
    if "S" not in plan:
        for copy in fetch[3:5]:
            copy.wait()
    if "o" not in plan:
        keep[0].wait()
    if "W" in plan and "H" not in plan:
        load_out.wait()
    keep[1].wait()
    keep[2].wait()


def mlp_kernel(plan, hhat, dy_hbm, wg_hbm, wu_own, wdown_hbm, sum_h, sum_o, col_out, down_out,
               h_all, dy_all, wg, wu, wd, mid, dgate, dup, stage_h, stage_o, stage, stage_2, slots_h, slots_o,
               col_sent, col_near, col_far, down_sent, down_near, down_far, local, *sems):
    place = Place()
    h_sems, sum_h_sems, sum_o_sems, col_seq, down_seq, up_seq = pairs_of(sems)
    greet([place.right, place.left, place.core_peer, place.far_peer])
    rows, width = hhat.shape
    ff = wg.shape[1]
    bf16, f32 = jnp.bfloat16, jnp.float32
    up_blocks = Blocks(wu, wu_own.shape[0])
    keep = [
        pltpu.make_async_copy(src, dst, local.at[i])
        for i, (src, dst) in enumerate(
            ((hhat, h_all.at[pl.ds(0, rows)]), (wg_hbm, wg), (wu_own, up_blocks[place.s]), (wdown_hbm, wd), (dy_hbm, dy_all))
        )
    ]
    for copy in keep:
        copy.start()
    gather = ring_gather(hhat, Rows(h_all, rows), h_sems, place)
    up_flow = seq_gather(wu_own, up_blocks, up_seq, place)

    def hidden_rows(start, count):
        at = pl.ds(start, count)

        def body(cols):
            gate = dot(h_all[at, :], wg[:, cols])
            up = dot(h_all[at, :], wu[:, cols])
            dmid = dot(dy_all[at, :], wd[cols, :], (1, 1))
            sig = jax.nn.sigmoid(gate)
            active = gate * sig
            mid[at, cols] = (active * up).astype(bf16)
            dgate[at, cols] = (dmid * up * sig * (1.0 + gate * (1.0 - sig))).astype(bf16)
            dup[at, cols] = (dmid * active).astype(bf16)

        chunks(ff, 512, body)

    def part_h(start, count, dst):
        at = pl.ds(start, count)

        def body(cols):
            dst[:, cols] = (dot(dgate[at, :], wg[cols, :], (1, 1)) + dot(dup[at, :], wu[cols, :], (1, 1))).astype(bf16)

        chunks(width, 512, body)

    def part_o(start, count, dst):
        at = pl.ds(start, count)

        def body(cols):
            dst[:, cols] = dot(mid[at, :], wd[:, cols]).astype(bf16)

        chunks(width, 1024, body)

    def col_grad(s, dst, add):
        def body(cols):
            lhs = h_all[:, pl.ds(pl.multiple_of(s * dst.shape[0] + cols.start, 256), 256)]
            for side, grad in enumerate((dgate, dup)):
                there = pl.ds(side * ff, ff)
                value = dot(lhs, grad[...], (0, 0))
                if add:
                    value = value + dst[cols, there].astype(f32)
                dst[cols, there] = value.astype(bf16)

        chunks(dst.shape[0], 256, body)

    def down_grad(s, dst, add):
        lhs = pl.ds(pl.multiple_of(s * dst.shape[0], 256), dst.shape[0])

        def body(cols):
            value = dot(mid[:, lhs], dy_all[:, cols], (0, 0))
            if add:
                value = value + dst[:, cols].astype(f32)
            dst[:, cols] = value.astype(bf16)

        chunks(width, 1024, body)

    def pair(ref):
        return (ref.at[pl.ds(rows, rows)], ref.at[pl.ds(0, rows)])

    col_sum = SeqSum(col_grad, col_sent, col_near, col_far, col_seq, place)
    down_sum = SeqSum(down_grad, down_sent, down_near, down_far, down_seq, place)
    ring_h, ring_o = RingSum(slots_h, sum_h_sems, place), RingSum(slots_o, sum_o_sems, place)
    top_h, top_o = stage_h.at[pl.ds(2 * rows, rows)], stage_o.at[pl.ds(2 * rows, rows)]
    next_h, next_o = stage_h.at[pl.ds(0, 2 * rows)], stage_o.at[pl.ds(0, 2 * rows)]

    def in_turn(*actions):
        return iter(actions)

    def parts(part, top, following, later):
        return in_turn(
            lambda: part(7 * rows, rows, top),
            lambda: part(5 * rows, 2 * rows, following),
            lambda: part(3 * rows, 2 * rows, later),
            lambda: part(rows, 2 * rows, later),
            lambda: part(0, rows, later.at[pl.ds(0, rows)]),
        )

    def sums(ring, top, following, later, out):
        return in_turn(
            lambda: ring.first(top),
            lambda: ring.relay(1, pair(following)),
            lambda: ring.relay(2, pair(later)),
            lambda: ring.relay(3, pair(later)),
            lambda: ring.last(later.at[pl.ds(0, rows)], out),
        )

    def wait_loads():
        for copy in keep:
            copy.wait()

    turns = {
        "k": in_turn(wait_loads),
        "a": in_turn(lambda: hidden_rows(0, rows)),
        "b": in_turn(lambda: hidden_rows(rows, 2 * rows)),
        "c": in_turn(lambda: hidden_rows(3 * rows, 2 * rows)),
        "d": in_turn(lambda: hidden_rows(5 * rows, 2 * rows)),
        "e": in_turn(lambda: hidden_rows(7 * rows, rows)),
        "P": parts(part_h, top_h, next_h, stage),
        "r": sums(ring_h, top_h, next_h, stage, sum_h),
        "O": parts(part_o, top_o, next_o, stage_2),
        "s": sums(ring_o, top_o, next_o, stage_2, sum_o),
        "n": in_turn(lambda: col_sum.near(0), lambda: col_sum.near(1)),
        "m": in_turn(col_sum.across),
        "w": in_turn(col_sum.own),
        "l": in_turn(col_sum.last),
        "N": in_turn(lambda: down_sum.near(0), lambda: down_sum.near(1)),
        "M": in_turn(down_sum.across),
        "W": in_turn(down_sum.own),
        "L": in_turn(down_sum.last),
    }
    for step in plan:
        if step == "x":
            next(gather)
        elif step == "u":
            next(up_flow)
        else:
            next(turns[step])()
    ends = []
    for i, (total, out) in enumerate(((col_sum, col_out), (down_sum, down_out))):
        ends.append(pltpu.make_async_copy(total.far, out, local.at[i]))
        ends[-1].start()
    for copy in ends:
        copy.wait()
    for flow in (ring_h, ring_o, col_sum, down_sum):
        flow.end()
    for flow in (gather, up_flow):
        for _ in flow:
            pass


def backward_kernel(plan, weighted, hidden, dy, x, pos_cols, q_hbm, k_hbm, v_hbm, ob_hbm, cos_hbm, sin_hbm, pos_hbm, start_hbm,
                    x_all, wqkv_all, wout_all, col,
                    grad_x, out_grad, qkv_raw, gate_raw, up_raw, col_hbm,
                    q, k, v, ob_local, cos, sin, pos_rows, start_rows,
                    x_v, wqkv_v, wout_v, branch, datt_own, datt, dqkv, dk, dv, sum_x, over_x, line_x,
                    qkv_sent, qkv_near, qkv_far, qkv_in, out_sent, out_near, out_far, slots_o, local, early, *sems):
    place = Place()
    att_swap, qkv_seq, qkv_swap, out_seq, out_ring = pairs_of(sems[:10])
    x_grid, col_swap = sems[10:14], sems[14:]
    bf16, f32 = jnp.bfloat16, jnp.float32
    rows, width = x.shape
    seq_len, head = q.shape
    shard = out_grad.shape[0]
    loads = [
        pltpu.make_async_copy(src, dst, local.at[i])
        for i, (src, dst) in enumerate(((wout_all, wout_v), (x_all, x_v), (wqkv_all, wqkv_v)))
    ]
    for copy in loads:
        copy.start()
    qkv_blocks = Blocks(qkv_far, shard)
    fetched = [
        pltpu.make_async_copy(src, dst, early.at[i])
        for i, (src, dst) in enumerate(
            (
                (ob_hbm, ob_local), (q_hbm, q), (k_hbm, k), (v_hbm, v),
                (cos_hbm, cos), (sin_hbm, sin), (pos_hbm, pos_rows), (start_hbm, start_rows),
            )
        )
    ]
    for copy in fetched:
        copy.start()
    def norm_back(tensor, grads):
        scale = lax.rsqrt(jnp.mean(tensor * tensor, axis=-1, keepdims=True) + EPSILON)
        inner = jnp.mean(grads * tensor, axis=-1, keepdims=True)
        return scale * grads - tensor * (scale * scale * scale) * inner

    def hidden_back(at):
        grads = dy[at, :].astype(f32) + norm_back(hidden[at, :], weighted[at, :])
        grad_x[at, :] = grads
        branch[at, :] = grads.astype(bf16)

    greet(place.peers() + [place.core_peer, place.far_peer], lambda: chunks(rows, 16, hidden_back))

    def heads_back():
        loads[0].wait()
        fetched[0].wait()

        def att_back(cols):
            datt_own[:, cols] = dot(branch[...], wout_v[cols, :], (1, 1)).astype(bf16)

        chunks(width, head, att_back)

    mine = block_at(place.c, rows)
    att_flow = exchange(
        lambda o: [(datt_own.at[:, block_at(place.at(o), head)], datt.at[mine])],
        lambda o: datt.at[block_at(place.at(o), rows)],
        att_swap,
        place,
    )
    def rows_grad(left, right):
        def grad(s, dst, add):
            def body(cols):
                lhs = left[:, pl.ds(pl.multiple_of(s * dst.shape[0] + cols.start, 256), 256)]
                value = dot(lhs, right[...], (0, 0))
                if add:
                    value = value + dst[cols, :].astype(f32)
                dst[cols, :] = value.astype(bf16)

            chunks(dst.shape[0], 256, body)

        return grad

    out_sum = SeqSum(rows_grad(ob_local, branch), out_sent, out_near, out_far, out_seq, place)
    qkv_sum = SeqSum(rows_grad(x_v, dqkv), qkv_sent, qkv_near, qkv_far, qkv_seq, place)
    def attend_back(at):
        prob = probabilities(q[at, :], k[...], pos_rows[at, :], start_rows[at, :], pos_cols[...])
        dprob = dot(datt[at, :], v[...], (1, 1))
        delta = jnp.sum(prob * dprob, axis=-1, keepdims=True)
        dscore = (prob * (dprob - delta)).astype(bf16)
        dq = dot(dscore, k[...]) * HDIM ** (-0.5)
        dqkv[at, pl.ds(0, head)] = turned(dq, cos[at, :], sin[at, :], -1.0).astype(bf16)
        dk[...] += dot(dscore, q[at, :], (0, 0))
        dv[...] += dot(prob.astype(bf16), datt[at, :], (0, 0))

    def finish_back(at):
        turned_dk = turned(dk[at, :] * HDIM ** (-0.5), cos[at, :], sin[at, :], -1.0)
        dqkv[at, pl.ds(head, head)] = turned_dk.astype(bf16)
        dqkv[at, pl.ds(2 * head, head)] = dv[at, :].astype(bf16)

    def all_back():
        dk[...] = jnp.zeros_like(dk)
        dv[...] = jnp.zeros_like(dv)
        datt[mine, :] = datt_own[:, block_at(place.c, head)]
        for copy in loads[1:] + fetched[1:]:
            copy.wait()
        chunks(seq_len, 256, attend_back)
        chunks(seq_len, 128, finish_back)

    part = wout_v.at[pl.ds(0, seq_len)]
    col_in = wout_v.at[pl.ds(seq_len, RING * shard)]
    total = GridSum(part, over_x, line_x, x_grid, place)

    def part_x(i):
        at = block_at(total.plane(i), 2 * rows)

        def body(cols):
            part[at, cols] = dot(dqkv[at, :], wqkv_v[cols, :], (1, 1)).astype(bf16)

        chunks(width, 1024, body)
        total.across(i)

    unit = gate_raw.shape[1] // (RING * SEQ)
    groups = H // KVH

    def fetch_columns():
        for k in (0,) + OFFSETS:
            c = place.at(k)
            source = Blocks(col_hbm if k else col, shard)
            pltpu.make_async_copy(source[c], Blocks(col_in, shard)[c], local.at[4]).start()

    def move_columns():
        pltpu.make_async_copy(col_in, col_in, local.at[4]).wait()
        for c in range(RING):
            for side, raw in enumerate((gate_raw, up_raw)):
                for i in range(SEQ):
                    value = col_in[pl.ds(c * shard, shard), pl.ds((side * SEQ + i) * unit, unit)]
                    raw[:, pl.ds((i * RING + c) * unit, unit)] = value

    def qkv_last():
        qkv_sum.last()
        qkv_in[place.c] = qkv_blocks[place.c][...]

    def tokens_back():
        total.last(sum_x)

        def token_back(at):
            grad_x[at, :] = grad_x[at, :] + norm_back(x[at, :].astype(f32), sum_x[at, :])

        chunks(rows, 16, token_back)

    def finish_qkv():
        for t in range(H):
            qkv_raw[:, pl.ds(t * head, head)] = qkv_in[t, :, pl.ds(0, head)].astype(f32)
        for side in (1, 2):
            for t in range(KVH):
                value = sum(qkv_in[t * groups + g, :, pl.ds(side * head, head)].astype(f32) for g in range(groups))
                qkv_raw[:, pl.ds((H + (side - 1) * KVH + t) * head, head)] = value

    def each(action, count=4):
        return iter([functools.partial(action, i) for i in range(count)])

    out_blocks = Owners(Blocks(out_far, shard), place)
    flows = {
        "a": att_flow,
        "c": by_owner(Blocks(col, shard), Blocks(col_hbm, shard), col_swap, place, 2),
        "o": ring_scatter(out_blocks, out_grad, slots_o, out_ring, place),
        "t": by_owner(qkv_blocks, qkv_in, qkv_swap, place),
    }
    works = {
        "h": heads_back, "B": all_back, "m": out_sum.across, "w": out_sum.own, "e": out_sum.last,
        "M": qkv_sum.across, "W": qkv_sum.own, "E": qkv_last, "C": fetch_columns, "V": move_columns, "Z": tokens_back, "F": finish_qkv,
    }
    turns = {"n": each(out_sum.near, 2), "N": each(qkv_sum.near, 2), "p": each(part_x), "l": each(total.along, 3)}
    for step in plan:
        if step in flows:
            next(flows[step])
        elif step in turns:
            next(turns[step])()
        else:
            works[step]()
    for name, flow in flows.items():
        if name in plan:
            for _ in flow:
                pass
    for flow in (total, out_sum, qkv_sum):
        flow.end()


class Blocks:
    def __init__(self, ref, rows):
        self.ref, self.rows = ref, rows
        self.shape = (ref.shape[0] // rows, rows) + tuple(ref.shape[1:])

    @property
    def at(self):
        return self

    def __getitem__(self, i):
        return self.ref.at[pl.ds(pl.multiple_of(i * self.rows, self.rows), self.rows)]


DMA = pltpu.SemaphoreType.DMA
HBM = pl.ANY


ATTENTION_PLAN = "doooooooooooxxqxxqqRSggggqqxLyPPAAbgygyuuuuyoogWbHydgu"


def attention_stage(
    tokens, cotangent, gain_attn, w_query, w_key, w_value, w_out, gain_mlp, w_gate, w_up, w_down, pair_order, segments, plan
):
    bf16, f32 = jnp.bfloat16, jnp.float32
    n = RING
    rows, width = tokens.shape[1], tokens.shape[2]
    seq_len = segments.shape[1]
    shard = w_query.shape[0]
    ff_own = w_down.shape[0]
    ff_mine = SEQ * ff_own
    head = HDIM
    frequency = THETA ** (-(np.arange(head // 2) * 2.0 / head))
    half = rows // 2
    block_angles = np.arange(2 * n)[:, None] * half * frequency[None, :]
    row_angles = np.arange(half)[:, None] * frequency[None, :]
    tables = tuple(jnp.asarray(f(angles), f32) for angles in (block_angles, row_angles) for f in (np.cos, np.sin))

    return call(
        functools.partial(attention_kernel, plan),
        [
            shaped((rows, width), f32),
            shaped((rows, width)),
            shaped((rows, H * head)),
            shaped((seq_len, head // 2), f32),
            shaped((seq_len, head // 2), f32),
            shaped((seq_len, 1), f32),
            shaped((seq_len, 1), f32),
            shaped((1, seq_len), f32),
            shaped((seq_len, head)),
            shaped((seq_len, head)),
            shaped((seq_len, head)),
            shaped((seq_len, width)),
            shaped((seq_len, width)),
            shaped((SEQ, n, shard, 3 * head)),
            shaped((SEQ, n, shard, width)),
            shaped((SEQ, n, shard, ff_mine)),
            shaped((n, shard, ff_mine)),
            shaped((SEQ, ff_own, width)),
        ],
        (tokens[0], gain_attn[None], gain_mlp[None], pair_order, segments)
        + tables
        + (cotangent[0], w_query, w_key, w_value, w_out, w_gate, w_up, w_down),
        [VMEM] * 3 + [pltpu.SMEM] + [VMEM] * 5 + [HBM] * 8,
        [VMEM] * 8 + [HBM] * 10,
        [
            VMEM((rows, width), bf16),
            VMEM(w_query.shape, bf16),
            VMEM(w_key.shape, bf16),
            VMEM(w_value.shape, bf16),
            VMEM(w_gate.shape, bf16),
            VMEM(w_up.shape, bf16),
            VMEM(w_out.shape, bf16),
            VMEM(w_down.shape, bf16),
            VMEM((rows, width), bf16),
            VMEM((n, shard, 3 * head), bf16),
            VMEM((n, shard, ff_mine), bf16),
            VMEM((n, shard, ff_mine), bf16),
            VMEM((seq_len, width), bf16),
            VMEM((SEQ, n, shard, 3 * head), bf16),
            VMEM((SEQ, n, shard, width), bf16),
        ]
        + [VMEM((seq_len, head), bf16)] * 4
        + [DMA((7,)), DMA((8,))]
        + pair_sems()
        + seq_sems()
        + ring_sems()
        + seq_sems()
        + pair_sems()
        + (pair_sems() + seq_sems()) * 2
        + grid_sems() * 2,
        1,
    )


MLP_PLAN = "xuxkxxuxxuabxxxcdxePrnPrnmOsPrOsNPrNMOsPwrOsOWslL"


def mlp_stage(hhat, dy_all, wg_all, wu_own, wdown_all, plan):
    bf16, f32, n = jnp.bfloat16, jnp.float32, RING
    (rows, width), seq_len = hhat.shape, dy_all.shape[0]
    ff_mine = wg_all.shape[1]
    shard, ff_own = width // (SEQ * n), ff_mine // SEQ
    slot_shape = VMEM((2, n // 2, rows, width), bf16)
    col_piece, down_piece = (n * shard, 2 * ff_mine), (ff_own, width)
    return call(
        functools.partial(mlp_kernel, plan),
        [shaped((rows, width), f32)] * 2 + [shaped(col_piece), shaped(down_piece)],
        (hhat, dy_all, wg_all, wu_own, wdown_all),
        [HBM] * 5,
        [VMEM] * 2 + [HBM] * 2,
        [VMEM((seq_len, width), bf16)] * 2
        + [VMEM((width, ff_mine), bf16)] * 2
        + [VMEM((ff_mine, width), bf16)]
        + [VMEM((seq_len, ff_mine), bf16)] * 3
        + [VMEM((3 * rows, width), bf16)] * 2
        + [VMEM((2 * rows, width), bf16)] * 2
        + [slot_shape] * 2
        + [VMEM((2,) + col_piece, bf16), VMEM((2,) + col_piece, bf16), VMEM(col_piece, bf16)]
        + [VMEM((2,) + down_piece, bf16), VMEM((2,) + down_piece, bf16), VMEM(down_piece, bf16)]
        + [DMA((5,))]
        + ring_sems() * 3
        + seq_sems() * 3,
        2,
    )


BACKWARD_PLAN = "hannmaccccBpNpNplMplwWlEtcCZVteoooooF"


def backward_stage(args, columns, plan):
    bf16, f32, n, head = jnp.bfloat16, jnp.float32, RING, HDIM
    (rows, width), seq_len, shard = args[0].shape, args[5].shape[0], columns[0]
    ff_mine = columns[1] // n
    piece = (n * shard, width)
    qkv_piece = (n * shard, 3 * head)
    outs = call(
        functools.partial(backward_kernel, plan),
        [
            shaped((rows, width), f32),
            shaped((shard, width), f32),
            shaped((shard, (H + 2 * KVH) * head), f32),
            shaped(columns),
            shaped(columns),
            shaped((n * shard, 2 * ff_mine)),
        ],
        args,
        [VMEM] * 5 + [HBM] * 12,
        [VMEM] * 5 + [HBM],
        [VMEM((seq_len, head), bf16)] * 3
        + [VMEM((rows, H * head), bf16)]
        + [VMEM((seq_len, head // 2), f32)] * 2
        + [VMEM((seq_len, 1), f32)] * 2
        + [
            VMEM((seq_len, width), bf16),
            VMEM((width, 3 * head), bf16),
            VMEM((H * head, width), bf16),
            VMEM((rows, width), bf16),
            VMEM((rows, width), bf16),
            VMEM((seq_len, head), bf16),
            VMEM((seq_len, 3 * head), bf16),
            VMEM((seq_len, head), f32),
            VMEM((seq_len, head), f32),
            VMEM((rows, width), f32),
            VMEM((n // 2, rows, width), bf16),
            VMEM((2, n // 2, rows, width), bf16),
        ]
        + [VMEM((2,) + qkv_piece, bf16), VMEM((2,) + qkv_piece, bf16), VMEM(qkv_piece, bf16)]
        + [VMEM((n, shard, 3 * head), bf16)]
        + [VMEM((2,) + piece, bf16), VMEM((2,) + piece, bf16), VMEM(piece, bf16)]
        + [VMEM((2, n // 2, shard, width), bf16), DMA((7,)), DMA((8,))]
        + pair_sems()
        + seq_sems()
        + pair_sems()
        + seq_sems()
        + ring_sems()
        + grid_sum_sems()
        + pair_sems(),
        5,
    )
    return outs[:-1]


def ring_device(
    tokens, cotangent, gain_attn, w_query, w_key, w_value, w_out, gain_mlp, w_gate, w_up, w_down, pair_order, segments
):
    bf16, f32 = jnp.bfloat16, jnp.float32
    n = RING
    rows, width = tokens.shape[1], tokens.shape[2]
    seq_len = segments.shape[1]
    shard = w_query.shape[0]
    ff_own = w_down.shape[0]
    ff_mine = SEQ * ff_own
    head = HDIM
    outs = attention_stage(
        tokens, cotangent, gain_attn, w_query, w_key, w_value, w_out, gain_mlp, w_gate, w_up, w_down,
        pair_order, segments, ATTENTION_PLAN,
    )
    hidden, hhat, ob_local = outs[:3]
    where = outs[3:8]
    q, k, v, x_all, dy_all, wqkv_all, wout_all, wg_all, wu_own, wdown_all = outs[8:]
    wqkv_all = wqkv_all.reshape(width, 3 * head)
    wout_all = wout_all.reshape(H * head, width)
    wg_all = wg_all.reshape(width, ff_mine)
    wu_own = wu_own.reshape(n * shard, ff_mine)
    wdown_all = wdown_all.reshape(ff_mine, width)
    dweighted, out_sum, col_sum, down_sum = mlp_stage(hhat, dy_all, wg_all, wu_own, wdown_all, MLP_PLAN)
    output = (hidden + out_sum).astype(bf16)[None]

    grad_tokens, out_grad, qkv_raw, gate_raw, up_raw = backward_stage(
        (dweighted, hidden, cotangent[0], tokens[0], where[4], q, k, v, ob_local)
        + tuple(where[:4])
        + (x_all, wqkv_all, wout_all, col_sum),
        w_gate.shape, BACKWARD_PLAN,
    )
    gain_one = gain_attn.astype(f32)[:, None]
    gain_two = gain_mlp.astype(f32)[:, None]
    raw_q = qkv_raw[:, : H * head]
    raw_k = qkv_raw[:, H * head : (H + KVH) * head]
    raw_v = qkv_raw[:, (H + KVH) * head :]

    def gain_part(raw, w):
        return jnp.sum(raw.astype(f32) * w.astype(f32), axis=1)

    grad_gain_one = gain_part(raw_q, w_query) + gain_part(raw_k, w_key) + gain_part(raw_v, w_value)
    grad_gain_two = gain_part(gate_raw, w_gate) + gain_part(up_raw, w_up)
    return (
        output,
        grad_tokens[None],
        grad_gain_one,
        raw_q * gain_one,
        raw_k * gain_one,
        raw_v * gain_one,
        out_grad,
        grad_gain_two,
        gate_raw.astype(f32) * gain_two,
        up_raw.astype(f32) * gain_two,
        down_sum.astype(f32),
    )


def solution(mesh):
    placed = (
        P("seq", "ctx", None),
        P("seq", "ctx", None),
        P(("seq", "ctx")),
        P(("seq", "ctx"), None),
        P(("seq", "ctx"), None),
        P(("seq", "ctx"), None),
        P(("seq", "ctx"), None),
        P(("seq", "ctx")),
        P(("seq", "ctx"), None),
        P(("seq", "ctx"), None),
        P(("seq", "ctx"), None),
        P("seq", None),
        P("seq", None),
    )
    fits = mesh.shape["ctx"] == H and mesh.shape["seq"] == 4
    chosen = ring_device if fits else general_device
    return jax.shard_map(
        chosen,
        mesh=mesh,
        in_specs=placed,
        out_specs=(
            P("seq", "ctx", None),
            P("seq", "ctx", None),
            P(("seq", "ctx")),
            P(("seq", "ctx"), None),
            P(("seq", "ctx"), None),
            P(("seq", "ctx"), None),
            P(("seq", "ctx"), None),
            P(("seq", "ctx")),
            P(("seq", "ctx"), None),
            P(("seq", "ctx"), None),
            P(("seq", "ctx"), None),
        ),
        check_vma=False,
    )
```

```python
import functools
import math

import jax
import jax.numpy as jnp
import numpy as np
from jax import lax
from jax.experimental import pallas as pl
from jax.experimental.pallas import tpu as pltpu
from jax.sharding import PartitionSpec as P

H = 8
KVH = 4
HDIM = 256
DOCS = 4


EPSILON = 1e-06
THETA = 1000042.0
NEG_FILL = -1e30


def slot_positions(pair_row, half_rows, pair_count):
    offsets = jnp.arange(half_rows, dtype=jnp.int32)
    low_slots = pair_row[:, None] * half_rows + offsets[None, :]
    high_slots = (2 * pair_count - 1 - pair_row)[:, None] * half_rows + offsets[None, :]
    return jnp.concatenate([low_slots, high_slots], axis=1).reshape(-1)


def rotary_tables(positions, head_dim):
    half_dim = head_dim // 2
    frequency = THETA ** (-(jnp.arange(half_dim, dtype=jnp.float32) * 2.0 / head_dim))
    angles = positions.astype(jnp.float32)[:, None] * frequency[None, :]
    return (jnp.cos(angles)[:, None, :], jnp.sin(angles)[:, None, :])


def rotary(tensor, table_cos, table_sin):
    half_dim = tensor.shape[-1] // 2
    lead_half = tensor[..., :half_dim]
    tail_half = tensor[..., half_dim:]
    return jnp.concatenate(
        [
            lead_half * table_cos - tail_half * table_sin,
            tail_half * table_cos + lead_half * table_sin,
        ],
        axis=-1,
    )


def rms_scale(tensor):
    return lax.rsqrt(jnp.mean(tensor * tensor, axis=-1, keepdims=True) + EPSILON)


def rms_backward(tensor, scale_rows, gain_full, grad_rows):
    weighted = gain_full * grad_rows
    inner_mean = jnp.mean(weighted * tensor, axis=-1, keepdims=True)
    return scale_rows * weighted - tensor * (scale_rows * scale_rows * scale_rows) * inner_mean


def contract_rows(first_mat, second_mat):
    return lax.dot_general(
        first_mat, second_mat, (((0,), (0,)), ((), ())), preferred_element_type=jnp.float32
    )


def contract_cols(first_mat, second_mat):
    return lax.dot_general(
        first_mat, second_mat, (((1,), (1,)), ((), ())), preferred_element_type=jnp.float32
    )


def attention_weights(gain_attn, gain_mlp, w_query, w_key, w_value, w_out):
    return (
        lax.all_gather(gain_attn, ("seq", "ctx"), axis=0, tiled=True),
        lax.all_gather(gain_mlp, ("seq", "ctx"), axis=0, tiled=True),
        lax.all_gather(w_query, ("seq", "ctx"), axis=0, tiled=True),
        lax.all_gather(w_key, ("seq", "ctx"), axis=0, tiled=True),
        lax.all_gather(w_value, ("seq", "ctx"), axis=0, tiled=True),
        lax.all_gather(w_out, ("seq", "ctx"), axis=0, tiled=True),
    )


def mlp_weights(w_gate, w_up, w_down):
    return (
        lax.all_gather(w_gate, ("seq", "ctx"), axis=0, tiled=True),
        lax.all_gather(w_up, ("seq", "ctx"), axis=0, tiled=True),
        lax.all_gather(w_down, ("seq", "ctx"), axis=0, tiled=True),
    )


def reduce_grads(grad_one, grad_two, grad_three):
    seq_count = lax.axis_size("seq")
    grad_one = grad_one.reshape((seq_count, grad_one.shape[0] // seq_count) + grad_one.shape[1:])
    grad_two = grad_two.reshape((seq_count, grad_two.shape[0] // seq_count) + grad_two.shape[1:])
    grad_three = grad_three.reshape(
        (seq_count, grad_three.shape[0] // seq_count) + grad_three.shape[1:]
    )
    grad_one, grad_two, grad_three = (
        lax.psum_scatter(
            grad_one.astype(jnp.bfloat16), "ctx", scatter_dimension=1, tiled=True
        ).astype(jnp.float32),
        lax.psum_scatter(
            grad_two.astype(jnp.bfloat16), "ctx", scatter_dimension=1, tiled=True
        ).astype(jnp.float32),
        lax.psum_scatter(
            grad_three.astype(jnp.bfloat16), "ctx", scatter_dimension=1, tiled=True
        ).astype(jnp.float32),
    )
    grad_one, grad_two, grad_three = (
        lax.psum_scatter(
            grad_one.astype(jnp.bfloat16), "seq", scatter_dimension=0, tiled=True
        ).astype(jnp.float32),
        lax.psum_scatter(
            grad_two.astype(jnp.bfloat16), "seq", scatter_dimension=0, tiled=True
        ).astype(jnp.float32),
        lax.psum_scatter(
            grad_three.astype(jnp.bfloat16), "seq", scatter_dimension=0, tiled=True
        ).astype(jnp.float32),
    )
    return (grad_one[0], grad_two[0], grad_three[0])


def general_device(
    tokens,
    cotangent,
    gain_attn,
    w_query,
    w_key,
    w_value,
    w_out,
    gain_mlp,
    w_gate,
    w_up,
    w_down,
    pair_order,
    segments,
):
    pair_count = lax.axis_size("ctx")
    my_index = lax.axis_index("ctx")
    row_count = tokens.shape[1]
    half_rows = row_count // 2
    seq_len = segments.shape[1]
    head_groups = H // KVH
    score_scale = HDIM ** (-0.5)
    key_rows = math.gcd(seq_len, 512)
    key_steps = seq_len // key_rows
    key_pos = slot_positions(pair_order[0], half_rows, pair_count)
    key_doc = jnp.take(segments[0], key_pos)
    query_pos = lax.dynamic_slice_in_dim(key_pos, my_index * row_count, row_count)
    query_doc = lax.dynamic_slice_in_dim(key_doc, my_index * row_count, row_count)
    rot_cos, rot_sin = rotary_tables(query_pos, HDIM)
    gain_one, gain_two, query_w, key_w, value_w, out_w = attention_weights(
        gain_attn, gain_mlp, w_query, w_key, w_value, w_out
    )
    gain_one = gain_one.astype(jnp.float32)
    gain_two = gain_two.astype(jnp.float32)
    inputs = tokens[0].astype(jnp.float32)
    scale_one = rms_scale(inputs)
    normed = (inputs * scale_one * gain_one).astype(jnp.bfloat16)
    query_proj = jnp.dot(normed, query_w, preferred_element_type=jnp.float32).reshape(
        row_count, H, HDIM
    )
    key_proj = jnp.dot(normed, key_w, preferred_element_type=jnp.float32).reshape(
        row_count, KVH, HDIM
    )
    value_proj = jnp.dot(normed, value_w, preferred_element_type=jnp.float32)
    query_rot = (
        rotary(query_proj, rot_cos, rot_sin)
        .astype(jnp.bfloat16)
        .reshape(row_count, KVH, head_groups, HDIM)
    )
    key_rot = rotary(key_proj, rot_cos, rot_sin).astype(jnp.bfloat16).reshape(row_count, KVH * HDIM)
    value_low = value_proj.astype(jnp.bfloat16)
    key_width = key_rot.shape[1]
    key_all, value_all = (
        lax.all_gather(key_rot, "ctx", axis=0, tiled=True),
        lax.all_gather(value_low, "ctx", axis=0, tiled=True),
    )
    pos_blocks = key_pos.reshape(key_steps, key_rows)
    doc_blocks = key_doc.reshape(key_steps, key_rows)

    def scores_of(key_blk, pos_blk, doc_blk):
        key_heads = key_blk.reshape(key_rows, KVH, HDIM)
        raw_scores = (
            jnp.einsum("qkgd,tkd->kgqt", query_rot, key_heads, preferred_element_type=jnp.float32)
            * score_scale
        )
        visible = (doc_blk[None, :] == query_doc[:, None]) & (
            pos_blk[None, :] <= query_pos[:, None]
        )
        return (raw_scores, visible[None, None])

    def first_pass(carried, step_data):
        running_top, running_sum = carried
        key_blk, pos_blk, doc_blk = step_data
        raw_scores, visible = scores_of(key_blk, pos_blk, doc_blk)
        masked = jnp.where(visible, raw_scores, NEG_FILL)
        new_top = jnp.maximum(running_top, jnp.max(masked, axis=-1))
        added = jnp.sum(jnp.where(visible, jnp.exp(masked - new_top[..., None]), 0.0), axis=-1)
        return ((new_top, running_sum * jnp.exp(running_top - new_top) + added), None)

    start_top = jnp.full((KVH, head_groups, row_count), NEG_FILL, jnp.float32)
    start_sum = jnp.zeros((KVH, head_groups, row_count), jnp.float32)
    key_stack = key_all.reshape(key_steps, key_rows, key_width)
    value_stack = value_all.reshape(key_steps, key_rows, key_width)
    (final_top, final_sum), _ = lax.scan(
        first_pass, (start_top, start_sum), (key_stack, pos_blocks, doc_blocks)
    )
    log_total = final_top + jnp.log(final_sum)

    def second_pass(carried, step_data):
        acc_out, acc_rest = carried
        key_blk, value_blk, pos_blk, doc_blk = step_data
        raw_scores, visible = scores_of(key_blk, pos_blk, doc_blk)
        prob_full = jnp.where(visible, jnp.exp(raw_scores - log_total[..., None]), 0.0)
        prob_low = prob_full.astype(jnp.bfloat16)
        prob_rest = (prob_full - prob_low.astype(jnp.float32)).astype(jnp.bfloat16)
        value_heads = value_blk.reshape(key_rows, KVH, HDIM)
        acc_out = acc_out + jnp.einsum(
            "kgqt,tkd->qkgd", prob_low, value_heads, preferred_element_type=jnp.float32
        )
        acc_rest = acc_rest + jnp.einsum(
            "kgqt,tkd->qkgd", prob_rest, value_heads, preferred_element_type=jnp.float32
        )
        return ((acc_out, acc_rest), None)

    start_acc = jnp.zeros((row_count, KVH, head_groups, HDIM), jnp.float32)
    (attended, attended_rest), _ = lax.scan(
        second_pass, (start_acc, start_acc), (key_stack, value_stack, pos_blocks, doc_blocks)
    )
    exact_out = attended + attended_rest
    out_low = attended.reshape(row_count, H * HDIM).astype(jnp.bfloat16)
    hidden = inputs + jnp.dot(out_low, out_w, preferred_element_type=jnp.float32)
    scale_two = rms_scale(hidden)
    normed_two = (hidden * scale_two * gain_two).astype(jnp.bfloat16)
    grad_out = cotangent[0]
    gate_w, up_w, down_w = mlp_weights(w_gate, w_up, w_down)
    gate_proj = jnp.dot(normed_two, gate_w, preferred_element_type=jnp.float32)
    up_proj = jnp.dot(normed_two, up_w, preferred_element_type=jnp.float32)
    gate_sig = jax.nn.sigmoid(gate_proj)
    active = gate_proj * gate_sig
    middle = (active * up_proj).astype(jnp.bfloat16)
    result = hidden + jnp.dot(middle, down_w, preferred_element_type=jnp.float32)
    output = result.astype(jnp.bfloat16)[None]
    gate_w, up_w, down_w = mlp_weights(w_gate, w_up, w_down)
    grad_mid = contract_cols(grad_out, down_w)
    grad_gate = (grad_mid * up_proj * gate_sig * (1.0 + gate_proj * (1.0 - gate_sig))).astype(
        jnp.bfloat16
    )
    grad_up = (grad_mid * active).astype(jnp.bfloat16)
    grad_norm_two = contract_cols(grad_gate, gate_w) + contract_cols(grad_up, up_w)
    grad_gain_two = jnp.sum(grad_norm_two * hidden * scale_two, axis=0)
    grad_hidden = grad_out.astype(jnp.float32) + rms_backward(
        hidden, scale_two, gain_two, grad_norm_two
    )
    grad_w_gate = contract_rows(normed_two, grad_gate)
    grad_w_up = contract_rows(normed_two, grad_up)
    shard_gain_two, shard_gate, shard_up = reduce_grads(grad_gain_two, grad_w_gate, grad_w_up)
    gain_one, gain_two, query_w, key_w, value_w, out_w = attention_weights(
        gain_attn, gain_mlp, w_query, w_key, w_value, w_out
    )
    gain_one = gain_one.astype(jnp.float32)
    grad_branch = grad_hidden.astype(jnp.bfloat16)
    grad_w_out = contract_rows(out_low, grad_branch)
    grad_att = (
        contract_cols(grad_branch, out_w)
        .astype(jnp.bfloat16)
        .reshape(row_count, KVH, head_groups, HDIM)
    )
    row_delta = jnp.transpose(jnp.sum(grad_att.astype(jnp.float32) * exact_out, axis=-1), (1, 2, 0))
    key_back, value_back = (key_all, value_all)

    def backward_step(grad_query, step_data):
        key_blk, value_blk, pos_blk, doc_blk = step_data
        raw_scores, visible = scores_of(key_blk, pos_blk, doc_blk)
        prob_full = jnp.where(visible, jnp.exp(raw_scores - log_total[..., None]), 0.0)
        prob_low = prob_full.astype(jnp.bfloat16)
        key_heads = key_blk.reshape(key_rows, KVH, HDIM)
        value_heads = value_blk.reshape(key_rows, KVH, HDIM)
        grad_value_blk = jnp.einsum(
            "kgqt,qkgd->tkd", prob_low, grad_att, preferred_element_type=jnp.float32
        )
        grad_probs = jnp.einsum(
            "qkgd,tkd->kgqt", grad_att, value_heads, preferred_element_type=jnp.float32
        )
        grad_scores = (prob_full * (grad_probs - row_delta[..., None])).astype(jnp.bfloat16)
        grad_query = (
            grad_query
            + jnp.einsum(
                "kgqt,tkd->qkgd", grad_scores, key_heads, preferred_element_type=jnp.float32
            )
            * score_scale
        )
        grad_key_blk = (
            jnp.einsum("kgqt,qkgd->tkd", grad_scores, query_rot, preferred_element_type=jnp.float32)
            * score_scale
        )
        return (
            grad_query,
            (
                grad_key_blk.reshape(key_rows, key_width),
                grad_value_blk.reshape(key_rows, key_width),
            ),
        )

    back_keys = key_back.reshape(key_steps, key_rows, key_width)
    back_values = value_back.reshape(key_steps, key_rows, key_width)
    grad_query, (grad_key_steps, grad_value_steps) = lax.scan(
        backward_step, start_acc, (back_keys, back_values, pos_blocks, doc_blocks)
    )
    grad_key_all = grad_key_steps.reshape(seq_len, key_width)
    grad_value_all = grad_value_steps.reshape(seq_len, key_width)
    grad_key_own, grad_value_own = (
        lax.psum_scatter(
            grad_key_all.astype(jnp.bfloat16), "ctx", scatter_dimension=0, tiled=True
        ).astype(jnp.float32),
        lax.psum_scatter(
            grad_value_all.astype(jnp.bfloat16), "ctx", scatter_dimension=0, tiled=True
        ).astype(jnp.float32),
    )
    grad_query = (
        rotary(grad_query.reshape(row_count, H, HDIM), rot_cos, -rot_sin)
        .astype(jnp.bfloat16)
        .reshape(row_count, H * HDIM)
    )
    grad_key = (
        rotary(grad_key_own.reshape(row_count, KVH, HDIM), rot_cos, -rot_sin)
        .astype(jnp.bfloat16)
        .reshape(row_count, key_width)
    )
    grad_value = grad_value_own.astype(jnp.bfloat16)
    grad_w_query = contract_rows(normed, grad_query)
    grad_w_key = contract_rows(normed, grad_key)
    grad_w_value = contract_rows(normed, grad_value)
    grad_normed = (
        contract_cols(grad_query, query_w)
        + contract_cols(grad_key, key_w)
        + contract_cols(grad_value, value_w)
    )
    grad_gain_one = jnp.sum(grad_normed * inputs * scale_one, axis=0)
    grad_tokens = grad_hidden + rms_backward(inputs, scale_one, gain_one, grad_normed)
    grad_w_down = contract_rows(middle, grad_out)
    shard_gain_one, shard_out, shard_down = reduce_grads(grad_gain_one, grad_w_out, grad_w_down)
    shard_query, shard_key, shard_value = reduce_grads(grad_w_query, grad_w_key, grad_w_value)
    return (
        output,
        grad_tokens[None],
        shard_gain_one,
        shard_query,
        shard_key,
        shard_value,
        shard_out,
        shard_gain_two,
        shard_gate,
        shard_up,
        shard_down,
    )


MESH = pl.DeviceIdType.MESH
VMEM = pltpu.VMEM
RING = 8
SEQ = 4


class Place:
    def __init__(self):
        self.c = lax.axis_index("ctx")
        self.s = lax.axis_index("seq")
        self.z, self.x = self.c // 2, lax.rem(self.c, 2)
        self.p = self.z + self.x * (7 - 2 * self.z)
        self.up, self.down = {"ctx": self.c + 2}, {"ctx": self.c - 2}
        self.side = {"ctx": self.c + 1 - 2 * self.x}
        self.right = {"ctx": self.at(1)}
        self.left = {"ctx": self.at(-1)}
        self.s_core = self.s + 1 - 2 * lax.rem(self.s, 2)
        self.s_far = lax.rem(self.s + 2, 4)
        self.s_both = 3 - self.s
        self.core_peer = {"seq": self.s_core}
        self.far_peer = {"seq": self.s_far}

    def at(self, offset):
        q = lax.rem(self.p + offset + 2 * RING, RING)
        return 2 * q + (q // 4) * (15 - 4 * q)

    def peers(self):
        return [{"ctx": lax.rem(self.c + k, RING)} for k in range(1, RING)]


def greet(devices, work=None):
    barrier = pltpu.get_barrier_semaphore()
    for device in devices:
        pl.semaphore_signal(barrier, inc=1, device_id=device, device_id_type=MESH)
    if work is not None:
        work()
    pl.semaphore_wait(barrier, len(devices))


def remote(src, dst, send_sem, recv_sem, device):
    return pltpu.make_async_remote_copy(
        src_ref=src, dst_ref=dst, send_sem=send_sem, recv_sem=recv_sem, device_id=device, device_id_type=MESH
    )


def arrived(ref, sems, index, device):
    remote(ref, ref, sems[0].at[index], sems[1].at[index], device).wait_recv()


def together(*flows):
    live = list(flows)
    while live:
        live = [flow for flow in live if next(flow, "end") != "end"]


def ring_sems():
    return [pltpu.SemaphoreType.DMA((2, RING // 2, 2))] * 2


def slot(offset):
    return 0 if offset == 0 else min(RING - 1, 2 * offset if offset > 0 else -2 * offset - 1)


class Rows:
    def __init__(self, ref, rows):
        self.ref, self.rows = ref, rows

    def here(self, offset):
        return self.ref.at[pl.ds(slot(offset) * self.rows, self.rows)]

    def there(self, offset, d):
        return self.here(offset - 1 if d == 0 else offset + 1)


class Owners:
    def __init__(self, ref, place):
        self.ref, self.place = ref, place

    def here(self, offset):
        return self.ref.at[self.place.at(offset)]

    def there(self, offset, d):
        return self.here(offset)


def ring_gather(own, blocks, sems, place):
    half = own.shape[0] // 2
    steps = RING // 2
    sent = []

    def part(ref, j):
        return ref.at[pl.ds(j * half, half)]

    def wait_for(d, s, j):
        offset = -(s + 1) if d == 0 else s + 1
        arrived(part(blocks.here(offset), j), sems, (d, s, j), place.right if d == 0 else place.left)

    for s in range(steps):
        for j in range(2):
            for d in range(2):
                if s == steps - 1 and j != d:
                    continue
                if s > 0:
                    wait_for(d, s - 1, j)
                offset = -s if d == 0 else s
                copy = remote(
                    part(own if s == 0 else blocks.here(offset), j),
                    part(blocks.there(offset, d), j),
                    sems[0].at[d, s, j],
                    sems[1].at[d, s, j],
                    place.right if d == 0 else place.left,
                )
                copy.start()
                sent.append(copy)
            yield
    for d in range(2):
        wait_for(d, steps - 2, 1 - d)
    yield
    for d in range(2):
        wait_for(d, steps - 1, d)
    yield
    for copy in sent:
        copy.wait_send()


class RingSum:
    def __init__(self, slots, sems, place):
        self.slots, self.sems, self.sent = slots, sems, []
        self.sides = (place.right, place.left)
        self.half = slots.shape[2] // 2

    def rows(self, ref, j):
        return ref.at[pl.ds(j * self.half, self.half)]

    def send(self, d, s, j, source):
        to = self.rows(self.slots.at[d, s], j)
        copy = remote(source, to, self.sems[0].at[d, s, j], self.sems[1].at[d, s, j], self.sides[d])
        copy.start()
        self.sent.append(copy)

    def held(self, d, s, j):
        ref = self.rows(self.slots.at[d, s], j)
        arrived(ref, self.sems, (d, s, j), self.sides[d])
        return ref

    def first(self, part):
        for d in range(2):
            self.send(d, 0, d, self.rows(part, d))

    def relay(self, s, parts):
        for j in range(2):
            for d in range(2):
                source = self.rows(parts[d], j)
                if s > 1 or j == d:
                    held = self.held(d, s - 1, j)
                    add_into(held, source)
                    source = held
                self.send(d, s, j, source)

    def last(self, part, out):
        for j in range(2):
            held = [self.held(d, RING // 2 - 1, j) for d in range(2)]
            sum_of_three(self.rows(out, j), self.rows(part, j), *held)

    def end(self):
        for copy in self.sent:
            copy.wait_send()


def ring_scatter(blocks, out, slots, sems, place):
    ring = RingSum(slots, sems, place)
    ring.first(blocks.here(RING // 2))
    yield
    for s in range(1, RING // 2):
        k = RING // 2 - s
        ring.relay(s, (blocks.here(k), blocks.here(-k)))
        yield
    ring.last(blocks.here(0), out)
    ring.end()
    yield


def pair_sems():
    return [pltpu.SemaphoreType.DMA((RING,))] * 2


OFFSETS = (1, -1, 2, -2, 3, -3, 4)


def exchange(pieces, here, sems, place, group=RING):
    for i in range(0, len(OFFSETS), group):
        for k in OFFSETS[i : i + group]:
            at = slot(k)
            for src, dst in pieces(k):
                remote(src, dst, sems[0].at[at], sems[1].at[at], {"ctx": place.at(k)}).start()
        yield
    for k in OFFSETS:
        arrived(here(k), sems, RING - 1 if k == RING // 2 else slot(-k), {"ctx": place.at(k)})
    for k in OFFSETS:
        remote(here(k), here(k), sems[0].at[slot(k)], sems[1].at[slot(k)], {"ctx": place.at(k)}).wait_send()
    yield


def by_owner(src, dst, sems, place, group=RING):
    return exchange(lambda k: [(src.at[place.at(k)], dst.at[place.c])], lambda k: dst.at[place.at(k)], sems, place, group)


def block_at(i, size):
    return pl.ds(pl.multiple_of(i * size, size), size)


class ByOwner:
    def __init__(self, ref, rows):
        self.ref, self.rows = ref, rows

    def owner(self, c, side=None):
        return self.ref.at[block_at(c, self.rows)]


class ByArrival:
    def __init__(self, ref, rows, place):
        self.ref, self.rows, self.place = ref, rows, place

    def owner(self, c, side="here"):
        far = {"here": 0, "up": 2, "down": -2, "side": 1 - 2 * self.place.x}[side]
        mine = self.place.c + far
        z, x = mine // 2, lax.rem(mine, 2)
        p = z + x * (7 - 2 * z)
        z, x = c // 2, lax.rem(c, 2)
        k = lax.rem(z + x * (7 - 2 * z) - p + 2 * RING, RING)
        late = jnp.where(k == RING // 2, RING - 1, 2 * (RING - k) - 1)
        return self.ref.at[block_at(jnp.where(k < RING // 2, 2 * k, late), self.rows)]


def grid_sems():
    return [pltpu.SemaphoreType.DMA((2, 3))] * 2 + [pltpu.SemaphoreType.DMA((4,))] * 2


def grid_gather(own, blocks, sems, place, late=False):
    z_sems, x_sems = sems[:2], sems[2:]
    z, x = place.z, place.x
    sent = []

    def send(when, src, c, side, pair, index, device):
        copy = remote(src, blocks.owner(c, side), pair[0].at[index], pair[1].at[index], device)
        pl.when(when)(copy.start)
        sent.append((when, copy))

    def across(when, src, line):
        send(when, src, 2 * line + x, "side", x_sems, line, place.side)

    send(z < 3, own, place.c, "up", z_sems, (0, 0), place.up)
    send(z > 0, own, place.c, "down", z_sems, (1, 0), place.down)
    if not late:
        across(z >= 0, own, z)
    yield
    for hop in range(1, 4):
        for d, (line, here, further) in enumerate(((z - hop, z >= hop, z < 3), (z + hop, z <= 3 - hop, z > 0))):
            index = 2 * line + x
            ref = blocks.owner(jnp.clip(index, 0, RING - 1))
            device = (place.down, place.up)[d]

            @pl.when(here)
            def _():
                arrived(ref, z_sems, (d, hop - 1), device)

            if hop < 3:
                send(here & further, ref, jnp.clip(index, 0, RING - 1), ("up", "down")[d], z_sems, (d, hop), (place.up, place.down)[d])
            if not late:
                across_line = jnp.clip(line, 0, 3)
                send(here, ref, 2 * across_line + x, "side", x_sems, across_line, place.side)
        yield
    if late:
        across(z >= 0, own, z)
        for hop in range(1, 4):
            line = lax.rem(z + hop, 4)
            across(z >= 0, blocks.owner(2 * line + x), line)
        yield
    for line in range(4):
        arrived(blocks.owner(2 * line + 1 - x), x_sems, line, place.side)
    for when, copy in sent:
        pl.when(when)(copy.wait_send)
    yield


def grid_sum_sems():
    return [pltpu.SemaphoreType.DMA((4,))] * 2 + [pltpu.SemaphoreType.DMA((2, 4))] * 2


class GridSum:
    def __init__(self, part, over, line, sems, place):
        self.part, self.over, self.line, self.place = part, over, line, place
        self.x_sems, self.z_sems = sems[:2], sems[2:]
        self.rows = over.shape[1]
        self.sent = []

    def plane(self, i):
        z = self.place.z
        inner = jnp.where((z == 1) | (z == 2), 1, 0)
        plain, mid = (3, 2, 1, 0)[i], (3, 0, 2, 1)[i]
        order = plain + inner * (mid - plain)
        return jnp.where(z < 2, order, 3 - order)

    def send(self, when, src, dst, pair, index, device):
        copy = remote(src, dst, pair[0].at[index], pair[1].at[index], device)
        pl.when(when)(copy.start)
        self.sent.append((when, copy))

    def mine(self, z, x):
        return self.part.at[block_at(2 * z + x, self.rows)]

    def across(self, i):
        z = self.plane(i)
        self.send(self.place.z >= 0, self.mine(z, 1 - self.place.x), self.over.at[z], self.x_sems, z, self.place.side)

    def along(self, i):
        z, me = self.plane(i), self.place.z
        held = self.over.at[z]
        arrived(held, self.x_sems, z, self.place.side)
        add_into(held, self.mine(z, self.place.x))
        for d, (when, more, source, device) in enumerate(
            (
                (z > me, me > 0, self.place.down, self.place.up),
                (z < me, me < 3, self.place.up, self.place.down),
            )
        ):

            @pl.when(when & more)
            def _():
                arrived(self.line.at[d, z], self.z_sems, (d, z), source)
                add_into(held, self.line.at[d, z])

            self.send(when, held, self.line.at[d, z], self.z_sems, (d, z), device)

    def last(self, out):
        z = self.place.z
        held = self.over.at[z]
        arrived(held, self.x_sems, z, self.place.side)
        add_to(out, held, self.mine(z, self.place.x))
        for d, (when, source) in enumerate(((z > 0, self.place.down), (z < 3, self.place.up))):

            @pl.when(when)
            def _():
                arrived(self.line.at[d, z], self.z_sems, (d, z), source)
                add_to(out, out, self.line.at[d, z])

    def end(self):
        for when, copy in self.sent:
            pl.when(when)(copy.wait_send)


def pairs_of(sems):
    return [sems[i : i + 2] for i in range(0, len(sems), 2)]


def seq_sems():
    return [pltpu.SemaphoreType.DMA((3,))] * 2


def seq_gather(own, buf, sems, place):
    first = remote(own, buf.at[place.s], sems[0].at[0], sems[1].at[0], place.far_peer)
    second = remote(own, buf.at[place.s], sems[0].at[1], sems[1].at[1], place.core_peer)
    first.start()
    second.start()
    yield
    arrived(buf.at[place.s_far], sems, 0, place.far_peer)
    third = remote(buf.at[place.s_far], buf.at[place.s_far], sems[0].at[2], sems[1].at[2], place.core_peer)
    third.start()
    yield
    arrived(buf.at[place.s_core], sems, 1, place.core_peer)
    arrived(buf.at[place.s_both], sems, 2, place.core_peer)
    for copy in (first, second, third):
        copy.wait_send()
    yield


def sum_of_three(dst, *terms):
    step = math.gcd(dst.shape[0], 16)

    @pl.loop(0, dst.shape[0] // step)
    def _(i):
        at = pl.ds(pl.multiple_of(i * step, step), step)
        one, two, three = (term[at].astype(jnp.float32) for term in terms)
        dst[at] = one + two + three


def add_to(dst, one, two):
    step = math.gcd(dst.shape[0], 16)

    @pl.loop(0, dst.shape[0] // step)
    def _(i):
        at = pl.ds(pl.multiple_of(i * step, step), step)
        dst[at] = one[at].astype(jnp.float32) + two[at].astype(jnp.float32)


def add_into(dst, other):
    rows = dst.shape[0]
    step = math.gcd(rows, 16)

    @pl.loop(0, rows // step)
    def _(i):
        at = pl.ds(pl.multiple_of(i * step, step), step)
        dst[at] = (dst[at].astype(jnp.float32) + other[at].astype(jnp.float32)).astype(dst.dtype)


class SeqSum:
    def __init__(self, grad, block, near, far, sems, place):
        self.grad, self.block, self.near_ref, self.far, self.sems, self.place = grad, block, near, far, sems, place
        self.low, self.row = lax.rem(place.s, 2), place.s // 2
        self.sent = []

    def send(self, src, dst, i, device):
        copy = remote(src, dst, self.sems[0].at[i], self.sems[1].at[i], device)
        copy.start()
        self.sent.append(copy)

    def near(self, i):
        r = (1 - self.row, self.row)[i]
        self.grad(r * 2 + 1 - self.low, self.block.at[i], False)
        self.send(self.block.at[i], self.near_ref.at[i], i, self.place.core_peer)

    def across(self):
        arrived(self.near_ref.at[0], self.sems, 0, self.place.core_peer)
        self.grad((1 - self.row) * 2 + self.low, self.near_ref.at[0], True)
        self.send(self.near_ref.at[0], self.far, 2, self.place.far_peer)

    def own(self):
        arrived(self.near_ref.at[1], self.sems, 1, self.place.core_peer)
        self.grad(self.row * 2 + self.low, self.near_ref.at[1], True)

    def last(self):
        arrived(self.far, self.sems, 2, self.place.far_peer)
        add_into(self.far, self.near_ref.at[1])

    def end(self):
        for copy in self.sent:
            copy.wait_send()


def call(body, outs, args, spaces, out_spaces, scratch, ident):
    return pl.pallas_call(
        body,
        out_shape=outs,
        in_specs=[pl.BlockSpec(memory_space=space) for space in spaces],
        out_specs=[pl.BlockSpec(memory_space=space) for space in out_spaces],
        scratch_shapes=scratch,
        compiler_params=pltpu.CompilerParams(
            collective_id=ident, has_side_effects=True, vmem_limit_bytes=63 * 1024 * 1024
        ),
    )(*args)


def shaped(shape, dtype=jnp.bfloat16):
    return jax.ShapeDtypeStruct(shape, dtype)


def dot(a, b, at=(1, 0)):
    return lax.dot_general(a, b, (((at[0],), (at[1],)), ((), ())), preferred_element_type=jnp.float32)


def chunks(total, size, body):
    @pl.loop(0, total // size)
    def _(i):
        body(pl.ds(pl.multiple_of(i * size, size), size))


def turned(t, cos, sin, sign):
    half = t.shape[1] // 2
    a, b = t[:, :half], t[:, half:]
    return jnp.concatenate([a * cos - sign * b * sin, b * cos + sign * a * sin], axis=-1)


def probabilities(q, k, pos_rows, start_rows, pos_cols):
    scores = dot(q, k, (1, 1)) * HDIM ** (-0.5)
    visible = (pos_cols >= start_rows) & (pos_cols <= pos_rows)
    scores = jnp.where(visible, scores, NEG_FILL)
    weight = jnp.exp(scores - jnp.max(scores, axis=-1, keepdims=True))
    return weight / jnp.sum(weight, axis=-1, keepdims=True)


def place_rows(pairs, segments, block_cos, block_sin, row_cos, row_sin, cos, sin, pos_rows, start_rows, pos_cols):
    f32 = jnp.float32
    half = row_cos.shape[0]
    bounds = [
        jnp.sum(jnp.where(segments[...] < d, 1.0, 0.0).astype(f32), axis=1, keepdims=True) for d in range(1, DOCS)
    ]
    numbers = lax.broadcasted_iota(jnp.int32, block_cos.shape, 0)
    for c in range(RING):
        blocks = (pairs[0, c], 2 * RING - 1 - pairs[0, c])
        lanes = lax.broadcasted_iota(jnp.int32, (1, 2 * half), 1)
        low = blocks[0] * half + lanes
        pos_cols[:, pl.ds(c * 2 * half, 2 * half)] = jnp.where(lanes < half, low, blocks[1] * half + lanes - half).astype(f32)
        for j, block in enumerate(blocks):
            at = pl.ds((2 * c + j) * half, half)
            near_cos = jnp.sum(jnp.where(numbers == block, block_cos[...], 0.0), axis=0, keepdims=True)
            near_sin = jnp.sum(jnp.where(numbers == block, block_sin[...], 0.0), axis=0, keepdims=True)
            cos[at, :] = near_cos * row_cos[...] - near_sin * row_sin[...]
            sin[at, :] = near_sin * row_cos[...] + near_cos * row_sin[...]
            pos = (block * half + lax.broadcasted_iota(jnp.int32, (half, 1), 0)).astype(f32)
            start = jnp.zeros((half, 1), f32)
            for bound in bounds:
                start = jnp.where(pos >= bound, bound, start)
            pos_rows[at, :] = pos
            start_rows[at, :] = start


def column(row):
    n = row.shape[1]
    same = lax.broadcasted_iota(jnp.int32, (n, n), 0) == lax.broadcasted_iota(jnp.int32, (n, n), 1)
    return jnp.sum(jnp.where(same, row, 0.0), axis=1, keepdims=True)


def attention_kernel(plan, x, gain_one, gain_two, pairs, segments, block_cos, block_sin, row_cos, row_sin,
                     dy, w_query, w_key, w_value, wout, w_gate, w_up, wdown,
                     hidden, hhat, ob_local, cos, sin, pos_rows, start_rows, pos_cols,
                     q_out, k_out, v_out, x_all, dy_all, wqkv_all, wout_all, wg_all, wu_own, wdown_all,
                     xhat, wq, wk, wv, wg, wu, wout_s, wdown_s, dy_s, heads, gate_units, up_units, x_v, wqkv_v, wout_v, q, k, v, ob, local, loads, *sems):
    place = Place()
    qkv_swap, qkv_seq, out_ring, out_seq, ob_swap, gate_swap, gate_seq, up_swap, down_seq = pairs_of(sems[:18])
    x_grid, dy_grid = sems[18:22], sems[22:26]
    bf16, f32 = jnp.bfloat16, jnp.float32
    rows, width = x.shape
    head, shard = ob.shape[1], wout.shape[0]
    groups = H // KVH
    fetch = [
        pltpu.make_async_copy(src, dst, loads.at[i])
        for i, (src, dst) in enumerate(
            (
                (w_query, wq), (w_key, wk), (w_value, wv), (w_gate, wg), (w_up, wu),
                (wout, wout_s), (wdown, wdown_s), (dy, dy_s),
            )
        )
    ]
    for copy in fetch:
        copy.start()
    keep = [
        pltpu.make_async_copy(wout_s, wout_all.at[place.s, place.c], local.at[0]),
        pltpu.make_async_copy(wdown_s, wdown_all.at[place.s], local.at[1]),
        pltpu.make_async_copy(dy_s, ByArrival(dy_all, rows, place).owner(place.c), local.at[2]),
    ]

    def normed(at):
        t = x[at, :].astype(f32)
        xhat[at, :] = (t * lax.rsqrt(jnp.mean(t * t, axis=-1, keepdims=True) + EPSILON)).astype(bf16)

    def scale(ref, gain, columns, into, at):
        @pl.loop(0, RING)
        def _(t):
            for j, cols in enumerate(columns(t)):
                part = (ref[:, cols].astype(f32) * gain).astype(bf16)
                into[t, :, pl.ds(at + j * cols.size, cols.size)] = part

    def prepare():
        chunks(rows, 16, normed)
        for loaded, kept in zip(fetch[5:], keep):
            loaded.wait()
            kept.start()
        for copy in fetch[:3]:
            copy.wait()
        gain = column(gain_one[...].astype(f32))
        scale(wq, gain, lambda t: [block_at(t, head)], heads, 0)
        scale(wk, gain, lambda t: [block_at(t // groups, head)], heads, head)
        scale(wv, gain, lambda t: [block_at(t // groups, head)], heads, 2 * head)

    greet(place.peers() + [place.core_peer, place.far_peer], prepare)
    down_w = seq_gather(wdown, wdown_all, down_seq, place)
    x_blocks, dy_blocks = ByOwner(x_all, rows), ByArrival(dy_all, rows, place)

    def out_flow():
        yield from ring_gather(wout, Owners(wout_all.at[place.s], place), out_ring, place)
        keep[0].wait()
        yield from seq_gather(wout_all.at[place.s], wout_all, out_seq, place)

    out_w = out_flow()

    def spread(src, dst, swap, seq, sem, group=RING):
        rows_of_s = dst if seq is None else dst.at[place.s]
        own = pltpu.make_async_copy(src.at[place.c], rows_of_s.at[place.c], sem)
        own.start()
        yield from by_owner(src, rows_of_s, swap, place, group)
        own.wait()
        if seq is not None:
            yield from seq_gather(rows_of_s, dst, seq, place)

    qkv_w = spread(heads, wqkv_all, qkv_swap, qkv_seq, local.at[3])
    gate_w = spread(gate_units, wg_all, gate_swap, gate_seq, local.at[4], 2)
    up_w = spread(up_units, wu_own, up_swap, None, local.at[5], 2)
    x_flow = grid_gather(xhat, x_blocks, x_grid, place)
    dy_flow = grid_gather(dy, dy_blocks, dy_grid, place)
    own_x = pltpu.make_async_copy(xhat, x_blocks.owner(place.c), local.at[6])

    flows = {"q": qkv_w, "g": gate_w, "u": up_w, "d": down_w, "o": out_w, "x": x_flow, "y": dy_flow}
    mine = block_at(place.c, head)
    flows["b"] = exchange(
        lambda o: [(ob.at[block_at(place.at(o), rows)], ob_local.at[:, mine])],
        lambda o: ob_local.at[:, block_at(place.at(o), head)],
        ob_swap,
        place,
    )
    load = [pltpu.make_async_copy(x_all, x_v, loads.at[0]), pltpu.make_async_copy(wqkv_all, wqkv_v, loads.at[1])]
    saves = [pltpu.make_async_copy(src, dst, loads.at[2 + i]) for i, (src, dst) in enumerate(((q, q_out), (k, k_out), (v, v_out)))]
    load_out = pltpu.make_async_copy(wout_all, wout_v, local.at[0])

    def scale_units():
        for copy in fetch[3:5]:
            copy.wait()
        gain = column(gain_two[...].astype(f32))
        own = wdown.shape[0]
        for ref, into in ((wg, gate_units), (wu, up_units)):
            scale(ref, gain, lambda t: [block_at(i * RING + t, own) for i in range(SEQ)], into, 0)

    def find_rows():
        place_rows(
            pairs, segments, block_cos, block_sin, row_cos, row_sin, cos, sin, pos_rows, start_rows, pos_cols
        )

    def load_attention():
        own_x.start()
        own_x.wait()
        for copy in load:
            copy.start()

    halves = x_v.shape[0] // 2

    def project(at):
        qkv = dot(x_v[at, :], wqkv_v[...].reshape(width, 3 * head))
        c, s = cos[at, :], sin[at, :]
        q[at, :] = turned(qkv[:, :head], c, s, 1.0).astype(bf16)
        k[at, :] = turned(qkv[:, head : 2 * head], c, s, 1.0).astype(bf16)
        v[at, :] = qkv[:, 2 * head :].astype(bf16)

    def project_half(i):
        if i == 0:
            for copy in load:
                copy.wait()
        chunks(halves, 256, lambda at: project(pl.ds(pl.multiple_of(i * halves + at.start, 256), 256)))
        if i == 1:
            for copy in saves:
                copy.start()

    def attend(at):
        prob = probabilities(q[at, :], k[...], pos_rows[at, :], start_rows[at, :], pos_cols[...])
        ob[at, :] = dot(prob.astype(bf16), v[...]).astype(bf16)

    def attend_half(i):
        chunks(halves, 256, lambda at: attend(pl.ds(pl.multiple_of(i * halves + at.start, 256), 256)))
        if i == 1:
            ob_local[:, mine] = ob[block_at(place.c, rows), :]

    def finish_hidden():
        load_out.wait()

        def residual(cols):
            part = dot(ob_local[...], wout_v[:, :, :, cols].reshape(width, cols.size))
            hidden[:, cols] = x[:, cols].astype(f32) + part

        chunks(width, 256, residual)

        def normed_two(at):
            t = hidden[at, :]
            hhat[at, :] = (t * lax.rsqrt(jnp.mean(t * t, axis=-1, keepdims=True) + EPSILON)).astype(bf16)

        chunks(rows, 16, normed_two)

    works = {
        "S": scale_units, "R": find_rows, "L": load_attention, "W": load_out.start, "H": finish_hidden,
    }
    turns = {"P": iter((0, 1)), "A": iter((0, 1))}
    for step in plan:
        if step in flows:
            next(flows[step], None)
        elif step in turns:
            (project_half if step == "P" else attend_half)(next(turns[step]))
        else:
            works[step]()
    for name, flow in flows.items():
        if name in plan:
            for _ in flow:
                pass
    if "P" in plan:
        for copy in saves:
            copy.wait()
    elif "L" in plan:
        for copy in load:
            copy.wait()
    if "S" not in plan:
        for copy in fetch[3:5]:
            copy.wait()
    if "o" not in plan:
        keep[0].wait()
    if "W" in plan and "H" not in plan:
        load_out.wait()
    keep[1].wait()
    keep[2].wait()


def mlp_kernel(plan, hhat, dy_hbm, wg_hbm, wu_own, wdown_hbm, sum_h, sum_o, col_out, down_out,
               h_all, dy_all, wg, wu, wd, mid, dgate, dup, stage_h, stage_o, stage, stage_2, slots_h, slots_o,
               col_sent, col_near, col_far, down_sent, down_near, down_far, local, *sems):
    place = Place()
    h_sems, sum_h_sems, sum_o_sems, col_seq, down_seq, up_seq = pairs_of(sems)
    greet([place.right, place.left, place.core_peer, place.far_peer])
    rows, width = hhat.shape
    ff = wg.shape[1]
    bf16, f32 = jnp.bfloat16, jnp.float32
    up_blocks = Blocks(wu, wu_own.shape[0])
    keep = [
        pltpu.make_async_copy(src, dst, local.at[i])
        for i, (src, dst) in enumerate(
            ((hhat, h_all.at[pl.ds(0, rows)]), (wg_hbm, wg), (wu_own, up_blocks[place.s]), (wdown_hbm, wd), (dy_hbm, dy_all))
        )
    ]
    for copy in keep:
        copy.start()
    gather = ring_gather(hhat, Rows(h_all, rows), h_sems, place)
    up_flow = seq_gather(wu_own, up_blocks, up_seq, place)

    def hidden_rows(start, count):
        at = pl.ds(start, count)

        def body(cols):
            gate = dot(h_all[at, :], wg[:, cols])
            up = dot(h_all[at, :], wu[:, cols])
            dmid = dot(dy_all[at, :], wd[cols, :], (1, 1))
            sig = jax.nn.sigmoid(gate)
            active = gate * sig
            mid[at, cols] = (active * up).astype(bf16)
            dgate[at, cols] = (dmid * up * sig * (1.0 + gate * (1.0 - sig))).astype(bf16)
            dup[at, cols] = (dmid * active).astype(bf16)

        chunks(ff, 512, body)

    def part_h(start, count, dst):
        at = pl.ds(start, count)

        def body(cols):
            dst[:, cols] = (dot(dgate[at, :], wg[cols, :], (1, 1)) + dot(dup[at, :], wu[cols, :], (1, 1))).astype(bf16)

        chunks(width, 512, body)

    def part_o(start, count, dst):
        at = pl.ds(start, count)

        def body(cols):
            dst[:, cols] = dot(mid[at, :], wd[:, cols]).astype(bf16)

        chunks(width, 1024, body)

    def col_grad(s, dst, add):
        def body(cols):
            lhs = h_all[:, pl.ds(pl.multiple_of(s * dst.shape[0] + cols.start, 256), 256)]
            for side, grad in enumerate((dgate, dup)):
                there = pl.ds(side * ff, ff)
                value = dot(lhs, grad[...], (0, 0))
                if add:
                    value = value + dst[cols, there].astype(f32)
                dst[cols, there] = value.astype(bf16)

        chunks(dst.shape[0], 256, body)

    def down_grad(s, dst, add):
        lhs = pl.ds(pl.multiple_of(s * dst.shape[0], 256), dst.shape[0])

        def body(cols):
            value = dot(mid[:, lhs], dy_all[:, cols], (0, 0))
            if add:
                value = value + dst[:, cols].astype(f32)
            dst[:, cols] = value.astype(bf16)

        chunks(width, 1024, body)

    def pair(ref):
        return (ref.at[pl.ds(rows, rows)], ref.at[pl.ds(0, rows)])

    col_sum = SeqSum(col_grad, col_sent, col_near, col_far, col_seq, place)
    down_sum = SeqSum(down_grad, down_sent, down_near, down_far, down_seq, place)
    ring_h, ring_o = RingSum(slots_h, sum_h_sems, place), RingSum(slots_o, sum_o_sems, place)
    top_h, top_o = stage_h.at[pl.ds(2 * rows, rows)], stage_o.at[pl.ds(2 * rows, rows)]
    next_h, next_o = stage_h.at[pl.ds(0, 2 * rows)], stage_o.at[pl.ds(0, 2 * rows)]

    def in_turn(*actions):
        return iter(actions)

    def parts(part, top, following, later):
        return in_turn(
            lambda: part(7 * rows, rows, top),
            lambda: part(5 * rows, 2 * rows, following),
            lambda: part(3 * rows, 2 * rows, later),
            lambda: part(rows, 2 * rows, later),
            lambda: part(0, rows, later.at[pl.ds(0, rows)]),
        )

    def sums(ring, top, following, later, out):
        return in_turn(
            lambda: ring.first(top),
            lambda: ring.relay(1, pair(following)),
            lambda: ring.relay(2, pair(later)),
            lambda: ring.relay(3, pair(later)),
            lambda: ring.last(later.at[pl.ds(0, rows)], out),
        )

    def wait_loads():
        for copy in keep:
            copy.wait()

    turns = {
        "k": in_turn(wait_loads),
        "a": in_turn(lambda: hidden_rows(0, rows)),
        "b": in_turn(lambda: hidden_rows(rows, 2 * rows)),
        "c": in_turn(lambda: hidden_rows(3 * rows, 2 * rows)),
        "d": in_turn(lambda: hidden_rows(5 * rows, 2 * rows)),
        "e": in_turn(lambda: hidden_rows(7 * rows, rows)),
        "P": parts(part_h, top_h, next_h, stage),
        "r": sums(ring_h, top_h, next_h, stage, sum_h),
        "O": parts(part_o, top_o, next_o, stage_2),
        "s": sums(ring_o, top_o, next_o, stage_2, sum_o),
        "n": in_turn(lambda: col_sum.near(0), lambda: col_sum.near(1)),
        "m": in_turn(col_sum.across),
        "w": in_turn(col_sum.own),
        "l": in_turn(col_sum.last),
        "N": in_turn(lambda: down_sum.near(0), lambda: down_sum.near(1)),
        "M": in_turn(down_sum.across),
        "W": in_turn(down_sum.own),
        "L": in_turn(down_sum.last),
    }
    for step in plan:
        if step == "x":
            next(gather)
        elif step == "u":
            next(up_flow)
        else:
            next(turns[step])()
    ends = []
    for i, (total, out) in enumerate(((col_sum, col_out), (down_sum, down_out))):
        ends.append(pltpu.make_async_copy(total.far, out, local.at[i]))
        ends[-1].start()
    for copy in ends:
        copy.wait()
    for flow in (ring_h, ring_o, col_sum, down_sum):
        flow.end()
    for flow in (gather, up_flow):
        for _ in flow:
            pass


def backward_kernel(plan, weighted, hidden, dy, x, pos_cols, q_hbm, k_hbm, v_hbm, ob_hbm, cos_hbm, sin_hbm, pos_hbm, start_hbm,
                    x_all, wqkv_all, wout_all, col,
                    grad_x, out_grad, qkv_raw, gate_raw, up_raw, col_hbm,
                    q, k, v, ob_local, cos, sin, pos_rows, start_rows,
                    x_v, wqkv_v, wout_v, branch, datt_own, datt, dqkv, dk, dv, sum_x, over_x, line_x,
                    qkv_sent, qkv_near, qkv_far, qkv_in, out_sent, out_near, out_far, slots_o, local, early, *sems):
    place = Place()
    att_swap, qkv_seq, qkv_swap, out_seq, out_ring = pairs_of(sems[:10])
    x_grid, col_swap = sems[10:14], sems[14:]
    bf16, f32 = jnp.bfloat16, jnp.float32
    rows, width = x.shape
    seq_len, head = q.shape
    shard = out_grad.shape[0]
    loads = [
        pltpu.make_async_copy(src, dst, local.at[i])
        for i, (src, dst) in enumerate(((wout_all, wout_v), (x_all, x_v), (wqkv_all, wqkv_v)))
    ]
    for copy in loads:
        copy.start()
    qkv_blocks = Blocks(qkv_far, shard)
    fetched = [
        pltpu.make_async_copy(src, dst, early.at[i])
        for i, (src, dst) in enumerate(
            (
                (ob_hbm, ob_local), (q_hbm, q), (k_hbm, k), (v_hbm, v),
                (cos_hbm, cos), (sin_hbm, sin), (pos_hbm, pos_rows), (start_hbm, start_rows),
            )
        )
    ]
    for copy in fetched:
        copy.start()
    def norm_back(tensor, grads):
        scale = lax.rsqrt(jnp.mean(tensor * tensor, axis=-1, keepdims=True) + EPSILON)
        inner = jnp.mean(grads * tensor, axis=-1, keepdims=True)
        return scale * grads - tensor * (scale * scale * scale) * inner

    def hidden_back(at):
        grads = dy[at, :].astype(f32) + norm_back(hidden[at, :], weighted[at, :])
        grad_x[at, :] = grads
        branch[at, :] = grads.astype(bf16)

    greet(place.peers() + [place.core_peer, place.far_peer], lambda: chunks(rows, 16, hidden_back))

    def heads_back():
        loads[0].wait()
        fetched[0].wait()

        def att_back(cols):
            datt_own[:, cols] = dot(branch[...], wout_v[cols, :], (1, 1)).astype(bf16)

        chunks(width, head, att_back)

    mine = block_at(place.c, rows)
    att_flow = exchange(
        lambda o: [(datt_own.at[:, block_at(place.at(o), head)], datt.at[mine])],
        lambda o: datt.at[block_at(place.at(o), rows)],
        att_swap,
        place,
    )
    def rows_grad(left, right):
        def grad(s, dst, add):
            def body(cols):
                lhs = left[:, pl.ds(pl.multiple_of(s * dst.shape[0] + cols.start, 256), 256)]
                value = dot(lhs, right[...], (0, 0))
                if add:
                    value = value + dst[cols, :].astype(f32)
                dst[cols, :] = value.astype(bf16)

            chunks(dst.shape[0], 256, body)

        return grad

    out_sum = SeqSum(rows_grad(ob_local, branch), out_sent, out_near, out_far, out_seq, place)
    qkv_sum = SeqSum(rows_grad(x_v, dqkv), qkv_sent, qkv_near, qkv_far, qkv_seq, place)
    def attend_back(at):
        prob = probabilities(q[at, :], k[...], pos_rows[at, :], start_rows[at, :], pos_cols[...])
        dprob = dot(datt[at, :], v[...], (1, 1))
        delta = jnp.sum(prob * dprob, axis=-1, keepdims=True)
        dscore = (prob * (dprob - delta)).astype(bf16)
        dq = dot(dscore, k[...]) * HDIM ** (-0.5)
        dqkv[at, pl.ds(0, head)] = turned(dq, cos[at, :], sin[at, :], -1.0).astype(bf16)
        dk[...] += dot(dscore, q[at, :], (0, 0))
        dv[...] += dot(prob.astype(bf16), datt[at, :], (0, 0))

    def finish_back(at):
        turned_dk = turned(dk[at, :] * HDIM ** (-0.5), cos[at, :], sin[at, :], -1.0)
        dqkv[at, pl.ds(head, head)] = turned_dk.astype(bf16)
        dqkv[at, pl.ds(2 * head, head)] = dv[at, :].astype(bf16)

    def all_back():
        dk[...] = jnp.zeros_like(dk)
        dv[...] = jnp.zeros_like(dv)
        datt[mine, :] = datt_own[:, block_at(place.c, head)]
        for copy in loads[1:] + fetched[1:]:
            copy.wait()
        chunks(seq_len, 256, attend_back)
        chunks(seq_len, 128, finish_back)

    part = wout_v.at[pl.ds(0, seq_len)]
    col_in = wout_v.at[pl.ds(seq_len, RING * shard)]
    total = GridSum(part, over_x, line_x, x_grid, place)

    def part_x(i):
        at = block_at(total.plane(i), 2 * rows)

        def body(cols):
            part[at, cols] = dot(dqkv[at, :], wqkv_v[cols, :], (1, 1)).astype(bf16)

        chunks(width, 1024, body)
        total.across(i)

    unit = gate_raw.shape[1] // (RING * SEQ)
    groups = H // KVH

    def fetch_columns():
        for k in (0,) + OFFSETS:
            c = place.at(k)
            source = Blocks(col_hbm if k else col, shard)
            pltpu.make_async_copy(source[c], Blocks(col_in, shard)[c], local.at[4]).start()

    def move_columns():
        pltpu.make_async_copy(col_in, col_in, local.at[4]).wait()
        for c in range(RING):
            for side, raw in enumerate((gate_raw, up_raw)):
                for i in range(SEQ):
                    value = col_in[pl.ds(c * shard, shard), pl.ds((side * SEQ + i) * unit, unit)]
                    raw[:, pl.ds((i * RING + c) * unit, unit)] = value

    def qkv_last():
        qkv_sum.last()
        qkv_in[place.c] = qkv_blocks[place.c][...]

    def tokens_back():
        total.last(sum_x)

        def token_back(at):
            grad_x[at, :] = grad_x[at, :] + norm_back(x[at, :].astype(f32), sum_x[at, :])

        chunks(rows, 16, token_back)

    def finish_qkv():
        for t in range(H):
            qkv_raw[:, pl.ds(t * head, head)] = qkv_in[t, :, pl.ds(0, head)].astype(f32)
        for side in (1, 2):
            for t in range(KVH):
                value = sum(qkv_in[t * groups + g, :, pl.ds(side * head, head)].astype(f32) for g in range(groups))
                qkv_raw[:, pl.ds((H + (side - 1) * KVH + t) * head, head)] = value

    def each(action, count=4):
        return iter([functools.partial(action, i) for i in range(count)])

    out_blocks = Owners(Blocks(out_far, shard), place)
    flows = {
        "a": att_flow,
        "c": by_owner(Blocks(col, shard), Blocks(col_hbm, shard), col_swap, place, 2),
        "o": ring_scatter(out_blocks, out_grad, slots_o, out_ring, place),
        "t": by_owner(qkv_blocks, qkv_in, qkv_swap, place),
    }
    works = {
        "h": heads_back, "B": all_back, "m": out_sum.across, "w": out_sum.own, "e": out_sum.last,
        "M": qkv_sum.across, "W": qkv_sum.own, "E": qkv_last, "C": fetch_columns, "V": move_columns, "Z": tokens_back, "F": finish_qkv,
    }
    turns = {"n": each(out_sum.near, 2), "N": each(qkv_sum.near, 2), "p": each(part_x), "l": each(total.along, 3)}
    for step in plan:
        if step in flows:
            next(flows[step])
        elif step in turns:
            next(turns[step])()
        else:
            works[step]()
    for name, flow in flows.items():
        if name in plan:
            for _ in flow:
                pass
    for flow in (total, out_sum, qkv_sum):
        flow.end()


class Blocks:
    def __init__(self, ref, rows):
        self.ref, self.rows = ref, rows
        self.shape = (ref.shape[0] // rows, rows) + tuple(ref.shape[1:])

    @property
    def at(self):
        return self

    def __getitem__(self, i):
        return self.ref.at[pl.ds(pl.multiple_of(i * self.rows, self.rows), self.rows)]


DMA = pltpu.SemaphoreType.DMA
HBM = pl.ANY


ATTENTION_PLAN = "doooooooooooxxqxxqqRSggggqqxLyPPAAbgygyuuuuyoogWbHydgu"


def attention_stage(
    tokens, cotangent, gain_attn, w_query, w_key, w_value, w_out, gain_mlp, w_gate, w_up, w_down, pair_order, segments, plan
):
    bf16, f32 = jnp.bfloat16, jnp.float32
    n = RING
    rows, width = tokens.shape[1], tokens.shape[2]
    seq_len = segments.shape[1]
    shard = w_query.shape[0]
    ff_own = w_down.shape[0]
    ff_mine = SEQ * ff_own
    head = HDIM
    frequency = THETA ** (-(np.arange(head // 2) * 2.0 / head))
    half = rows // 2
    block_angles = np.arange(2 * n)[:, None] * half * frequency[None, :]
    row_angles = np.arange(half)[:, None] * frequency[None, :]
    tables = tuple(jnp.asarray(f(angles), f32) for angles in (block_angles, row_angles) for f in (np.cos, np.sin))

    return call(
        functools.partial(attention_kernel, plan),
        [
            shaped((rows, width), f32),
            shaped((rows, width)),
            shaped((rows, H * head)),
            shaped((seq_len, head // 2), f32),
            shaped((seq_len, head // 2), f32),
            shaped((seq_len, 1), f32),
            shaped((seq_len, 1), f32),
            shaped((1, seq_len), f32),
            shaped((seq_len, head)),
            shaped((seq_len, head)),
            shaped((seq_len, head)),
            shaped((seq_len, width)),
            shaped((seq_len, width)),
            shaped((SEQ, n, shard, 3 * head)),
            shaped((SEQ, n, shard, width)),
            shaped((SEQ, n, shard, ff_mine)),
            shaped((n, shard, ff_mine)),
            shaped((SEQ, ff_own, width)),
        ],
        (tokens[0], gain_attn[None], gain_mlp[None], pair_order, segments)
        + tables
        + (cotangent[0], w_query, w_key, w_value, w_out, w_gate, w_up, w_down),
        [VMEM] * 3 + [pltpu.SMEM] + [VMEM] * 5 + [HBM] * 8,
        [VMEM] * 8 + [HBM] * 10,
        [
            VMEM((rows, width), bf16),
            VMEM(w_query.shape, bf16),
            VMEM(w_key.shape, bf16),
            VMEM(w_value.shape, bf16),
            VMEM(w_gate.shape, bf16),
            VMEM(w_up.shape, bf16),
            VMEM(w_out.shape, bf16),
            VMEM(w_down.shape, bf16),
            VMEM((rows, width), bf16),
            VMEM((n, shard, 3 * head), bf16),
            VMEM((n, shard, ff_mine), bf16),
            VMEM((n, shard, ff_mine), bf16),
            VMEM((seq_len, width), bf16),
            VMEM((SEQ, n, shard, 3 * head), bf16),
            VMEM((SEQ, n, shard, width), bf16),
        ]
        + [VMEM((seq_len, head), bf16)] * 4
        + [DMA((7,)), DMA((8,))]
        + pair_sems()
        + seq_sems()
        + ring_sems()
        + seq_sems()
        + pair_sems()
        + (pair_sems() + seq_sems()) * 2
        + grid_sems() * 2,
        1,
    )


MLP_PLAN = "xuxkxxuxxuabxxxcdxePrnPrnmOsPrOsNPrNMOsPwrOsOWslL"


def mlp_stage(hhat, dy_all, wg_all, wu_own, wdown_all, plan):
    bf16, f32, n = jnp.bfloat16, jnp.float32, RING
    (rows, width), seq_len = hhat.shape, dy_all.shape[0]
    ff_mine = wg_all.shape[1]
    shard, ff_own = width // (SEQ * n), ff_mine // SEQ
    slot_shape = VMEM((2, n // 2, rows, width), bf16)
    col_piece, down_piece = (n * shard, 2 * ff_mine), (ff_own, width)
    return call(
        functools.partial(mlp_kernel, plan),
        [shaped((rows, width), f32)] * 2 + [shaped(col_piece), shaped(down_piece)],
        (hhat, dy_all, wg_all, wu_own, wdown_all),
        [HBM] * 5,
        [VMEM] * 2 + [HBM] * 2,
        [VMEM((seq_len, width), bf16)] * 2
        + [VMEM((width, ff_mine), bf16)] * 2
        + [VMEM((ff_mine, width), bf16)]
        + [VMEM((seq_len, ff_mine), bf16)] * 3
        + [VMEM((3 * rows, width), bf16)] * 2
        + [VMEM((2 * rows, width), bf16)] * 2
        + [slot_shape] * 2
        + [VMEM((2,) + col_piece, bf16), VMEM((2,) + col_piece, bf16), VMEM(col_piece, bf16)]
        + [VMEM((2,) + down_piece, bf16), VMEM((2,) + down_piece, bf16), VMEM(down_piece, bf16)]
        + [DMA((5,))]
        + ring_sems() * 3
        + seq_sems() * 3,
        2,
    )


BACKWARD_PLAN = "hannmaccccBpNpNplMplwWlEteoZocCoVtooF"


def backward_stage(args, columns, plan):
    bf16, f32, n, head = jnp.bfloat16, jnp.float32, RING, HDIM
    (rows, width), seq_len, shard = args[0].shape, args[5].shape[0], columns[0]
    ff_mine = columns[1] // n
    piece = (n * shard, width)
    qkv_piece = (n * shard, 3 * head)
    outs = call(
        functools.partial(backward_kernel, plan),
        [
            shaped((rows, width), f32),
            shaped((shard, width), f32),
            shaped((shard, (H + 2 * KVH) * head), f32),
            shaped(columns),
            shaped(columns),
            shaped((n * shard, 2 * ff_mine)),
        ],
        args,
        [VMEM] * 5 + [HBM] * 12,
        [VMEM] * 5 + [HBM],
        [VMEM((seq_len, head), bf16)] * 3
        + [VMEM((rows, H * head), bf16)]
        + [VMEM((seq_len, head // 2), f32)] * 2
        + [VMEM((seq_len, 1), f32)] * 2
        + [
            VMEM((seq_len, width), bf16),
            VMEM((width, 3 * head), bf16),
            VMEM((H * head, width), bf16),
            VMEM((rows, width), bf16),
            VMEM((rows, width), bf16),
            VMEM((seq_len, head), bf16),
            VMEM((seq_len, 3 * head), bf16),
            VMEM((seq_len, head), f32),
            VMEM((seq_len, head), f32),
            VMEM((rows, width), f32),
            VMEM((n // 2, rows, width), bf16),
            VMEM((2, n // 2, rows, width), bf16),
        ]
        + [VMEM((2,) + qkv_piece, bf16), VMEM((2,) + qkv_piece, bf16), VMEM(qkv_piece, bf16)]
        + [VMEM((n, shard, 3 * head), bf16)]
        + [VMEM((2,) + piece, bf16), VMEM((2,) + piece, bf16), VMEM(piece, bf16)]
        + [VMEM((2, n // 2, shard, width), bf16), DMA((7,)), DMA((8,))]
        + pair_sems()
        + seq_sems()
        + pair_sems()
        + seq_sems()
        + ring_sems()
        + grid_sum_sems()
        + pair_sems(),
        5,
    )
    return outs[:-1]


def ring_device(
    tokens, cotangent, gain_attn, w_query, w_key, w_value, w_out, gain_mlp, w_gate, w_up, w_down, pair_order, segments
):
    bf16, f32 = jnp.bfloat16, jnp.float32
    n = RING
    rows, width = tokens.shape[1], tokens.shape[2]
    seq_len = segments.shape[1]
    shard = w_query.shape[0]
    ff_own = w_down.shape[0]
    ff_mine = SEQ * ff_own
    head = HDIM
    outs = attention_stage(
        tokens, cotangent, gain_attn, w_query, w_key, w_value, w_out, gain_mlp, w_gate, w_up, w_down,
        pair_order, segments, ATTENTION_PLAN,
    )
    hidden, hhat, ob_local = outs[:3]
    where = outs[3:8]
    q, k, v, x_all, dy_all, wqkv_all, wout_all, wg_all, wu_own, wdown_all = outs[8:]
    wqkv_all = wqkv_all.reshape(width, 3 * head)
    wout_all = wout_all.reshape(H * head, width)
    wg_all = wg_all.reshape(width, ff_mine)
    wu_own = wu_own.reshape(n * shard, ff_mine)
    wdown_all = wdown_all.reshape(ff_mine, width)
    dweighted, out_sum, col_sum, down_sum = mlp_stage(hhat, dy_all, wg_all, wu_own, wdown_all, MLP_PLAN)
    output = (hidden + out_sum).astype(bf16)[None]

    grad_tokens, out_grad, qkv_raw, gate_raw, up_raw = backward_stage(
        (dweighted, hidden, cotangent[0], tokens[0], where[4], q, k, v, ob_local)
        + tuple(where[:4])
        + (x_all, wqkv_all, wout_all, col_sum),
        w_gate.shape, BACKWARD_PLAN,
    )
    gain_one = gain_attn.astype(f32)[:, None]
    gain_two = gain_mlp.astype(f32)[:, None]
    raw_q = qkv_raw[:, : H * head]
    raw_k = qkv_raw[:, H * head : (H + KVH) * head]
    raw_v = qkv_raw[:, (H + KVH) * head :]

    def gain_part(raw, w):
        return jnp.sum(raw.astype(f32) * w.astype(f32), axis=1)

    grad_gain_one = gain_part(raw_q, w_query) + gain_part(raw_k, w_key) + gain_part(raw_v, w_value)
    grad_gain_two = gain_part(gate_raw, w_gate) + gain_part(up_raw, w_up)
    return (
        output,
        grad_tokens[None],
        grad_gain_one,
        raw_q * gain_one,
        raw_k * gain_one,
        raw_v * gain_one,
        out_grad,
        grad_gain_two,
        gate_raw.astype(f32) * gain_two,
        up_raw.astype(f32) * gain_two,
        down_sum.astype(f32),
    )


def solution(mesh):
    placed = (
        P("seq", "ctx", None),
        P("seq", "ctx", None),
        P(("seq", "ctx")),
        P(("seq", "ctx"), None),
        P(("seq", "ctx"), None),
        P(("seq", "ctx"), None),
        P(("seq", "ctx"), None),
        P(("seq", "ctx")),
        P(("seq", "ctx"), None),
        P(("seq", "ctx"), None),
        P(("seq", "ctx"), None),
        P("seq", None),
        P("seq", None),
    )
    fits = mesh.shape["ctx"] == H and mesh.shape["seq"] == 4
    chosen = ring_device if fits else general_device
    return jax.shard_map(
        chosen,
        mesh=mesh,
        in_specs=placed,
        out_specs=(
            P("seq", "ctx", None),
            P("seq", "ctx", None),
            P(("seq", "ctx")),
            P(("seq", "ctx"), None),
            P(("seq", "ctx"), None),
            P(("seq", "ctx"), None),
            P(("seq", "ctx"), None),
            P(("seq", "ctx")),
            P(("seq", "ctx"), None),
            P(("seq", "ctx"), None),
            P(("seq", "ctx"), None),
        ),
        check_vma=False,
    )
```

```python
import functools
import math

import jax
import jax.numpy as jnp
import numpy as np
from jax import lax
from jax.experimental import pallas as pl
from jax.experimental.pallas import tpu as pltpu
from jax.sharding import PartitionSpec as P

H = 8
KVH = 4
HDIM = 256
DOCS = 4


EPSILON = 1e-06
THETA = 1000042.0
NEG_FILL = -1e30


def slot_positions(pair_row, half_rows, pair_count):
    offsets = jnp.arange(half_rows, dtype=jnp.int32)
    low_slots = pair_row[:, None] * half_rows + offsets[None, :]
    high_slots = (2 * pair_count - 1 - pair_row)[:, None] * half_rows + offsets[None, :]
    return jnp.concatenate([low_slots, high_slots], axis=1).reshape(-1)


def rotary_tables(positions, head_dim):
    half_dim = head_dim // 2
    frequency = THETA ** (-(jnp.arange(half_dim, dtype=jnp.float32) * 2.0 / head_dim))
    angles = positions.astype(jnp.float32)[:, None] * frequency[None, :]
    return (jnp.cos(angles)[:, None, :], jnp.sin(angles)[:, None, :])


def rotary(tensor, table_cos, table_sin):
    half_dim = tensor.shape[-1] // 2
    lead_half = tensor[..., :half_dim]
    tail_half = tensor[..., half_dim:]
    return jnp.concatenate(
        [
            lead_half * table_cos - tail_half * table_sin,
            tail_half * table_cos + lead_half * table_sin,
        ],
        axis=-1,
    )


def rms_scale(tensor):
    return lax.rsqrt(jnp.mean(tensor * tensor, axis=-1, keepdims=True) + EPSILON)


def rms_backward(tensor, scale_rows, gain_full, grad_rows):
    weighted = gain_full * grad_rows
    inner_mean = jnp.mean(weighted * tensor, axis=-1, keepdims=True)
    return scale_rows * weighted - tensor * (scale_rows * scale_rows * scale_rows) * inner_mean


def contract_rows(first_mat, second_mat):
    return lax.dot_general(
        first_mat, second_mat, (((0,), (0,)), ((), ())), preferred_element_type=jnp.float32
    )


def contract_cols(first_mat, second_mat):
    return lax.dot_general(
        first_mat, second_mat, (((1,), (1,)), ((), ())), preferred_element_type=jnp.float32
    )


def attention_weights(gain_attn, gain_mlp, w_query, w_key, w_value, w_out):
    return (
        lax.all_gather(gain_attn, ("seq", "ctx"), axis=0, tiled=True),
        lax.all_gather(gain_mlp, ("seq", "ctx"), axis=0, tiled=True),
        lax.all_gather(w_query, ("seq", "ctx"), axis=0, tiled=True),
        lax.all_gather(w_key, ("seq", "ctx"), axis=0, tiled=True),
        lax.all_gather(w_value, ("seq", "ctx"), axis=0, tiled=True),
        lax.all_gather(w_out, ("seq", "ctx"), axis=0, tiled=True),
    )


def mlp_weights(w_gate, w_up, w_down):
    return (
        lax.all_gather(w_gate, ("seq", "ctx"), axis=0, tiled=True),
        lax.all_gather(w_up, ("seq", "ctx"), axis=0, tiled=True),
        lax.all_gather(w_down, ("seq", "ctx"), axis=0, tiled=True),
    )


def reduce_grads(grad_one, grad_two, grad_three):
    seq_count = lax.axis_size("seq")
    grad_one = grad_one.reshape((seq_count, grad_one.shape[0] // seq_count) + grad_one.shape[1:])
    grad_two = grad_two.reshape((seq_count, grad_two.shape[0] // seq_count) + grad_two.shape[1:])
    grad_three = grad_three.reshape(
        (seq_count, grad_three.shape[0] // seq_count) + grad_three.shape[1:]
    )
    grad_one, grad_two, grad_three = (
        lax.psum_scatter(
            grad_one.astype(jnp.bfloat16), "ctx", scatter_dimension=1, tiled=True
        ).astype(jnp.float32),
        lax.psum_scatter(
            grad_two.astype(jnp.bfloat16), "ctx", scatter_dimension=1, tiled=True
        ).astype(jnp.float32),
        lax.psum_scatter(
            grad_three.astype(jnp.bfloat16), "ctx", scatter_dimension=1, tiled=True
        ).astype(jnp.float32),
    )
    grad_one, grad_two, grad_three = (
        lax.psum_scatter(
            grad_one.astype(jnp.bfloat16), "seq", scatter_dimension=0, tiled=True
        ).astype(jnp.float32),
        lax.psum_scatter(
            grad_two.astype(jnp.bfloat16), "seq", scatter_dimension=0, tiled=True
        ).astype(jnp.float32),
        lax.psum_scatter(
            grad_three.astype(jnp.bfloat16), "seq", scatter_dimension=0, tiled=True
        ).astype(jnp.float32),
    )
    return (grad_one[0], grad_two[0], grad_three[0])


def general_device(
    tokens,
    cotangent,
    gain_attn,
    w_query,
    w_key,
    w_value,
    w_out,
    gain_mlp,
    w_gate,
    w_up,
    w_down,
    pair_order,
    segments,
):
    pair_count = lax.axis_size("ctx")
    my_index = lax.axis_index("ctx")
    row_count = tokens.shape[1]
    half_rows = row_count // 2
    seq_len = segments.shape[1]
    head_groups = H // KVH
    score_scale = HDIM ** (-0.5)
    key_rows = math.gcd(seq_len, 512)
    key_steps = seq_len // key_rows
    key_pos = slot_positions(pair_order[0], half_rows, pair_count)
    key_doc = jnp.take(segments[0], key_pos)
    query_pos = lax.dynamic_slice_in_dim(key_pos, my_index * row_count, row_count)
    query_doc = lax.dynamic_slice_in_dim(key_doc, my_index * row_count, row_count)
    rot_cos, rot_sin = rotary_tables(query_pos, HDIM)
    gain_one, gain_two, query_w, key_w, value_w, out_w = attention_weights(
        gain_attn, gain_mlp, w_query, w_key, w_value, w_out
    )
    gain_one = gain_one.astype(jnp.float32)
    gain_two = gain_two.astype(jnp.float32)
    inputs = tokens[0].astype(jnp.float32)
    scale_one = rms_scale(inputs)
    normed = (inputs * scale_one * gain_one).astype(jnp.bfloat16)
    query_proj = jnp.dot(normed, query_w, preferred_element_type=jnp.float32).reshape(
        row_count, H, HDIM
    )
    key_proj = jnp.dot(normed, key_w, preferred_element_type=jnp.float32).reshape(
        row_count, KVH, HDIM
    )
    value_proj = jnp.dot(normed, value_w, preferred_element_type=jnp.float32)
    query_rot = (
        rotary(query_proj, rot_cos, rot_sin)
        .astype(jnp.bfloat16)
        .reshape(row_count, KVH, head_groups, HDIM)
    )
    key_rot = rotary(key_proj, rot_cos, rot_sin).astype(jnp.bfloat16).reshape(row_count, KVH * HDIM)
    value_low = value_proj.astype(jnp.bfloat16)
    key_width = key_rot.shape[1]
    key_all, value_all = (
        lax.all_gather(key_rot, "ctx", axis=0, tiled=True),
        lax.all_gather(value_low, "ctx", axis=0, tiled=True),
    )
    pos_blocks = key_pos.reshape(key_steps, key_rows)
    doc_blocks = key_doc.reshape(key_steps, key_rows)

    def scores_of(key_blk, pos_blk, doc_blk):
        key_heads = key_blk.reshape(key_rows, KVH, HDIM)
        raw_scores = (
            jnp.einsum("qkgd,tkd->kgqt", query_rot, key_heads, preferred_element_type=jnp.float32)
            * score_scale
        )
        visible = (doc_blk[None, :] == query_doc[:, None]) & (
            pos_blk[None, :] <= query_pos[:, None]
        )
        return (raw_scores, visible[None, None])

    def first_pass(carried, step_data):
        running_top, running_sum = carried
        key_blk, pos_blk, doc_blk = step_data
        raw_scores, visible = scores_of(key_blk, pos_blk, doc_blk)
        masked = jnp.where(visible, raw_scores, NEG_FILL)
        new_top = jnp.maximum(running_top, jnp.max(masked, axis=-1))
        added = jnp.sum(jnp.where(visible, jnp.exp(masked - new_top[..., None]), 0.0), axis=-1)
        return ((new_top, running_sum * jnp.exp(running_top - new_top) + added), None)

    start_top = jnp.full((KVH, head_groups, row_count), NEG_FILL, jnp.float32)
    start_sum = jnp.zeros((KVH, head_groups, row_count), jnp.float32)
    key_stack = key_all.reshape(key_steps, key_rows, key_width)
    value_stack = value_all.reshape(key_steps, key_rows, key_width)
    (final_top, final_sum), _ = lax.scan(
        first_pass, (start_top, start_sum), (key_stack, pos_blocks, doc_blocks)
    )
    log_total = final_top + jnp.log(final_sum)

    def second_pass(carried, step_data):
        acc_out, acc_rest = carried
        key_blk, value_blk, pos_blk, doc_blk = step_data
        raw_scores, visible = scores_of(key_blk, pos_blk, doc_blk)
        prob_full = jnp.where(visible, jnp.exp(raw_scores - log_total[..., None]), 0.0)
        prob_low = prob_full.astype(jnp.bfloat16)
        prob_rest = (prob_full - prob_low.astype(jnp.float32)).astype(jnp.bfloat16)
        value_heads = value_blk.reshape(key_rows, KVH, HDIM)
        acc_out = acc_out + jnp.einsum(
            "kgqt,tkd->qkgd", prob_low, value_heads, preferred_element_type=jnp.float32
        )
        acc_rest = acc_rest + jnp.einsum(
            "kgqt,tkd->qkgd", prob_rest, value_heads, preferred_element_type=jnp.float32
        )
        return ((acc_out, acc_rest), None)

    start_acc = jnp.zeros((row_count, KVH, head_groups, HDIM), jnp.float32)
    (attended, attended_rest), _ = lax.scan(
        second_pass, (start_acc, start_acc), (key_stack, value_stack, pos_blocks, doc_blocks)
    )
    exact_out = attended + attended_rest
    out_low = attended.reshape(row_count, H * HDIM).astype(jnp.bfloat16)
    hidden = inputs + jnp.dot(out_low, out_w, preferred_element_type=jnp.float32)
    scale_two = rms_scale(hidden)
    normed_two = (hidden * scale_two * gain_two).astype(jnp.bfloat16)
    grad_out = cotangent[0]
    gate_w, up_w, down_w = mlp_weights(w_gate, w_up, w_down)
    gate_proj = jnp.dot(normed_two, gate_w, preferred_element_type=jnp.float32)
    up_proj = jnp.dot(normed_two, up_w, preferred_element_type=jnp.float32)
    gate_sig = jax.nn.sigmoid(gate_proj)
    active = gate_proj * gate_sig
    middle = (active * up_proj).astype(jnp.bfloat16)
    result = hidden + jnp.dot(middle, down_w, preferred_element_type=jnp.float32)
    output = result.astype(jnp.bfloat16)[None]
    gate_w, up_w, down_w = mlp_weights(w_gate, w_up, w_down)
    grad_mid = contract_cols(grad_out, down_w)
    grad_gate = (grad_mid * up_proj * gate_sig * (1.0 + gate_proj * (1.0 - gate_sig))).astype(
        jnp.bfloat16
    )
    grad_up = (grad_mid * active).astype(jnp.bfloat16)
    grad_norm_two = contract_cols(grad_gate, gate_w) + contract_cols(grad_up, up_w)
    grad_gain_two = jnp.sum(grad_norm_two * hidden * scale_two, axis=0)
    grad_hidden = grad_out.astype(jnp.float32) + rms_backward(
        hidden, scale_two, gain_two, grad_norm_two
    )
    grad_w_gate = contract_rows(normed_two, grad_gate)
    grad_w_up = contract_rows(normed_two, grad_up)
    shard_gain_two, shard_gate, shard_up = reduce_grads(grad_gain_two, grad_w_gate, grad_w_up)
    gain_one, gain_two, query_w, key_w, value_w, out_w = attention_weights(
        gain_attn, gain_mlp, w_query, w_key, w_value, w_out
    )
    gain_one = gain_one.astype(jnp.float32)
    grad_branch = grad_hidden.astype(jnp.bfloat16)
    grad_w_out = contract_rows(out_low, grad_branch)
    grad_att = (
        contract_cols(grad_branch, out_w)
        .astype(jnp.bfloat16)
        .reshape(row_count, KVH, head_groups, HDIM)
    )
    row_delta = jnp.transpose(jnp.sum(grad_att.astype(jnp.float32) * exact_out, axis=-1), (1, 2, 0))
    key_back, value_back = (key_all, value_all)

    def backward_step(grad_query, step_data):
        key_blk, value_blk, pos_blk, doc_blk = step_data
        raw_scores, visible = scores_of(key_blk, pos_blk, doc_blk)
        prob_full = jnp.where(visible, jnp.exp(raw_scores - log_total[..., None]), 0.0)
        prob_low = prob_full.astype(jnp.bfloat16)
        key_heads = key_blk.reshape(key_rows, KVH, HDIM)
        value_heads = value_blk.reshape(key_rows, KVH, HDIM)
        grad_value_blk = jnp.einsum(
            "kgqt,qkgd->tkd", prob_low, grad_att, preferred_element_type=jnp.float32
        )
        grad_probs = jnp.einsum(
            "qkgd,tkd->kgqt", grad_att, value_heads, preferred_element_type=jnp.float32
        )
        grad_scores = (prob_full * (grad_probs - row_delta[..., None])).astype(jnp.bfloat16)
        grad_query = (
            grad_query
            + jnp.einsum(
                "kgqt,tkd->qkgd", grad_scores, key_heads, preferred_element_type=jnp.float32
            )
            * score_scale
        )
        grad_key_blk = (
            jnp.einsum("kgqt,qkgd->tkd", grad_scores, query_rot, preferred_element_type=jnp.float32)
            * score_scale
        )
        return (
            grad_query,
            (
                grad_key_blk.reshape(key_rows, key_width),
                grad_value_blk.reshape(key_rows, key_width),
            ),
        )

    back_keys = key_back.reshape(key_steps, key_rows, key_width)
    back_values = value_back.reshape(key_steps, key_rows, key_width)
    grad_query, (grad_key_steps, grad_value_steps) = lax.scan(
        backward_step, start_acc, (back_keys, back_values, pos_blocks, doc_blocks)
    )
    grad_key_all = grad_key_steps.reshape(seq_len, key_width)
    grad_value_all = grad_value_steps.reshape(seq_len, key_width)
    grad_key_own, grad_value_own = (
        lax.psum_scatter(
            grad_key_all.astype(jnp.bfloat16), "ctx", scatter_dimension=0, tiled=True
        ).astype(jnp.float32),
        lax.psum_scatter(
            grad_value_all.astype(jnp.bfloat16), "ctx", scatter_dimension=0, tiled=True
        ).astype(jnp.float32),
    )
    grad_query = (
        rotary(grad_query.reshape(row_count, H, HDIM), rot_cos, -rot_sin)
        .astype(jnp.bfloat16)
        .reshape(row_count, H * HDIM)
    )
    grad_key = (
        rotary(grad_key_own.reshape(row_count, KVH, HDIM), rot_cos, -rot_sin)
        .astype(jnp.bfloat16)
        .reshape(row_count, key_width)
    )
    grad_value = grad_value_own.astype(jnp.bfloat16)
    grad_w_query = contract_rows(normed, grad_query)
    grad_w_key = contract_rows(normed, grad_key)
    grad_w_value = contract_rows(normed, grad_value)
    grad_normed = (
        contract_cols(grad_query, query_w)
        + contract_cols(grad_key, key_w)
        + contract_cols(grad_value, value_w)
    )
    grad_gain_one = jnp.sum(grad_normed * inputs * scale_one, axis=0)
    grad_tokens = grad_hidden + rms_backward(inputs, scale_one, gain_one, grad_normed)
    grad_w_down = contract_rows(middle, grad_out)
    shard_gain_one, shard_out, shard_down = reduce_grads(grad_gain_one, grad_w_out, grad_w_down)
    shard_query, shard_key, shard_value = reduce_grads(grad_w_query, grad_w_key, grad_w_value)
    return (
        output,
        grad_tokens[None],
        shard_gain_one,
        shard_query,
        shard_key,
        shard_value,
        shard_out,
        shard_gain_two,
        shard_gate,
        shard_up,
        shard_down,
    )


MESH = pl.DeviceIdType.MESH
VMEM = pltpu.VMEM
RING = 8
SEQ = 4


class Place:
    def __init__(self):
        self.c = lax.axis_index("ctx")
        self.s = lax.axis_index("seq")
        self.z, self.x = self.c // 2, lax.rem(self.c, 2)
        self.p = self.z + self.x * (7 - 2 * self.z)
        self.up, self.down = {"ctx": self.c + 2}, {"ctx": self.c - 2}
        self.side = {"ctx": self.c + 1 - 2 * self.x}
        self.right = {"ctx": self.at(1)}
        self.left = {"ctx": self.at(-1)}
        self.s_core = self.s + 1 - 2 * lax.rem(self.s, 2)
        self.s_far = lax.rem(self.s + 2, 4)
        self.s_both = 3 - self.s
        self.core_peer = {"seq": self.s_core}
        self.far_peer = {"seq": self.s_far}

    def at(self, offset):
        q = lax.rem(self.p + offset + 2 * RING, RING)
        return 2 * q + (q // 4) * (15 - 4 * q)

    def peers(self):
        return [{"ctx": lax.rem(self.c + k, RING)} for k in range(1, RING)]


def greet(devices, work=None):
    barrier = pltpu.get_barrier_semaphore()
    for device in devices:
        pl.semaphore_signal(barrier, inc=1, device_id=device, device_id_type=MESH)
    if work is not None:
        work()
    pl.semaphore_wait(barrier, len(devices))


def remote(src, dst, send_sem, recv_sem, device):
    return pltpu.make_async_remote_copy(
        src_ref=src, dst_ref=dst, send_sem=send_sem, recv_sem=recv_sem, device_id=device, device_id_type=MESH
    )


def arrived(ref, sems, index, device):
    remote(ref, ref, sems[0].at[index], sems[1].at[index], device).wait_recv()


def together(*flows):
    live = list(flows)
    while live:
        live = [flow for flow in live if next(flow, "end") != "end"]


def ring_sems():
    return [pltpu.SemaphoreType.DMA((2, RING // 2, 2))] * 2


def slot(offset):
    return 0 if offset == 0 else min(RING - 1, 2 * offset if offset > 0 else -2 * offset - 1)


class Rows:
    def __init__(self, ref, rows):
        self.ref, self.rows = ref, rows

    def here(self, offset):
        return self.ref.at[pl.ds(slot(offset) * self.rows, self.rows)]

    def there(self, offset, d):
        return self.here(offset - 1 if d == 0 else offset + 1)


class Owners:
    def __init__(self, ref, place):
        self.ref, self.place = ref, place

    def here(self, offset):
        return self.ref.at[self.place.at(offset)]

    def there(self, offset, d):
        return self.here(offset)


def ring_gather(own, blocks, sems, place):
    half = own.shape[0] // 2
    steps = RING // 2
    sent = []

    def part(ref, j):
        return ref.at[pl.ds(j * half, half)]

    def wait_for(d, s, j):
        offset = -(s + 1) if d == 0 else s + 1
        arrived(part(blocks.here(offset), j), sems, (d, s, j), place.right if d == 0 else place.left)

    for s in range(steps):
        for j in range(2):
            for d in range(2):
                if s == steps - 1 and j != d:
                    continue
                if s > 0:
                    wait_for(d, s - 1, j)
                offset = -s if d == 0 else s
                copy = remote(
                    part(own if s == 0 else blocks.here(offset), j),
                    part(blocks.there(offset, d), j),
                    sems[0].at[d, s, j],
                    sems[1].at[d, s, j],
                    place.right if d == 0 else place.left,
                )
                copy.start()
                sent.append(copy)
            yield
    for d in range(2):
        wait_for(d, steps - 2, 1 - d)
    yield
    for d in range(2):
        wait_for(d, steps - 1, d)
    yield
    for copy in sent:
        copy.wait_send()


class RingSum:
    def __init__(self, slots, sems, place):
        self.slots, self.sems, self.sent = slots, sems, []
        self.sides = (place.right, place.left)
        self.half = slots.shape[2] // 2

    def rows(self, ref, j):
        return ref.at[pl.ds(j * self.half, self.half)]

    def send(self, d, s, j, source):
        to = self.rows(self.slots.at[d, s], j)
        copy = remote(source, to, self.sems[0].at[d, s, j], self.sems[1].at[d, s, j], self.sides[d])
        copy.start()
        self.sent.append(copy)

    def held(self, d, s, j):
        ref = self.rows(self.slots.at[d, s], j)
        arrived(ref, self.sems, (d, s, j), self.sides[d])
        return ref

    def first(self, part):
        for d in range(2):
            self.send(d, 0, d, self.rows(part, d))

    def relay(self, s, parts):
        for j in range(2):
            for d in range(2):
                source = self.rows(parts[d], j)
                if s > 1 or j == d:
                    held = self.held(d, s - 1, j)
                    add_into(held, source)
                    source = held
                self.send(d, s, j, source)

    def last(self, part, out):
        for j in range(2):
            held = [self.held(d, RING // 2 - 1, j) for d in range(2)]
            sum_of_three(self.rows(out, j), self.rows(part, j), *held)

    def end(self):
        for copy in self.sent:
            copy.wait_send()


def ring_scatter(blocks, out, slots, sems, place):
    ring = RingSum(slots, sems, place)
    ring.first(blocks.here(RING // 2))
    yield
    for s in range(1, RING // 2):
        k = RING // 2 - s
        ring.relay(s, (blocks.here(k), blocks.here(-k)))
        yield
    ring.last(blocks.here(0), out)
    ring.end()
    yield


def pair_sems():
    return [pltpu.SemaphoreType.DMA((RING,))] * 2


OFFSETS = (1, -1, 2, -2, 3, -3, 4)


def exchange(pieces, here, sems, place, group=RING):
    for i in range(0, len(OFFSETS), group):
        for k in OFFSETS[i : i + group]:
            at = slot(k)
            for src, dst in pieces(k):
                remote(src, dst, sems[0].at[at], sems[1].at[at], {"ctx": place.at(k)}).start()
        yield
    for k in OFFSETS:
        arrived(here(k), sems, RING - 1 if k == RING // 2 else slot(-k), {"ctx": place.at(k)})
    for k in OFFSETS:
        remote(here(k), here(k), sems[0].at[slot(k)], sems[1].at[slot(k)], {"ctx": place.at(k)}).wait_send()
    yield


def by_owner(src, dst, sems, place, group=RING):
    return exchange(lambda k: [(src.at[place.at(k)], dst.at[place.c])], lambda k: dst.at[place.at(k)], sems, place, group)


def block_at(i, size):
    return pl.ds(pl.multiple_of(i * size, size), size)


class ByOwner:
    def __init__(self, ref, rows):
        self.ref, self.rows = ref, rows

    def owner(self, c, side=None):
        return self.ref.at[block_at(c, self.rows)]


class ByArrival:
    def __init__(self, ref, rows, place):
        self.ref, self.rows, self.place = ref, rows, place

    def owner(self, c, side="here"):
        far = {"here": 0, "up": 2, "down": -2, "side": 1 - 2 * self.place.x}[side]
        mine = self.place.c + far
        z, x = mine // 2, lax.rem(mine, 2)
        p = z + x * (7 - 2 * z)
        z, x = c // 2, lax.rem(c, 2)
        k = lax.rem(z + x * (7 - 2 * z) - p + 2 * RING, RING)
        late = jnp.where(k == RING // 2, RING - 1, 2 * (RING - k) - 1)
        return self.ref.at[block_at(jnp.where(k < RING // 2, 2 * k, late), self.rows)]


def grid_sems():
    return [pltpu.SemaphoreType.DMA((2, 3))] * 2 + [pltpu.SemaphoreType.DMA((4,))] * 2


def grid_gather(own, blocks, sems, place, late=False):
    z_sems, x_sems = sems[:2], sems[2:]
    z, x = place.z, place.x
    sent = []

    def send(when, src, c, side, pair, index, device):
        copy = remote(src, blocks.owner(c, side), pair[0].at[index], pair[1].at[index], device)
        pl.when(when)(copy.start)
        sent.append((when, copy))

    def across(when, src, line):
        send(when, src, 2 * line + x, "side", x_sems, line, place.side)

    send(z < 3, own, place.c, "up", z_sems, (0, 0), place.up)
    send(z > 0, own, place.c, "down", z_sems, (1, 0), place.down)
    if not late:
        across(z >= 0, own, z)
    yield
    for hop in range(1, 4):
        for d, (line, here, further) in enumerate(((z - hop, z >= hop, z < 3), (z + hop, z <= 3 - hop, z > 0))):
            index = 2 * line + x
            ref = blocks.owner(jnp.clip(index, 0, RING - 1))
            device = (place.down, place.up)[d]

            @pl.when(here)
            def _():
                arrived(ref, z_sems, (d, hop - 1), device)

            if hop < 3:
                send(here & further, ref, jnp.clip(index, 0, RING - 1), ("up", "down")[d], z_sems, (d, hop), (place.up, place.down)[d])
            if not late:
                across_line = jnp.clip(line, 0, 3)
                send(here, ref, 2 * across_line + x, "side", x_sems, across_line, place.side)
        yield
    if late:
        across(z >= 0, own, z)
        for hop in range(1, 4):
            line = lax.rem(z + hop, 4)
            across(z >= 0, blocks.owner(2 * line + x), line)
        yield
    for line in range(4):
        arrived(blocks.owner(2 * line + 1 - x), x_sems, line, place.side)
    for when, copy in sent:
        pl.when(when)(copy.wait_send)
    yield


def grid_sum_sems():
    return [pltpu.SemaphoreType.DMA((4,))] * 2 + [pltpu.SemaphoreType.DMA((2, 4))] * 2


class GridSum:
    def __init__(self, part, over, line, sems, place):
        self.part, self.over, self.line, self.place = part, over, line, place
        self.x_sems, self.z_sems = sems[:2], sems[2:]
        self.rows = over.shape[1]
        self.sent = []

    def plane(self, i):
        z = self.place.z
        inner = jnp.where((z == 1) | (z == 2), 1, 0)
        plain, mid = (3, 2, 1, 0)[i], (3, 0, 2, 1)[i]
        order = plain + inner * (mid - plain)
        return jnp.where(z < 2, order, 3 - order)

    def send(self, when, src, dst, pair, index, device):
        copy = remote(src, dst, pair[0].at[index], pair[1].at[index], device)
        pl.when(when)(copy.start)
        self.sent.append((when, copy))

    def mine(self, z, x):
        return self.part.at[block_at(2 * z + x, self.rows)]

    def across(self, i):
        z = self.plane(i)
        self.send(self.place.z >= 0, self.mine(z, 1 - self.place.x), self.over.at[z], self.x_sems, z, self.place.side)

    def along(self, i):
        z, me = self.plane(i), self.place.z
        held = self.over.at[z]
        arrived(held, self.x_sems, z, self.place.side)
        add_into(held, self.mine(z, self.place.x))
        for d, (when, more, source, device) in enumerate(
            (
                (z > me, me > 0, self.place.down, self.place.up),
                (z < me, me < 3, self.place.up, self.place.down),
            )
        ):

            @pl.when(when & more)
            def _():
                arrived(self.line.at[d, z], self.z_sems, (d, z), source)
                add_into(held, self.line.at[d, z])

            self.send(when, held, self.line.at[d, z], self.z_sems, (d, z), device)

    def last(self, out):
        z = self.place.z
        held = self.over.at[z]
        arrived(held, self.x_sems, z, self.place.side)
        add_to(out, held, self.mine(z, self.place.x))
        for d, (when, source) in enumerate(((z > 0, self.place.down), (z < 3, self.place.up))):

            @pl.when(when)
            def _():
                arrived(self.line.at[d, z], self.z_sems, (d, z), source)
                add_to(out, out, self.line.at[d, z])

    def end(self):
        for when, copy in self.sent:
            pl.when(when)(copy.wait_send)


def pairs_of(sems):
    return [sems[i : i + 2] for i in range(0, len(sems), 2)]


def seq_sems():
    return [pltpu.SemaphoreType.DMA((3,))] * 2


def seq_gather(own, buf, sems, place):
    first = remote(own, buf.at[place.s], sems[0].at[0], sems[1].at[0], place.far_peer)
    second = remote(own, buf.at[place.s], sems[0].at[1], sems[1].at[1], place.core_peer)
    first.start()
    second.start()
    yield
    arrived(buf.at[place.s_far], sems, 0, place.far_peer)
    third = remote(buf.at[place.s_far], buf.at[place.s_far], sems[0].at[2], sems[1].at[2], place.core_peer)
    third.start()
    yield
    arrived(buf.at[place.s_core], sems, 1, place.core_peer)
    arrived(buf.at[place.s_both], sems, 2, place.core_peer)
    for copy in (first, second, third):
        copy.wait_send()
    yield


def sum_of_three(dst, *terms):
    step = math.gcd(dst.shape[0], 16)

    @pl.loop(0, dst.shape[0] // step)
    def _(i):
        at = pl.ds(pl.multiple_of(i * step, step), step)
        one, two, three = (term[at].astype(jnp.float32) for term in terms)
        dst[at] = one + two + three


def add_to(dst, one, two):
    step = math.gcd(dst.shape[0], 16)

    @pl.loop(0, dst.shape[0] // step)
    def _(i):
        at = pl.ds(pl.multiple_of(i * step, step), step)
        dst[at] = one[at].astype(jnp.float32) + two[at].astype(jnp.float32)


def add_into(dst, other):
    rows = dst.shape[0]
    step = math.gcd(rows, 16)

    @pl.loop(0, rows // step)
    def _(i):
        at = pl.ds(pl.multiple_of(i * step, step), step)
        dst[at] = (dst[at].astype(jnp.float32) + other[at].astype(jnp.float32)).astype(dst.dtype)


class SeqSum:
    def __init__(self, grad, block, near, far, sems, place):
        self.grad, self.block, self.near_ref, self.far, self.sems, self.place = grad, block, near, far, sems, place
        self.low, self.row = lax.rem(place.s, 2), place.s // 2
        self.sent = []

    def send(self, src, dst, i, device):
        copy = remote(src, dst, self.sems[0].at[i], self.sems[1].at[i], device)
        copy.start()
        self.sent.append(copy)

    def near(self, i):
        r = (1 - self.row, self.row)[i]
        self.grad(r * 2 + 1 - self.low, self.block.at[i], False)
        self.send(self.block.at[i], self.near_ref.at[i], i, self.place.core_peer)

    def across(self):
        arrived(self.near_ref.at[0], self.sems, 0, self.place.core_peer)
        self.grad((1 - self.row) * 2 + self.low, self.near_ref.at[0], True)
        self.send(self.near_ref.at[0], self.far, 2, self.place.far_peer)

    def own(self):
        arrived(self.near_ref.at[1], self.sems, 1, self.place.core_peer)
        self.grad(self.row * 2 + self.low, self.near_ref.at[1], True)

    def last(self):
        arrived(self.far, self.sems, 2, self.place.far_peer)
        add_into(self.far, self.near_ref.at[1])

    def end(self):
        for copy in self.sent:
            copy.wait_send()


def call(body, outs, args, spaces, out_spaces, scratch, ident):
    return pl.pallas_call(
        body,
        out_shape=outs,
        in_specs=[pl.BlockSpec(memory_space=space) for space in spaces],
        out_specs=[pl.BlockSpec(memory_space=space) for space in out_spaces],
        scratch_shapes=scratch,
        compiler_params=pltpu.CompilerParams(
            collective_id=ident, has_side_effects=True, vmem_limit_bytes=63 * 1024 * 1024
        ),
    )(*args)


def shaped(shape, dtype=jnp.bfloat16):
    return jax.ShapeDtypeStruct(shape, dtype)


def dot(a, b, at=(1, 0)):
    return lax.dot_general(a, b, (((at[0],), (at[1],)), ((), ())), preferred_element_type=jnp.float32)


def chunks(total, size, body):
    @pl.loop(0, total // size)
    def _(i):
        body(pl.ds(pl.multiple_of(i * size, size), size))


def turned(t, cos, sin, sign):
    half = t.shape[1] // 2
    a, b = t[:, :half], t[:, half:]
    return jnp.concatenate([a * cos - sign * b * sin, b * cos + sign * a * sin], axis=-1)


def probabilities(q, k, pos_rows, start_rows, pos_cols):
    scores = dot(q, k, (1, 1)) * HDIM ** (-0.5)
    visible = (pos_cols >= start_rows) & (pos_cols <= pos_rows)
    scores = jnp.where(visible, scores, NEG_FILL)
    weight = jnp.exp(scores - jnp.max(scores, axis=-1, keepdims=True))
    return weight / jnp.sum(weight, axis=-1, keepdims=True)


def place_rows(pairs, segments, block_cos, block_sin, row_cos, row_sin, cos, sin, pos_rows, start_rows, pos_cols):
    f32 = jnp.float32
    half = row_cos.shape[0]
    bounds = [
        jnp.sum(jnp.where(segments[...] < d, 1.0, 0.0).astype(f32), axis=1, keepdims=True) for d in range(1, DOCS)
    ]
    numbers = lax.broadcasted_iota(jnp.int32, block_cos.shape, 0)
    for c in range(RING):
        blocks = (pairs[0, c], 2 * RING - 1 - pairs[0, c])
        lanes = lax.broadcasted_iota(jnp.int32, (1, 2 * half), 1)
        low = blocks[0] * half + lanes
        pos_cols[:, pl.ds(c * 2 * half, 2 * half)] = jnp.where(lanes < half, low, blocks[1] * half + lanes - half).astype(f32)
        for j, block in enumerate(blocks):
            at = pl.ds((2 * c + j) * half, half)
            near_cos = jnp.sum(jnp.where(numbers == block, block_cos[...], 0.0), axis=0, keepdims=True)
            near_sin = jnp.sum(jnp.where(numbers == block, block_sin[...], 0.0), axis=0, keepdims=True)
            cos[at, :] = near_cos * row_cos[...] - near_sin * row_sin[...]
            sin[at, :] = near_sin * row_cos[...] + near_cos * row_sin[...]
            pos = (block * half + lax.broadcasted_iota(jnp.int32, (half, 1), 0)).astype(f32)
            start = jnp.zeros((half, 1), f32)
            for bound in bounds:
                start = jnp.where(pos >= bound, bound, start)
            pos_rows[at, :] = pos
            start_rows[at, :] = start


def column(row):
    n = row.shape[1]
    same = lax.broadcasted_iota(jnp.int32, (n, n), 0) == lax.broadcasted_iota(jnp.int32, (n, n), 1)
    return jnp.sum(jnp.where(same, row, 0.0), axis=1, keepdims=True)


def attention_kernel(plan, x, gain_one, gain_two, pairs, segments, block_cos, block_sin, row_cos, row_sin,
                     dy, w_query, w_key, w_value, wout, w_gate, w_up, wdown,
                     hidden, hhat, ob_local, cos, sin, pos_rows, start_rows, pos_cols,
                     q_out, k_out, v_out, x_all, dy_all, wqkv_all, wout_all, wg_all, wu_own, wdown_all,
                     xhat, wq, wk, wv, wg, wu, wout_s, wdown_s, dy_s, heads, gate_units, up_units, x_v, wqkv_v, wout_v, q, k, v, ob, local, loads, *sems):
    place = Place()
    qkv_swap, qkv_seq, out_ring, out_seq, ob_swap, gate_swap, gate_seq, up_swap, down_seq = pairs_of(sems[:18])
    x_grid, dy_grid = sems[18:22], sems[22:26]
    bf16, f32 = jnp.bfloat16, jnp.float32
    rows, width = x.shape
    head, shard = ob.shape[1], wout.shape[0]
    groups = H // KVH
    fetch = [
        pltpu.make_async_copy(src, dst, loads.at[i])
        for i, (src, dst) in enumerate(
            (
                (w_query, wq), (w_key, wk), (w_value, wv), (w_gate, wg), (w_up, wu),
                (wout, wout_s), (wdown, wdown_s), (dy, dy_s),
            )
        )
    ]
    for copy in fetch:
        copy.start()
    keep = [
        pltpu.make_async_copy(wout_s, wout_all.at[place.s, place.c], local.at[0]),
        pltpu.make_async_copy(wdown_s, wdown_all.at[place.s], local.at[1]),
        pltpu.make_async_copy(dy_s, ByArrival(dy_all, rows, place).owner(place.c), local.at[2]),
    ]

    def normed(at):
        t = x[at, :].astype(f32)
        xhat[at, :] = (t * lax.rsqrt(jnp.mean(t * t, axis=-1, keepdims=True) + EPSILON)).astype(bf16)

    def scale(ref, gain, columns, into, at):
        @pl.loop(0, RING)
        def _(t):
            for j, cols in enumerate(columns(t)):
                part = (ref[:, cols].astype(f32) * gain).astype(bf16)
                into[t, :, pl.ds(at + j * cols.size, cols.size)] = part

    def prepare():
        chunks(rows, 16, normed)
        for loaded, kept in zip(fetch[5:], keep):
            loaded.wait()
            kept.start()
        for copy in fetch[:3]:
            copy.wait()
        gain = column(gain_one[...].astype(f32))
        scale(wq, gain, lambda t: [block_at(t, head)], heads, 0)
        scale(wk, gain, lambda t: [block_at(t // groups, head)], heads, head)
        scale(wv, gain, lambda t: [block_at(t // groups, head)], heads, 2 * head)

    greet(place.peers() + [place.core_peer, place.far_peer], prepare)
    down_w = seq_gather(wdown, wdown_all, down_seq, place)
    x_blocks, dy_blocks = ByOwner(x_all, rows), ByArrival(dy_all, rows, place)

    def out_flow():
        yield from ring_gather(wout, Owners(wout_all.at[place.s], place), out_ring, place)
        keep[0].wait()
        yield from seq_gather(wout_all.at[place.s], wout_all, out_seq, place)

    out_w = out_flow()

    def spread(src, dst, swap, seq, sem, group=RING):
        rows_of_s = dst if seq is None else dst.at[place.s]
        own = pltpu.make_async_copy(src.at[place.c], rows_of_s.at[place.c], sem)
        own.start()
        yield from by_owner(src, rows_of_s, swap, place, group)
        own.wait()
        if seq is not None:
            yield from seq_gather(rows_of_s, dst, seq, place)

    qkv_w = spread(heads, wqkv_all, qkv_swap, qkv_seq, local.at[3])
    gate_w = spread(gate_units, wg_all, gate_swap, gate_seq, local.at[4], 2)
    up_w = spread(up_units, wu_own, up_swap, None, local.at[5], 2)
    x_flow = grid_gather(xhat, x_blocks, x_grid, place)
    dy_flow = grid_gather(dy, dy_blocks, dy_grid, place)
    own_x = pltpu.make_async_copy(xhat, x_blocks.owner(place.c), local.at[6])

    flows = {"q": qkv_w, "g": gate_w, "u": up_w, "d": down_w, "o": out_w, "x": x_flow, "y": dy_flow}
    mine = block_at(place.c, head)
    flows["b"] = exchange(
        lambda o: [(ob.at[block_at(place.at(o), rows)], ob_local.at[:, mine])],
        lambda o: ob_local.at[:, block_at(place.at(o), head)],
        ob_swap,
        place,
    )
    load = [pltpu.make_async_copy(x_all, x_v, loads.at[0]), pltpu.make_async_copy(wqkv_all, wqkv_v, loads.at[1])]
    saves = [pltpu.make_async_copy(src, dst, loads.at[2 + i]) for i, (src, dst) in enumerate(((q, q_out), (k, k_out), (v, v_out)))]
    load_out = pltpu.make_async_copy(wout_all, wout_v, local.at[0])

    def scale_units():
        for copy in fetch[3:5]:
            copy.wait()
        gain = column(gain_two[...].astype(f32))
        own = wdown.shape[0]
        for ref, into in ((wg, gate_units), (wu, up_units)):
            scale(ref, gain, lambda t: [block_at(i * RING + t, own) for i in range(SEQ)], into, 0)

    def find_rows():
        place_rows(
            pairs, segments, block_cos, block_sin, row_cos, row_sin, cos, sin, pos_rows, start_rows, pos_cols
        )

    def load_attention():
        own_x.start()
        own_x.wait()
        for copy in load:
            copy.start()

    halves = x_v.shape[0] // 2

    def project(at):
        qkv = dot(x_v[at, :], wqkv_v[...].reshape(width, 3 * head))
        c, s = cos[at, :], sin[at, :]
        q[at, :] = turned(qkv[:, :head], c, s, 1.0).astype(bf16)
        k[at, :] = turned(qkv[:, head : 2 * head], c, s, 1.0).astype(bf16)
        v[at, :] = qkv[:, 2 * head :].astype(bf16)

    def project_half(i):
        if i == 0:
            for copy in load:
                copy.wait()
        chunks(halves, 256, lambda at: project(pl.ds(pl.multiple_of(i * halves + at.start, 256), 256)))
        if i == 1:
            for copy in saves:
                copy.start()

    def attend(at):
        prob = probabilities(q[at, :], k[...], pos_rows[at, :], start_rows[at, :], pos_cols[...])
        ob[at, :] = dot(prob.astype(bf16), v[...]).astype(bf16)

    def attend_half(i):
        chunks(halves, 256, lambda at: attend(pl.ds(pl.multiple_of(i * halves + at.start, 256), 256)))
        if i == 1:
            ob_local[:, mine] = ob[block_at(place.c, rows), :]

    def finish_hidden():
        load_out.wait()

        def residual(cols):
            part = dot(ob_local[...], wout_v[:, :, :, cols].reshape(width, cols.size))
            hidden[:, cols] = x[:, cols].astype(f32) + part

        chunks(width, 256, residual)

        def normed_two(at):
            t = hidden[at, :]
            hhat[at, :] = (t * lax.rsqrt(jnp.mean(t * t, axis=-1, keepdims=True) + EPSILON)).astype(bf16)

        chunks(rows, 16, normed_two)

    works = {
        "S": scale_units, "R": find_rows, "L": load_attention, "W": load_out.start, "H": finish_hidden,
    }
    turns = {"P": iter((0, 1)), "A": iter((0, 1))}
    for step in plan:
        if step in flows:
            next(flows[step], None)
        elif step in turns:
            (project_half if step == "P" else attend_half)(next(turns[step]))
        else:
            works[step]()
    for name, flow in flows.items():
        if name in plan:
            for _ in flow:
                pass
    if "P" in plan:
        for copy in saves:
            copy.wait()
    elif "L" in plan:
        for copy in load:
            copy.wait()
    if "S" not in plan:
        for copy in fetch[3:5]:
            copy.wait()
    if "o" not in plan:
        keep[0].wait()
    if "W" in plan and "H" not in plan:
        load_out.wait()
    keep[1].wait()
    keep[2].wait()


def mlp_kernel(plan, hhat, dy_hbm, wg_hbm, wu_own, wdown_hbm, sum_h, sum_o, col_out, down_out,
               h_all, dy_all, wg, wu, wd, mid, dgate, dup, stage_h, stage_o, stage, stage_2, slots_h, slots_o,
               col_sent, col_near, col_far, down_sent, down_near, down_far, local, *sems):
    place = Place()
    h_sems, sum_h_sems, sum_o_sems, col_seq, down_seq, up_seq = pairs_of(sems)
    greet([place.right, place.left, place.core_peer, place.far_peer])
    rows, width = hhat.shape
    ff = wg.shape[1]
    bf16, f32 = jnp.bfloat16, jnp.float32
    up_blocks = Blocks(wu, wu_own.shape[0])
    keep = [
        pltpu.make_async_copy(src, dst, local.at[i])
        for i, (src, dst) in enumerate(
            ((hhat, h_all.at[pl.ds(0, rows)]), (wg_hbm, wg), (wu_own, up_blocks[place.s]), (wdown_hbm, wd), (dy_hbm, dy_all))
        )
    ]
    for copy in keep:
        copy.start()
    gather = ring_gather(hhat, Rows(h_all, rows), h_sems, place)
    up_flow = seq_gather(wu_own, up_blocks, up_seq, place)

    def hidden_rows(start, count):
        at = pl.ds(start, count)

        def body(cols):
            gate = dot(h_all[at, :], wg[:, cols])
            up = dot(h_all[at, :], wu[:, cols])
            dmid = dot(dy_all[at, :], wd[cols, :], (1, 1))
            sig = jax.nn.sigmoid(gate)
            active = gate * sig
            mid[at, cols] = (active * up).astype(bf16)
            dgate[at, cols] = (dmid * up * sig * (1.0 + gate * (1.0 - sig))).astype(bf16)
            dup[at, cols] = (dmid * active).astype(bf16)

        chunks(ff, 512, body)

    def part_h(start, count, dst):
        at = pl.ds(start, count)

        def body(cols):
            dst[:, cols] = (dot(dgate[at, :], wg[cols, :], (1, 1)) + dot(dup[at, :], wu[cols, :], (1, 1))).astype(bf16)

        chunks(width, 1024, body)

    def part_o(start, count, dst):
        at = pl.ds(start, count)

        def body(cols):
            dst[:, cols] = dot(mid[at, :], wd[:, cols]).astype(bf16)

        chunks(width, 1024, body)

    def col_grad(s, dst, add):
        def body(cols):
            lhs = h_all[:, pl.ds(pl.multiple_of(s * dst.shape[0] + cols.start, 256), 256)]
            for side, grad in enumerate((dgate, dup)):
                there = pl.ds(side * ff, ff)
                value = dot(lhs, grad[...], (0, 0))
                if add:
                    value = value + dst[cols, there].astype(f32)
                dst[cols, there] = value.astype(bf16)

        chunks(dst.shape[0], 256, body)

    def down_grad(s, dst, add):
        lhs = pl.ds(pl.multiple_of(s * dst.shape[0], 256), dst.shape[0])

        def body(cols):
            value = dot(mid[:, lhs], dy_all[:, cols], (0, 0))
            if add:
                value = value + dst[:, cols].astype(f32)
            dst[:, cols] = value.astype(bf16)

        chunks(width, 1024, body)

    def pair(ref):
        return (ref.at[pl.ds(rows, rows)], ref.at[pl.ds(0, rows)])

    col_sum = SeqSum(col_grad, col_sent, col_near, col_far, col_seq, place)
    down_sum = SeqSum(down_grad, down_sent, down_near, down_far, down_seq, place)
    ring_h, ring_o = RingSum(slots_h, sum_h_sems, place), RingSum(slots_o, sum_o_sems, place)
    top_h, top_o = stage_h.at[pl.ds(2 * rows, rows)], stage_o.at[pl.ds(2 * rows, rows)]
    next_h, next_o = stage_h.at[pl.ds(0, 2 * rows)], stage_o.at[pl.ds(0, 2 * rows)]

    def in_turn(*actions):
        return iter(actions)

    def parts(part, top, following, later):
        return in_turn(
            lambda: part(7 * rows, rows, top),
            lambda: part(5 * rows, 2 * rows, following),
            lambda: part(3 * rows, 2 * rows, later),
            lambda: part(rows, 2 * rows, later),
            lambda: part(0, rows, later.at[pl.ds(0, rows)]),
        )

    def sums(ring, top, following, later, out):
        return in_turn(
            lambda: ring.first(top),
            lambda: ring.relay(1, pair(following)),
            lambda: ring.relay(2, pair(later)),
            lambda: ring.relay(3, pair(later)),
            lambda: ring.last(later.at[pl.ds(0, rows)], out),
        )

    def wait_loads():
        for copy in keep:
            copy.wait()

    turns = {
        "k": in_turn(wait_loads),
        "a": in_turn(lambda: hidden_rows(0, rows)),
        "b": in_turn(lambda: hidden_rows(rows, 2 * rows)),
        "c": in_turn(lambda: hidden_rows(3 * rows, 2 * rows)),
        "d": in_turn(lambda: hidden_rows(5 * rows, 2 * rows)),
        "e": in_turn(lambda: hidden_rows(7 * rows, rows)),
        "P": parts(part_h, top_h, next_h, stage),
        "r": sums(ring_h, top_h, next_h, stage, sum_h),
        "O": parts(part_o, top_o, next_o, stage_2),
        "s": sums(ring_o, top_o, next_o, stage_2, sum_o),
        "n": in_turn(lambda: col_sum.near(0), lambda: col_sum.near(1)),
        "m": in_turn(col_sum.across),
        "w": in_turn(col_sum.own),
        "l": in_turn(col_sum.last),
        "N": in_turn(lambda: down_sum.near(0), lambda: down_sum.near(1)),
        "M": in_turn(down_sum.across),
        "W": in_turn(down_sum.own),
        "L": in_turn(down_sum.last),
    }
    for step in plan:
        if step == "x":
            next(gather)
        elif step == "u":
            next(up_flow)
        else:
            next(turns[step])()
    ends = []
    for i, (total, out) in enumerate(((col_sum, col_out), (down_sum, down_out))):
        ends.append(pltpu.make_async_copy(total.far, out, local.at[i]))
        ends[-1].start()
    for copy in ends:
        copy.wait()
    for flow in (ring_h, ring_o, col_sum, down_sum):
        flow.end()
    for flow in (gather, up_flow):
        for _ in flow:
            pass


def backward_kernel(plan, weighted, hidden, dy, x, pos_cols, q_hbm, k_hbm, v_hbm, ob_hbm, cos_hbm, sin_hbm, pos_hbm, start_hbm,
                    x_all, wqkv_all, wout_all, col,
                    grad_x, out_grad, qkv_raw, gate_raw, up_raw, col_hbm,
                    q, k, v, ob_local, cos, sin, pos_rows, start_rows,
                    x_v, wqkv_v, wout_v, branch, datt_own, datt, dqkv, dk, dv, sum_x, over_x, line_x,
                    qkv_sent, qkv_near, qkv_far, qkv_in, out_sent, out_near, out_far, slots_o, local, early, *sems):
    place = Place()
    att_swap, qkv_seq, qkv_swap, out_seq, out_ring = pairs_of(sems[:10])
    x_grid, col_swap = sems[10:14], sems[14:]
    bf16, f32 = jnp.bfloat16, jnp.float32
    rows, width = x.shape
    seq_len, head = q.shape
    shard = out_grad.shape[0]
    loads = [
        pltpu.make_async_copy(src, dst, local.at[i])
        for i, (src, dst) in enumerate(((wout_all, wout_v), (x_all, x_v), (wqkv_all, wqkv_v)))
    ]
    for copy in loads:
        copy.start()
    qkv_blocks = Blocks(qkv_far, shard)
    fetched = [
        pltpu.make_async_copy(src, dst, early.at[i])
        for i, (src, dst) in enumerate(
            (
                (ob_hbm, ob_local), (q_hbm, q), (k_hbm, k), (v_hbm, v),
                (cos_hbm, cos), (sin_hbm, sin), (pos_hbm, pos_rows), (start_hbm, start_rows),
            )
        )
    ]
    for copy in fetched:
        copy.start()
    def norm_back(tensor, grads):
        scale = lax.rsqrt(jnp.mean(tensor * tensor, axis=-1, keepdims=True) + EPSILON)
        inner = jnp.mean(grads * tensor, axis=-1, keepdims=True)
        return scale * grads - tensor * (scale * scale * scale) * inner

    def hidden_back(at):
        grads = dy[at, :].astype(f32) + norm_back(hidden[at, :], weighted[at, :])
        grad_x[at, :] = grads
        branch[at, :] = grads.astype(bf16)

    greet(place.peers() + [place.core_peer, place.far_peer], lambda: chunks(rows, 16, hidden_back))

    def heads_back():
        loads[0].wait()
        fetched[0].wait()

        def att_back(cols):
            datt_own[:, cols] = dot(branch[...], wout_v[cols, :], (1, 1)).astype(bf16)

        chunks(width, head, att_back)

    mine = block_at(place.c, rows)
    att_flow = exchange(
        lambda o: [(datt_own.at[:, block_at(place.at(o), head)], datt.at[mine])],
        lambda o: datt.at[block_at(place.at(o), rows)],
        att_swap,
        place,
    )
    def rows_grad(left, right):
        def grad(s, dst, add):
            def body(cols):
                lhs = left[:, pl.ds(pl.multiple_of(s * dst.shape[0] + cols.start, 256), 256)]
                value = dot(lhs, right[...], (0, 0))
                if add:
                    value = value + dst[cols, :].astype(f32)
                dst[cols, :] = value.astype(bf16)

            chunks(dst.shape[0], 256, body)

        return grad

    out_sum = SeqSum(rows_grad(ob_local, branch), out_sent, out_near, out_far, out_seq, place)
    qkv_sum = SeqSum(rows_grad(x_v, dqkv), qkv_sent, qkv_near, qkv_far, qkv_seq, place)
    def attend_back(at):
        prob = probabilities(q[at, :], k[...], pos_rows[at, :], start_rows[at, :], pos_cols[...])
        dprob = dot(datt[at, :], v[...], (1, 1))
        delta = jnp.sum(prob * dprob, axis=-1, keepdims=True)
        dscore = (prob * (dprob - delta)).astype(bf16)
        dq = dot(dscore, k[...]) * HDIM ** (-0.5)
        dqkv[at, pl.ds(0, head)] = turned(dq, cos[at, :], sin[at, :], -1.0).astype(bf16)
        dk[...] += dot(dscore, q[at, :], (0, 0))
        dv[...] += dot(prob.astype(bf16), datt[at, :], (0, 0))

    def finish_back(at):
        turned_dk = turned(dk[at, :] * HDIM ** (-0.5), cos[at, :], sin[at, :], -1.0)
        dqkv[at, pl.ds(head, head)] = turned_dk.astype(bf16)
        dqkv[at, pl.ds(2 * head, head)] = dv[at, :].astype(bf16)

    def all_back():
        dk[...] = jnp.zeros_like(dk)
        dv[...] = jnp.zeros_like(dv)
        datt[mine, :] = datt_own[:, block_at(place.c, head)]
        for copy in loads[1:] + fetched[1:]:
            copy.wait()
        chunks(seq_len, 256, attend_back)
        chunks(seq_len, 128, finish_back)

    part = wout_v.at[pl.ds(0, seq_len)]
    col_in = wout_v.at[pl.ds(seq_len, RING * shard)]
    total = GridSum(part, over_x, line_x, x_grid, place)

    def part_x(i):
        at = block_at(total.plane(i), 2 * rows)

        def body(cols):
            part[at, cols] = dot(dqkv[at, :], wqkv_v[cols, :], (1, 1)).astype(bf16)

        chunks(width, 1024, body)
        total.across(i)

    unit = gate_raw.shape[1] // (RING * SEQ)
    groups = H // KVH

    def fetch_columns():
        for k in (0,) + OFFSETS:
            c = place.at(k)
            source = Blocks(col_hbm if k else col, shard)
            pltpu.make_async_copy(source[c], Blocks(col_in, shard)[c], local.at[4]).start()

    def move_columns():
        pltpu.make_async_copy(col_in, col_in, local.at[4]).wait()
        for c in range(RING):
            for side, raw in enumerate((gate_raw, up_raw)):
                for i in range(SEQ):
                    value = col_in[pl.ds(c * shard, shard), pl.ds((side * SEQ + i) * unit, unit)]
                    raw[:, pl.ds((i * RING + c) * unit, unit)] = value

    def qkv_last():
        qkv_sum.last()
        qkv_in[place.c] = qkv_blocks[place.c][...]

    def tokens_back():
        total.last(sum_x)

        def token_back(at):
            grad_x[at, :] = grad_x[at, :] + norm_back(x[at, :].astype(f32), sum_x[at, :])

        chunks(rows, 16, token_back)

    def finish_qkv():
        for t in range(H):
            qkv_raw[:, pl.ds(t * head, head)] = qkv_in[t, :, pl.ds(0, head)].astype(f32)
        for side in (1, 2):
            for t in range(KVH):
                value = sum(qkv_in[t * groups + g, :, pl.ds(side * head, head)].astype(f32) for g in range(groups))
                qkv_raw[:, pl.ds((H + (side - 1) * KVH + t) * head, head)] = value

    def each(action, count=4):
        return iter([functools.partial(action, i) for i in range(count)])

    out_blocks = Owners(Blocks(out_far, shard), place)
    flows = {
        "a": att_flow,
        "c": by_owner(Blocks(col, shard), Blocks(col_hbm, shard), col_swap, place, 2),
        "o": ring_scatter(out_blocks, out_grad, slots_o, out_ring, place),
        "t": by_owner(qkv_blocks, qkv_in, qkv_swap, place),
    }
    works = {
        "h": heads_back, "B": all_back, "m": out_sum.across, "w": out_sum.own, "e": out_sum.last,
        "M": qkv_sum.across, "W": qkv_sum.own, "E": qkv_last, "C": fetch_columns, "V": move_columns, "Z": tokens_back, "F": finish_qkv,
    }
    turns = {"n": each(out_sum.near, 2), "N": each(qkv_sum.near, 2), "p": each(part_x), "l": each(total.along, 3)}
    for step in plan:
        if step in flows:
            next(flows[step])
        elif step in turns:
            next(turns[step])()
        else:
            works[step]()
    for name, flow in flows.items():
        if name in plan:
            for _ in flow:
                pass
    for flow in (total, out_sum, qkv_sum):
        flow.end()


class Blocks:
    def __init__(self, ref, rows):
        self.ref, self.rows = ref, rows
        self.shape = (ref.shape[0] // rows, rows) + tuple(ref.shape[1:])

    @property
    def at(self):
        return self

    def __getitem__(self, i):
        return self.ref.at[pl.ds(pl.multiple_of(i * self.rows, self.rows), self.rows)]


DMA = pltpu.SemaphoreType.DMA
HBM = pl.ANY


ATTENTION_PLAN = "doooooooooooxxqxxqqRSggggqqxLyPPAAbgygyuuuuyoogWbHydgu"


def attention_stage(
    tokens, cotangent, gain_attn, w_query, w_key, w_value, w_out, gain_mlp, w_gate, w_up, w_down, pair_order, segments, plan
):
    bf16, f32 = jnp.bfloat16, jnp.float32
    n = RING
    rows, width = tokens.shape[1], tokens.shape[2]
    seq_len = segments.shape[1]
    shard = w_query.shape[0]
    ff_own = w_down.shape[0]
    ff_mine = SEQ * ff_own
    head = HDIM
    frequency = THETA ** (-(np.arange(head // 2) * 2.0 / head))
    half = rows // 2
    block_angles = np.arange(2 * n)[:, None] * half * frequency[None, :]
    row_angles = np.arange(half)[:, None] * frequency[None, :]
    tables = tuple(jnp.asarray(f(angles), f32) for angles in (block_angles, row_angles) for f in (np.cos, np.sin))

    return call(
        functools.partial(attention_kernel, plan),
        [
            shaped((rows, width), f32),
            shaped((rows, width)),
            shaped((rows, H * head)),
            shaped((seq_len, head // 2), f32),
            shaped((seq_len, head // 2), f32),
            shaped((seq_len, 1), f32),
            shaped((seq_len, 1), f32),
            shaped((1, seq_len), f32),
            shaped((seq_len, head)),
            shaped((seq_len, head)),
            shaped((seq_len, head)),
            shaped((seq_len, width)),
            shaped((seq_len, width)),
            shaped((SEQ, n, shard, 3 * head)),
            shaped((SEQ, n, shard, width)),
            shaped((SEQ, n, shard, ff_mine)),
            shaped((n, shard, ff_mine)),
            shaped((SEQ, ff_own, width)),
        ],
        (tokens[0], gain_attn[None], gain_mlp[None], pair_order, segments)
        + tables
        + (cotangent[0], w_query, w_key, w_value, w_out, w_gate, w_up, w_down),
        [VMEM] * 3 + [pltpu.SMEM] + [VMEM] * 5 + [HBM] * 8,
        [VMEM] * 8 + [HBM] * 10,
        [
            VMEM((rows, width), bf16),
            VMEM(w_query.shape, bf16),
            VMEM(w_key.shape, bf16),
            VMEM(w_value.shape, bf16),
            VMEM(w_gate.shape, bf16),
            VMEM(w_up.shape, bf16),
            VMEM(w_out.shape, bf16),
            VMEM(w_down.shape, bf16),
            VMEM((rows, width), bf16),
            VMEM((n, shard, 3 * head), bf16),
            VMEM((n, shard, ff_mine), bf16),
            VMEM((n, shard, ff_mine), bf16),
            VMEM((seq_len, width), bf16),
            VMEM((SEQ, n, shard, 3 * head), bf16),
            VMEM((SEQ, n, shard, width), bf16),
        ]
        + [VMEM((seq_len, head), bf16)] * 4
        + [DMA((7,)), DMA((8,))]
        + pair_sems()
        + seq_sems()
        + ring_sems()
        + seq_sems()
        + pair_sems()
        + (pair_sems() + seq_sems()) * 2
        + grid_sems() * 2,
        1,
    )


MLP_PLAN = "xuxkxxuxxuabxxxcdxePrnPrnmOsPrOsNPrNMOsPwrOsOWslL"


def mlp_stage(hhat, dy_all, wg_all, wu_own, wdown_all, plan):
    bf16, f32, n = jnp.bfloat16, jnp.float32, RING
    (rows, width), seq_len = hhat.shape, dy_all.shape[0]
    ff_mine = wg_all.shape[1]
    shard, ff_own = width // (SEQ * n), ff_mine // SEQ
    slot_shape = VMEM((2, n // 2, rows, width), bf16)
    col_piece, down_piece = (n * shard, 2 * ff_mine), (ff_own, width)
    return call(
        functools.partial(mlp_kernel, plan),
        [shaped((rows, width), f32)] * 2 + [shaped(col_piece), shaped(down_piece)],
        (hhat, dy_all, wg_all, wu_own, wdown_all),
        [HBM] * 5,
        [VMEM] * 2 + [HBM] * 2,
        [VMEM((seq_len, width), bf16)] * 2
        + [VMEM((width, ff_mine), bf16)] * 2
        + [VMEM((ff_mine, width), bf16)]
        + [VMEM((seq_len, ff_mine), bf16)] * 3
        + [VMEM((3 * rows, width), bf16)] * 2
        + [VMEM((2 * rows, width), bf16)] * 2
        + [slot_shape] * 2
        + [VMEM((2,) + col_piece, bf16), VMEM((2,) + col_piece, bf16), VMEM(col_piece, bf16)]
        + [VMEM((2,) + down_piece, bf16), VMEM((2,) + down_piece, bf16), VMEM(down_piece, bf16)]
        + [DMA((5,))]
        + ring_sems() * 3
        + seq_sems() * 3,
        2,
    )


BACKWARD_PLAN = "hannmaccccBpNpNplMplwWlEteoZocCoVtooF"


def backward_stage(args, columns, plan):
    bf16, f32, n, head = jnp.bfloat16, jnp.float32, RING, HDIM
    (rows, width), seq_len, shard = args[0].shape, args[5].shape[0], columns[0]
    ff_mine = columns[1] // n
    piece = (n * shard, width)
    qkv_piece = (n * shard, 3 * head)
    outs = call(
        functools.partial(backward_kernel, plan),
        [
            shaped((rows, width), f32),
            shaped((shard, width), f32),
            shaped((shard, (H + 2 * KVH) * head), f32),
            shaped(columns),
            shaped(columns),
            shaped((n * shard, 2 * ff_mine)),
        ],
        args,
        [VMEM] * 5 + [HBM] * 12,
        [VMEM] * 5 + [HBM],
        [VMEM((seq_len, head), bf16)] * 3
        + [VMEM((rows, H * head), bf16)]
        + [VMEM((seq_len, head // 2), f32)] * 2
        + [VMEM((seq_len, 1), f32)] * 2
        + [
            VMEM((seq_len, width), bf16),
            VMEM((width, 3 * head), bf16),
            VMEM((H * head, width), bf16),
            VMEM((rows, width), bf16),
            VMEM((rows, width), bf16),
            VMEM((seq_len, head), bf16),
            VMEM((seq_len, 3 * head), bf16),
            VMEM((seq_len, head), f32),
            VMEM((seq_len, head), f32),
            VMEM((rows, width), f32),
            VMEM((n // 2, rows, width), bf16),
            VMEM((2, n // 2, rows, width), bf16),
        ]
        + [VMEM((2,) + qkv_piece, bf16), VMEM((2,) + qkv_piece, bf16), VMEM(qkv_piece, bf16)]
        + [VMEM((n, shard, 3 * head), bf16)]
        + [VMEM((2,) + piece, bf16), VMEM((2,) + piece, bf16), VMEM(piece, bf16)]
        + [VMEM((2, n // 2, shard, width), bf16), DMA((7,)), DMA((8,))]
        + pair_sems()
        + seq_sems()
        + pair_sems()
        + seq_sems()
        + ring_sems()
        + grid_sum_sems()
        + pair_sems(),
        5,
    )
    return outs[:-1]


def ring_device(
    tokens, cotangent, gain_attn, w_query, w_key, w_value, w_out, gain_mlp, w_gate, w_up, w_down, pair_order, segments
):
    bf16, f32 = jnp.bfloat16, jnp.float32
    n = RING
    rows, width = tokens.shape[1], tokens.shape[2]
    seq_len = segments.shape[1]
    shard = w_query.shape[0]
    ff_own = w_down.shape[0]
    ff_mine = SEQ * ff_own
    head = HDIM
    outs = attention_stage(
        tokens, cotangent, gain_attn, w_query, w_key, w_value, w_out, gain_mlp, w_gate, w_up, w_down,
        pair_order, segments, ATTENTION_PLAN,
    )
    hidden, hhat, ob_local = outs[:3]
    where = outs[3:8]
    q, k, v, x_all, dy_all, wqkv_all, wout_all, wg_all, wu_own, wdown_all = outs[8:]
    wqkv_all = wqkv_all.reshape(width, 3 * head)
    wout_all = wout_all.reshape(H * head, width)
    wg_all = wg_all.reshape(width, ff_mine)
    wu_own = wu_own.reshape(n * shard, ff_mine)
    wdown_all = wdown_all.reshape(ff_mine, width)
    dweighted, out_sum, col_sum, down_sum = mlp_stage(hhat, dy_all, wg_all, wu_own, wdown_all, MLP_PLAN)
    output = (hidden + out_sum).astype(bf16)[None]

    grad_tokens, out_grad, qkv_raw, gate_raw, up_raw = backward_stage(
        (dweighted, hidden, cotangent[0], tokens[0], where[4], q, k, v, ob_local)
        + tuple(where[:4])
        + (x_all, wqkv_all, wout_all, col_sum),
        w_gate.shape, BACKWARD_PLAN,
    )
    gain_one = gain_attn.astype(f32)[:, None]
    gain_two = gain_mlp.astype(f32)[:, None]
    raw_q = qkv_raw[:, : H * head]
    raw_k = qkv_raw[:, H * head : (H + KVH) * head]
    raw_v = qkv_raw[:, (H + KVH) * head :]

    def gain_part(raw, w):
        return jnp.sum(raw.astype(f32) * w.astype(f32), axis=1)

    grad_gain_one = gain_part(raw_q, w_query) + gain_part(raw_k, w_key) + gain_part(raw_v, w_value)
    grad_gain_two = gain_part(gate_raw, w_gate) + gain_part(up_raw, w_up)
    return (
        output,
        grad_tokens[None],
        grad_gain_one,
        raw_q * gain_one,
        raw_k * gain_one,
        raw_v * gain_one,
        out_grad,
        grad_gain_two,
        gate_raw.astype(f32) * gain_two,
        up_raw.astype(f32) * gain_two,
        down_sum.astype(f32),
    )


def solution(mesh):
    placed = (
        P("seq", "ctx", None),
        P("seq", "ctx", None),
        P(("seq", "ctx")),
        P(("seq", "ctx"), None),
        P(("seq", "ctx"), None),
        P(("seq", "ctx"), None),
        P(("seq", "ctx"), None),
        P(("seq", "ctx")),
        P(("seq", "ctx"), None),
        P(("seq", "ctx"), None),
        P(("seq", "ctx"), None),
        P("seq", None),
        P("seq", None),
    )
    fits = mesh.shape["ctx"] == H and mesh.shape["seq"] == 4
    chosen = ring_device if fits else general_device
    return jax.shard_map(
        chosen,
        mesh=mesh,
        in_specs=placed,
        out_specs=(
            P("seq", "ctx", None),
            P("seq", "ctx", None),
            P(("seq", "ctx")),
            P(("seq", "ctx"), None),
            P(("seq", "ctx"), None),
            P(("seq", "ctx"), None),
            P(("seq", "ctx"), None),
            P(("seq", "ctx")),
            P(("seq", "ctx"), None),
            P(("seq", "ctx"), None),
            P(("seq", "ctx"), None),
        ),
        check_vma=False,
    )
```
